32 devices in a mesh: member: 2 (over y), domain: 4 (over z), role: 4 (over x, core).
Axes of the slice: x: 2, y: 2, z: 4, core: 2. Of those that a mesh axis runs over, the one named last changes fastest.
Arguments:
- ensemble: float32 [256, 32, 512], P('member', 'domain', 'role'), may hold values from -6 to 6
- diffusion: float32 [32, 512], P('domain', 'role'), may hold values from 0.02 to 0.1
- drift_rows: float32 [32, 512], P('domain', 'role'), may hold values from 0.05 to 0.3
- drift_cols: float32 [32, 512], P('domain', 'role'), may hold values from 0.05 to 0.3
- observed_cells: int32 [4, 1024], P('domain'), may hold values from 0 to 4095
- observed_count: int32 [4], P('domain'), may hold values from 256 to 1024
- observed_values: float32 [4, 1024], P('domain'), may hold values from -6 to 6
- observed_weights: float32 [4, 1024], P('domain'), may hold values from 0.5 to 4
Outputs:
- analysis: float32 [256, 32, 512], P('member', 'domain', 'role')
The draws below stay inside these ranges and needn't reach their ends.
All inputs are finite; a program needn't handle non-finite values.
Results may differ from the reference program's by a relative error of at most 0.0003.
Values sent between devices are 32-bit elements; how exact they have to be, the bound alone decides.
No kernel may reach another device: no remote copies, remote signals or barrier semaphores. Data moves between devices by JAX's collectives and lax.ppermute only.
A program may use at most 64 MiB of HBM per device.

```python
import math
import jax
import jax.numpy as jnp
import numpy as np
from jax import lax

ENSEMBLE_SIZE = 256
OBS_REG = 1024
STEPS = 4
ITERS = 6
CX = 8
REGIONS = 4
GRID_ROWS = 32
GRID_COLUMNS = 512
N_MEMBER = 2


def place_ends(array, own_key, smallest, top_value):
    shape = array.shape
    spot = [jax.random.randint(jax.random.fold_in(own_key, axis), (), 0, shape[axis]) for axis in range(len(shape))]
    array = array.at[tuple(spot)].set(smallest)
    longest = shape.index(max(shape))
    spot[longest] = (spot[longest] + 1) % shape[longest]
    return array.at[tuple(spot)].set(top_value)


def shard_levels(own_key, shape, pieces, least, top_value):
    level = 1.0
    for dim, blocks in pieces:
        heights = jax.random.uniform(jax.random.fold_in(jax.random.fold_in(own_key, 6), dim), (blocks,), jnp.float32, least / len(pieces), top_value / len(pieces))
        level = level * jnp.repeat(jnp.exp(heights), shape[dim] // blocks).reshape((-1,) + (1,) * (len(shape) - 1 - dim))
    return level


def rank_table(amount, skew):
    weights = [(1 << 20) // math.isqrt(grade ** skew) + 1 for grade in range(1, amount + 1)]
    scale = 1 + sum(weights) // (1 << 30)
    return np.cumsum(np.array([max(1, weight // scale) for weight in weights]))


def ranked_ids(own_key, shape, amount, lean):
    grid = rank_table(amount, lean)
    lot = jax.random.randint(jax.random.fold_in(own_key, 1), shape, 0, int(grid[amount - 1]))
    grade = jnp.searchsorted(jnp.asarray(grid, jnp.int32), lot, side="right")
    return jax.random.permutation(jax.random.fold_in(own_key, 2), amount)[grade].astype(jnp.int32)


def centred(rng, shape, scale, most, cuts=(), kind=jnp.bfloat16):
    loudness = shard_levels(rng, shape, cuts, -0.22, 0.18) if cuts else 1.0
    values = jax.random.normal(rng, shape, jnp.float32) * scale * loudness
    return jnp.minimum(jnp.maximum(values, -most), most).astype(kind)


def setup_inputs(seed: int = 0) -> dict:
    keys = jax.random.split(jax.random.key(seed), 9)
    ensemble = centred(keys[0], (ENSEMBLE_SIZE, GRID_ROWS, GRID_COLUMNS), 1.0, 6.0, ((0, 2), (1, 4), (2, 4)), jnp.float32)
    diffusion = jnp.clip(0.02 + 0.08 * jax.random.uniform(keys[1], (GRID_ROWS, GRID_COLUMNS), jnp.float32) ** shard_levels(keys[1], (GRID_ROWS, GRID_COLUMNS), ((0, 4), (1, 4)), -0.2, 0.2), 0.02, 0.1)
    drift_rows = jnp.clip(0.05 + 0.25 * jax.random.uniform(keys[2], (GRID_ROWS, GRID_COLUMNS), jnp.float32) ** shard_levels(keys[2], (GRID_ROWS, GRID_COLUMNS), ((0, 4), (1, 4)), -0.2, 0.2), 0.05, 0.3)
    drift_cols = jnp.clip(0.05 + 0.25 * jax.random.uniform(keys[3], (GRID_ROWS, GRID_COLUMNS), jnp.float32) ** shard_levels(keys[3], (GRID_ROWS, GRID_COLUMNS), ((0, 4), (1, 4)), -0.2, 0.2), 0.05, 0.3)
    observed_cells = place_ends(ranked_ids(keys[4], (REGIONS, OBS_REG), CX * GRID_COLUMNS, 2), jax.random.fold_in(keys[4], 3), 0, (CX * GRID_COLUMNS) - 1).astype(jnp.int32)
    observed_count = place_ends(jax.random.randint(keys[5], (REGIONS,), OBS_REG // 4, OBS_REG + 1), jax.random.fold_in(keys[5], 1), OBS_REG // 4, OBS_REG).astype(jnp.int32)
    observed_values = centred(keys[6], (REGIONS, OBS_REG), 1.0, 6.0, ((0, 4),), jnp.float32)
    observed_weights = jnp.clip(jnp.exp(math.log(4.0) - 2.0794415 * jax.random.uniform(keys[7], (REGIONS, OBS_REG), jnp.float32) ** shard_levels(keys[7], (REGIONS, OBS_REG), ((0, 4),), -0.2, 0.2)), 0.5, 4.0)
    return {"ensemble": ensemble, "diffusion": diffusion, "drift_rows": drift_rows, "drift_cols": drift_cols, "observed_cells": observed_cells, "observed_count": observed_count, "observed_values": observed_values, "observed_weights": observed_weights}


precise = lax.Precision.HIGHEST

def advance(values, diffusion, drift_rows, drift_cols):
    ahead_rows = jnp.roll(values, -1, 1)
    behind_rows = jnp.roll(values, 1, 1)
    ahead_cols = jnp.roll(values, -1, 2)
    behind_cols = jnp.roll(values, 1, 2)
    spread = ahead_rows + behind_rows + ahead_cols + behind_cols - 4.0 * values
    return values + diffusion * spread - drift_rows * (values - behind_rows) - drift_cols * (values - behind_cols)

def inverse_root(matrix):
    extent = matrix.shape[0]
    identity = jnp.eye(extent, dtype=jnp.float32)
    scaling = jnp.sqrt(jnp.sum(matrix * matrix))
    current = matrix / scaling
    inverse = identity
    for repeat in range(ITERS):
        middle = 0.5 * (3.0 * identity - jnp.dot(inverse, current, precision=precise))
        current = jnp.dot(current, middle, precision=precise)
        inverse = jnp.dot(middle, inverse, precision=precise)
    return (inverse, scaling)

def analysis_weights(gram_sum, innovation):
    extent = gram_sum.shape[0]
    matrix = gram_sum + (extent - 1.0) * jnp.eye(extent, dtype=jnp.float32)
    inverse, scaling = inverse_root(matrix)
    spread = jnp.sqrt((extent - 1.0) / scaling) * inverse
    shifted = jnp.dot(inverse, jnp.dot(inverse, innovation, precision=precise), precision=precise) / scaling
    return spread + shifted[:, None]

def stripe_analysis(stripe, cell_index, counts, values, weights):
    flattened = stripe.reshape(stripe.shape[0], -1)
    observed = jnp.take(flattened, cell_index, axis=1)
    centre_obs = lax.optimization_barrier(jnp.mean(observed, axis=0))
    deviation = observed - centre_obs
    usable = jnp.arange(cell_index.shape[0]) < counts
    weighted = deviation * jnp.where(usable, weights, jnp.float32(0.0))
    gram_sum = jnp.dot(weighted, deviation.T, precision=precise)
    innovation = jnp.dot(weighted, values - centre_obs, precision=precise)
    mixing = analysis_weights(gram_sum, innovation)
    centre = lax.optimization_barrier(jnp.mean(flattened, axis=0))
    updated = centre + jnp.dot(mixing.T, flattened - centre, precision=precise)
    return updated.reshape(stripe.shape)

def reference(ensemble, diffusion, drift_rows, drift_cols, observed_cells, observed_count, observed_values, observed_weights):
    partition_sets = ensemble.reshape(N_MEMBER, ENSEMBLE_SIZE // N_MEMBER, GRID_ROWS, GRID_COLUMNS)

    def predicted_fields(ensemble_states):
        for repeat in range(STEPS):
            ensemble_states = advance(ensemble_states, diffusion, drift_rows, drift_cols)
        return ensemble_states
    stepped_forward = lax.map(predicted_fields, partition_sets).reshape(ENSEMBLE_SIZE, GRID_ROWS, GRID_COLUMNS)

    def analyse(region):
        stripe = lax.dynamic_slice_in_dim(stepped_forward, (region * CX).astype(jnp.int32), CX, 1)
        return stripe_analysis(stripe, observed_cells[region], observed_count[region], observed_values[region], observed_weights[region])
    result = lax.map(analyse, jnp.arange(REGIONS, dtype=jnp.int32))
    return jnp.transpose(result, (1, 0, 2, 3)).reshape(ENSEMBLE_SIZE, GRID_ROWS, GRID_COLUMNS)
```

```python
import functools

import jax
import jax.numpy as jnp
from jax import lax
from jax.experimental import pallas as pl
from jax.experimental.pallas import tpu as pltpu
from jax.sharding import PartitionSpec as P

STEPS = 4
ITERS = 6
LEAD = 16


VMEM = pl.BlockSpec(memory_space=pltpu.VMEM)


def struct(*shape, kind=jnp.float32):
    return jax.ShapeDtypeStruct(shape, kind)


def call(body, outs, *args, scratch=(), name=None):
    return pl.pallas_call(
        body,
        out_shape=outs,
        in_specs=[VMEM] * len(args),
        out_specs=jax.tree.map(lambda _: VMEM, outs),
        scratch_shapes=scratch,
        name=name,
    )(*args)


def halves(value):
    upper = value.astype(jnp.bfloat16)
    lower = (value - upper.astype(jnp.float32)).astype(jnp.bfloat16)
    return upper, lower


def dot(a, b, dims=((1,), (0,))):
    return lax.dot_general(a, b, (dims, ((), ())), preferred_element_type=jnp.float32)


def dot3(a, b, dims=((1,), (0,))):
    return dot(a[0], b[0], dims) + (dot(a[0], b[1], dims) + dot(a[1], b[0], dims))


def loop(count, body):
    if count <= 8:
        for i in range(count):
            body(i)
    else:
        lax.fori_loop(0, count, lambda i, c: (body(i), c)[1], 0)


def pack_kernel(ens, field, top, bottom, left, right, tl, tr, bl, br):
    _, rows, cols = ens.shape
    width = STEPS

    def row(r):
        turned = ens[:, r, :].T
        field[r] = turned
        return turned

    for r in range(width):
        turned = row(r)
        top[r] = turned
        tl[r * width : (r + 1) * width] = turned[:width]
        tr[r * width : (r + 1) * width] = turned[cols - width :]
        left[r * width : (r + 1) * width] = turned[:width]
        right[r * width : (r + 1) * width] = turned[cols - width :]
    for r in range(width, rows):
        turned = row(r)
        left[r * width : (r + 1) * width] = turned[:width]
        right[r * width : (r + 1) * width] = turned[cols - width :]
    for i in range(width):
        r = rows - width + i
        turned = field[r]
        bottom[i] = turned
        bl[i * width : (i + 1) * width] = turned[:width]
        br[i * width : (i + 1) * width] = turned[cols - width :]


def coefficient_kernel(source, spread):
    _, rows, cols, members = spread.shape
    for r in range(1, rows - 1):
        diffusion = jnp.broadcast_to(source[0][:, r : r + 1], (cols, members))
        drift_rows = jnp.broadcast_to(source[1][:, r : r + 1], (cols, members))
        drift_cols = jnp.broadcast_to(source[2][:, r : r + 1], (cols, members))
        spread[0, r] = 1.0 - 4.0 * diffusion - drift_rows - drift_cols
        spread[1, r] = diffusion
        spread[2, r] = diffusion + drift_rows
        spread[3, r] = diffusion + drift_cols


def forecast_kernel(
    field, above, below, left, right, nw, ne, sw, se, spread, out, even, odd
):
    rows, cols, members = field.shape
    width = STEPS
    own = pl.ds(LEAD, cols)
    before = pl.ds(LEAD - width, width)
    after = pl.ds(LEAD + cols, width)
    for i in range(width):
        part = slice(i * width, (i + 1) * width)
        even[i, own] = above[i]
        even[i, before] = nw[part]
        even[i, after] = ne[part]
        j = width + rows + i
        even[j, own] = below[i]
        even[j, before] = sw[part]
        even[j, after] = se[part]
    for r in range(rows):
        part = slice(r * width, (r + 1) * width)
        even[width + r, own] = field[r]
        even[width + r, before] = left[part]
        even[width + r, after] = right[part]
    span = cols + 16
    start = LEAD - 8
    source, target = even, odd
    for step in range(1, STEPS + 1):
        last = step == STEPS
        at, size = (LEAD, cols) if last else (start, span)
        here = pl.ds(at, size)

        def advance(r, source=source, target=target, at=at, size=size, here=here, last=last):
            value = (
                spread[0, r, here] * source[r, here]
                + spread[1, r, here] * (source[r + 1, here] + source[r, pl.ds(at + 1, size)])
                + spread[2, r, here] * source[r - 1, here]
                + spread[3, r, here] * source[r, pl.ds(at - 1, size)]
            )
            if last:
                out[r - width] = value
            else:
                target[r, here] = value

        lax.fori_loop(
            step, rows + 2 * width - step, lambda r, c, f=advance: (f(r), c)[1], 0
        )
        source, target = target, source


def weight_kernel(row_of, col_of, plain, valued, out):
    cols, twice = out.shape
    rows = twice // 2
    slots = row_of.shape[1]
    here = lax.broadcasted_iota(jnp.int32, (cols, slots), 0) == col_of[...]
    here = jnp.where(here, 1.0, 0.0).astype(jnp.bfloat16)
    line = lax.broadcasted_iota(jnp.int32, (rows, slots), 0) == row_of[...]
    value = jnp.concatenate(
        [jnp.where(line, plain[...], 0.0), jnp.where(line, valued[...], 0.0)], axis=0
    )
    total = jnp.zeros((cols, twice), jnp.float32)
    for piece in range(3):
        part = value.astype(jnp.bfloat16)
        value = value - part.astype(jnp.float32)
        total = total + dot(here, part, ((1,), (1,)))
    out[...] = total


def gram_kernel(groups, own, others, weight, gram, upper, lower, centre, total):
    rows, cols, _ = own.shape
    members = total.shape[0]
    total[...] = jnp.zeros_like(total)
    pull = gram.shape[0] - 8

    def line(r, innovation):
        parts = [own[r]] + [others[g * rows + r] for g in range(groups - 1)]
        value = jnp.concatenate(parts, axis=1) if groups > 1 else parts[0]
        mean = jnp.sum(value, axis=1, keepdims=True) * (1.0 / members)
        deviation = value - mean
        picked = jnp.where(
            lax.broadcasted_iota(jnp.int32, weight.shape, 1) == r, weight[...], 0.0
        )
        plain = jnp.sum(picked, axis=1, keepdims=True)
        picked = jnp.where(
            lax.broadcasted_iota(jnp.int32, weight.shape, 1) == r + rows, weight[...], 0.0
        )
        valued = jnp.sum(picked, axis=1, keepdims=True)
        centre[r] = jnp.broadcast_to(mean, (cols, centre.shape[2]))
        high, low = halves(deviation)
        at = pl.ds(r * cols, cols)
        upper[at] = high
        lower[at] = low
        turned = (deviation * plain).T
        total[...] += dot3(halves(turned), (high, low))
        return innovation + jnp.sum(
            deviation * (valued - plain * mean), axis=0, keepdims=True
        )

    innovation = jnp.zeros((1, members), jnp.float32)
    if rows <= 8:
        for r in range(rows):
            innovation = line(r, innovation)
    else:
        innovation = lax.fori_loop(0, rows, line, innovation)
    blocks = members // 128
    at = 0
    gram[pl.ds(pull, 8)] = jnp.zeros((8, 128), jnp.float32)
    for i in range(blocks):
        gram[pl.ds(pull + i, 1)] = innovation[:, i * 128 : (i + 1) * 128]
        for j in range(i, blocks):
            gram[pl.ds(at, 128)] = total[i * 128 : (i + 1) * 128, j * 128 : (j + 1) * 128]
            at += 128


def analysis_kernel(first, second, upper, lower, centre, out, whole, chosen):
    local, rows, cols = out.shape
    members = whole.shape[0]
    blocks = members // 128
    pull = first.shape[0] - 8
    at = 0
    for i in range(blocks):
        for j in range(i, blocks):
            block = first[pl.ds(at, 128)] + second[pl.ds(at, 128)]
            whole[i * 128 : (i + 1) * 128, j * 128 : (j + 1) * 128] = block
            if j > i:
                whole[j * 128 : (j + 1) * 128, i * 128 : (i + 1) * 128] = block.T
            at += 128
    innovation = jnp.concatenate(
        [first[pl.ds(pull + i, 1)] + second[pl.ds(pull + i, 1)] for i in range(blocks)],
        axis=1,
    )
    down = lax.broadcasted_iota(jnp.int32, (members, members), 0)
    across = lax.broadcasted_iota(jnp.int32, (members, members), 1)
    identity = jnp.where(down == across, 1.0, 0.0)
    matrix = whole[...] + (members - 1.0) * identity
    squares = jnp.sum(jnp.sum(matrix * matrix, axis=1, keepdims=True), axis=0, keepdims=True)
    scaling = jnp.sqrt(squares)
    current = matrix * (1.0 / scaling)
    middle = 1.5 * identity - 0.5 * current
    inverse = middle
    current = dot3(halves(current), halves(middle))
    for repeat in range(1, ITERS):
        inverse_parts = halves(inverse)
        current_parts = halves(current)
        middle = 1.5 * identity - 0.5 * dot3(inverse_parts, current_parts)
        middle_parts = halves(middle)
        if repeat < ITERS - 1:
            current = dot3(current_parts, middle_parts)
        inverse = dot3(middle_parts, inverse_parts)
    once = jnp.sum(inverse * innovation, axis=1, keepdims=True)
    once_row = jnp.sum(jnp.where(down == across, once, 0.0), axis=0, keepdims=True)
    shifted = jnp.sum(inverse * once_row, axis=1, keepdims=True) * (1.0 / scaling)
    factor = jnp.sqrt((members - 1.0) / scaling)
    mixing = (factor * inverse + shifted)[:, :local]
    high, low = halves(mixing)
    chosen[0] = high
    chosen[1] = low

    def line(r):
        at = pl.ds(r * cols, cols)
        value = dot(upper[at], chosen[0]) + (dot(upper[at], chosen[1]) + dot(lower[at], chosen[0]))
        out[:, r, :] = (value + centre[r]).T

    loop(rows, line)


def shift(value, axes, *moves):
    sizes = [lax.axis_size(a) for a in axes]
    pairs = []
    total = 1
    for s in sizes:
        total *= s
    for flat in range(total):
        rest, place = flat, []
        for s in reversed(sizes):
            place.append(rest % s)
            rest //= s
        place = place[::-1]
        to = 0
        for s, p, m in zip(sizes, place, moves):
            to = to * s + (p + m) % s
        pairs.append((flat, to))
    return lax.ppermute(value, axes if len(axes) > 1 else axes[0], pairs)


def extended(value, sides, width):
    for axis, dim in sides:
        length = value.shape[dim]
        before = shift(lax.slice_in_dim(value, length - width, length, axis=dim), (axis,), 1)
        after = shift(lax.slice_in_dim(value, 0, width, axis=dim), (axis,), -1)
        value = jnp.concatenate([before, value, after], axis=dim)
    return value


def role_sum(value):
    size = lax.axis_size("role")
    if size & (size - 1) or size == 1:
        return lax.psum(value, "role"), jnp.zeros_like(value)
    other = jnp.zeros_like(value)
    step = 1
    while step < size:
        if step > 1:
            value = value + other
        other = lax.ppermute(value, "role", [(i, i ^ step) for i in range(size)])
        step *= 2
    return value, other


def shards(
    ensemble,
    diffusion,
    drift_rows,
    drift_cols,
    observed_cells,
    observed_count,
    observed_values,
    observed_weights,
):
    groups = lax.axis_size("member")
    roles = lax.axis_size("role")
    local, rows, cols = ensemble.shape
    members = local * groups
    width = STEPS
    edge = struct(rows * width, local)
    corner = struct(width * width, local)
    strip = struct(width, cols, local)
    field, top, bottom, left, right, tl, tr, bl, br = call(
        pack_kernel,
        (struct(rows, cols, local), strip, strip, edge, edge, corner, corner, corner, corner),
        ensemble,
        name="pack",
    )
    z, x, zx = ("domain",), ("role",), ("domain", "role")
    above = shift(bottom, z, 1)
    below = shift(top, z, -1)
    left_halo = shift(right, x, 1)
    right_halo = shift(left, x, -1)
    nw = shift(br, zx, 1, 1)
    ne = shift(bl, zx, 1, -1)
    sw = shift(tr, zx, -1, 1)
    se = shift(tl, zx, -1, -1)

    coefficients = jnp.stack([diffusion, drift_rows, drift_cols])
    coefficients = extended(coefficients, (("role", 2), ("domain", 1)), width)
    coefficients = jnp.transpose(coefficients, (0, 2, 1))
    coefficients = jnp.pad(coefficients, ((0, 0), (LEAD - width, LEAD - width), (0, 0)))
    spread = call(
        coefficient_kernel,
        struct(4, rows + 2 * width, cols + 2 * LEAD, local),
        coefficients,
        name="coefficients",
    )

    full_cols = cols * roles
    row_of = observed_cells // full_cols
    col_of = observed_cells % full_cols - lax.axis_index("role") * cols
    slot = lax.broadcasted_iota(jnp.int32, observed_cells.shape, 1)
    plain = jnp.where(slot < observed_count[0], observed_weights, 0.0)
    weight = call(
        weight_kernel,
        struct(cols, 2 * rows),
        row_of,
        col_of,
        plain,
        plain * observed_values,
        name="weights",
    )

    padded = pltpu.VMEM((rows + 2 * width, cols + 2 * LEAD, local), jnp.float32)
    forecast = call(
        forecast_kernel,
        struct(rows, cols, local),
        field,
        above,
        below,
        left_halo,
        right_halo,
        nw,
        ne,
        sw,
        se,
        spread,
        scratch=(padded, padded),
        name="forecast",
    )
    others = [shift(forecast, ("member",), s) for s in range(1, groups)]
    others = jnp.concatenate(others, axis=0) if len(others) > 1 else others[0]

    blocks = members // 128
    size = blocks * (blocks + 1) // 2 * 128 + 8
    gram, upper, lower, centre = call(
        functools.partial(gram_kernel, groups),
        (
            struct(size, 128),
            struct(rows * cols, members, kind=jnp.bfloat16),
            struct(rows * cols, members, kind=jnp.bfloat16),
            struct(rows, cols, local),
        ),
        forecast,
        others,
        weight,
        scratch=(pltpu.VMEM((members, members), jnp.float32),),
        name="gram",
    )
    first, second = role_sum(gram)
    return call(
        analysis_kernel,
        struct(local, rows, cols),
        first,
        second,
        upper,
        lower,
        centre,
        scratch=(
            pltpu.VMEM((members, members), jnp.float32),
            pltpu.VMEM((2, members, local), jnp.bfloat16),
        ),
        name="analysis",
    )


def solution(mesh):
    placed = (
        P("member", "domain", "role"),
        P("domain", "role"),
        P("domain", "role"),
        P("domain", "role"),
        P("domain", None),
        P("domain"),
        P("domain", None),
        P("domain", None),
    )
    return jax.shard_map(
        shards, mesh=mesh, in_specs=placed, out_specs=P("member", "domain", "role"), check_vma=False
    )
```

```python
import functools

import jax
import jax.numpy as jnp
from jax import lax
from jax.experimental import pallas as pl
from jax.experimental.pallas import tpu as pltpu
from jax.sharding import PartitionSpec as P

STEPS = 4
ITERS = 6
LEAD = 16


VMEM = pl.BlockSpec(memory_space=pltpu.VMEM)
SMEM = pl.BlockSpec(memory_space=pltpu.SMEM)
ROOM = 3 << 20


def struct(*shape, kind=jnp.float32):
    return jax.ShapeDtypeStruct(shape, kind)


def near(shape, kind):
    size = jnp.dtype(kind).itemsize
    for place, extent in enumerate(shape[::-1]):
        unit = (128, 32 // jnp.dtype(kind).itemsize, 1)[min(place, 2)]
        size *= -(-extent // unit) * unit
    return size <= ROOM


def call(body, outs, *args, scratch=(), name=None, scalars=0, raw=0, result=False):
    placed = list(args[: scalars + raw])
    for value in args[scalars + raw :]:
        if near(value.shape, value.dtype):
            value = pltpu.with_memory_space_constraint(value, pltpu.VMEM)
        placed.append(value)
    if not result:
        outs = jax.tree.map(
            lambda s: pltpu.VMEM(s.shape, s.dtype) if near(s.shape, s.dtype) else s, outs
        )
    return pl.pallas_call(
        body,
        out_shape=outs,
        in_specs=[SMEM] * scalars + [VMEM] * (len(args) - scalars),
        out_specs=tuple(VMEM for _ in outs) if isinstance(outs, tuple) else VMEM,
        scratch_shapes=scratch,
        name=name,
    )(*placed)


def halves(value):
    upper = value.astype(jnp.bfloat16)
    lower = (value - upper.astype(jnp.float32)).astype(jnp.bfloat16)
    return upper, lower


def dot(a, b, dims=((1,), (0,))):
    return lax.dot_general(a, b, (dims, ((), ())), preferred_element_type=jnp.float32)


def dot3(a, b, dims=((1,), (0,))):
    return dot(a[0], b[0], dims) + (dot(a[0], b[1], dims) + dot(a[1], b[0], dims))


def loop(count, body):
    if count <= 16:
        for i in range(count):
            body(i)
    else:
        lax.fori_loop(0, count, lambda i, c: (body(i), c)[1], 0)


def pack_kernel(ens, diffusion, drift_rows, drift_cols, field, kept, top, bottom, left, right):
    _, rows, cols = ens.shape
    members = field.shape[2]
    width = STEPS
    lanes = pl.ds(0, members)
    for r in range(rows):
        turned = ens[:, r, :].T
        field[r] = turned
        part = pl.ds(r * width, width)
        left[part, lanes] = turned[:width]
        right[part, lanes] = turned[cols - width :]
        if r < width:
            top[pl.ds(r * cols, cols), lanes] = turned
        if r >= rows - width:
            bottom[pl.ds((r - rows + width) * cols, cols), lanes] = turned
    near_edge = jnp.zeros((rows, cols), jnp.float32)
    far_edge = near_edge
    lane = lax.broadcasted_iota(jnp.int32, (rows, cols), 1)
    for k, part in enumerate((diffusion, drift_rows, drift_cols)):
        at = pl.ds(width * cols + k * width, width)
        top[at, pl.ds(0, cols)] = part[:width]
        bottom[at, pl.ds(0, cols)] = part[rows - width :]
        value = part[...]
        kept[k] = value
        mine = (lane >= k * width) & (lane < (k + 1) * width)
        if k:
            near_edge = jnp.where(mine, pltpu.roll(value, k * width, 1), near_edge)
        else:
            near_edge = jnp.where(mine, value, near_edge)
        far_edge = jnp.where(mine, pltpu.roll(value, (k + 1) * width, 1), far_edge)
    left[pl.ds(rows * width, rows), pl.ds(0, cols)] = near_edge
    right[pl.ds(rows * width, rows), pl.ds(0, cols)] = far_edge


def turn_kernel(rows, left, right, up, down):
    width = STEPS
    area = width * width
    for i, side in enumerate((left, right)):
        up[pl.ds(i * area, area)] = side[pl.ds(0, area)]
        down[pl.ds(i * area, area)] = side[pl.ds((rows - width) * width, area)]
        at = pl.ds(2 * area + i * width, width)
        up[at] = side[pl.ds(rows * width, width)]
        down[at] = side[pl.ds(rows * width + rows - width, width)]


def widen(line, write, parts, left, right, members):
    cols = parts[0].shape[0]
    width = STEPS
    pieces = []
    for k in range(3):
        at = slice(k * width, (k + 1) * width)
        pieces.append(
            (
                (LEAD - width, left[at, line : line + 1], width),
                (LEAD, parts[k][:, line : line + 1], cols),
                (LEAD + cols, right[at, line : line + 1], width),
            )
        )
    for (at, a, size), (_, b, _), (_, c, _) in zip(*pieces):
        diffusion = jnp.broadcast_to(a, (size, members))
        rowwise = jnp.broadcast_to(b, (size, members))
        colwise = jnp.broadcast_to(c, (size, members))
        here = pl.ds(at, size)
        write(0, here, 1.0 - 4.0 * diffusion - rowwise - colwise)
        write(1, here, diffusion)
        write(2, here, diffusion + rowwise)
        write(3, here, diffusion + colwise)


def forecast_kernel(
    field,
    kept,
    above,
    below,
    left,
    right,
    corner_above,
    corner_below,
    out,
    even,
    odd,
    spread,
    stage,
):
    rows, cols, members = field.shape
    width = STEPS
    area = width * width
    lanes = pl.ds(0, members)
    own = pl.ds(LEAD, cols)
    before = pl.ds(LEAD - width, width)
    after = pl.ds(LEAD + cols, width)
    for i, (strip, corner) in enumerate(((above, corner_above), (below, corner_below))):
        at = pl.ds(i * width, width)
        for k in range(3):
            stage[k, at] = strip[pl.ds(width * cols + k * width, width), pl.ds(0, cols)]
        for side in range(2):
            stage[3 + side, at] = corner[pl.ds(2 * area + side * width, width), pl.ds(0, cols)]
    def fill(parts, near_part, far_part, lines):
        for line, row in lines:

            def write(k, here, value, row=row):
                spread[k, row, here] = value

            widen(line, write, parts, near_part, far_part, members)

    turned = [stage[k].T for k in range(5)]
    lines = [(i, i) for i in range(1, width)]
    lines += [(width + i, width + rows + i) for i in range(width - 1)]
    fill(turned[:3], turned[3], turned[4], lines)
    edge = pl.ds(rows * width, rows), pl.ds(0, cols)
    parts = [kept[k].T for k in range(3)]
    fill(parts, left[edge].T, right[edge].T, [(r, width + r) for r in range(rows)])
    for i in range(width):
        part = pl.ds(i * cols, cols)
        near_part, far_part = pl.ds(i * width, width), pl.ds(area + i * width, width)
        for j, strip, corner in (
            (i, above, corner_above),
            (width + rows + i, below, corner_below),
        ):
            even[j, own] = strip[part, lanes]
            even[j, before] = corner[near_part, lanes]
            even[j, after] = corner[far_part, lanes]
    for r in range(rows):
        part = pl.ds(r * width, width)
        even[width + r, own] = field[r]
        even[width + r, before] = left[part, lanes]
        even[width + r, after] = right[part, lanes]
    span = cols + 16
    source, target = even, odd
    for step in range(1, STEPS + 1):
        last = step == STEPS
        at, size = (LEAD, cols) if last else (LEAD - 8, span)
        here = pl.ds(at, size)

        def advance(r):
            value = (
                spread[0, r, here] * source[r, here]
                + spread[1, r, here] * (source[r + 1, here] + source[r, pl.ds(at + 1, size)])
                + spread[2, r, here] * source[r - 1, here]
                + spread[3, r, here] * source[r, pl.ds(at - 1, size)]
            )
            if last:
                out[r - width] = value
            else:
                target[r, here] = value

        loop(rows + 2 * width - 2 * step, lambda i: advance(i + step))
        source, target = target, source


def weight_kernel(axis, count, cells, values, weights, out):
    cols, twice = out.shape
    rows = twice // 2
    slots = cells.shape[1]
    full = cols * lax.axis_size(axis)
    cell = cells[...]
    if full & (full - 1):
        row_of = lax.div(cell, full)
    else:
        row_of = lax.shift_right_logical(cell, full.bit_length() - 1)
    col_of = cell - row_of * full - lax.axis_index(axis) * cols
    slot = lax.broadcasted_iota(jnp.int32, (1, slots), 1)
    plain = jnp.where(slot < count[0], weights[...], 0.0)
    valued = plain * values[...]
    here = lax.broadcasted_iota(jnp.int32, (cols, slots), 0) == col_of
    here = jnp.where(here, 1.0, 0.0).astype(jnp.bfloat16)
    line = lax.broadcasted_iota(jnp.int32, (rows, slots), 0) == row_of
    value = jnp.concatenate([jnp.where(line, plain, 0.0), jnp.where(line, valued, 0.0)], axis=0)
    total = jnp.zeros((cols, twice), jnp.float32)
    for piece in range(3):
        part = value.astype(jnp.bfloat16)
        value = value - part.astype(jnp.float32)
        total = total + dot(here, part, ((1,), (1,)))
    out[...] = total


def gram_kernel(groups, own, others, weight, gram, upper, lower, centre, total):
    rows, cols, _ = own.shape
    members = total.shape[0]
    total[...] = jnp.zeros_like(total)
    pull = gram.shape[0] - 8
    diagonal = lax.broadcasted_iota(jnp.int32, (cols, cols), 0) == lax.broadcasted_iota(
        jnp.int32, (cols, cols), 1
    )

    def line(r, innovation):
        parts = [own[r]] + [others[g * rows + r] for g in range(groups - 1)]
        value = jnp.concatenate(parts, axis=1) if groups > 1 else parts[0]
        mean = jnp.sum(value, axis=1, keepdims=True) * (1.0 / members)
        deviation = value - mean
        picked = jnp.where(
            lax.broadcasted_iota(jnp.int32, weight.shape, 1) == r, weight[...], 0.0
        )
        plain = jnp.sum(picked, axis=1, keepdims=True)
        picked = jnp.where(
            lax.broadcasted_iota(jnp.int32, weight.shape, 1) == r + rows, weight[...], 0.0
        )
        valued = jnp.sum(picked, axis=1, keepdims=True)
        centre[pl.ds(r, 1)] = jnp.sum(jnp.where(diagonal, mean, 0.0), axis=0, keepdims=True)
        high, low = halves(deviation)
        at = pl.ds(r * cols, cols)
        upper[at] = high
        lower[at] = low
        turned = (deviation * plain).T
        total[...] += dot3(halves(turned), (high, low))
        return innovation + jnp.sum(
            deviation * (valued - plain * mean), axis=0, keepdims=True
        )

    innovation = jnp.zeros((1, members), jnp.float32)
    if rows <= 8:
        for r in range(rows):
            innovation = line(r, innovation)
    else:
        innovation = lax.fori_loop(0, rows, line, innovation)
    blocks = members // 128
    at = 0
    gram[pl.ds(pull, 8)] = jnp.zeros((8, 128), jnp.float32)
    for i in range(blocks):
        gram[pl.ds(pull + i, 1)] = innovation[:, i * 128 : (i + 1) * 128]
        for j in range(i, blocks):
            gram[pl.ds(at, 128)] = total[i * 128 : (i + 1) * 128, j * 128 : (j + 1) * 128]
            at += 128


def analysis_kernel(first, second, upper, lower, centre, out, whole, chosen):
    local, rows, cols = out.shape
    members = whole.shape[0]
    blocks = members // 128
    pull = first.shape[0] - 8
    at = 0
    for i in range(blocks):
        for j in range(i, blocks):
            block = first[pl.ds(at, 128)] + second[pl.ds(at, 128)]
            whole[i * 128 : (i + 1) * 128, j * 128 : (j + 1) * 128] = block
            if j > i:
                whole[j * 128 : (j + 1) * 128, i * 128 : (i + 1) * 128] = block.T
            at += 128
    innovation = jnp.concatenate(
        [first[pl.ds(pull + i, 1)] + second[pl.ds(pull + i, 1)] for i in range(blocks)],
        axis=1,
    )
    down = lax.broadcasted_iota(jnp.int32, (members, members), 0)
    across = lax.broadcasted_iota(jnp.int32, (members, members), 1)
    identity = jnp.where(down == across, 1.0, 0.0)
    matrix = whole[...] + (members - 1.0) * identity
    squares = jnp.sum(jnp.sum(matrix * matrix, axis=1, keepdims=True), axis=0, keepdims=True)
    scaling = jnp.sqrt(squares)
    current = matrix * (1.0 / scaling)
    middle = 1.5 * identity - 0.5 * current
    inverse = middle
    current = dot3(halves(current), halves(middle))
    for repeat in range(1, ITERS):
        current_parts = halves(current)
        inverse_parts = halves(inverse)
        middle = 1.5 * identity - 0.5 * dot3(inverse_parts, current_parts)
        middle_parts = halves(middle)
        if repeat < ITERS - 1:
            current = dot3(current_parts, middle_parts)
        inverse = dot3(inverse_parts, middle_parts)
    once = jnp.sum(inverse * innovation, axis=1, keepdims=True)
    once_row = jnp.sum(jnp.where(down == across, once, 0.0), axis=0, keepdims=True)
    shifted = jnp.sum(inverse * once_row, axis=1, keepdims=True) * (1.0 / scaling)
    factor = jnp.sqrt((members - 1.0) / scaling)
    mixing = (factor * inverse + shifted)[:, :local]
    high, low = halves(mixing)
    chosen[0] = high
    chosen[1] = low

    def line(r):
        at = pl.ds(r * cols, cols)
        value = dot(upper[at], chosen[0]) + (dot(upper[at], chosen[1]) + dot(lower[at], chosen[0]))
        out[:, r, :] = value.T + centre[pl.ds(r, 1)]

    loop(rows, line)


def shift(value, axes, *moves):
    sizes = [lax.axis_size(a) for a in axes]
    pairs = []
    total = 1
    for s in sizes:
        total *= s
    for flat in range(total):
        rest, place = flat, []
        for s in reversed(sizes):
            place.append(rest % s)
            rest //= s
        place = place[::-1]
        to = 0
        for s, p, m in zip(sizes, place, moves):
            to = to * s + (p + m) % s
        pairs.append((flat, to))
    return lax.ppermute(value, axes if len(axes) > 1 else axes[0], pairs)


def role_sum(value):
    size = lax.axis_size("role")
    if size & (size - 1) or size == 1:
        return lax.psum(value, "role"), jnp.zeros_like(value)
    other = jnp.zeros_like(value)
    step = 1
    while step < size:
        if step > 1:
            value = value + other
        other = lax.ppermute(value, "role", [(i, i ^ step) for i in range(size)])
        step *= 2
    return value, other


def shards(
    ensemble,
    diffusion,
    drift_rows,
    drift_cols,
    observed_cells,
    observed_count,
    observed_values,
    observed_weights,
):
    groups = lax.axis_size("member")
    roles = lax.axis_size("role")
    local, rows, cols = ensemble.shape
    members = local * groups
    width = STEPS
    lanes = max(local, cols)
    strip = struct(width * cols + 4 * width, lanes)
    edge = struct(rows * width + rows, lanes)
    corner = struct(2 * width * width + 2 * width, lanes)
    field, kept, top, bottom, left, right = call(
        pack_kernel,
        (struct(rows, cols, local), struct(3, rows, cols), strip, strip, edge, edge),
        ensemble,
        diffusion,
        drift_rows,
        drift_cols,
        name="pack",
        raw=4,
    )
    z, x = ("domain",), ("role",)
    above = shift(bottom, z, 1)
    below = shift(top, z, -1)
    left, right = shift(right, x, 1), shift(left, x, -1)
    up, down = call(
        functools.partial(turn_kernel, rows), (corner, corner), left, right, name="turn"
    )
    corner_above = shift(down, z, 1)
    corner_below = shift(up, z, -1)
    weight = call(
        functools.partial(weight_kernel, "role"),
        struct(cols, 2 * rows),
        observed_count,
        observed_cells,
        observed_values,
        observed_weights,
        scalars=1,
        raw=3,
        name="weights",
    )
    padded = pltpu.VMEM((rows + 2 * width, cols + 2 * LEAD, local), jnp.float32)
    forecast = call(
        forecast_kernel,
        struct(rows, cols, local),
        field,
        kept,
        above,
        below,
        left,
        right,
        corner_above,
        corner_below,
        scratch=(
            padded,
            padded,
            pltpu.VMEM((4, rows + 2 * width, cols + 2 * LEAD, local), jnp.float32),
            pltpu.VMEM((5, 2 * width, cols), jnp.float32),
        ),
        name="forecast",
    )
    others = [shift(forecast, ("member",), s) for s in range(1, groups)]
    others = jnp.concatenate(others, axis=0) if len(others) > 1 else others[0]

    blocks = members // 128
    size = blocks * (blocks + 1) // 2 * 128 + 8
    gram, upper, lower, centre = call(
        functools.partial(gram_kernel, groups),
        (
            struct(size, 128),
            struct(rows * cols, members, kind=jnp.bfloat16),
            struct(rows * cols, members, kind=jnp.bfloat16),
            struct(rows, cols),
        ),
        forecast,
        others,
        weight,
        scratch=(pltpu.VMEM((members, members), jnp.float32),),
        name="gram",
    )
    first, second = role_sum(gram)
    return call(
        analysis_kernel,
        struct(local, rows, cols),
        first,
        second,
        upper,
        lower,
        centre,
        scratch=(
            pltpu.VMEM((members, members), jnp.float32),
            pltpu.VMEM((2, members, local), jnp.bfloat16),
        ),
        name="analysis",
        result=True,
    )


def solution(mesh):
    placed = (
        P("member", "domain", "role"),
        P("domain", "role"),
        P("domain", "role"),
        P("domain", "role"),
        P("domain", None),
        P("domain"),
        P("domain", None),
        P("domain", None),
    )
    return jax.shard_map(
        shards, mesh=mesh, in_specs=placed, out_specs=P("member", "domain", "role"), check_vma=False
    )
```

```python
import functools

import jax
import jax.numpy as jnp
from jax import lax
from jax.experimental import pallas as pl
from jax.experimental.pallas import tpu as pltpu
from jax.sharding import PartitionSpec as P

STEPS = 4
ITERS = 6
LEAD = 16


VMEM = pl.BlockSpec(memory_space=pltpu.VMEM)
SMEM = pl.BlockSpec(memory_space=pltpu.SMEM)
ROOM = 1 << 20


def struct(*shape, kind=jnp.float32):
    return jax.ShapeDtypeStruct(shape, kind)


def near(shape, kind):
    size = jnp.dtype(kind).itemsize
    for place, extent in enumerate(shape[::-1]):
        unit = (128, 32 // jnp.dtype(kind).itemsize, 1)[min(place, 2)]
        size *= -(-extent // unit) * unit
    return size <= ROOM


def call(body, outs, *args, scratch=(), name=None, scalars=0, raw=0, result=False):
    placed = list(args[: scalars + raw])
    for value in args[scalars + raw :]:
        if near(value.shape, value.dtype):
            value = pltpu.with_memory_space_constraint(value, pltpu.VMEM)
        placed.append(value)
    if not result:
        outs = jax.tree.map(
            lambda s: pltpu.VMEM(s.shape, s.dtype) if near(s.shape, s.dtype) else s, outs
        )
    return pl.pallas_call(
        body,
        out_shape=outs,
        in_specs=[SMEM] * scalars + [VMEM] * (len(args) - scalars),
        out_specs=tuple(VMEM for _ in outs) if isinstance(outs, tuple) else VMEM,
        scratch_shapes=scratch,
        name=name,
    )(*placed)


def halves(value):
    upper = value.astype(jnp.bfloat16)
    lower = (value - upper.astype(jnp.float32)).astype(jnp.bfloat16)
    return upper, lower


def dot(a, b, dims=((1,), (0,))):
    return lax.dot_general(a, b, (dims, ((), ())), preferred_element_type=jnp.float32)


def dot3(a, b, dims=((1,), (0,))):
    return dot(a[0], b[0], dims) + (dot(a[0], b[1], dims) + dot(a[1], b[0], dims))


def loop(count, body):
    if count <= 16:
        for i in range(count):
            body(i)
    else:
        lax.fori_loop(0, count, lambda i, c: (body(i), c)[1], 0)


def parted(cols):
    cut = (cols // 2 + 16) // 8 * 8
    return cut, 8, cut - 8


def pack_kernel(ens, diffusion, drift_rows, drift_cols, field, kept, top, bottom, left, right):
    _, rows, cols = ens.shape
    members = field.shape[2]
    width = STEPS
    cut = parted(cols)[0]
    lanes = pl.ds(0, members)
    for r in range(rows):
        turned = ens[:, r, :].T
        field[r] = turned
        part = pl.ds(r * width, width)
        left[part, lanes] = turned[:width]
        right[part, lanes] = turned[cols - width :]
        if r < width:
            top[pl.ds(r * cut, cut), lanes] = turned[:cut]
        if r >= rows - width:
            bottom[pl.ds((r - rows + width) * cut, cut), lanes] = turned[:cut]
    near_edge = jnp.zeros((rows, cols), jnp.float32)
    far_edge = near_edge
    lane = lax.broadcasted_iota(jnp.int32, (rows, cols), 1)
    for k, part in enumerate((diffusion, drift_rows, drift_cols)):
        at = pl.ds(width * cut + k * width, width)
        top[at, pl.ds(0, cols)] = part[:width]
        bottom[at, pl.ds(0, cols)] = part[rows - width :]
        value = part[...]
        kept[k] = value
        mine = (lane >= k * width) & (lane < (k + 1) * width)
        if k:
            near_edge = jnp.where(mine, pltpu.roll(value, k * width, 1), near_edge)
        else:
            near_edge = jnp.where(mine, value, near_edge)
        far_edge = jnp.where(mine, pltpu.roll(value, (k + 1) * width, 1), far_edge)
    left[pl.ds(rows * width, rows), pl.ds(0, cols)] = near_edge
    right[pl.ds(rows * width, rows), pl.ds(0, cols)] = far_edge


def turn_kernel(field, left, right, up, down):
    rows, cols, members = field.shape
    width = STEPS
    area = width * width
    cut = parted(cols)[0]
    size = cols - cut
    lanes = pl.ds(0, members)
    for i in range(width):
        at = pl.ds(i * size, size)
        up[at, lanes] = field[i, pl.ds(cut, size)]
        down[at, lanes] = field[rows - width + i, pl.ds(cut, size)]
    base = width * size
    for i, side in enumerate((left, right)):
        at = pl.ds(base + i * area, area)
        up[at] = side[pl.ds(0, area)]
        down[at] = side[pl.ds((rows - width) * width, area)]
        at = pl.ds(base + 2 * area + i * width, width)
        up[at] = side[pl.ds(rows * width, width)]
        down[at] = side[pl.ds(rows * width + rows - width, width)]


def widen(write, line, columns, members):
    for at, parts in columns:
        size = parts[0].shape[0]
        diffusion, rowwise, colwise = (
            jnp.broadcast_to(p[:, line : line + 1], (size, members)) for p in parts
        )
        here = pl.ds(at, size)
        write(0, here, 1.0 - 4.0 * diffusion - rowwise - colwise)
        write(1, here, diffusion)
        write(2, here, diffusion + rowwise)
        write(3, here, diffusion + colwise)


def spread_rows(spread, lines, columns, members):
    for line, row in lines:

        def write(k, here, value, row=row):
            spread[k, row, here] = value

        widen(write, line, columns, members)


def march(rows, even, odd, spread, ranges, finals, store):
    width = STEPS
    source, target = even, odd
    for step in range(1, STEPS + 1):
        last = step == STEPS

        def advance(r, source=source, target=target, last=last):
            for at, size in finals if last else ranges:
                here = pl.ds(at, size)
                value = (
                    spread[0, r, here] * source[r, here]
                    + spread[1, r, here] * (source[r + 1, here] + source[r, pl.ds(at + 1, size)])
                    + spread[2, r, here] * source[r - 1, here]
                    + spread[3, r, here] * source[r, pl.ds(at - 1, size)]
                )
                if last:
                    store(r - width, at, value)
                else:
                    target[r, here] = value

        loop(rows + 2 * width - 2 * step, lambda i: advance(i + step))
        source, target = target, source


def coefficient_rows(kept, above, below, stage, cut):
    rows, cols = kept.shape[1:]
    width = STEPS
    for i, strip in enumerate((above, below)):
        for k in range(3):
            stage[k, pl.ds(i * width, width)] = strip[
                pl.ds(width * cut + k * width, width), pl.ds(0, cols)
            ]
    lines = [(i, i) for i in range(1, width)]
    lines += [(width + i, width + rows + i) for i in range(width - 1)]
    inside = [(r, width + r) for r in range(rows)]
    return [kept[k].T for k in range(3)], inside, [stage[k].T for k in range(3)], lines


def middle_kernel(field, kept, above, below, out, even, odd, spread, stage):
    rows, cols, members = field.shape
    width = STEPS
    cut, low, high = parted(cols)
    lanes = pl.ds(0, members)
    own, inside, beyond, lines = coefficient_rows(kept, above, below, stage, cut)
    for parts, places in ((beyond, lines), (own, inside)):
        spread_rows(spread, places, [(LEAD, [p[:cut] for p in parts])], members)
    here = pl.ds(LEAD, cut)
    for i in range(width):
        part = pl.ds(i * cut, cut)
        even[i, here] = above[part, lanes]
        even[width + rows + i, here] = below[part, lanes]
    for r in range(rows):
        even[width + r, here] = field[r, pl.ds(0, cut)]

    def store(r, at, value):
        out[r] = value

    march(rows, even, odd, spread, [(LEAD, cut)], [(LEAD + low, high - low)], store)


def sides_kernel(
    field, kept, above, below, left, right, above_rest, below_rest, out, even, odd, spread, stage
):
    rows, cols, members = field.shape
    width = STEPS
    area = width * width
    cut, low, high = parted(cols)
    first, second = low + 8, high - 8
    size = cols - cut
    base = width * size
    lanes = pl.ds(0, members)
    own, inside, beyond, lines = coefficient_rows(kept, above, below, stage, cut)
    for i, strip in enumerate((above_rest, below_rest)):
        for side in range(2):
            stage[3 + side, pl.ds(i * width, width)] = strip[
                pl.ds(base + 2 * area + side * width, width), pl.ds(0, cols)
            ]
    edge = pl.ds(rows * width, rows), pl.ds(0, cols)
    for parts, near_part, far_part, places in (
        (beyond, stage[3].T, stage[4].T, lines),
        (own, left[edge].T, right[edge].T, inside),
    ):
        halo = [slice(k * width, (k + 1) * width) for k in range(3)]
        columns = [
            (LEAD - width, [near_part[h] for h in halo]),
            (LEAD, [p[:first] for p in parts]),
            (LEAD + second, [p[second:] for p in parts]),
            (LEAD + cols, [far_part[h] for h in halo]),
        ]
        spread_rows(spread, places, columns, members)
    before = pl.ds(LEAD - width, width)
    after = pl.ds(LEAD + cols, width)
    for i in range(width):
        for j, strip, rest in (
            (i, above, above_rest),
            (width + rows + i, below, below_rest),
        ):
            even[j, before] = rest[pl.ds(base + i * width, width), lanes]
            even[j, pl.ds(LEAD, first)] = strip[pl.ds(i * cut, first), lanes]
            even[j, pl.ds(LEAD + second, cut - second)] = strip[
                pl.ds(i * cut + second, cut - second), lanes
            ]
            even[j, pl.ds(LEAD + cut, size)] = rest[pl.ds(i * size, size), lanes]
            even[j, after] = rest[pl.ds(base + area + i * width, width), lanes]
    for r in range(rows):
        part = pl.ds(r * width, width)
        even[width + r, before] = left[part, lanes]
        even[width + r, pl.ds(LEAD, first)] = field[r, pl.ds(0, first)]
        even[width + r, pl.ds(LEAD + second, cols - second)] = field[
            r, pl.ds(second, cols - second)
        ]
        even[width + r, after] = right[part, lanes]

    def store(r, at, value):
        if at == LEAD:
            out[r, pl.ds(cols - high, low)] = value
        else:
            out[r, pl.ds(0, cols - high)] = value

    march(
        rows,
        even,
        odd,
        spread,
        [(LEAD + second, cols - second + 8), (LEAD - 8, first + 8)],
        [(LEAD + high, cols - high), (LEAD, low)],
        store,
    )


def weight_kernel(axis, count, cells, values, weights, out):
    cols, twice = out.shape
    rows = twice // 2
    slots = cells.shape[1]
    full = cols * lax.axis_size(axis)
    cell = cells[...]
    if full & (full - 1):
        row_of = lax.div(cell, full)
    else:
        row_of = lax.shift_right_logical(cell, full.bit_length() - 1)
    col_of = cell - row_of * full - lax.axis_index(axis) * cols
    slot = lax.broadcasted_iota(jnp.int32, (1, slots), 1)
    plain = jnp.where(slot < count[0], weights[...], 0.0)
    valued = plain * values[...]
    here = lax.broadcasted_iota(jnp.int32, (cols, slots), 0) == col_of
    here = jnp.where(here, 1.0, 0.0).astype(jnp.bfloat16)
    line = lax.broadcasted_iota(jnp.int32, (rows, slots), 0) == row_of
    value = jnp.concatenate([jnp.where(line, plain, 0.0), jnp.where(line, valued, 0.0)], axis=0)
    total = jnp.zeros((cols, twice), jnp.float32)
    for piece in range(3):
        part = value.astype(jnp.bfloat16)
        value = value - part.astype(jnp.float32)
        total = total + dot(here, part, ((1,), (1,)))
    out[...] = total


def gram_kernel(groups, pieces, own, others, weight, upper, lower, centre, total, tilt):
    rows, size, _ = own.shape
    members = total.shape[0]
    cols = weight.shape[0]
    many = next(n for n in (4, 2, 1) if rows % n == 0)
    depth = many * size

    def block(b):
        def cells(ref, start):
            value = ref[pl.ds(start + b * many, many)]
            return value.reshape(depth, value.shape[2])

        parts = [cells(own, 0)] + [cells(others, g * rows) for g in range(groups - 1)]
        value = jnp.concatenate(parts, axis=1) if groups > 1 else parts[0]
        mean = jnp.sum(value, axis=1, keepdims=True) * (1.0 / members)
        deviation = value - mean
        plain, valued = [], []
        for i in range(many):
            r = b * many + i
            row = jnp.zeros((1, cols), jnp.float32)
            for start, column, length in pieces:
                place = lax.broadcasted_iota(jnp.int32, (length, cols), 0) + column
                here = place == lax.broadcasted_iota(jnp.int32, (length, cols), 1)
                part = mean[i * size + start : i * size + start + length]
                row = row + jnp.sum(jnp.where(here, part, 0.0), axis=0, keepdims=True)
                source = weight[pl.ds(column, length)]
                line = lax.broadcasted_iota(jnp.int32, source.shape, 1)
                plain.append(jnp.sum(jnp.where(line == r, source, 0.0), axis=1, keepdims=True))
                valued.append(
                    jnp.sum(jnp.where(line == r + rows, source, 0.0), axis=1, keepdims=True)
                )
            centre[pl.ds(r, 1)] = row
        plain = jnp.concatenate(plain, axis=0)
        valued = jnp.concatenate(valued, axis=0)
        high, low = halves(deviation)
        at = pl.ds(b * depth, depth)
        upper[at] = high
        lower[at] = low
        turned = (deviation * plain).T
        total[...] += dot3(halves(turned), (high, low))
        tilt[...] += jnp.sum(deviation * (valued - plain * mean), axis=0, keepdims=True)

    loop(rows // many, block)


def first_gram_kernel(groups, pieces, own, others, weight, upper, lower, centre, total, tilt):
    total[...] = jnp.zeros_like(total)
    tilt[...] = jnp.zeros_like(tilt)
    gram_kernel(groups, pieces, own, others, weight, upper, lower, centre, total, tilt)


def last_gram_kernel(
    groups, pieces, own, others, weight, before, tilted, gram, upper, lower, centre, total, tilt
):
    total[...] = before[...]
    tilt[...] = tilted[...]
    gram_kernel(groups, pieces, own, others, weight, upper, lower, centre, total, tilt)
    pull = gram.shape[0] - 8
    blocks = total.shape[0] // 128
    innovation = tilt[...]
    at = 0
    gram[pl.ds(pull, 8)] = jnp.zeros((8, 128), jnp.float32)
    for i in range(blocks):
        gram[pl.ds(pull + i, 1)] = innovation[:, i * 128 : (i + 1) * 128]
        for j in range(i, blocks):
            gram[pl.ds(at, 128)] = total[i * 128 : (i + 1) * 128, j * 128 : (j + 1) * 128]
            at += 128


def analysis_kernel(parts, first, second, *rest):
    uppers, lowers, centres = rest[0:2], rest[2:4], rest[4:6]
    out, whole, chosen, natural = rest[6:]
    local, rows, cols = out.shape
    members = whole.shape[0]
    blocks = members // 128
    pull = first.shape[0] - 8
    at = 0
    for i in range(blocks):
        for j in range(i, blocks):
            block = first[pl.ds(at, 128)] + second[pl.ds(at, 128)]
            whole[i * 128 : (i + 1) * 128, j * 128 : (j + 1) * 128] = block
            if j > i:
                whole[j * 128 : (j + 1) * 128, i * 128 : (i + 1) * 128] = block.T
            at += 128
    innovation = jnp.concatenate(
        [first[pl.ds(pull + i, 1)] + second[pl.ds(pull + i, 1)] for i in range(blocks)],
        axis=1,
    )
    down = lax.broadcasted_iota(jnp.int32, (members, members), 0)
    across = lax.broadcasted_iota(jnp.int32, (members, members), 1)
    identity = jnp.where(down == across, 1.0, 0.0)
    matrix = whole[...] + (members - 1.0) * identity
    squares = jnp.sum(jnp.sum(matrix * matrix, axis=1, keepdims=True), axis=0, keepdims=True)
    scaling = jnp.sqrt(squares)
    current = matrix * (1.0 / scaling)
    middle = 1.5 * identity - 0.5 * current
    inverse = middle
    current = dot3(halves(current), halves(middle))
    for repeat in range(1, ITERS):
        current_parts = halves(current)
        inverse_parts = halves(inverse)
        middle = 1.5 * identity - 0.5 * dot3(inverse_parts, current_parts)
        middle_parts = halves(middle)
        if repeat < ITERS - 1:
            current = dot3(current_parts, middle_parts)
        inverse = dot3(inverse_parts, middle_parts)
    once = jnp.sum(inverse * innovation, axis=1, keepdims=True)
    once_row = jnp.sum(jnp.where(down == across, once, 0.0), axis=0, keepdims=True)
    shifted = jnp.sum(inverse * once_row, axis=1, keepdims=True) * (1.0 / scaling)
    factor = jnp.sqrt((members - 1.0) / scaling)
    mixing = (factor * inverse + shifted)[:, :local]
    high, low = halves(mixing)
    chosen[0] = high
    chosen[1] = low
    many = next(n for n in (4, 2, 1) if rows % n == 0)

    def block(b):
        for pieces, upper, lower in zip(parts, uppers, lowers):
            size = upper.shape[0] // rows
            at = pl.ds(b * many * size, many * size)
            value = dot(upper[at], chosen[0]) + (
                dot(upper[at], chosen[1]) + dot(lower[at], chosen[0])
            )
            for i in range(many):
                for start, column, length in pieces:
                    natural[i, pl.ds(column, length)] = value[
                        i * size + start : i * size + start + length
                    ]
        for i in range(many):
            r = b * many + i
            middle_row = centres[0][pl.ds(r, 1)] + centres[1][pl.ds(r, 1)]
            out[:, r, :] = natural[i].T + middle_row

    loop(rows // many, block)


def shift(value, axes, *moves):
    sizes = [lax.axis_size(a) for a in axes]
    pairs = []
    total = 1
    for s in sizes:
        total *= s
    for flat in range(total):
        rest, place = flat, []
        for s in reversed(sizes):
            place.append(rest % s)
            rest //= s
        place = place[::-1]
        to = 0
        for s, p, m in zip(sizes, place, moves):
            to = to * s + (p + m) % s
        pairs.append((flat, to))
    return lax.ppermute(value, axes if len(axes) > 1 else axes[0], pairs)


def role_sum(value):
    size = lax.axis_size("role")
    if size & (size - 1) or size == 1:
        return lax.psum(value, "role"), jnp.zeros_like(value)
    other = jnp.zeros_like(value)
    step = 1
    while step < size:
        if step > 1:
            value = value + other
        other = lax.ppermute(value, "role", [(i, i ^ step) for i in range(size)])
        step *= 2
    return value, other


def shards(
    ensemble,
    diffusion,
    drift_rows,
    drift_cols,
    observed_cells,
    observed_count,
    observed_values,
    observed_weights,
):
    groups = lax.axis_size("member")
    roles = lax.axis_size("role")
    local, rows, cols = ensemble.shape
    members = local * groups
    width = STEPS
    lanes = max(local, cols)
    cut, low, high = parted(cols)
    strip = struct(width * cut + 4 * width, lanes)
    rest = struct(width * (cols - cut) + 2 * width * width + 2 * width, lanes)
    edge = struct(rows * width + rows, lanes)
    field, kept, top, bottom, left, right = call(
        pack_kernel,
        (struct(rows, cols, local), struct(3, rows, cols), strip, strip, edge, edge),
        ensemble,
        diffusion,
        drift_rows,
        drift_cols,
        name="pack",
        raw=4,
    )
    z, x = ("domain",), ("role",)
    above = shift(bottom, z, 1)
    below = shift(top, z, -1)
    left, right = shift(right, x, 1), shift(left, x, -1)
    up, down = call(turn_kernel, (rest, rest), field, left, right, name="turn")
    above_rest = shift(down, z, 1)
    below_rest = shift(up, z, -1)
    weight = call(
        functools.partial(weight_kernel, "role"),
        struct(cols, 2 * rows),
        observed_count,
        observed_cells,
        observed_values,
        observed_weights,
        scalars=1,
        raw=3,
        name="weights",
    )
    padded = pltpu.VMEM((rows + 2 * width, cols + 2 * LEAD, local), jnp.float32)
    scratch = (
        padded,
        padded,
        pltpu.VMEM((4, rows + 2 * width, cols + 2 * LEAD, local), jnp.float32),
        pltpu.VMEM((5, 2 * width, cols), jnp.float32),
    )
    middle = call(
        middle_kernel,
        struct(rows, high - low, local),
        field,
        kept,
        above,
        below,
        scratch=scratch,
        name="middle",
    )
    sides = call(
        sides_kernel,
        struct(rows, cols - high + low, local),
        field,
        kept,
        above,
        below,
        left,
        right,
        above_rest,
        below_rest,
        scratch=scratch,
        name="sides",
    )

    def gathered(value):
        others = [shift(value, ("member",), s) for s in range(1, groups)]
        return jnp.concatenate(others, axis=0) if len(others) > 1 else others[0]

    middle_others = gathered(middle)
    sides_others = gathered(sides)
    parts = (
        ((0, low, high - low),),
        ((0, high, cols - high), (cols - high, 0, low)),
    )
    blocks = members // 128
    size = blocks * (blocks + 1) // 2 * 128 + 8
    square = struct(members, members)
    vector = struct(1, members)

    def deviations(columns):
        one = struct(rows * columns, members, kind=jnp.bfloat16)
        return one, one, struct(rows, cols)

    upper_a, lower_a, centre_a, total, tilt = call(
        functools.partial(first_gram_kernel, groups, parts[0]),
        (*deviations(high - low), square, vector),
        middle,
        middle_others,
        weight,
        name="first_gram",
    )
    gram, upper_b, lower_b, centre_b = call(
        functools.partial(last_gram_kernel, groups, parts[1]),
        (struct(size, 128), *deviations(cols - high + low)),
        sides,
        sides_others,
        weight,
        total,
        tilt,
        scratch=(
            pltpu.VMEM((members, members), jnp.float32),
            pltpu.VMEM((1, members), jnp.float32),
        ),
        name="last_gram",
    )
    first, second = role_sum(gram)
    return call(
        functools.partial(analysis_kernel, parts),
        struct(local, rows, cols),
        first,
        second,
        upper_a,
        upper_b,
        lower_a,
        lower_b,
        centre_a,
        centre_b,
        scratch=(
            pltpu.VMEM((members, members), jnp.float32),
            pltpu.VMEM((2, members, local), jnp.bfloat16),
            pltpu.VMEM((4, cols, local), jnp.float32),
        ),
        name="analysis",
        result=True,
    )


def solution(mesh):
    placed = (
        P("member", "domain", "role"),
        P("domain", "role"),
        P("domain", "role"),
        P("domain", "role"),
        P("domain", None),
        P("domain"),
        P("domain", None),
        P("domain", None),
    )
    return jax.shard_map(
        shards, mesh=mesh, in_specs=placed, out_specs=P("member", "domain", "role"), check_vma=False
    )
```

```python
import functools

import jax
import jax.numpy as jnp
from jax import lax
from jax.experimental import pallas as pl
from jax.experimental.pallas import tpu as pltpu
from jax.sharding import PartitionSpec as P

STEPS = 4
ITERS = 6
LEAD = 16


VMEM = pl.BlockSpec(memory_space=pltpu.VMEM)
SMEM = pl.BlockSpec(memory_space=pltpu.SMEM)
ROOM = 1 << 20


def struct(*shape, kind=jnp.float32):
    return jax.ShapeDtypeStruct(shape, kind)


def near(shape, kind):
    size = jnp.dtype(kind).itemsize
    for place, extent in enumerate(shape[::-1]):
        unit = (128, 32 // jnp.dtype(kind).itemsize, 1)[min(place, 2)]
        size *= -(-extent // unit) * unit
    return size <= ROOM


def call(body, outs, *args, scratch=(), name=None, scalars=0, raw=0, result=False):
    placed = list(args[: scalars + raw])
    for value in args[scalars + raw :]:
        if near(value.shape, value.dtype):
            value = pltpu.with_memory_space_constraint(value, pltpu.VMEM)
        placed.append(value)
    if not result:
        outs = jax.tree.map(
            lambda s: pltpu.VMEM(s.shape, s.dtype) if near(s.shape, s.dtype) else s, outs
        )
    return pl.pallas_call(
        body,
        out_shape=outs,
        in_specs=[SMEM] * scalars + [VMEM] * (len(args) - scalars),
        out_specs=tuple(VMEM for _ in outs) if isinstance(outs, tuple) else VMEM,
        scratch_shapes=scratch,
        name=name,
    )(*placed)


def halves(value):
    upper = value.astype(jnp.bfloat16)
    lower = (value - upper.astype(jnp.float32)).astype(jnp.bfloat16)
    return upper, lower


def dot(a, b, dims=((1,), (0,))):
    return lax.dot_general(a, b, (dims, ((), ())), preferred_element_type=jnp.float32)


def dot3(a, b, dims=((1,), (0,))):
    return dot(a[0], b[0], dims) + (dot(a[0], b[1], dims) + dot(a[1], b[0], dims))


def loop(count, body):
    if count <= 16:
        for i in range(count):
            body(i)
    else:
        lax.fori_loop(0, count, lambda i, c: (body(i), c)[1], 0)


def parted(cols):
    cut = (cols // 2 + 16) // 8 * 8
    return cut, 8, cut - 8


def parity(axis):
    return lax.rem(lax.axis_index(axis), 2)


def pack_kernel(axis, ens, diffusion, drift_rows, drift_cols, field, kept, early, late, left, right):
    odd = parity(axis)
    _, rows, cols = ens.shape
    members = field.shape[2]
    width = STEPS
    cut = parted(cols)[0]
    lanes = pl.ds(0, members)
    for r in range(rows):
        turned = ens[:, r, :].T
        field[r] = turned
        part = pl.ds(r * width, width)
        left[part, lanes] = turned[:width]
        right[part, lanes] = turned[cols - width :]
    for i in range(width):
        part = pl.ds(i * cut, cut)
        early[part, lanes] = field[i + odd * (rows - width), pl.ds(0, cut)]
        late[part, lanes] = field[i + (1 - odd) * (rows - width), pl.ds(0, cut)]
    near_edge = jnp.zeros((rows, cols), jnp.float32)
    far_edge = near_edge
    lane = lax.broadcasted_iota(jnp.int32, (rows, cols), 1)
    for k, part in enumerate((diffusion, drift_rows, drift_cols)):
        at = pl.ds(width * cut + k * width, width)
        top, bottom = part[:width], part[rows - width :]
        early[at, pl.ds(0, cols)] = jnp.where(odd == 0, top, bottom)
        late[at, pl.ds(0, cols)] = jnp.where(odd == 0, bottom, top)
        value = part[...]
        kept[k] = value
        mine = (lane >= k * width) & (lane < (k + 1) * width)
        if k:
            near_edge = jnp.where(mine, pltpu.roll(value, k * width, 1), near_edge)
        else:
            near_edge = jnp.where(mine, value, near_edge)
        far_edge = jnp.where(mine, pltpu.roll(value, (k + 1) * width, 1), far_edge)
    left[pl.ds(rows * width, rows), pl.ds(0, cols)] = near_edge
    right[pl.ds(rows * width, rows), pl.ds(0, cols)] = far_edge


def turn_kernel(axis, field, left, right, early, late):
    rows, cols, members = field.shape
    odd = parity(axis)
    width = STEPS
    area = width * width
    cut = parted(cols)[0]
    size = cols - cut
    lanes = pl.ds(0, members)
    for i in range(width):
        at = pl.ds(i * size, size)
        early[at, lanes] = field[i + odd * (rows - width), pl.ds(cut, size)]
        late[at, lanes] = field[i + (1 - odd) * (rows - width), pl.ds(cut, size)]
    base = width * size
    for i, side in enumerate((left, right)):
        at = pl.ds(base + i * area, area)
        top, bottom = side[pl.ds(0, area)], side[pl.ds((rows - width) * width, area)]
        early[at] = jnp.where(odd == 0, top, bottom)
        late[at] = jnp.where(odd == 0, bottom, top)
        at = pl.ds(base + 2 * area + i * width, width)
        top = side[pl.ds(rows * width, width)]
        bottom = side[pl.ds(rows * width + rows - width, width)]
        early[at] = jnp.where(odd == 0, top, bottom)
        late[at] = jnp.where(odd == 0, bottom, top)


def widen(write, line, columns, members):
    for at, parts in columns:
        size = parts[0].shape[0]
        diffusion, rowwise, colwise = (
            jnp.broadcast_to(p[:, line : line + 1], (size, members)) for p in parts
        )
        here = pl.ds(at, size)
        write(0, here, 1.0 - 4.0 * diffusion - rowwise - colwise)
        write(1, here, diffusion)
        write(2, here, diffusion + rowwise)
        write(3, here, diffusion + colwise)


def spread_rows(spread, lines, columns, members):
    for line, row in lines:

        def write(k, here, value, row=row):
            spread[k, row, here] = value

        widen(write, line, columns, members)


def march(rows, even, odd, spread, ranges, finals, store):
    width = STEPS
    source, target = even, odd
    for step in range(1, STEPS + 1):
        last = step == STEPS

        def advance(r, source=source, target=target, last=last):
            for at, size in finals if last else ranges:
                here = pl.ds(at, size)
                value = (
                    spread[0, r, here] * source[r, here]
                    + spread[1, r, here] * (source[r + 1, here] + source[r, pl.ds(at + 1, size)])
                    + spread[2, r, here] * source[r - 1, here]
                    + spread[3, r, here] * source[r, pl.ds(at - 1, size)]
                )
                if last:
                    store(r - width, at, value)
                else:
                    target[r, here] = value

        loop(rows + 2 * width - 2 * step, lambda i: advance(i + step))
        source, target = target, source


def coefficient_rows(odd, kept, early, late, stage, cut):
    rows, cols = kept.shape[1:]
    width = STEPS
    for k in range(3):
        at = pl.ds(width * cut + k * width, width), pl.ds(0, cols)
        stage[k, pl.ds(0, width)] = jnp.where(odd == 0, early[at], late[at])
        stage[k, pl.ds(width, width)] = jnp.where(odd == 0, late[at], early[at])
    lines = [(i, i) for i in range(1, width)]
    lines += [(width + i, width + rows + i) for i in range(width - 1)]
    inside = [(r, width + r) for r in range(rows)]
    return [kept[k].T for k in range(3)], inside, [stage[k].T for k in range(3)], lines


def middle_kernel(axis, field, kept, early, late, out, one, two, spread, stage):
    rows, cols, members = field.shape
    width = STEPS
    cut, low, high = parted(cols)
    lanes = pl.ds(0, members)
    odd = parity(axis)
    own, inside, beyond, lines = coefficient_rows(odd, kept, early, late, stage, cut)
    for parts, places in ((beyond, lines), (own, inside)):
        spread_rows(spread, places, [(LEAD, [p[:cut] for p in parts])], members)
    here = pl.ds(LEAD, cut)
    for i in range(width):
        part = pl.ds(i * cut, cut)
        one[i + odd * (rows + width), here] = early[part, lanes]
        one[i + (1 - odd) * (rows + width), here] = late[part, lanes]
    for r in range(rows):
        one[width + r, here] = field[r, pl.ds(0, cut)]

    def store(r, at, value):
        out[r] = value

    march(rows, one, two, spread, [(LEAD, cut)], [(LEAD + low, high - low)], store)


def sides_kernel(
    axis,
    field,
    kept,
    early,
    late,
    left,
    right,
    early_rest,
    late_rest,
    out,
    one,
    two,
    spread,
    stage,
):
    rows, cols, members = field.shape
    width = STEPS
    area = width * width
    cut, low, high = parted(cols)
    first, second = low + 8, high - 8
    size = cols - cut
    base = width * size
    lanes = pl.ds(0, members)
    odd = parity(axis)
    own, inside, beyond, lines = coefficient_rows(odd, kept, early, late, stage, cut)
    for side in range(2):
        at = pl.ds(base + 2 * area + side * width, width), pl.ds(0, cols)
        stage[3 + side, pl.ds(0, width)] = jnp.where(odd == 0, early_rest[at], late_rest[at])
        stage[3 + side, pl.ds(width, width)] = jnp.where(odd == 0, late_rest[at], early_rest[at])
    edge = pl.ds(rows * width, rows), pl.ds(0, cols)
    for parts, near_part, far_part, places in (
        (beyond, stage[3].T, stage[4].T, lines),
        (own, left[edge].T, right[edge].T, inside),
    ):
        halo = [slice(k * width, (k + 1) * width) for k in range(3)]
        columns = [
            (LEAD - width, [near_part[h] for h in halo]),
            (LEAD, [p[:first] for p in parts]),
            (LEAD + second, [p[second:] for p in parts]),
            (LEAD + cols, [far_part[h] for h in halo]),
        ]
        spread_rows(spread, places, columns, members)
    before = pl.ds(LEAD - width, width)
    after = pl.ds(LEAD + cols, width)
    for i in range(width):
        for j, strip, rest in (
            (i + odd * (rows + width), early, early_rest),
            (i + (1 - odd) * (rows + width), late, late_rest),
        ):
            one[j, before] = rest[pl.ds(base + i * width, width), lanes]
            one[j, pl.ds(LEAD, first)] = strip[pl.ds(i * cut, first), lanes]
            one[j, pl.ds(LEAD + second, cut - second)] = strip[
                pl.ds(i * cut + second, cut - second), lanes
            ]
            one[j, pl.ds(LEAD + cut, size)] = rest[pl.ds(i * size, size), lanes]
            one[j, after] = rest[pl.ds(base + area + i * width, width), lanes]
    for r in range(rows):
        part = pl.ds(r * width, width)
        one[width + r, before] = left[part, lanes]
        one[width + r, pl.ds(LEAD, first)] = field[r, pl.ds(0, first)]
        one[width + r, pl.ds(LEAD + second, cols - second)] = field[
            r, pl.ds(second, cols - second)
        ]
        one[width + r, after] = right[part, lanes]

    def store(r, at, value):
        if at == LEAD:
            out[r, pl.ds(cols - high, low)] = value
        else:
            out[r, pl.ds(0, cols - high)] = value

    march(
        rows,
        one,
        two,
        spread,
        [(LEAD + second, cols - second + 8), (LEAD - 8, first + 8)],
        [(LEAD + high, cols - high), (LEAD, low)],
        store,
    )


def weight_kernel(axis, count, cells, values, weights, out):
    cols, twice = out.shape
    rows = twice // 2
    slots = cells.shape[1]
    full = cols * lax.axis_size(axis)
    cell = cells[...]
    if full & (full - 1):
        row_of = lax.div(cell, full)
    else:
        row_of = lax.shift_right_logical(cell, full.bit_length() - 1)
    col_of = cell - row_of * full - lax.axis_index(axis) * cols
    slot = lax.broadcasted_iota(jnp.int32, (1, slots), 1)
    plain = jnp.where(slot < count[0], weights[...], 0.0)
    valued = plain * values[...]
    here = lax.broadcasted_iota(jnp.int32, (cols, slots), 0) == col_of
    here = jnp.where(here, 1.0, 0.0).astype(jnp.bfloat16)
    line = lax.broadcasted_iota(jnp.int32, (rows, slots), 0) == row_of
    value = jnp.concatenate([jnp.where(line, plain, 0.0), jnp.where(line, valued, 0.0)], axis=0)
    total = jnp.zeros((cols, twice), jnp.float32)
    for piece in range(3):
        part = value.astype(jnp.bfloat16)
        value = value - part.astype(jnp.float32)
        total = total + dot(here, part, ((1,), (1,)))
    out[...] = total


def gram_kernel(groups, pieces, own, others, weight, upper, lower, centre, total, tilt):
    rows, size, _ = own.shape
    members = total.shape[0]
    cols = weight.shape[0]
    many = next(n for n in (4, 2, 1) if rows % n == 0)
    depth = many * size

    def block(b):
        def cells(ref, start):
            value = ref[pl.ds(start + b * many, many)]
            return value.reshape(depth, value.shape[2])

        parts = [cells(own, 0)] + [cells(others, g * rows) for g in range(groups - 1)]
        value = jnp.concatenate(parts, axis=1) if groups > 1 else parts[0]
        mean = jnp.sum(value, axis=1, keepdims=True) * (1.0 / members)
        deviation = value - mean
        plain, valued = [], []
        for i in range(many):
            r = b * many + i
            row = jnp.zeros((1, cols), jnp.float32)
            for start, column, length in pieces:
                place = lax.broadcasted_iota(jnp.int32, (length, cols), 0) + column
                here = place == lax.broadcasted_iota(jnp.int32, (length, cols), 1)
                part = mean[i * size + start : i * size + start + length]
                row = row + jnp.sum(jnp.where(here, part, 0.0), axis=0, keepdims=True)
                source = weight[pl.ds(column, length)]
                line = lax.broadcasted_iota(jnp.int32, source.shape, 1)
                plain.append(jnp.sum(jnp.where(line == r, source, 0.0), axis=1, keepdims=True))
                valued.append(
                    jnp.sum(jnp.where(line == r + rows, source, 0.0), axis=1, keepdims=True)
                )
            centre[pl.ds(r, 1)] = row
        plain = jnp.concatenate(plain, axis=0)
        valued = jnp.concatenate(valued, axis=0)
        high, low = halves(deviation)
        at = pl.ds(b * depth, depth)
        upper[at] = high
        lower[at] = low
        turned = (deviation * plain).T
        total[...] += dot3(halves(turned), (high, low))
        tilt[...] += jnp.sum(deviation * (valued - plain * mean), axis=0, keepdims=True)

    loop(rows // many, block)


def first_gram_kernel(groups, pieces, own, others, weight, upper, lower, centre, total, tilt):
    total[...] = jnp.zeros_like(total)
    tilt[...] = jnp.zeros_like(tilt)
    gram_kernel(groups, pieces, own, others, weight, upper, lower, centre, total, tilt)


def last_gram_kernel(
    groups, pieces, own, others, weight, before, tilted, gram, upper, lower, centre, total, tilt
):
    total[...] = before[...]
    tilt[...] = tilted[...]
    gram_kernel(groups, pieces, own, others, weight, upper, lower, centre, total, tilt)
    pull = gram.shape[0] - 8
    blocks = total.shape[0] // 128
    innovation = tilt[...]
    at = 0
    gram[pl.ds(pull, 8)] = jnp.zeros((8, 128), jnp.float32)
    for i in range(blocks):
        gram[pl.ds(pull + i, 1)] = innovation[:, i * 128 : (i + 1) * 128]
        for j in range(i, blocks):
            gram[pl.ds(at, 128)] = total[i * 128 : (i + 1) * 128, j * 128 : (j + 1) * 128]
            at += 128


def analysis_kernel(parts, first, second, *rest):
    uppers, lowers, centres = rest[0:2], rest[2:4], rest[4:6]
    out, whole, chosen, natural = rest[6:]
    local, rows, cols = out.shape
    members = whole.shape[0]
    blocks = members // 128
    pull = first.shape[0] - 8
    at = 0
    for i in range(blocks):
        for j in range(i, blocks):
            block = first[pl.ds(at, 128)] + second[pl.ds(at, 128)]
            whole[i * 128 : (i + 1) * 128, j * 128 : (j + 1) * 128] = block
            if j > i:
                whole[j * 128 : (j + 1) * 128, i * 128 : (i + 1) * 128] = block.T
            at += 128
    innovation = jnp.concatenate(
        [first[pl.ds(pull + i, 1)] + second[pl.ds(pull + i, 1)] for i in range(blocks)],
        axis=1,
    )
    down = lax.broadcasted_iota(jnp.int32, (members, members), 0)
    across = lax.broadcasted_iota(jnp.int32, (members, members), 1)
    identity = jnp.where(down == across, 1.0, 0.0)
    matrix = whole[...] + (members - 1.0) * identity
    squares = jnp.sum(jnp.sum(matrix * matrix, axis=1, keepdims=True), axis=0, keepdims=True)
    scaling = jnp.sqrt(squares)
    current = matrix * (1.0 / scaling)
    middle = 1.5 * identity - 0.5 * current
    inverse = middle
    current = dot3(halves(current), halves(middle))
    for repeat in range(1, ITERS):
        current_parts = halves(current)
        inverse_parts = halves(inverse)
        middle = 1.5 * identity - 0.5 * dot3(inverse_parts, current_parts)
        middle_parts = halves(middle)
        if repeat < ITERS - 1:
            current = dot3(current_parts, middle_parts)
        inverse = dot3(inverse_parts, middle_parts)
    once = jnp.sum(inverse * innovation, axis=1, keepdims=True)
    once_row = jnp.sum(jnp.where(down == across, once, 0.0), axis=0, keepdims=True)
    shifted = jnp.sum(inverse * once_row, axis=1, keepdims=True) * (1.0 / scaling)
    factor = jnp.sqrt((members - 1.0) / scaling)
    mixing = (factor * inverse + shifted)[:, :local]
    high, low = halves(mixing)
    chosen[0] = high
    chosen[1] = low
    many = next(n for n in (4, 2, 1) if rows % n == 0)

    def block(b):
        for pieces, upper, lower in zip(parts, uppers, lowers):
            size = upper.shape[0] // rows
            at = pl.ds(b * many * size, many * size)
            value = dot(upper[at], chosen[0]) + (
                dot(upper[at], chosen[1]) + dot(lower[at], chosen[0])
            )
            for i in range(many):
                for start, column, length in pieces:
                    natural[i, pl.ds(column, length)] = value[
                        i * size + start : i * size + start + length
                    ]
        for i in range(many):
            r = b * many + i
            middle_row = centres[0][pl.ds(r, 1)] + centres[1][pl.ds(r, 1)]
            out[:, r, :] = natural[i].T + middle_row

    loop(rows // many, block)


def shift(value, axes, *moves):
    sizes = [lax.axis_size(a) for a in axes]
    pairs = []
    total = 1
    for s in sizes:
        total *= s
    for flat in range(total):
        rest, place = flat, []
        for s in reversed(sizes):
            place.append(rest % s)
            rest //= s
        place = place[::-1]
        to = 0
        for s, p, m in zip(sizes, place, moves):
            to = to * s + (p + m) % s
        pairs.append((flat, to))
    return lax.ppermute(value, axes if len(axes) > 1 else axes[0], pairs)


def trade(value, axis, first):
    size = lax.axis_size(axis)
    if size % 2:
        raise ValueError("odd ring")
    start = 1 if first else 0
    pairs = [(i % size, (i + 1) % size) for i in range(start, size, 2)]
    return lax.ppermute(value, axis, pairs + [(j, i) for i, j in pairs])


def role_sum(value):
    size = lax.axis_size("role")
    if size & (size - 1) or size == 1:
        return lax.psum(value, "role"), jnp.zeros_like(value)
    other = jnp.zeros_like(value)
    step = 1
    while step < size:
        if step > 1:
            value = value + other
        other = lax.ppermute(value, "role", [(i, i ^ step) for i in range(size)])
        step *= 2
    return value, other


def shards(
    ensemble,
    diffusion,
    drift_rows,
    drift_cols,
    observed_cells,
    observed_count,
    observed_values,
    observed_weights,
):
    groups = lax.axis_size("member")
    roles = lax.axis_size("role")
    local, rows, cols = ensemble.shape
    members = local * groups
    width = STEPS
    lanes = max(local, cols)
    cut, low, high = parted(cols)
    strip = struct(width * cut + 4 * width, lanes)
    rest = struct(width * (cols - cut) + 2 * width * width + 2 * width, lanes)
    edge = struct(rows * width + rows, lanes)
    field, kept, early, late, left, right = call(
        functools.partial(pack_kernel, "domain"),
        (struct(rows, cols, local), struct(3, rows, cols), strip, strip, edge, edge),
        ensemble,
        diffusion,
        drift_rows,
        drift_cols,
        name="pack",
        raw=4,
    )
    early = trade(early, "domain", True)
    late = trade(late, "domain", False)
    left, right = shift(right, ("role",), 1), shift(left, ("role",), -1)
    early_rest, late_rest = call(
        functools.partial(turn_kernel, "domain"), (rest, rest), field, left, right, name="turn"
    )
    early_rest = trade(early_rest, "domain", True)
    late_rest = trade(late_rest, "domain", False)
    weight = call(
        functools.partial(weight_kernel, "role"),
        struct(cols, 2 * rows),
        observed_count,
        observed_cells,
        observed_values,
        observed_weights,
        scalars=1,
        raw=3,
        name="weights",
    )
    padded = pltpu.VMEM((rows + 2 * width, cols + 2 * LEAD, local), jnp.float32)
    scratch = (
        padded,
        padded,
        pltpu.VMEM((4, rows + 2 * width, cols + 2 * LEAD, local), jnp.float32),
        pltpu.VMEM((5, 2 * width, cols), jnp.float32),
    )
    middle = call(
        functools.partial(middle_kernel, "domain"),
        struct(rows, high - low, local),
        field,
        kept,
        early,
        late,
        scratch=scratch,
        name="middle",
    )
    sides = call(
        functools.partial(sides_kernel, "domain"),
        struct(rows, cols - high + low, local),
        field,
        kept,
        early,
        late,
        left,
        right,
        early_rest,
        late_rest,
        scratch=scratch,
        name="sides",
    )

    def gathered(value):
        others = [shift(value, ("member",), s) for s in range(1, groups)]
        return jnp.concatenate(others, axis=0) if len(others) > 1 else others[0]

    middle_others = gathered(middle)
    sides_others = gathered(sides)
    parts = (
        ((0, low, high - low),),
        ((0, high, cols - high), (cols - high, 0, low)),
    )
    blocks = members // 128
    size = blocks * (blocks + 1) // 2 * 128 + 8
    square = struct(members, members)
    vector = struct(1, members)

    def deviations(columns):
        one = struct(rows * columns, members, kind=jnp.bfloat16)
        return one, one, struct(rows, cols)

    upper_a, lower_a, centre_a, total, tilt = call(
        functools.partial(first_gram_kernel, groups, parts[0]),
        (*deviations(high - low), square, vector),
        middle,
        middle_others,
        weight,
        name="first_gram",
    )
    gram, upper_b, lower_b, centre_b = call(
        functools.partial(last_gram_kernel, groups, parts[1]),
        (struct(size, 128), *deviations(cols - high + low)),
        sides,
        sides_others,
        weight,
        total,
        tilt,
        scratch=(
            pltpu.VMEM((members, members), jnp.float32),
            pltpu.VMEM((1, members), jnp.float32),
        ),
        name="last_gram",
    )
    first, second = role_sum(gram)
    return call(
        functools.partial(analysis_kernel, parts),
        struct(local, rows, cols),
        first,
        second,
        upper_a,
        upper_b,
        lower_a,
        lower_b,
        centre_a,
        centre_b,
        scratch=(
            pltpu.VMEM((members, members), jnp.float32),
            pltpu.VMEM((2, members, local), jnp.bfloat16),
            pltpu.VMEM((4, cols, local), jnp.float32),
        ),
        name="analysis",
        result=True,
    )


def solution(mesh):
    placed = (
        P("member", "domain", "role"),
        P("domain", "role"),
        P("domain", "role"),
        P("domain", "role"),
        P("domain", None),
        P("domain"),
        P("domain", None),
        P("domain", None),
    )
    return jax.shard_map(
        shards, mesh=mesh, in_specs=placed, out_specs=P("member", "domain", "role"), check_vma=False
    )
```

```python
import functools

import jax
import jax.numpy as jnp
from jax import lax
from jax.experimental import pallas as pl
from jax.experimental.pallas import tpu as pltpu
from jax.sharding import PartitionSpec as P

STEPS = 4
ITERS = 6
LEAD = 16


VMEM = pl.BlockSpec(memory_space=pltpu.VMEM)
SMEM = pl.BlockSpec(memory_space=pltpu.SMEM)
ROOM = 1 << 20


def struct(*shape, kind=jnp.float32):
    return jax.ShapeDtypeStruct(shape, kind)


def near(shape, kind):
    size = jnp.dtype(kind).itemsize
    for place, extent in enumerate(shape[::-1]):
        unit = (128, 32 // jnp.dtype(kind).itemsize, 1)[min(place, 2)]
        size *= -(-extent // unit) * unit
    return size <= ROOM


def call(body, outs, *args, scratch=(), name=None, scalars=0, raw=0, result=False):
    placed = list(args[: scalars + raw])
    for value in args[scalars + raw :]:
        if near(value.shape, value.dtype):
            value = pltpu.with_memory_space_constraint(value, pltpu.VMEM)
        placed.append(value)
    if not result:
        outs = jax.tree.map(
            lambda s: pltpu.VMEM(s.shape, s.dtype) if near(s.shape, s.dtype) else s, outs
        )
    return pl.pallas_call(
        body,
        out_shape=outs,
        in_specs=[SMEM] * scalars + [VMEM] * (len(args) - scalars),
        out_specs=tuple(VMEM for _ in outs) if isinstance(outs, tuple) else VMEM,
        scratch_shapes=scratch,
        name=name,
    )(*placed)


def halves(value):
    upper = value.astype(jnp.bfloat16)
    lower = (value - upper.astype(jnp.float32)).astype(jnp.bfloat16)
    return upper, lower


def dot(a, b, dims=((1,), (0,))):
    return lax.dot_general(a, b, (dims, ((), ())), preferred_element_type=jnp.float32)


def dot3(a, b, dims=((1,), (0,))):
    return dot(a[0], b[0], dims) + (dot(a[0], b[1], dims) + dot(a[1], b[0], dims))


def loop(count, body):
    if count <= 16:
        for i in range(count):
            body(i)
    else:
        lax.fori_loop(0, count, lambda i, c: (body(i), c)[1], 0)


def parted(cols):
    cut = (cols // 2 + 16) // 8 * 8
    return cut, 8, cut - 8


def parity(axis):
    return lax.rem(lax.axis_index(axis), 2)


def pack_kernel(axis, ens, diffusion, drift_rows, drift_cols, field, kept, early, late, left, right):
    odd = parity(axis)
    _, rows, cols = ens.shape
    members = field.shape[2]
    width = STEPS
    cut = parted(cols)[0]
    lanes = pl.ds(0, members)
    for r in range(rows):
        turned = ens[:, r, :].T
        field[r] = turned
        part = pl.ds(r * width, width)
        left[part, lanes] = turned[:width]
        right[part, lanes] = turned[cols - width :]
    for i in range(width):
        part = pl.ds(i * cut, cut)
        early[part, lanes] = field[i + odd * (rows - width), pl.ds(0, cut)]
        late[part, lanes] = field[i + (1 - odd) * (rows - width), pl.ds(0, cut)]
    near_edge = jnp.zeros((rows, cols), jnp.float32)
    far_edge = near_edge
    lane = lax.broadcasted_iota(jnp.int32, (rows, cols), 1)
    for k, part in enumerate((diffusion, drift_rows, drift_cols)):
        at = pl.ds(width * cut + k * width, width)
        top, bottom = part[:width], part[rows - width :]
        early[at, pl.ds(0, cols)] = jnp.where(odd == 0, top, bottom)
        late[at, pl.ds(0, cols)] = jnp.where(odd == 0, bottom, top)
        value = part[...]
        kept[k] = value
        mine = (lane >= k * width) & (lane < (k + 1) * width)
        if k:
            near_edge = jnp.where(mine, pltpu.roll(value, k * width, 1), near_edge)
        else:
            near_edge = jnp.where(mine, value, near_edge)
        far_edge = jnp.where(mine, pltpu.roll(value, (k + 1) * width, 1), far_edge)
    left[pl.ds(rows * width, rows), pl.ds(0, cols)] = near_edge
    right[pl.ds(rows * width, rows), pl.ds(0, cols)] = far_edge


def turn_kernel(axis, field, left, right, early, late):
    rows, cols, members = field.shape
    odd = parity(axis)
    width = STEPS
    area = width * width
    cut = parted(cols)[0]
    size = cols - cut
    lanes = pl.ds(0, members)
    for i in range(width):
        at = pl.ds(i * size, size)
        early[at, lanes] = field[i + odd * (rows - width), pl.ds(cut, size)]
        late[at, lanes] = field[i + (1 - odd) * (rows - width), pl.ds(cut, size)]
    base = width * size
    for i, side in enumerate((left, right)):
        at = pl.ds(base + i * area, area)
        top, bottom = side[pl.ds(0, area)], side[pl.ds((rows - width) * width, area)]
        early[at] = jnp.where(odd == 0, top, bottom)
        late[at] = jnp.where(odd == 0, bottom, top)
        at = pl.ds(base + 2 * area + i * width, width)
        top = side[pl.ds(rows * width, width)]
        bottom = side[pl.ds(rows * width + rows - width, width)]
        early[at] = jnp.where(odd == 0, top, bottom)
        late[at] = jnp.where(odd == 0, bottom, top)


def widen(write, line, columns, members):
    for at, parts in columns:
        size = parts[0].shape[0]
        diffusion, rowwise, colwise = (
            jnp.broadcast_to(p[:, line : line + 1], (size, members)) for p in parts
        )
        here = pl.ds(at, size)
        write(0, here, 1.0 - 4.0 * diffusion - rowwise - colwise)
        write(1, here, diffusion)
        write(2, here, diffusion + rowwise)
        write(3, here, diffusion + colwise)


def spread_rows(spread, lines, columns, members):
    for line, row in lines:

        def write(k, here, value, row=row):
            spread[k, row, here] = value

        widen(write, line, columns, members)


def march(rows, even, odd, spread, ranges, finals, store):
    width = STEPS
    source, target = even, odd
    for step in range(1, STEPS + 1):
        last = step == STEPS

        def advance(r, source=source, target=target, last=last):
            for at, size in finals if last else ranges:
                here = pl.ds(at, size)
                value = (
                    spread[0, r, here] * source[r, here]
                    + spread[1, r, here] * (source[r + 1, here] + source[r, pl.ds(at + 1, size)])
                    + spread[2, r, here] * source[r - 1, here]
                    + spread[3, r, here] * source[r, pl.ds(at - 1, size)]
                )
                if last:
                    store(r - width, at, value)
                else:
                    target[r, here] = value

        loop(rows + 2 * width - 2 * step, lambda i: advance(i + step))
        source, target = target, source


def coefficient_rows(odd, kept, early, late, stage, cut):
    rows, cols = kept.shape[1:]
    width = STEPS
    for k in range(3):
        at = pl.ds(width * cut + k * width, width), pl.ds(0, cols)
        stage[k, pl.ds(0, width)] = jnp.where(odd == 0, early[at], late[at])
        stage[k, pl.ds(width, width)] = jnp.where(odd == 0, late[at], early[at])
    lines = [(i, i) for i in range(1, width)]
    lines += [(width + i, width + rows + i) for i in range(width - 1)]
    inside = [(r, width + r) for r in range(rows)]
    return [kept[k].T for k in range(3)], inside, [stage[k].T for k in range(3)], lines


def middle_kernel(axis, field, kept, early, late, out, one, two, spread, stage):
    rows, cols, members = field.shape
    width = STEPS
    cut, low, high = parted(cols)
    lanes = pl.ds(0, members)
    odd = parity(axis)
    own, inside, beyond, lines = coefficient_rows(odd, kept, early, late, stage, cut)
    for parts, places in ((beyond, lines), (own, inside)):
        spread_rows(spread, places, [(LEAD, [p[:cut] for p in parts])], members)
    here = pl.ds(LEAD, cut)
    for i in range(width):
        part = pl.ds(i * cut, cut)
        one[i + odd * (rows + width), here] = early[part, lanes]
        one[i + (1 - odd) * (rows + width), here] = late[part, lanes]
    for r in range(rows):
        one[width + r, here] = field[r, pl.ds(0, cut)]

    def store(r, at, value):
        out[r] = value

    march(rows, one, two, spread, [(LEAD, cut)], [(LEAD + low, high - low)], store)


def sides_kernel(
    axis,
    field,
    kept,
    early,
    late,
    left,
    right,
    early_rest,
    late_rest,
    out,
    one,
    two,
    spread,
    stage,
):
    rows, cols, members = field.shape
    width = STEPS
    area = width * width
    cut, low, high = parted(cols)
    first, second = low + 8, high - 8
    size = cols - cut
    base = width * size
    lanes = pl.ds(0, members)
    odd = parity(axis)
    own, inside, beyond, lines = coefficient_rows(odd, kept, early, late, stage, cut)
    for side in range(2):
        at = pl.ds(base + 2 * area + side * width, width), pl.ds(0, cols)
        stage[3 + side, pl.ds(0, width)] = jnp.where(odd == 0, early_rest[at], late_rest[at])
        stage[3 + side, pl.ds(width, width)] = jnp.where(odd == 0, late_rest[at], early_rest[at])
    edge = pl.ds(rows * width, rows), pl.ds(0, cols)
    for parts, near_part, far_part, places in (
        (beyond, stage[3].T, stage[4].T, lines),
        (own, left[edge].T, right[edge].T, inside),
    ):
        halo = [slice(k * width, (k + 1) * width) for k in range(3)]
        columns = [
            (LEAD - width, [near_part[h] for h in halo]),
            (LEAD, [p[:first] for p in parts]),
            (LEAD + second, [p[second:] for p in parts]),
            (LEAD + cols, [far_part[h] for h in halo]),
        ]
        spread_rows(spread, places, columns, members)
    before = pl.ds(LEAD - width, width)
    after = pl.ds(LEAD + cols, width)
    for i in range(width):
        for j, strip, rest in (
            (i + odd * (rows + width), early, early_rest),
            (i + (1 - odd) * (rows + width), late, late_rest),
        ):
            one[j, before] = rest[pl.ds(base + i * width, width), lanes]
            one[j, pl.ds(LEAD, first)] = strip[pl.ds(i * cut, first), lanes]
            one[j, pl.ds(LEAD + second, cut - second)] = strip[
                pl.ds(i * cut + second, cut - second), lanes
            ]
            one[j, pl.ds(LEAD + cut, size)] = rest[pl.ds(i * size, size), lanes]
            one[j, after] = rest[pl.ds(base + area + i * width, width), lanes]
    for r in range(rows):
        part = pl.ds(r * width, width)
        one[width + r, before] = left[part, lanes]
        one[width + r, pl.ds(LEAD, first)] = field[r, pl.ds(0, first)]
        one[width + r, pl.ds(LEAD + second, cols - second)] = field[
            r, pl.ds(second, cols - second)
        ]
        one[width + r, after] = right[part, lanes]

    def store(r, at, value):
        if at == LEAD:
            out[r, pl.ds(cols - high, low)] = value
        else:
            out[r, pl.ds(0, cols - high)] = value

    march(
        rows,
        one,
        two,
        spread,
        [(LEAD + second, cols - second + 8), (LEAD - 8, first + 8)],
        [(LEAD + high, cols - high), (LEAD, low)],
        store,
    )


def weight_kernel(axis, count, cells, values, weights, out):
    cols, twice = out.shape
    rows = twice // 2
    slots = cells.shape[1]
    full = cols * lax.axis_size(axis)
    cell = cells[...]
    if full & (full - 1):
        row_of = lax.div(cell, full)
    else:
        row_of = lax.shift_right_logical(cell, full.bit_length() - 1)
    col_of = cell - row_of * full - lax.axis_index(axis) * cols
    slot = lax.broadcasted_iota(jnp.int32, (1, slots), 1)
    plain = jnp.where(slot < count[0], weights[...], 0.0)
    valued = plain * values[...]
    here = lax.broadcasted_iota(jnp.int32, (cols, slots), 0) == col_of
    here = jnp.where(here, 1.0, 0.0).astype(jnp.bfloat16)
    line = lax.broadcasted_iota(jnp.int32, (rows, slots), 0) == row_of
    value = jnp.concatenate([jnp.where(line, plain, 0.0), jnp.where(line, valued, 0.0)], axis=0)
    total = jnp.zeros((cols, twice), jnp.float32)
    for piece in range(3):
        part = value.astype(jnp.bfloat16)
        value = value - part.astype(jnp.float32)
        total = total + dot(here, part, ((1,), (1,)))
    out[...] = total


def gram_kernel(groups, pieces, own, others, weight, upper, lower, centre, total, tilt):
    rows, size, _ = own.shape
    members = total.shape[0]
    cols = weight.shape[0]
    many = next(n for n in (4, 2, 1) if rows % n == 0)
    depth = many * size

    def block(b):
        def cells(ref, start):
            value = ref[pl.ds(start + b * many, many)]
            return value.reshape(depth, value.shape[2])

        parts = [cells(own, 0)] + [cells(others, g * rows) for g in range(groups - 1)]
        value = jnp.concatenate(parts, axis=1) if groups > 1 else parts[0]
        mean = jnp.sum(value, axis=1, keepdims=True) * (1.0 / members)
        deviation = value - mean
        plain, valued = [], []
        for i in range(many):
            r = b * many + i
            row = jnp.zeros((1, cols), jnp.float32)
            for start, column, length in pieces:
                place = lax.broadcasted_iota(jnp.int32, (length, cols), 0) + column
                here = place == lax.broadcasted_iota(jnp.int32, (length, cols), 1)
                part = mean[i * size + start : i * size + start + length]
                row = row + jnp.sum(jnp.where(here, part, 0.0), axis=0, keepdims=True)
                source = weight[pl.ds(column, length)]
                line = lax.broadcasted_iota(jnp.int32, source.shape, 1)
                plain.append(jnp.sum(jnp.where(line == r, source, 0.0), axis=1, keepdims=True))
                valued.append(
                    jnp.sum(jnp.where(line == r + rows, source, 0.0), axis=1, keepdims=True)
                )
            centre[pl.ds(r, 1)] = row
        plain = jnp.concatenate(plain, axis=0)
        valued = jnp.concatenate(valued, axis=0)
        high, low = halves(deviation)
        at = pl.ds(b * depth, depth)
        upper[at] = high
        lower[at] = low
        turned = (deviation * plain).T
        total[...] += dot3(halves(turned), (high, low))
        tilt[...] += jnp.sum(deviation * (valued - plain * mean), axis=0, keepdims=True)

    loop(rows // many, block)


def first_gram_kernel(groups, pieces, own, others, weight, upper, lower, centre, total, tilt):
    total[...] = jnp.zeros_like(total)
    tilt[...] = jnp.zeros_like(tilt)
    gram_kernel(groups, pieces, own, others, weight, upper, lower, centre, total, tilt)


def last_gram_kernel(
    groups, pieces, own, others, weight, before, tilted, gram, upper, lower, centre, total, tilt
):
    total[...] = before[...]
    tilt[...] = tilted[...]
    gram_kernel(groups, pieces, own, others, weight, upper, lower, centre, total, tilt)
    pull = gram.shape[0] - 8
    blocks = total.shape[0] // 128
    innovation = tilt[...]
    at = 0
    gram[pl.ds(pull, 8)] = jnp.zeros((8, 128), jnp.float32)
    for i in range(blocks):
        gram[pl.ds(pull + i, 1)] = innovation[:, i * 128 : (i + 1) * 128]
        for j in range(i, blocks):
            gram[pl.ds(at, 128)] = total[i * 128 : (i + 1) * 128, j * 128 : (j + 1) * 128]
            at += 128


def analysis_kernel(layout, first, second, *rest):
    uppers, lowers, centres = rest[0:2], rest[2:4], rest[4:6]
    out, whole, chosen, natural = rest[6:]
    local, rows, cols = out.shape
    members = whole.shape[0]
    blocks = members // 128
    pull = first.shape[0] - 8
    at = 0
    for i in range(blocks):
        for j in range(i, blocks):
            block = first[pl.ds(at, 128)] + second[pl.ds(at, 128)]
            whole[i * 128 : (i + 1) * 128, j * 128 : (j + 1) * 128] = block
            if j > i:
                whole[j * 128 : (j + 1) * 128, i * 128 : (i + 1) * 128] = block.T
            at += 128
    innovation = jnp.concatenate(
        [first[pl.ds(pull + i, 1)] + second[pl.ds(pull + i, 1)] for i in range(blocks)],
        axis=1,
    )
    down = lax.broadcasted_iota(jnp.int32, (members, members), 0)
    across = lax.broadcasted_iota(jnp.int32, (members, members), 1)
    identity = jnp.where(down == across, 1.0, 0.0)
    matrix = whole[...] + (members - 1.0) * identity
    parts = halves(matrix)
    square = dot3(parts, parts)
    squares = jnp.sum(jnp.sum(matrix * matrix, axis=1, keepdims=True), axis=0, keepdims=True)
    scaling = jnp.sqrt(squares)
    current = matrix * (1.0 / scaling)
    square = square * (1.0 / scaling) * (1.0 / scaling)
    inverse = None
    for repeat in range(0, ITERS, 2):
        if repeat:
            parts = halves(current)
            square = dot3(parts, parts)
        inner = 0.0625 * square - 0.5625 * current
        outer = 2.25 * identity - 2.4375 * current + 1.6875 * square
        both = outer + dot3(halves(square), halves(inner))
        both_parts = halves(both)
        if repeat + 2 < ITERS:
            twice = dot3(both_parts, both_parts)
            current = dot3(halves(current), halves(twice))
        inverse = both if inverse is None else dot3(halves(inverse), both_parts)
    once = jnp.sum(inverse * innovation, axis=1, keepdims=True)
    once_row = jnp.sum(jnp.where(down == across, once, 0.0), axis=0, keepdims=True)
    shifted = jnp.sum(inverse * once_row, axis=1, keepdims=True) * (1.0 / scaling)
    factor = jnp.sqrt((members - 1.0) / scaling)
    mixing = (factor * inverse + shifted)[:, :local]
    high, low = halves(mixing)
    chosen[:, :local] = high
    chosen[:, local:] = low
    many = next(n for n in (4, 2, 1) if rows % n == 0)

    def block(b):
        for pieces, upper, lower in zip(layout, uppers, lowers):
            size = upper.shape[0] // rows
            at = pl.ds(b * many * size, many * size)
            value = dot(upper[at], chosen[...])
            value = value[:, :local] + value[:, local:] + dot(lower[at], chosen[:, :local])
            for i in range(many):
                for start, column, length in pieces:
                    natural[i, pl.ds(column, length)] = value[
                        i * size + start : i * size + start + length
                    ]
        for i in range(many):
            r = b * many + i
            middle_row = centres[0][pl.ds(r, 1)] + centres[1][pl.ds(r, 1)]
            out[:, r, :] = natural[i].T + middle_row

    loop(rows // many, block)


def shift(value, axes, *moves):
    sizes = [lax.axis_size(a) for a in axes]
    pairs = []
    total = 1
    for s in sizes:
        total *= s
    for flat in range(total):
        rest, place = flat, []
        for s in reversed(sizes):
            place.append(rest % s)
            rest //= s
        place = place[::-1]
        to = 0
        for s, p, m in zip(sizes, place, moves):
            to = to * s + (p + m) % s
        pairs.append((flat, to))
    return lax.ppermute(value, axes if len(axes) > 1 else axes[0], pairs)


def trade(value, axis, first):
    size = lax.axis_size(axis)
    if size % 2:
        raise ValueError("odd ring")
    start = 1 if first else 0
    pairs = [(i % size, (i + 1) % size) for i in range(start, size, 2)]
    return lax.ppermute(value, axis, pairs + [(j, i) for i, j in pairs])


def role_sum(value):
    size = lax.axis_size("role")
    if size & (size - 1) or size == 1:
        return lax.psum(value, "role"), jnp.zeros_like(value)
    other = jnp.zeros_like(value)
    step = 1
    while step < size:
        if step > 1:
            value = value + other
        other = lax.ppermute(value, "role", [(i, i ^ step) for i in range(size)])
        step *= 2
    return value, other


def shards(
    ensemble,
    diffusion,
    drift_rows,
    drift_cols,
    observed_cells,
    observed_count,
    observed_values,
    observed_weights,
):
    groups = lax.axis_size("member")
    roles = lax.axis_size("role")
    local, rows, cols = ensemble.shape
    members = local * groups
    width = STEPS
    lanes = max(local, cols)
    cut, low, high = parted(cols)
    strip = struct(width * cut + 4 * width, lanes)
    rest = struct(width * (cols - cut) + 2 * width * width + 2 * width, lanes)
    edge = struct(rows * width + rows, lanes)
    field, kept, early, late, left, right = call(
        functools.partial(pack_kernel, "domain"),
        (struct(rows, cols, local), struct(3, rows, cols), strip, strip, edge, edge),
        ensemble,
        diffusion,
        drift_rows,
        drift_cols,
        name="pack",
        raw=4,
    )
    early = trade(early, "domain", True)
    late = trade(late, "domain", False)
    left, right = shift(right, ("role",), 1), shift(left, ("role",), -1)
    early_rest, late_rest = call(
        functools.partial(turn_kernel, "domain"), (rest, rest), field, left, right, name="turn"
    )
    early_rest = trade(early_rest, "domain", True)
    late_rest = trade(late_rest, "domain", False)
    weight = call(
        functools.partial(weight_kernel, "role"),
        struct(cols, 2 * rows),
        observed_count,
        observed_cells,
        observed_values,
        observed_weights,
        scalars=1,
        raw=3,
        name="weights",
    )
    padded = pltpu.VMEM((rows + 2 * width, cols + 2 * LEAD, local), jnp.float32)
    scratch = (
        padded,
        padded,
        pltpu.VMEM((4, rows + 2 * width, cols + 2 * LEAD, local), jnp.float32),
        pltpu.VMEM((5, 2 * width, cols), jnp.float32),
    )
    middle = call(
        functools.partial(middle_kernel, "domain"),
        struct(rows, high - low, local),
        field,
        kept,
        early,
        late,
        scratch=scratch,
        name="middle",
    )
    sides = call(
        functools.partial(sides_kernel, "domain"),
        struct(rows, cols - high + low, local),
        field,
        kept,
        early,
        late,
        left,
        right,
        early_rest,
        late_rest,
        scratch=scratch,
        name="sides",
    )

    def gathered(value):
        others = [shift(value, ("member",), s) for s in range(1, groups)]
        return jnp.concatenate(others, axis=0) if len(others) > 1 else others[0]

    middle_others = gathered(middle)
    sides_others = gathered(sides)
    parts = (
        ((0, low, high - low),),
        ((0, high, cols - high), (cols - high, 0, low)),
    )
    blocks = members // 128
    size = blocks * (blocks + 1) // 2 * 128 + 8
    square = struct(members, members)
    vector = struct(1, members)

    def deviations(columns):
        one = struct(rows * columns, members, kind=jnp.bfloat16)
        return one, one, struct(rows, cols)

    upper_a, lower_a, centre_a, total, tilt = call(
        functools.partial(first_gram_kernel, groups, parts[0]),
        (*deviations(high - low), square, vector),
        middle,
        middle_others,
        weight,
        name="first_gram",
    )
    gram, upper_b, lower_b, centre_b = call(
        functools.partial(last_gram_kernel, groups, parts[1]),
        (struct(size, 128), *deviations(cols - high + low)),
        sides,
        sides_others,
        weight,
        total,
        tilt,
        scratch=(
            pltpu.VMEM((members, members), jnp.float32),
            pltpu.VMEM((1, members), jnp.float32),
        ),
        name="last_gram",
    )
    first, second = role_sum(gram)
    return call(
        functools.partial(analysis_kernel, parts),
        struct(local, rows, cols),
        first,
        second,
        upper_a,
        upper_b,
        lower_a,
        lower_b,
        centre_a,
        centre_b,
        scratch=(
            pltpu.VMEM((members, members), jnp.float32),
            pltpu.VMEM((members, 2 * local), jnp.bfloat16),
            pltpu.VMEM((4, cols, local), jnp.float32),
        ),
        name="analysis",
        result=True,
    )


def solution(mesh):
    placed = (
        P("member", "domain", "role"),
        P("domain", "role"),
        P("domain", "role"),
        P("domain", "role"),
        P("domain", None),
        P("domain"),
        P("domain", None),
        P("domain", None),
    )
    return jax.shard_map(
        shards, mesh=mesh, in_specs=placed, out_specs=P("member", "domain", "role"), check_vma=False
    )
```

```python
import functools

import jax
import jax.numpy as jnp
from jax import lax
from jax.experimental import pallas as pl
from jax.experimental.pallas import tpu as pltpu
from jax.sharding import PartitionSpec as P

STEPS = 4
ITERS = 6
LEAD = 16


VMEM = pl.BlockSpec(memory_space=pltpu.VMEM)
SMEM = pl.BlockSpec(memory_space=pltpu.SMEM)
ROOM = 1 << 20


def struct(*shape, kind=jnp.float32):
    return jax.ShapeDtypeStruct(shape, kind)


def near(shape, kind):
    size = jnp.dtype(kind).itemsize
    for place, extent in enumerate(shape[::-1]):
        unit = (128, 32 // jnp.dtype(kind).itemsize, 1)[min(place, 2)]
        size *= -(-extent // unit) * unit
    return size <= ROOM


def call(body, outs, *args, scratch=(), name=None, scalars=0, raw=0, result=False):
    placed = list(args[: scalars + raw])
    for value in args[scalars + raw :]:
        if near(value.shape, value.dtype):
            value = pltpu.with_memory_space_constraint(value, pltpu.VMEM)
        placed.append(value)
    if not result:
        outs = jax.tree.map(
            lambda s: pltpu.VMEM(s.shape, s.dtype) if near(s.shape, s.dtype) else s, outs
        )
    return pl.pallas_call(
        body,
        out_shape=outs,
        in_specs=[SMEM] * scalars + [VMEM] * (len(args) - scalars),
        out_specs=tuple(VMEM for _ in outs) if isinstance(outs, tuple) else VMEM,
        scratch_shapes=scratch,
        name=name,
    )(*placed)


def halves(value):
    upper = value.astype(jnp.bfloat16)
    lower = (value - upper.astype(jnp.float32)).astype(jnp.bfloat16)
    return upper, lower


def dot(a, b, dims=((1,), (0,))):
    return lax.dot_general(a, b, (dims, ((), ())), preferred_element_type=jnp.float32)


def dot3(a, b, dims=((1,), (0,))):
    return dot(a[0], b[0], dims) + (dot(a[0], b[1], dims) + dot(a[1], b[0], dims))


def loop(count, body):
    if count <= 16:
        for i in range(count):
            body(i)
    else:
        lax.fori_loop(0, count, lambda i, c: (body(i), c)[1], 0)


def parted(cols):
    cut = (cols // 2 + 16) // 8 * 8
    return cut, 8, cut - 8


def parity(axis):
    return lax.rem(lax.axis_index(axis), 2)


def pack_kernel(axis, ens, diffusion, drift_rows, drift_cols, field, kept, early, late, left, right):
    odd = parity(axis)
    _, rows, cols = ens.shape
    members = field.shape[2]
    width = STEPS
    cut = parted(cols)[0]
    lanes = pl.ds(0, members)
    for r in range(rows):
        turned = ens[:, r, :].T
        field[r] = turned
        part = pl.ds(r * width, width)
        left[part, lanes] = turned[:width]
        right[part, lanes] = turned[cols - width :]
    for i in range(width):
        part = pl.ds(i * cut, cut)
        early[part, lanes] = field[i + odd * (rows - width), pl.ds(0, cut)]
        late[part, lanes] = field[i + (1 - odd) * (rows - width), pl.ds(0, cut)]
    near_edge = jnp.zeros((rows, cols), jnp.float32)
    far_edge = near_edge
    lane = lax.broadcasted_iota(jnp.int32, (rows, cols), 1)
    for k, part in enumerate((diffusion, drift_rows, drift_cols)):
        at = pl.ds(width * cut + k * width, width)
        top, bottom = part[:width], part[rows - width :]
        early[at, pl.ds(0, cols)] = jnp.where(odd == 0, top, bottom)
        late[at, pl.ds(0, cols)] = jnp.where(odd == 0, bottom, top)
        value = part[...]
        kept[k] = value
        mine = (lane >= k * width) & (lane < (k + 1) * width)
        if k:
            near_edge = jnp.where(mine, pltpu.roll(value, k * width, 1), near_edge)
        else:
            near_edge = jnp.where(mine, value, near_edge)
        far_edge = jnp.where(mine, pltpu.roll(value, (k + 1) * width, 1), far_edge)
    left[pl.ds(rows * width, rows), pl.ds(0, cols)] = near_edge
    right[pl.ds(rows * width, rows), pl.ds(0, cols)] = far_edge


def turn_kernel(axis, field, left, right, early, late):
    rows, cols, members = field.shape
    odd = parity(axis)
    width = STEPS
    area = width * width
    cut = parted(cols)[0]
    size = cols - cut
    lanes = pl.ds(0, members)
    for i in range(width):
        at = pl.ds(i * size, size)
        early[at, lanes] = field[i + odd * (rows - width), pl.ds(cut, size)]
        late[at, lanes] = field[i + (1 - odd) * (rows - width), pl.ds(cut, size)]
    base = width * size
    for i, side in enumerate((left, right)):
        at = pl.ds(base + i * area, area)
        top, bottom = side[pl.ds(0, area)], side[pl.ds((rows - width) * width, area)]
        early[at] = jnp.where(odd == 0, top, bottom)
        late[at] = jnp.where(odd == 0, bottom, top)
        at = pl.ds(base + 2 * area + i * width, width)
        top = side[pl.ds(rows * width, width)]
        bottom = side[pl.ds(rows * width + rows - width, width)]
        early[at] = jnp.where(odd == 0, top, bottom)
        late[at] = jnp.where(odd == 0, bottom, top)


def widen(write, line, columns, members):
    for at, parts in columns:
        size = parts[0].shape[0]
        diffusion, rowwise, colwise = (
            jnp.broadcast_to(p[:, line : line + 1], (size, members)) for p in parts
        )
        here = pl.ds(at, size)
        write(0, here, 1.0 - 4.0 * diffusion - rowwise - colwise)
        write(1, here, diffusion)
        write(2, here, diffusion + rowwise)
        write(3, here, diffusion + colwise)


def spread_rows(spread, lines, columns, members):
    for line, row in lines:

        def write(k, here, value, row=row):
            spread[k, row, here] = value

        widen(write, line, columns, members)


def march(rows, even, odd, spread, ranges, finals, store):
    width = STEPS
    source, target = even, odd
    for step in range(1, STEPS + 1):
        last = step == STEPS

        def advance(r, source=source, target=target, last=last):
            for at, size in finals if last else ranges:
                here = pl.ds(at, size)
                value = (
                    spread[0, r, here] * source[r, here]
                    + spread[1, r, here] * (source[r + 1, here] + source[r, pl.ds(at + 1, size)])
                    + spread[2, r, here] * source[r - 1, here]
                    + spread[3, r, here] * source[r, pl.ds(at - 1, size)]
                )
                if last:
                    store(r - width, at, value)
                else:
                    target[r, here] = value

        loop(rows + 2 * width - 2 * step, lambda i: advance(i + step))
        source, target = target, source


def coefficient_rows(odd, kept, early, late, stage, cut):
    rows, cols = kept.shape[1:]
    width = STEPS
    for k in range(3):
        at = pl.ds(width * cut + k * width, width), pl.ds(0, cols)
        stage[k, pl.ds(0, width)] = jnp.where(odd == 0, early[at], late[at])
        stage[k, pl.ds(width, width)] = jnp.where(odd == 0, late[at], early[at])
    lines = [(i, i) for i in range(1, width)]
    lines += [(width + i, width + rows + i) for i in range(width - 1)]
    inside = [(r, width + r) for r in range(rows)]
    return [kept[k].T for k in range(3)], inside, [stage[k].T for k in range(3)], lines


def middle_kernel(axis, field, kept, early, late, after, out, one, two, spread, stage):
    rows, cols, members = field.shape
    width = STEPS
    cut, low, high = parted(cols)
    lanes = pl.ds(0, members)
    odd = parity(axis)
    own, inside, beyond, lines = coefficient_rows(odd, kept, early, late, stage, cut)
    for parts, places in ((beyond, lines), (own, inside)):
        spread_rows(spread, places, [(LEAD, [p[:cut] for p in parts])], members)
    here = pl.ds(LEAD, cut)
    for i in range(width):
        part = pl.ds(i * cut, cut)
        one[i + odd * (rows + width), here] = early[part, lanes]
        one[i + (1 - odd) * (rows + width), here] = late[part, lanes]
    for r in range(rows):
        one[width + r, here] = field[r, pl.ds(0, cut)]

    def store(r, at, value):
        out[r] = value

    march(rows, one, two, spread, [(LEAD, cut)], [(LEAD + low, high - low)], store)


def sides_kernel(
    axis,
    field,
    kept,
    early,
    late,
    left,
    right,
    early_rest,
    late_rest,
    out,
    one,
    two,
    spread,
    stage,
):
    rows, cols, members = field.shape
    width = STEPS
    area = width * width
    cut, low, high = parted(cols)
    first, second = low + 8, high - 8
    size = cols - cut
    base = width * size
    lanes = pl.ds(0, members)
    odd = parity(axis)
    own, inside, beyond, lines = coefficient_rows(odd, kept, early, late, stage, cut)
    for side in range(2):
        at = pl.ds(base + 2 * area + side * width, width), pl.ds(0, cols)
        stage[3 + side, pl.ds(0, width)] = jnp.where(odd == 0, early_rest[at], late_rest[at])
        stage[3 + side, pl.ds(width, width)] = jnp.where(odd == 0, late_rest[at], early_rest[at])
    edge = pl.ds(rows * width, rows), pl.ds(0, cols)
    for parts, near_part, far_part, places in (
        (beyond, stage[3].T, stage[4].T, lines),
        (own, left[edge].T, right[edge].T, inside),
    ):
        halo = [slice(k * width, (k + 1) * width) for k in range(3)]
        columns = [
            (LEAD - width, [near_part[h] for h in halo]),
            (LEAD, [p[:first] for p in parts]),
            (LEAD + second, [p[second:] for p in parts]),
            (LEAD + cols, [far_part[h] for h in halo]),
        ]
        spread_rows(spread, places, columns, members)
    before = pl.ds(LEAD - width, width)
    after = pl.ds(LEAD + cols, width)
    for i in range(width):
        for j, strip, rest in (
            (i + odd * (rows + width), early, early_rest),
            (i + (1 - odd) * (rows + width), late, late_rest),
        ):
            one[j, before] = rest[pl.ds(base + i * width, width), lanes]
            one[j, pl.ds(LEAD, first)] = strip[pl.ds(i * cut, first), lanes]
            one[j, pl.ds(LEAD + second, cut - second)] = strip[
                pl.ds(i * cut + second, cut - second), lanes
            ]
            one[j, pl.ds(LEAD + cut, size)] = rest[pl.ds(i * size, size), lanes]
            one[j, after] = rest[pl.ds(base + area + i * width, width), lanes]
    for r in range(rows):
        part = pl.ds(r * width, width)
        one[width + r, before] = left[part, lanes]
        one[width + r, pl.ds(LEAD, first)] = field[r, pl.ds(0, first)]
        one[width + r, pl.ds(LEAD + second, cols - second)] = field[
            r, pl.ds(second, cols - second)
        ]
        one[width + r, after] = right[part, lanes]

    def store(r, at, value):
        if at == LEAD:
            out[r, pl.ds(cols - high, low)] = value
        else:
            out[r, pl.ds(0, cols - high)] = value

    march(
        rows,
        one,
        two,
        spread,
        [(LEAD + second, cols - second + 8), (LEAD - 8, first + 8)],
        [(LEAD + high, cols - high), (LEAD, low)],
        store,
    )


def weight_kernel(axis, count, cells, values, weights, out):
    cols, twice = out.shape
    rows = twice // 2
    slots = cells.shape[1]
    full = cols * lax.axis_size(axis)
    cell = cells[...]
    if full & (full - 1):
        row_of = lax.div(cell, full)
    else:
        row_of = lax.shift_right_logical(cell, full.bit_length() - 1)
    col_of = cell - row_of * full - lax.axis_index(axis) * cols
    slot = lax.broadcasted_iota(jnp.int32, (1, slots), 1)
    plain = jnp.where(slot < count[0], weights[...], 0.0)
    valued = plain * values[...]
    here = lax.broadcasted_iota(jnp.int32, (cols, slots), 0) == col_of
    here = jnp.where(here, 1.0, 0.0).astype(jnp.bfloat16)
    line = lax.broadcasted_iota(jnp.int32, (rows, slots), 0) == row_of
    value = jnp.concatenate([jnp.where(line, plain, 0.0), jnp.where(line, valued, 0.0)], axis=0)
    total = jnp.zeros((cols, twice), jnp.float32)
    for piece in range(3):
        part = value.astype(jnp.bfloat16)
        value = value - part.astype(jnp.float32)
        total = total + dot(here, part, ((1,), (1,)))
    out[...] = total


def cell_weights(rows, pieces, weight, b, many):
    plain, valued = [], []
    for i in range(many):
        r = b * many + i
        for start, column, length in pieces:
            source = weight[pl.ds(column, length)]
            line = lax.broadcasted_iota(jnp.int32, source.shape, 1)
            plain.append(jnp.sum(jnp.where(line == r, source, 0.0), axis=1, keepdims=True))
            valued.append(jnp.sum(jnp.where(line == r + rows, source, 0.0), axis=1, keepdims=True))
    return jnp.concatenate(plain, axis=0), jnp.concatenate(valued, axis=0)


def lay_rows(pieces, column_of, size, centre, b, many):
    cols = centre.shape[1]
    for i in range(many):
        row = jnp.zeros((1, cols), jnp.float32)
        for start, column, length in pieces:
            place = lax.broadcasted_iota(jnp.int32, (length, cols), 0) + column
            here = place == lax.broadcasted_iota(jnp.int32, (length, cols), 1)
            part = column_of[i * size + start : i * size + start + length]
            row = row + jnp.sum(jnp.where(here, part, 0.0), axis=0, keepdims=True)
        centre[pl.ds(b * many + i, 1)] = row


def grouping(rows):
    return next(n for n in (4, 2, 1) if rows % n == 0)


def cells_of(ref, b, many, start=0):
    value = ref[pl.ds(start + b * many, many)]
    return value.reshape(many * value.shape[1], value.shape[2])


def lane_mean(value):
    return jnp.sum(value, axis=1, keepdims=True) * (1.0 / value.shape[1])


def wide(parts):
    return jnp.concatenate(parts, axis=1)


def dot_wide(a, both, size):
    value = dot(a[0], both)
    return value[:, :size] + value[:, size:] + dot(a[1], both[:, :size])


def gram_kernel(groups, pieces, own, others, weight, upper, lower, centre, total, tilt):
    rows, size, _ = own.shape
    members = total.shape[0]
    many = grouping(rows)
    depth = many * size

    def block(b):
        parts = [cells_of(own, b, many)]
        parts += [cells_of(others, b, many, g * rows) for g in range(groups - 1)]
        value = wide(parts) if groups > 1 else parts[0]
        mean = lane_mean(value)
        deviation = value - mean
        plain, valued = cell_weights(rows, pieces, weight, b, many)
        lay_rows(pieces, mean, size, centre, b, many)
        high, low = halves(deviation)
        at = pl.ds(b * depth, depth)
        upper[at] = high
        lower[at] = low
        turned = (deviation * plain).T
        total[...] += dot3(halves(turned), (high, low))
        tilt[...] += jnp.sum(deviation * (valued - plain * mean), axis=0, keepdims=True)

    loop(rows // many, block)


def own_gram_kernel(layout, middle, sides, weight, total):
    local = total.shape[0]
    total[...] = jnp.zeros_like(total)
    for pieces, own in zip(layout, (middle, sides)):
        rows, size, _ = own.shape
        many = grouping(rows)

        def block(b, pieces=pieces, own=own, rows=rows, many=many):
            value = cells_of(own, b, many)
            deviation = value - lane_mean(value)
            plain, _ = cell_weights(rows, pieces, weight, b, many)
            turned = (deviation * plain).T
            total[...] += dot_wide(halves(turned), wide(halves(deviation)), local)

        loop(rows // many, block)


def cross_kernel(pieces, own, other, weight, after, *rest):
    before, (upper, lower, centre, total) = rest[:-4], rest[-4:]
    total[...] = before[0][...] if before else jnp.zeros_like(total)
    rows, size, local = own.shape
    many = grouping(rows)
    depth = many * size
    left, right = pl.ds(0, local), pl.ds(local, local)

    def block(b):
        value, partner = cells_of(own, b, many), cells_of(other, b, many)
        mean_own, mean_partner = lane_mean(value), lane_mean(partner)
        mean = 0.5 * (mean_own + mean_partner)
        apart = 0.5 * (mean_own - mean_partner)
        deviation, counter = value - mean, partner - mean
        plain, valued = cell_weights(rows, pieces, weight, b, many)
        lay_rows(pieces, mean, size, centre, b, many)
        at = pl.ds(b * depth, depth)
        high, low = halves(deviation)
        upper[at, left] = high
        lower[at, left] = low
        high, low = halves(counter)
        upper[at, right] = high
        lower[at, right] = low
        turned = (deviation * plain).T
        total[pl.ds(0, local)] += dot_wide(halves(turned), wide((high, low)), local)
        pull = valued - plain * mean
        tie = plain * apart

        def add(row, columns):
            total[pl.ds(local + row, 1)] += jnp.sum(columns, axis=0, keepdims=True)

        add(0, deviation * pull)
        add(1, counter * pull)
        add(2, deviation * tie)
        add(3, counter * -tie)
        add(4, jnp.broadcast_to(tie * apart, deviation.shape))

    loop(rows // many, block)


def first_gram_kernel(groups, pieces, own, others, weight, upper, lower, centre, total, tilt):
    total[...] = jnp.zeros_like(total)
    tilt[...] = jnp.zeros_like(tilt)
    gram_kernel(groups, pieces, own, others, weight, upper, lower, centre, total, tilt)


def last_gram_kernel(
    groups, pieces, own, others, weight, before, tilted, gram, upper, lower, centre, total, tilt
):
    total[...] = before[...]
    tilt[...] = tilted[...]
    gram_kernel(groups, pieces, own, others, weight, upper, lower, centre, total, tilt)
    pull = gram.shape[0] - 8
    blocks = total.shape[0] // 128
    innovation = tilt[...]
    at = 0
    gram[pl.ds(pull, 8)] = jnp.zeros((8, 128), jnp.float32)
    for i in range(blocks):
        gram[pl.ds(pull + i, 1)] = innovation[:, i * 128 : (i + 1) * 128]
        for j in range(i, blocks):
            gram[pl.ds(at, 128)] = total[i * 128 : (i + 1) * 128, j * 128 : (j + 1) * 128]
            at += 128


def assemble(first, second, whole):
    blocks = whole.shape[0] // 128
    pull = first.shape[0] - 8
    at = 0
    for i in range(blocks):
        for j in range(i, blocks):
            block = first[pl.ds(at, 128)] + second[pl.ds(at, 128)]
            whole[i * 128 : (i + 1) * 128, j * 128 : (j + 1) * 128] = block
            if j > i:
                whole[j * 128 : (j + 1) * 128, i * 128 : (i + 1) * 128] = block.T
            at += 128
    return wide([first[pl.ds(pull + i, 1)] + second[pl.ds(pull + i, 1)] for i in range(blocks)])


def assemble_pair(first, second, own, other, whole):
    local = own.shape[1]
    cross = first[pl.ds(0, local)] + second[pl.ds(0, local)]
    rest = first[pl.ds(local, 8)] + second[pl.ds(local, 8)]
    whole[:local, local:] = cross
    whole[local:, :local] = cross.T
    square = rest[4:5]
    diagonal = lax.broadcasted_iota(jnp.int32, (local, local), 0) == lax.broadcasted_iota(
        jnp.int32, (local, local), 1
    )
    for i, part in enumerate((own, other)):
        tie = rest[2 + i : 3 + i]
        upright = jnp.sum(jnp.where(diagonal, tie, 0.0), axis=1, keepdims=True)
        at = slice(i * local, (i + 1) * local)
        whole[at, at] = part[...] + upright + (tie - square)
    return wide([rest[0:1], rest[1:2]])


def analysis_kernel(layout, pair, *rest):
    if pair:
        first, second, own, other, *rest = rest
    else:
        first, second, *rest = rest
    uppers, lowers, centres = rest[0:2], rest[2:4], rest[4:6]
    out, whole, chosen, natural = rest[6:]
    local, rows, cols = out.shape
    members = whole.shape[0]
    if pair:
        innovation = assemble_pair(first, second, own, other, whole)
    else:
        innovation = assemble(first, second, whole)
    down = lax.broadcasted_iota(jnp.int32, (members, members), 0)
    across = lax.broadcasted_iota(jnp.int32, (members, members), 1)
    identity = jnp.where(down == across, 1.0, 0.0)
    matrix = whole[...] + (members - 1.0) * identity
    parts = halves(matrix)
    square = dot3(parts, parts)
    squares = jnp.sum(jnp.sum(matrix * matrix, axis=1, keepdims=True), axis=0, keepdims=True)
    scaling = jnp.sqrt(squares)
    current = matrix * (1.0 / scaling)
    square = square * (1.0 / scaling) * (1.0 / scaling)
    inverse = None
    for repeat in range(0, ITERS, 2):
        if repeat:
            parts = halves(current)
            square = dot3(parts, parts)
        inner = 0.0625 * square - 0.5625 * current
        outer = 2.25 * identity - 2.4375 * current + 1.6875 * square
        both = outer + dot3(halves(square), halves(inner))
        both_parts = halves(both)
        if repeat + 2 < ITERS:
            twice = dot3(both_parts, both_parts)
            current = dot3(halves(current), halves(twice))
        inverse = both if inverse is None else dot3(halves(inverse), both_parts)
    once = jnp.sum(inverse * innovation, axis=1, keepdims=True)
    once_row = jnp.sum(jnp.where(down == across, once, 0.0), axis=0, keepdims=True)
    shifted = jnp.sum(inverse * once_row, axis=1, keepdims=True) * (1.0 / scaling)
    factor = jnp.sqrt((members - 1.0) / scaling)
    mixing = (factor * inverse + shifted)[:, :local]
    high, low = halves(mixing)
    chosen[:, :local] = high
    chosen[:, local:] = low
    many = grouping(rows)

    def block(b):
        for pieces, upper, lower in zip(layout, uppers, lowers):
            size = upper.shape[0] // rows
            at = pl.ds(b * many * size, many * size)
            value = dot(upper[at], chosen[...])
            value = value[:, :local] + value[:, local:] + dot(lower[at], chosen[:, :local])
            for i in range(many):
                for start, column, length in pieces:
                    natural[i, pl.ds(column, length)] = value[
                        i * size + start : i * size + start + length
                    ]
        for i in range(many):
            r = b * many + i
            middle_row = centres[0][pl.ds(r, 1)] + centres[1][pl.ds(r, 1)]
            out[:, r, :] = natural[i].T + middle_row

    loop(rows // many, block)


def shift(value, axes, *moves):
    sizes = [lax.axis_size(a) for a in axes]
    pairs = []
    total = 1
    for s in sizes:
        total *= s
    for flat in range(total):
        rest, place = flat, []
        for s in reversed(sizes):
            place.append(rest % s)
            rest //= s
        place = place[::-1]
        to = 0
        for s, p, m in zip(sizes, place, moves):
            to = to * s + (p + m) % s
        pairs.append((flat, to))
    return lax.ppermute(value, axes if len(axes) > 1 else axes[0], pairs)


def trade(value, axis, first):
    size = lax.axis_size(axis)
    if size % 2:
        raise ValueError("odd ring")
    start = 1 if first else 0
    pairs = [(i % size, (i + 1) % size) for i in range(start, size, 2)]
    return lax.ppermute(value, axis, pairs + [(j, i) for i, j in pairs])


def role_sums(value):
    size = lax.axis_size("role")
    if size & (size - 1) or size == 1:
        return [(lax.psum(value, "role"), jnp.zeros_like(value))]
    stages = []
    step = 1
    while step < size:
        other = lax.ppermute(value, "role", [(i, i ^ step) for i in range(size)])
        stages.append((value, other))
        value = value + other
        step *= 2
    return stages


def shards(
    ensemble,
    diffusion,
    drift_rows,
    drift_cols,
    observed_cells,
    observed_count,
    observed_values,
    observed_weights,
):
    groups = lax.axis_size("member")
    roles = lax.axis_size("role")
    local, rows, cols = ensemble.shape
    members = local * groups
    width = STEPS
    lanes = max(local, cols)
    cut, low, high = parted(cols)
    strip = struct(width * cut + 4 * width, lanes)
    rest = struct(width * (cols - cut) + 2 * width * width + 2 * width, lanes)
    edge = struct(rows * width + rows, lanes)
    field, kept, early, late, left, right = call(
        functools.partial(pack_kernel, "domain"),
        (struct(rows, cols, local), struct(3, rows, cols), strip, strip, edge, edge),
        ensemble,
        diffusion,
        drift_rows,
        drift_cols,
        name="pack",
        raw=4,
    )
    early = trade(early, "domain", True)
    late = trade(late, "domain", False)
    left, right = shift(right, ("role",), 1), shift(left, ("role",), -1)
    early_rest, late_rest = call(
        functools.partial(turn_kernel, "domain"), (rest, rest), field, left, right, name="turn"
    )
    early_rest = trade(early_rest, "domain", True)
    late_rest = trade(late_rest, "domain", False)
    weight = call(
        functools.partial(weight_kernel, "role"),
        struct(cols, 2 * rows),
        observed_count,
        observed_cells,
        observed_values,
        observed_weights,
        scalars=1,
        raw=3,
        name="weights",
    )
    padded = pltpu.VMEM((rows + 2 * width, cols + 2 * LEAD, local), jnp.float32)
    scratch = (
        padded,
        padded,
        pltpu.VMEM((4, rows + 2 * width, cols + 2 * LEAD, local), jnp.float32),
        pltpu.VMEM((5, 2 * width, cols), jnp.float32),
    )
    middle = call(
        functools.partial(middle_kernel, "domain"),
        struct(rows, high - low, local),
        field,
        kept,
        early,
        late,
        weight,
        scratch=scratch,
        name="middle",
    )
    sides = call(
        functools.partial(sides_kernel, "domain"),
        struct(rows, cols - high + low, local),
        field,
        kept,
        early,
        late,
        left,
        right,
        early_rest,
        late_rest,
        scratch=scratch,
        name="sides",
    )

    def gathered(value):
        others = [shift(value, ("member",), s) for s in range(1, groups)]
        return jnp.concatenate(others, axis=0) if len(others) > 1 else others[0]

    middle_others = gathered(middle)
    sides_others = gathered(sides)
    layout = (
        ((0, low, high - low),),
        ((0, high, cols - high), (cols - high, 0, low)),
    )

    def deviations(columns):
        one = struct(rows * columns, members, kind=jnp.bfloat16)
        return one, one, struct(rows, cols)

    pair = groups == 2 and local % 128 == 0
    if pair:
        alone = call(
            functools.partial(own_gram_kernel, layout),
            struct(local, local),
            middle,
            sides,
            weight,
            name="own_gram",
        )
        stages = role_sums(alone)
        started = sum(stages[0])
        cross = struct(local + 8, local)
        upper_a, lower_a, centre_a, total = call(
            functools.partial(cross_kernel, layout[0]),
            (*deviations(high - low), cross),
            middle,
            middle_others,
            weight,
            started,
            name="first_cross",
        )
        alone, arriving = stages[-1]
        total, alone = lax.optimization_barrier((total, alone))
        alone = alone + arriving
        upper_b, lower_b, centre_b, gram = call(
            functools.partial(cross_kernel, layout[1]),
            (*deviations(cols - high + low), cross),
            sides,
            sides_others,
            weight,
            alone,
            total,
            name="last_cross",
        )
        gram, alone = lax.optimization_barrier((gram, alone))
        grams = (*role_sums(gram)[-1], alone, shift(alone, ("member",), 1))
    else:
        blocks = members // 128
        size = blocks * (blocks + 1) // 2 * 128 + 8
        square = struct(members, members)
        vector = struct(1, members)
        upper_a, lower_a, centre_a, total, tilt = call(
            functools.partial(first_gram_kernel, groups, layout[0]),
            (*deviations(high - low), square, vector),
            middle,
            middle_others,
            weight,
            name="first_gram",
        )
        gram, upper_b, lower_b, centre_b = call(
            functools.partial(last_gram_kernel, groups, layout[1]),
            (struct(size, 128), *deviations(cols - high + low)),
            sides,
            sides_others,
            weight,
            total,
            tilt,
            scratch=(
                pltpu.VMEM((members, members), jnp.float32),
                pltpu.VMEM((1, members), jnp.float32),
            ),
            name="last_gram",
        )
        grams = role_sums(gram)[-1]
    return call(
        functools.partial(analysis_kernel, layout, pair),
        struct(local, rows, cols),
        *grams,
        upper_a,
        upper_b,
        lower_a,
        lower_b,
        centre_a,
        centre_b,
        scratch=(
            pltpu.VMEM((members, members), jnp.float32),
            pltpu.VMEM((members, 2 * local), jnp.bfloat16),
            pltpu.VMEM((4, cols, local), jnp.float32),
        ),
        name="analysis",
        result=True,
    )


def solution(mesh):
    placed = (
        P("member", "domain", "role"),
        P("domain", "role"),
        P("domain", "role"),
        P("domain", "role"),
        P("domain", None),
        P("domain"),
        P("domain", None),
        P("domain", None),
    )
    return jax.shard_map(
        shards, mesh=mesh, in_specs=placed, out_specs=P("member", "domain", "role"), check_vma=False
    )
```

```python
import functools

import jax
import jax.numpy as jnp
from jax import lax
from jax.experimental import pallas as pl
from jax.experimental.pallas import tpu as pltpu
from jax.sharding import PartitionSpec as P

STEPS = 4
ITERS = 6
LEAD = 16


VMEM = pl.BlockSpec(memory_space=pltpu.VMEM)
SMEM = pl.BlockSpec(memory_space=pltpu.SMEM)
ROOM = 1 << 20


def struct(*shape, kind=jnp.float32):
    return jax.ShapeDtypeStruct(shape, kind)


def near(shape, kind):
    size = jnp.dtype(kind).itemsize
    for place, extent in enumerate(shape[::-1]):
        unit = (128, 32 // jnp.dtype(kind).itemsize, 1)[min(place, 2)]
        size *= -(-extent // unit) * unit
    return size <= ROOM


def call(body, outs, *args, scratch=(), name=None, scalars=0, raw=0, result=False):
    placed = list(args[: scalars + raw])
    for value in args[scalars + raw :]:
        if near(value.shape, value.dtype):
            value = pltpu.with_memory_space_constraint(value, pltpu.VMEM)
        placed.append(value)
    if not result:
        outs = jax.tree.map(
            lambda s: pltpu.VMEM(s.shape, s.dtype) if near(s.shape, s.dtype) else s, outs
        )
    return pl.pallas_call(
        body,
        out_shape=outs,
        in_specs=[SMEM] * scalars + [VMEM] * (len(args) - scalars),
        out_specs=tuple(VMEM for _ in outs) if isinstance(outs, tuple) else VMEM,
        scratch_shapes=scratch,
        name=name,
    )(*placed)


def halves(value):
    upper = value.astype(jnp.bfloat16)
    lower = (value - upper.astype(jnp.float32)).astype(jnp.bfloat16)
    return upper, lower


def dot(a, b, dims=((1,), (0,))):
    return lax.dot_general(a, b, (dims, ((), ())), preferred_element_type=jnp.float32)


def dot3(a, b, dims=((1,), (0,))):
    return dot(a[0], b[0], dims) + (dot(a[0], b[1], dims) + dot(a[1], b[0], dims))


def loop(count, body):
    if count <= 16:
        for i in range(count):
            body(i)
    else:
        lax.fori_loop(0, count, lambda i, c: (body(i), c)[1], 0)


def parted(cols):
    cut = (cols // 2 + 16) // 8 * 8
    return cut, 8, cut - 8


def parity(axis):
    return lax.rem(lax.axis_index(axis), 2)


def pack_kernel(axis, ens, diffusion, drift_rows, drift_cols, field, kept, early, late, left, right):
    odd = parity(axis)
    rows, cols, members = field.shape
    width = STEPS
    cut = parted(cols)[0]
    lanes = pl.ds(0, members)
    for r in range(rows):
        turned = ens[pl.ds(r, members, stride=rows)].T
        field[r] = turned
        part = pl.ds(r * width, width)
        left[part, lanes] = turned[:width]
        right[part, lanes] = turned[cols - width :]
    for i in range(width):
        part = pl.ds(i * cut, cut)
        early[part, lanes] = field[i + odd * (rows - width), pl.ds(0, cut)]
        late[part, lanes] = field[i + (1 - odd) * (rows - width), pl.ds(0, cut)]
    near_edge = jnp.zeros((rows, cols), jnp.float32)
    far_edge = near_edge
    lane = lax.broadcasted_iota(jnp.int32, (rows, cols), 1)
    for k, part in enumerate((diffusion, drift_rows, drift_cols)):
        at = pl.ds(width * cut + k * width, width)
        top, bottom = part[:width], part[rows - width :]
        early[at, pl.ds(0, cols)] = jnp.where(odd == 0, top, bottom)
        late[at, pl.ds(0, cols)] = jnp.where(odd == 0, bottom, top)
        value = part[...]
        kept[k] = value
        mine = (lane >= k * width) & (lane < (k + 1) * width)
        if k:
            near_edge = jnp.where(mine, pltpu.roll(value, k * width, 1), near_edge)
        else:
            near_edge = jnp.where(mine, value, near_edge)
        far_edge = jnp.where(mine, pltpu.roll(value, (k + 1) * width, 1), far_edge)
    left[pl.ds(rows * width, rows), pl.ds(0, cols)] = near_edge
    right[pl.ds(rows * width, rows), pl.ds(0, cols)] = far_edge


def turn_kernel(axis, field, left, right, after, early, late):
    rows, cols, members = field.shape
    odd = parity(axis)
    width = STEPS
    area = width * width
    cut = parted(cols)[0]
    size = cols - cut
    lanes = pl.ds(0, members)
    for i in range(width):
        at = pl.ds(i * size, size)
        early[at, lanes] = field[i + odd * (rows - width), pl.ds(cut, size)]
        late[at, lanes] = field[i + (1 - odd) * (rows - width), pl.ds(cut, size)]
    base = width * size
    for i, side in enumerate((left, right)):
        at = pl.ds(base + i * area, area)
        top, bottom = side[pl.ds(0, area)], side[pl.ds((rows - width) * width, area)]
        early[at] = jnp.where(odd == 0, top, bottom)
        late[at] = jnp.where(odd == 0, bottom, top)
        at = pl.ds(base + 2 * area + i * width, width)
        top = side[pl.ds(rows * width, width)]
        bottom = side[pl.ds(rows * width + rows - width, width)]
        early[at] = jnp.where(odd == 0, top, bottom)
        late[at] = jnp.where(odd == 0, bottom, top)


def widen(write, line, columns, members):
    for at, parts in columns:
        size = parts[0].shape[0]
        diffusion, rowwise, colwise = (
            jnp.broadcast_to(p[:, line : line + 1], (size, members)) for p in parts
        )
        here = pl.ds(at, size)
        write(0, here, 1.0 - 4.0 * diffusion - rowwise - colwise)
        write(1, here, diffusion)
        write(2, here, diffusion + rowwise)
        write(3, here, diffusion + colwise)


def spread_rows(spread, lines, columns, members):
    for line, row in lines:

        def write(k, here, value, row=row):
            spread[k, row, here] = value

        widen(write, line, columns, members)


def march(rows, even, odd, spread, ranges, finals, store):
    width = STEPS
    source, target = even, odd
    for step in range(1, STEPS + 1):
        last = step == STEPS

        def advance(r, source=source, target=target, last=last):
            for at, size in finals if last else ranges:
                here = pl.ds(at, size)
                value = (
                    spread[0, r, here] * source[r, here]
                    + spread[1, r, here] * (source[r + 1, here] + source[r, pl.ds(at + 1, size)])
                    + spread[2, r, here] * source[r - 1, here]
                    + spread[3, r, here] * source[r, pl.ds(at - 1, size)]
                )
                if last:
                    store(r - width, at, value)
                else:
                    target[r, here] = value

        loop(rows + 2 * width - 2 * step, lambda i: advance(i + step))
        source, target = target, source


def coefficient_rows(odd, kept, early, late, stage, cut):
    rows, cols = kept.shape[1:]
    width = STEPS
    for k in range(3):
        at = pl.ds(width * cut + k * width, width), pl.ds(0, cols)
        stage[k, pl.ds(0, width)] = jnp.where(odd == 0, early[at], late[at])
        stage[k, pl.ds(width, width)] = jnp.where(odd == 0, late[at], early[at])
    lines = [(i, i) for i in range(1, width)]
    lines += [(width + i, width + rows + i) for i in range(width - 1)]
    inside = [(r, width + r) for r in range(rows)]
    return [kept[k].T for k in range(3)], inside, [stage[k].T for k in range(3)], lines


def middle_kernel(axis, field, kept, early, late, out, one, two, spread, stage):
    rows, cols, members = field.shape
    width = STEPS
    cut, low, high = parted(cols)
    lanes = pl.ds(0, members)
    odd = parity(axis)
    own, inside, beyond, lines = coefficient_rows(odd, kept, early, late, stage, cut)
    for parts, places in ((beyond, lines), (own, inside)):
        spread_rows(spread, places, [(LEAD, [p[:cut] for p in parts])], members)
    here = pl.ds(LEAD, cut)
    for i in range(width):
        part = pl.ds(i * cut, cut)
        one[i + odd * (rows + width), here] = early[part, lanes]
        one[i + (1 - odd) * (rows + width), here] = late[part, lanes]
    for r in range(rows):
        one[width + r, here] = field[r, pl.ds(0, cut)]

    def store(r, at, value):
        out[r] = value

    march(rows, one, two, spread, [(LEAD, cut)], [(LEAD + low, high - low)], store)


def sides_kernel(
    axis,
    field,
    kept,
    early,
    late,
    left,
    right,
    early_rest,
    late_rest,
    out,
    one,
    two,
    spread,
    stage,
):
    rows, cols, members = field.shape
    width = STEPS
    area = width * width
    cut, low, high = parted(cols)
    first, second = low + 8, high - 8
    size = cols - cut
    base = width * size
    lanes = pl.ds(0, members)
    odd = parity(axis)
    own, inside, beyond, lines = coefficient_rows(odd, kept, early, late, stage, cut)
    for side in range(2):
        at = pl.ds(base + 2 * area + side * width, width), pl.ds(0, cols)
        stage[3 + side, pl.ds(0, width)] = jnp.where(odd == 0, early_rest[at], late_rest[at])
        stage[3 + side, pl.ds(width, width)] = jnp.where(odd == 0, late_rest[at], early_rest[at])
    edge = pl.ds(rows * width, rows), pl.ds(0, cols)
    for parts, near_part, far_part, places in (
        (beyond, stage[3].T, stage[4].T, lines),
        (own, left[edge].T, right[edge].T, inside),
    ):
        halo = [slice(k * width, (k + 1) * width) for k in range(3)]
        columns = [
            (LEAD - width, [near_part[h] for h in halo]),
            (LEAD, [p[:first] for p in parts]),
            (LEAD + second, [p[second:] for p in parts]),
            (LEAD + cols, [far_part[h] for h in halo]),
        ]
        spread_rows(spread, places, columns, members)
    before = pl.ds(LEAD - width, width)
    after = pl.ds(LEAD + cols, width)
    for i in range(width):
        for j, strip, rest in (
            (i + odd * (rows + width), early, early_rest),
            (i + (1 - odd) * (rows + width), late, late_rest),
        ):
            one[j, before] = rest[pl.ds(base + i * width, width), lanes]
            one[j, pl.ds(LEAD, first)] = strip[pl.ds(i * cut, first), lanes]
            one[j, pl.ds(LEAD + second, cut - second)] = strip[
                pl.ds(i * cut + second, cut - second), lanes
            ]
            one[j, pl.ds(LEAD + cut, size)] = rest[pl.ds(i * size, size), lanes]
            one[j, after] = rest[pl.ds(base + area + i * width, width), lanes]
    for r in range(rows):
        part = pl.ds(r * width, width)
        one[width + r, before] = left[part, lanes]
        one[width + r, pl.ds(LEAD, first)] = field[r, pl.ds(0, first)]
        one[width + r, pl.ds(LEAD + second, cols - second)] = field[
            r, pl.ds(second, cols - second)
        ]
        one[width + r, after] = right[part, lanes]

    def store(r, at, value):
        if at == LEAD:
            out[r, pl.ds(cols - high, low)] = value
        else:
            out[r, pl.ds(0, cols - high)] = value

    march(
        rows,
        one,
        two,
        spread,
        [(LEAD + second, cols - second + 8), (LEAD - 8, first + 8)],
        [(LEAD + high, cols - high), (LEAD, low)],
        store,
    )


def weight_kernel(axis, count, cells, values, weights, out):
    cols, twice = out.shape
    rows = twice // 2
    slots = cells.shape[1]
    full = cols * lax.axis_size(axis)
    cell = cells[...]
    if full & (full - 1):
        row_of = lax.div(cell, full)
    else:
        row_of = lax.shift_right_logical(cell, full.bit_length() - 1)
    col_of = cell - row_of * full - lax.axis_index(axis) * cols
    slot = lax.broadcasted_iota(jnp.int32, (1, slots), 1)
    plain = jnp.where(slot < count[...], weights[...], 0.0)
    valued = plain * values[...]
    here = lax.broadcasted_iota(jnp.int32, (cols, slots), 0) == col_of
    here = jnp.where(here, 1.0, 0.0).astype(jnp.bfloat16)
    line = lax.broadcasted_iota(jnp.int32, (rows, slots), 0) == row_of
    value = jnp.concatenate([jnp.where(line, plain, 0.0), jnp.where(line, valued, 0.0)], axis=0)
    total = jnp.zeros((cols, twice), jnp.float32)
    for piece in range(3):
        part = value.astype(jnp.bfloat16)
        value = value - part.astype(jnp.float32)
        total = total + dot(here, part, ((1,), (1,)))
    out[...] = total


def cell_weights(rows, pieces, weight, b, many):
    plain, valued = [], []
    for i in range(many):
        r = b * many + i
        for start, column, length in pieces:
            source = weight[pl.ds(column, length)]
            line = lax.broadcasted_iota(jnp.int32, source.shape, 1)
            plain.append(jnp.sum(jnp.where(line == r, source, 0.0), axis=1, keepdims=True))
            valued.append(jnp.sum(jnp.where(line == r + rows, source, 0.0), axis=1, keepdims=True))
    return jnp.concatenate(plain, axis=0), jnp.concatenate(valued, axis=0)


def lay_rows(pieces, column_of, size, centre, b, many):
    cols = centre.shape[1]
    for i in range(many):
        row = jnp.zeros((1, cols), jnp.float32)
        for start, column, length in pieces:
            place = lax.broadcasted_iota(jnp.int32, (length, cols), 0) + column
            here = place == lax.broadcasted_iota(jnp.int32, (length, cols), 1)
            part = column_of[i * size + start : i * size + start + length]
            row = row + jnp.sum(jnp.where(here, part, 0.0), axis=0, keepdims=True)
        centre[pl.ds(b * many + i, 1)] = row


def grouping(rows):
    return next(n for n in (4, 2, 1) if rows % n == 0)


def cells_of(ref, b, many, start=0):
    value = ref[pl.ds(start + b * many, many)]
    return value.reshape(many * value.shape[1], value.shape[2])


def lane_mean(value):
    return jnp.sum(value, axis=1, keepdims=True) * (1.0 / value.shape[1])


def wide(parts):
    return jnp.concatenate(parts, axis=1)


def dot_wide(a, both, size):
    value = dot(a[0], both)
    return value[:, :size] + value[:, size:] + dot(a[1], both[:, :size])


def gram_kernel(groups, pieces, own, others, weight, upper, lower, centre, total, tilt):
    rows, size, _ = own.shape
    members = total.shape[0]
    many = grouping(rows)
    depth = many * size

    def block(b):
        parts = [cells_of(own, b, many)]
        parts += [cells_of(others, b, many, g * rows) for g in range(groups - 1)]
        value = wide(parts) if groups > 1 else parts[0]
        mean = lane_mean(value)
        deviation = value - mean
        plain, valued = cell_weights(rows, pieces, weight, b, many)
        lay_rows(pieces, mean, size, centre, b, many)
        high, low = halves(deviation)
        at = pl.ds(b * depth, depth)
        upper[at] = high
        lower[at] = low
        turned = (deviation * plain).T
        total[...] += dot3(halves(turned), (high, low))
        tilt[...] += jnp.sum(deviation * (valued - plain * mean), axis=0, keepdims=True)

    loop(rows // many, block)


def own_gram_kernel(layout, middle, sides, weight, total):
    local = total.shape[0]
    total[...] = jnp.zeros_like(total)
    for pieces, own in zip(layout, (middle, sides)):
        rows, size, _ = own.shape
        many = grouping(rows)

        def block(b, pieces=pieces, own=own, rows=rows, many=many):
            value = cells_of(own, b, many)
            deviation = value - lane_mean(value)
            plain, _ = cell_weights(rows, pieces, weight, b, many)
            turned = (deviation * plain).T
            total[...] += dot_wide(halves(turned), wide(halves(deviation)), local)

        loop(rows // many, block)


def cross_kernel(pieces, own, other, weight, after, *rest):
    before, (upper, lower, centre, total) = rest[:-4], rest[-4:]
    total[...] = before[0][...] if before else jnp.zeros_like(total)
    rows, size, local = own.shape
    many = grouping(rows)
    depth = many * size
    left, right = pl.ds(0, local), pl.ds(local, local)

    def block(b):
        value, partner = cells_of(own, b, many), cells_of(other, b, many)
        mean_own, mean_partner = lane_mean(value), lane_mean(partner)
        mean = 0.5 * (mean_own + mean_partner)
        apart = 0.5 * (mean_own - mean_partner)
        deviation, counter = value - mean, partner - mean
        plain, valued = cell_weights(rows, pieces, weight, b, many)
        lay_rows(pieces, mean, size, centre, b, many)
        at = pl.ds(b * depth, depth)
        high, low = halves(deviation)
        upper[at, left] = high
        lower[at, left] = low
        high, low = halves(counter)
        upper[at, right] = high
        lower[at, right] = low
        turned = (deviation * plain).T
        total[pl.ds(0, local)] += dot_wide(halves(turned), wide((high, low)), local)
        pull = valued - plain * mean
        tie = plain * apart

        def add(row, columns):
            total[pl.ds(local + row, 1)] += jnp.sum(columns, axis=0, keepdims=True)

        add(0, deviation * pull)
        add(1, counter * pull)
        add(2, deviation * tie)
        add(3, counter * -tie)
        add(4, jnp.broadcast_to(tie * apart, deviation.shape))

    loop(rows // many, block)


def first_gram_kernel(groups, pieces, own, others, weight, upper, lower, centre, total, tilt):
    total[...] = jnp.zeros_like(total)
    tilt[...] = jnp.zeros_like(tilt)
    gram_kernel(groups, pieces, own, others, weight, upper, lower, centre, total, tilt)


def last_gram_kernel(
    groups, pieces, own, others, weight, before, tilted, gram, upper, lower, centre, total, tilt
):
    total[...] = before[...]
    tilt[...] = tilted[...]
    gram_kernel(groups, pieces, own, others, weight, upper, lower, centre, total, tilt)
    pull = gram.shape[0] - 8
    blocks = total.shape[0] // 128
    innovation = tilt[...]
    at = 0
    gram[pl.ds(pull, 8)] = jnp.zeros((8, 128), jnp.float32)
    for i in range(blocks):
        gram[pl.ds(pull + i, 1)] = innovation[:, i * 128 : (i + 1) * 128]
        for j in range(i, blocks):
            gram[pl.ds(at, 128)] = total[i * 128 : (i + 1) * 128, j * 128 : (j + 1) * 128]
            at += 128


def assemble(first, second, whole):
    blocks = whole.shape[0] // 128
    pull = first.shape[0] - 8
    at = 0
    for i in range(blocks):
        for j in range(i, blocks):
            block = first[pl.ds(at, 128)] + second[pl.ds(at, 128)]
            whole[i * 128 : (i + 1) * 128, j * 128 : (j + 1) * 128] = block
            if j > i:
                whole[j * 128 : (j + 1) * 128, i * 128 : (i + 1) * 128] = block.T
            at += 128
    return wide([first[pl.ds(pull + i, 1)] + second[pl.ds(pull + i, 1)] for i in range(blocks)])


def assemble_pair(first, second, own, other, whole):
    local = own.shape[1]
    cross = first[pl.ds(0, local)] + second[pl.ds(0, local)]
    rest = first[pl.ds(local, 8)] + second[pl.ds(local, 8)]
    whole[:local, local:] = cross
    whole[local:, :local] = cross.T
    square = rest[4:5]
    diagonal = lax.broadcasted_iota(jnp.int32, (local, local), 0) == lax.broadcasted_iota(
        jnp.int32, (local, local), 1
    )
    for i, part in enumerate((own, other)):
        tie = rest[2 + i : 3 + i]
        upright = jnp.sum(jnp.where(diagonal, tie, 0.0), axis=1, keepdims=True)
        at = slice(i * local, (i + 1) * local)
        whole[at, at] = part[...] + upright + (tie - square)
    return wide([rest[0:1], rest[1:2]])


def analysis_kernel(layout, pair, *rest):
    if pair:
        first, second, own, other, *rest = rest
    else:
        first, second, *rest = rest
    uppers, lowers, centres = rest[0:2], rest[2:4], rest[4:6]
    out, whole, chosen, natural = rest[6:]
    rows, cols = centres[0].shape
    local = natural.shape[2]
    members = whole.shape[0]
    if pair:
        innovation = assemble_pair(first, second, own, other, whole)
    else:
        innovation = assemble(first, second, whole)
    down = lax.broadcasted_iota(jnp.int32, (members, members), 0)
    across = lax.broadcasted_iota(jnp.int32, (members, members), 1)
    identity = jnp.where(down == across, 1.0, 0.0)
    matrix = whole[...] + (members - 1.0) * identity
    parts = halves(matrix)
    square = dot3(parts, parts)
    squares = jnp.sum(jnp.sum(matrix * matrix, axis=1, keepdims=True), axis=0, keepdims=True)
    scaling = jnp.sqrt(squares)
    current = matrix * (1.0 / scaling)
    square = square * (1.0 / scaling) * (1.0 / scaling)
    inverse = None
    for repeat in range(0, ITERS, 2):
        if repeat:
            parts = halves(current)
            square = dot3(parts, parts)
        inner = 0.0625 * square - 0.5625 * current
        outer = 2.25 * identity - 2.4375 * current + 1.6875 * square
        both = outer + dot3(halves(square), halves(inner))
        both_parts = halves(both)
        if repeat + 2 < ITERS:
            twice = dot3(both_parts, both_parts)
            current = dot3(halves(current), halves(twice))
        inverse = both if inverse is None else dot3(halves(inverse), both_parts)
    once = jnp.sum(inverse * innovation, axis=1, keepdims=True)
    once_row = jnp.sum(jnp.where(down == across, once, 0.0), axis=0, keepdims=True)
    shifted = jnp.sum(inverse * once_row, axis=1, keepdims=True) * (1.0 / scaling)
    factor = jnp.sqrt((members - 1.0) / scaling)
    mixing = (factor * inverse + shifted)[:, :local]
    high, low = halves(mixing)
    chosen[:, :local] = high
    chosen[:, local:] = low
    many = grouping(rows)

    def block(b):
        for pieces, upper, lower in zip(layout, uppers, lowers):
            size = upper.shape[0] // rows
            at = pl.ds(b * many * size, many * size)
            value = dot(upper[at], chosen[...])
            value = value[:, :local] + value[:, local:] + dot(lower[at], chosen[:, :local])
            for i in range(many):
                for start, column, length in pieces:
                    natural[i, pl.ds(column, length)] = value[
                        i * size + start : i * size + start + length
                    ]
        for i in range(many):
            r = b * many + i
            middle_row = centres[0][pl.ds(r, 1)] + centres[1][pl.ds(r, 1)]
            out[pl.ds(r, local, stride=rows)] = natural[i].T + middle_row

    loop(rows // many, block)


def shift(value, axes, *moves):
    sizes = [lax.axis_size(a) for a in axes]
    pairs = []
    total = 1
    for s in sizes:
        total *= s
    for flat in range(total):
        rest, place = flat, []
        for s in reversed(sizes):
            place.append(rest % s)
            rest //= s
        place = place[::-1]
        to = 0
        for s, p, m in zip(sizes, place, moves):
            to = to * s + (p + m) % s
        pairs.append((flat, to))
    return lax.ppermute(value, axes if len(axes) > 1 else axes[0], pairs)


def trade(value, axis, first):
    size = lax.axis_size(axis)
    if size % 2:
        raise ValueError("odd ring")
    start = 1 if first else 0
    pairs = [(i % size, (i + 1) % size) for i in range(start, size, 2)]
    return lax.ppermute(value, axis, pairs + [(j, i) for i, j in pairs])


def role_sums(value):
    size = lax.axis_size("role")
    if size & (size - 1) or size == 1:
        return [(lax.psum(value, "role"), jnp.zeros_like(value))]
    stages = []
    step = 1
    while step < size:
        other = lax.ppermute(value, "role", [(i, i ^ step) for i in range(size)])
        stages.append((value, other))
        value = value + other
        step *= 2
    return stages


def shards(
    ensemble,
    diffusion,
    drift_rows,
    drift_cols,
    observed_cells,
    observed_count,
    observed_values,
    observed_weights,
):
    groups = lax.axis_size("member")
    roles = lax.axis_size("role")
    local, rows, cols = ensemble.shape
    members = local * groups
    width = STEPS
    lanes = max(local, cols)
    cut, low, high = parted(cols)
    strip = struct(width * cut + 4 * width, lanes)
    rest = struct(width * (cols - cut) + 2 * width * width + 2 * width, lanes)
    edge = struct(rows * width + rows, lanes)
    field, kept, early, late, left, right = call(
        functools.partial(pack_kernel, "domain"),
        (struct(rows, cols, local), struct(3, rows, cols), strip, strip, edge, edge),
        ensemble.reshape(local * rows, cols),
        diffusion,
        drift_rows,
        drift_cols,
        name="pack",
        raw=4,
    )
    early = trade(early, "domain", True)
    late = trade(late, "domain", False)
    left, right = shift(right, ("role",), 1), shift(left, ("role",), -1)
    weight = call(
        functools.partial(weight_kernel, "role"),
        struct(cols, 2 * rows),
        observed_count.reshape(1, 1),
        observed_cells,
        observed_values,
        observed_weights,
        raw=4,
        name="weights",
    )
    early_rest, late_rest = call(
        functools.partial(turn_kernel, "domain"),
        (rest, rest),
        field,
        left,
        right,
        weight,
        name="turn",
    )
    early_rest = trade(early_rest, "domain", True)
    late_rest = trade(late_rest, "domain", False)
    padded = pltpu.VMEM((rows + 2 * width, cols + 2 * LEAD, local), jnp.float32)
    scratch = (
        padded,
        padded,
        pltpu.VMEM((4, rows + 2 * width, cols + 2 * LEAD, local), jnp.float32),
        pltpu.VMEM((5, 2 * width, cols), jnp.float32),
    )
    middle = call(
        functools.partial(middle_kernel, "domain"),
        struct(rows, high - low, local),
        field,
        kept,
        early,
        late,
        scratch=scratch,
        name="middle",
    )
    sides = call(
        functools.partial(sides_kernel, "domain"),
        struct(rows, cols - high + low, local),
        field,
        kept,
        early,
        late,
        left,
        right,
        early_rest,
        late_rest,
        scratch=scratch,
        name="sides",
    )

    def gathered(value):
        others = [shift(value, ("member",), s) for s in range(1, groups)]
        return jnp.concatenate(others, axis=0) if len(others) > 1 else others[0]

    middle_others = gathered(middle)
    sides_others = gathered(sides)
    layout = (
        ((0, low, high - low),),
        ((0, high, cols - high), (cols - high, 0, low)),
    )

    def deviations(columns):
        one = struct(rows * columns, members, kind=jnp.bfloat16)
        return one, one, struct(rows, cols)

    pair = groups == 2 and local % 128 == 0
    if pair:
        alone = call(
            functools.partial(own_gram_kernel, layout),
            struct(local, local),
            middle,
            sides,
            weight,
            name="own_gram",
        )
        stages = role_sums(alone)
        started = sum(stages[0])
        cross = struct(local + 8, local)
        upper_a, lower_a, centre_a, total = call(
            functools.partial(cross_kernel, layout[0]),
            (*deviations(high - low), cross),
            middle,
            middle_others,
            weight,
            started,
            name="first_cross",
        )
        alone, arriving = stages[-1]
        total, alone = lax.optimization_barrier((total, alone))
        alone = alone + arriving
        upper_b, lower_b, centre_b, gram = call(
            functools.partial(cross_kernel, layout[1]),
            (*deviations(cols - high + low), cross),
            sides,
            sides_others,
            weight,
            alone,
            total,
            name="last_cross",
        )
        gram, alone = lax.optimization_barrier((gram, alone))
        grams = (*role_sums(gram)[-1], alone, shift(alone, ("member",), 1))
    else:
        blocks = members // 128
        size = blocks * (blocks + 1) // 2 * 128 + 8
        square = struct(members, members)
        vector = struct(1, members)
        upper_a, lower_a, centre_a, total, tilt = call(
            functools.partial(first_gram_kernel, groups, layout[0]),
            (*deviations(high - low), square, vector),
            middle,
            middle_others,
            weight,
            name="first_gram",
        )
        gram, upper_b, lower_b, centre_b = call(
            functools.partial(last_gram_kernel, groups, layout[1]),
            (struct(size, 128), *deviations(cols - high + low)),
            sides,
            sides_others,
            weight,
            total,
            tilt,
            scratch=(
                pltpu.VMEM((members, members), jnp.float32),
                pltpu.VMEM((1, members), jnp.float32),
            ),
            name="last_gram",
        )
        grams = role_sums(gram)[-1]
    return call(
        functools.partial(analysis_kernel, layout, pair),
        struct(local * rows, cols),
        *grams,
        upper_a,
        upper_b,
        lower_a,
        lower_b,
        centre_a,
        centre_b,
        scratch=(
            pltpu.VMEM((members, members), jnp.float32),
            pltpu.VMEM((members, 2 * local), jnp.bfloat16),
            pltpu.VMEM((4, cols, local), jnp.float32),
        ),
        name="analysis",
        result=True,
    ).reshape(local, rows, cols)


def solution(mesh):
    placed = (
        P("member", "domain", "role"),
        P("domain", "role"),
        P("domain", "role"),
        P("domain", "role"),
        P("domain", None),
        P("domain"),
        P("domain", None),
        P("domain", None),
    )
    return jax.shard_map(
        shards, mesh=mesh, in_specs=placed, out_specs=P("member", "domain", "role"), check_vma=False
    )
```

```python
import functools

import jax
import jax.numpy as jnp
from jax import lax
from jax.experimental import pallas as pl
from jax.experimental.pallas import tpu as pltpu
from jax.sharding import PartitionSpec as P

STEPS = 4
ITERS = 6
LEAD = 16


VMEM = pl.BlockSpec(memory_space=pltpu.VMEM)
SMEM = pl.BlockSpec(memory_space=pltpu.SMEM)
ROOM = 1 << 20


def struct(*shape, kind=jnp.float32):
    return jax.ShapeDtypeStruct(shape, kind)


def near(shape, kind):
    size = jnp.dtype(kind).itemsize
    for place, extent in enumerate(shape[::-1]):
        unit = (128, 32 // jnp.dtype(kind).itemsize, 1)[min(place, 2)]
        size *= -(-extent // unit) * unit
    return size <= ROOM


def call(body, outs, *args, scratch=(), name=None, scalars=0, raw=0, result=False):
    placed = list(args[: scalars + raw])
    for value in args[scalars + raw :]:
        if near(value.shape, value.dtype):
            value = pltpu.with_memory_space_constraint(value, pltpu.VMEM)
        placed.append(value)
    if not result:
        outs = jax.tree.map(
            lambda s: pltpu.VMEM(s.shape, s.dtype) if near(s.shape, s.dtype) else s, outs
        )
    return pl.pallas_call(
        body,
        out_shape=outs,
        in_specs=[SMEM] * scalars + [VMEM] * (len(args) - scalars),
        out_specs=tuple(VMEM for _ in outs) if isinstance(outs, tuple) else VMEM,
        scratch_shapes=scratch,
        name=name,
    )(*placed)


def halves(value):
    upper = value.astype(jnp.bfloat16)
    lower = (value - upper.astype(jnp.float32)).astype(jnp.bfloat16)
    return upper, lower


def dot(a, b, dims=((1,), (0,))):
    return lax.dot_general(a, b, (dims, ((), ())), preferred_element_type=jnp.float32)


def dot3(a, b, dims=((1,), (0,))):
    return dot(a[0], b[0], dims) + (dot(a[0], b[1], dims) + dot(a[1], b[0], dims))


def loop(count, body):
    if count <= 16:
        for i in range(count):
            body(i)
    else:
        lax.fori_loop(0, count, lambda i, c: (body(i), c)[1], 0)


def parted(cols):
    cut = (cols // 2 + 16) // 8 * 8
    return cut, 8, cut - 8


def parity(axis):
    return lax.rem(lax.axis_index(axis), 2)


def pack_kernel(axis, ens, diffusion, drift_rows, drift_cols, field, kept, early, late, left, right):
    odd = parity(axis)
    rows, cols, members = field.shape
    width = STEPS
    cut = parted(cols)[0]
    lanes = pl.ds(0, members)
    for r in range(rows):
        turned = ens[pl.ds(r, members, stride=rows)].T
        field[r] = turned
        part = pl.ds(r * width, width)
        left[part, lanes] = turned[:width]
        right[part, lanes] = turned[cols - width :]
    for i in range(width):
        part = pl.ds(i * cut, cut)
        early[part, lanes] = field[i + odd * (rows - width), pl.ds(0, cut)]
        late[part, lanes] = field[i + (1 - odd) * (rows - width), pl.ds(0, cut)]
    near_edge = jnp.zeros((rows, cols), jnp.float32)
    far_edge = near_edge
    lane = lax.broadcasted_iota(jnp.int32, (rows, cols), 1)
    for k, part in enumerate((diffusion, drift_rows, drift_cols)):
        at = pl.ds(width * cut + k * width, width)
        top, bottom = part[:width], part[rows - width :]
        early[at, pl.ds(0, cols)] = jnp.where(odd == 0, top, bottom)
        late[at, pl.ds(0, cols)] = jnp.where(odd == 0, bottom, top)
        value = part[...]
        kept[k] = value
        mine = (lane >= k * width) & (lane < (k + 1) * width)
        if k:
            near_edge = jnp.where(mine, pltpu.roll(value, k * width, 1), near_edge)
        else:
            near_edge = jnp.where(mine, value, near_edge)
        far_edge = jnp.where(mine, pltpu.roll(value, (k + 1) * width, 1), far_edge)
    left[pl.ds(rows * width, rows), pl.ds(0, cols)] = near_edge
    right[pl.ds(rows * width, rows), pl.ds(0, cols)] = far_edge


def turn_kernel(axis, field, left, right, after, early, late):
    rows, cols, members = field.shape
    odd = parity(axis)
    width = STEPS
    area = width * width
    cut = parted(cols)[0]
    size = cols - cut
    lanes = pl.ds(0, members)
    for i in range(width):
        at = pl.ds(i * size, size)
        early[at, lanes] = field[i + odd * (rows - width), pl.ds(cut, size)]
        late[at, lanes] = field[i + (1 - odd) * (rows - width), pl.ds(cut, size)]
    base = width * size
    for i, side in enumerate((left, right)):
        at = pl.ds(base + i * area, area)
        top, bottom = side[pl.ds(0, area)], side[pl.ds((rows - width) * width, area)]
        early[at] = jnp.where(odd == 0, top, bottom)
        late[at] = jnp.where(odd == 0, bottom, top)
        at = pl.ds(base + 2 * area + i * width, width)
        top = side[pl.ds(rows * width, width)]
        bottom = side[pl.ds(rows * width + rows - width, width)]
        early[at] = jnp.where(odd == 0, top, bottom)
        late[at] = jnp.where(odd == 0, bottom, top)


def widen(write, line, columns, members):
    for at, parts in columns:
        size = parts[0].shape[0]
        diffusion, rowwise, colwise = (
            jnp.broadcast_to(p[:, line : line + 1], (size, members)) for p in parts
        )
        here = pl.ds(at, size)
        write(0, here, 1.0 - 4.0 * diffusion - rowwise - colwise)
        write(1, here, diffusion)
        write(2, here, diffusion + rowwise)
        write(3, here, diffusion + colwise)


def spread_rows(spread, lines, columns, members):
    for line, row in lines:

        def write(k, here, value, row=row):
            spread[k, row, here] = value

        widen(write, line, columns, members)


def march(rows, even, odd, spread, ranges, finals, store):
    width = STEPS
    source, target = even, odd
    for step in range(1, STEPS + 1):
        last = step == STEPS

        def advance(r, source=source, target=target, last=last):
            for at, size in finals if last else ranges:
                here = pl.ds(at, size)
                value = (
                    spread[0, r, here] * source[r, here]
                    + spread[1, r, here] * (source[r + 1, here] + source[r, pl.ds(at + 1, size)])
                    + spread[2, r, here] * source[r - 1, here]
                    + spread[3, r, here] * source[r, pl.ds(at - 1, size)]
                )
                if last:
                    store(r - width, at, value)
                else:
                    target[r, here] = value

        loop(rows + 2 * width - 2 * step, lambda i: advance(i + step))
        source, target = target, source


def coefficient_rows(odd, kept, early, late, stage, cut):
    rows, cols = kept.shape[1:]
    width = STEPS
    for k in range(3):
        at = pl.ds(width * cut + k * width, width), pl.ds(0, cols)
        stage[k, pl.ds(0, width)] = jnp.where(odd == 0, early[at], late[at])
        stage[k, pl.ds(width, width)] = jnp.where(odd == 0, late[at], early[at])
    lines = [(i, i) for i in range(1, width)]
    lines += [(width + i, width + rows + i) for i in range(width - 1)]
    inside = [(r, width + r) for r in range(rows)]
    return [kept[k].T for k in range(3)], inside, [stage[k].T for k in range(3)], lines


def middle_kernel(axis, field, kept, early, late, out, one, two, spread, stage):
    rows, cols, members = field.shape
    width = STEPS
    cut, low, high = parted(cols)
    lanes = pl.ds(0, members)
    odd = parity(axis)
    own, inside, beyond, lines = coefficient_rows(odd, kept, early, late, stage, cut)
    for parts, places in ((beyond, lines), (own, inside)):
        spread_rows(spread, places, [(LEAD, [p[:cut] for p in parts])], members)
    here = pl.ds(LEAD, cut)
    for i in range(width):
        part = pl.ds(i * cut, cut)
        one[i + odd * (rows + width), here] = early[part, lanes]
        one[i + (1 - odd) * (rows + width), here] = late[part, lanes]
    for r in range(rows):
        one[width + r, here] = field[r, pl.ds(0, cut)]

    def store(r, at, value):
        out[r] = value

    march(rows, one, two, spread, [(LEAD, cut)], [(LEAD + low, high - low)], store)


def sides_kernel(
    axis,
    field,
    kept,
    early,
    late,
    left,
    right,
    early_rest,
    late_rest,
    out,
    one,
    two,
    spread,
    stage,
):
    rows, cols, members = field.shape
    width = STEPS
    area = width * width
    cut, low, high = parted(cols)
    first, second = low + 8, high - 8
    size = cols - cut
    base = width * size
    lanes = pl.ds(0, members)
    odd = parity(axis)
    own, inside, beyond, lines = coefficient_rows(odd, kept, early, late, stage, cut)
    for side in range(2):
        at = pl.ds(base + 2 * area + side * width, width), pl.ds(0, cols)
        stage[3 + side, pl.ds(0, width)] = jnp.where(odd == 0, early_rest[at], late_rest[at])
        stage[3 + side, pl.ds(width, width)] = jnp.where(odd == 0, late_rest[at], early_rest[at])
    edge = pl.ds(rows * width, rows), pl.ds(0, cols)
    for parts, near_part, far_part, places in (
        (beyond, stage[3].T, stage[4].T, lines),
        (own, left[edge].T, right[edge].T, inside),
    ):
        halo = [slice(k * width, (k + 1) * width) for k in range(3)]
        columns = [
            (LEAD - width, [near_part[h] for h in halo]),
            (LEAD, [p[:first] for p in parts]),
            (LEAD + second, [p[second:] for p in parts]),
            (LEAD + cols, [far_part[h] for h in halo]),
        ]
        spread_rows(spread, places, columns, members)
    before = pl.ds(LEAD - width, width)
    after = pl.ds(LEAD + cols, width)
    for i in range(width):
        for j, strip, rest in (
            (i + odd * (rows + width), early, early_rest),
            (i + (1 - odd) * (rows + width), late, late_rest),
        ):
            one[j, before] = rest[pl.ds(base + i * width, width), lanes]
            one[j, pl.ds(LEAD, first)] = strip[pl.ds(i * cut, first), lanes]
            one[j, pl.ds(LEAD + second, cut - second)] = strip[
                pl.ds(i * cut + second, cut - second), lanes
            ]
            one[j, pl.ds(LEAD + cut, size)] = rest[pl.ds(i * size, size), lanes]
            one[j, after] = rest[pl.ds(base + area + i * width, width), lanes]
    for r in range(rows):
        part = pl.ds(r * width, width)
        one[width + r, before] = left[part, lanes]
        one[width + r, pl.ds(LEAD, first)] = field[r, pl.ds(0, first)]
        one[width + r, pl.ds(LEAD + second, cols - second)] = field[
            r, pl.ds(second, cols - second)
        ]
        one[width + r, after] = right[part, lanes]

    def store(r, at, value):
        if at == LEAD:
            out[r, pl.ds(cols - high, low)] = value
        else:
            out[r, pl.ds(0, cols - high)] = value

    march(
        rows,
        one,
        two,
        spread,
        [(LEAD + second, cols - second + 8), (LEAD - 8, first + 8)],
        [(LEAD + high, cols - high), (LEAD, low)],
        store,
    )


def weight_kernel(axis, count, cells, values, weights, out):
    cols, twice = out.shape
    rows = twice // 2
    slots = cells.shape[1]
    full = cols * lax.axis_size(axis)
    cell = cells[...]
    if full & (full - 1):
        row_of = lax.div(cell, full)
    else:
        row_of = lax.shift_right_logical(cell, full.bit_length() - 1)
    col_of = cell - row_of * full - lax.axis_index(axis) * cols
    slot = lax.broadcasted_iota(jnp.int32, (1, slots), 1)
    plain = jnp.where(slot < count[...], weights[...], 0.0)
    valued = plain * values[...]
    here = lax.broadcasted_iota(jnp.int32, (cols, slots), 0) == col_of
    here = jnp.where(here, 1.0, 0.0).astype(jnp.bfloat16)
    line = lax.broadcasted_iota(jnp.int32, (rows, slots), 0) == row_of
    value = jnp.concatenate([jnp.where(line, plain, 0.0), jnp.where(line, valued, 0.0)], axis=0)
    total = jnp.zeros((cols, twice), jnp.float32)
    for piece in range(3):
        part = value.astype(jnp.bfloat16)
        value = value - part.astype(jnp.float32)
        total = total + dot(here, part, ((1,), (1,)))
    out[...] = total


def cell_weights(rows, pieces, weight, b, many):
    plain, valued = [], []
    for i in range(many):
        r = b * many + i
        for start, column, length in pieces:
            source = weight[pl.ds(column, length)]
            line = lax.broadcasted_iota(jnp.int32, source.shape, 1)
            plain.append(jnp.sum(jnp.where(line == r, source, 0.0), axis=1, keepdims=True))
            valued.append(jnp.sum(jnp.where(line == r + rows, source, 0.0), axis=1, keepdims=True))
    return jnp.concatenate(plain, axis=0), jnp.concatenate(valued, axis=0)


def lay_rows(pieces, column_of, size, centre, b, many):
    cols = centre.shape[1]
    for i in range(many):
        row = jnp.zeros((1, cols), jnp.float32)
        for start, column, length in pieces:
            place = lax.broadcasted_iota(jnp.int32, (length, cols), 0) + column
            here = place == lax.broadcasted_iota(jnp.int32, (length, cols), 1)
            part = column_of[i * size + start : i * size + start + length]
            row = row + jnp.sum(jnp.where(here, part, 0.0), axis=0, keepdims=True)
        centre[pl.ds(b * many + i, 1)] = row


def grouping(rows):
    return next(n for n in (4, 2, 1) if rows % n == 0)


def cells_of(ref, b, many, start=0):
    value = ref[pl.ds(start + b * many, many)]
    return value.reshape(many * value.shape[1], value.shape[2])


def lane_mean(value):
    return jnp.sum(value, axis=1, keepdims=True) * (1.0 / value.shape[1])


def wide(parts):
    return jnp.concatenate(parts, axis=1)


def dot_wide(a, both, size):
    value = dot(a[0], both)
    return value[:, :size] + value[:, size:] + dot(a[1], both[:, :size])


def gram_kernel(groups, pieces, own, others, weight, upper, lower, centre, total, tilt):
    rows, size, _ = own.shape
    members = total.shape[0]
    many = grouping(rows)
    depth = many * size

    def block(b):
        parts = [cells_of(own, b, many)]
        parts += [cells_of(others, b, many, g * rows) for g in range(groups - 1)]
        value = wide(parts) if groups > 1 else parts[0]
        mean = lane_mean(value)
        deviation = value - mean
        plain, valued = cell_weights(rows, pieces, weight, b, many)
        lay_rows(pieces, mean, size, centre, b, many)
        high, low = halves(deviation)
        at = pl.ds(b * depth, depth)
        upper[at] = high
        lower[at] = low
        turned = (deviation * plain).T
        total[...] += dot3(halves(turned), (high, low))
        tilt[...] += jnp.sum(deviation * (valued - plain * mean), axis=0, keepdims=True)

    loop(rows // many, block)


def own_gram_kernel(layout, middle, sides, weight, total, left, right, spread):
    local = total.shape[0]
    total[...] = jnp.zeros_like(total)
    for pieces, own in zip(layout, (middle, sides)):
        rows, size, _ = own.shape
        many = grouping(rows)
        depth = many * size

        def block(b, pieces=pieces, own=own, rows=rows, many=many, depth=depth):
            value = cells_of(own, b, many)
            mean = lane_mean(value)
            deviation = value - mean
            plain, valued = cell_weights(rows, pieces, weight, b, many)
            turned = halves((deviation * plain).T)
            total[...] += dot_wide(turned, wide(halves(deviation)), local)
            if own is sides:
                at = pl.ds(b * depth, depth)
                left[:, at], right[:, at] = turned
                lane = lax.broadcasted_iota(jnp.int32, (depth, local), 1)
                spread[at] = jnp.where(lane == 0, plain, jnp.where(lane == 1, valued, mean))

        loop(rows // many, block)


def tally(total, local, value, partner, plain, valued, mean_own):
    mean_partner = lane_mean(partner)
    counter = partner - mean_partner
    mean = 0.5 * (mean_own + mean_partner)
    apart = 0.5 * (mean_own - mean_partner)
    deviation = value - mean
    pull = valued - plain * mean
    tie = plain * apart

    def add(row, columns):
        total[pl.ds(local + row, 1)] += jnp.sum(columns, axis=0, keepdims=True)

    add(0, deviation * pull)
    add(1, (partner - mean) * pull)
    add(2, deviation * tie)
    add(3, (mean - partner) * tie)
    add(4, jnp.broadcast_to(tie * apart, deviation.shape))
    return counter


def part_deviations(pieces, value, partner, size, upper, lower, centre, b, many):
    value = wide([value, partner])
    mean = lane_mean(value)
    lay_rows(pieces, mean, size, centre, b, many)
    at = pl.ds(b * many * size, many * size)
    upper[at], lower[at] = halves(value - mean)


def first_cross_kernel(pieces, own, other, weight, after, upper, lower, centre, total):
    total[...] = jnp.zeros_like(total)
    rows, size, local = own.shape
    many = grouping(rows)

    def block(b):
        value, partner = cells_of(own, b, many), cells_of(other, b, many)
        mean = lane_mean(value)
        plain, valued = cell_weights(rows, pieces, weight, b, many)
        counter = tally(total, local, value, partner, plain, valued, mean)
        part_deviations(pieces, value, partner, size, upper, lower, centre, b, many)
        turned = ((value - mean) * plain).T
        total[pl.ds(0, local)] += dot_wide(halves(turned), wide(halves(counter)), local)

    loop(rows // many, block)


def last_cross_kernel(own, other, left, right, spread, before, after, total):
    total[...] = before[...]
    rows, size, local = own.shape
    many = grouping(rows)
    depth = many * size

    def block(b):
        at = pl.ds(b * depth, depth)
        value, partner = cells_of(own, b, many), cells_of(other, b, many)
        counter = tally(total, local, value, partner, *(spread[at, i : i + 1] for i in range(3)))
        total[pl.ds(0, local)] += dot_wide(
            (left[:, at], right[:, at]), wide(halves(counter)), local
        )

    loop(rows // many, block)


def deviation_kernel(pieces, own, other, after, upper, lower, centre):
    rows, size, _ = own.shape
    many = grouping(rows)

    def block(b):
        value, partner = cells_of(own, b, many), cells_of(other, b, many)
        part_deviations(pieces, value, partner, size, upper, lower, centre, b, many)

    loop(rows // many, block)


def first_gram_kernel(groups, pieces, own, others, weight, upper, lower, centre, total, tilt):
    total[...] = jnp.zeros_like(total)
    tilt[...] = jnp.zeros_like(tilt)
    gram_kernel(groups, pieces, own, others, weight, upper, lower, centre, total, tilt)


def last_gram_kernel(
    groups, pieces, own, others, weight, before, tilted, gram, upper, lower, centre, total, tilt
):
    total[...] = before[...]
    tilt[...] = tilted[...]
    gram_kernel(groups, pieces, own, others, weight, upper, lower, centre, total, tilt)
    pull = gram.shape[0] - 8
    blocks = total.shape[0] // 128
    innovation = tilt[...]
    at = 0
    gram[pl.ds(pull, 8)] = jnp.zeros((8, 128), jnp.float32)
    for i in range(blocks):
        gram[pl.ds(pull + i, 1)] = innovation[:, i * 128 : (i + 1) * 128]
        for j in range(i, blocks):
            gram[pl.ds(at, 128)] = total[i * 128 : (i + 1) * 128, j * 128 : (j + 1) * 128]
            at += 128


def assemble(first, second, whole):
    blocks = whole.shape[0] // 128
    pull = first.shape[0] - 8
    at = 0
    for i in range(blocks):
        for j in range(i, blocks):
            block = first[pl.ds(at, 128)] + second[pl.ds(at, 128)]
            whole[i * 128 : (i + 1) * 128, j * 128 : (j + 1) * 128] = block
            if j > i:
                whole[j * 128 : (j + 1) * 128, i * 128 : (i + 1) * 128] = block.T
            at += 128
    return wide([first[pl.ds(pull + i, 1)] + second[pl.ds(pull + i, 1)] for i in range(blocks)])


def assemble_pair(first, second, own, other, whole):
    local = own.shape[1]
    cross = first[pl.ds(0, local)] + second[pl.ds(0, local)]
    rest = first[pl.ds(local, 8)] + second[pl.ds(local, 8)]
    square = rest[4:5]
    diagonal = lax.broadcasted_iota(jnp.int32, (local, local), 0) == lax.broadcasted_iota(
        jnp.int32, (local, local), 1
    )
    uprights = []
    for i, part in enumerate((own, other)):
        tie = rest[2 + i : 3 + i]
        upright = jnp.sum(jnp.where(diagonal, tie, 0.0), axis=1, keepdims=True)
        uprights.append(upright)
        at = slice(i * local, (i + 1) * local)
        whole[at, at] = part[...] + upright + (tie - square)
    cross = cross - uprights[0] + (square - rest[3:4])
    whole[:local, local:] = cross
    whole[local:, :local] = cross.T
    return wide([rest[0:1], rest[1:2]])


def analysis_kernel(layout, pair, *rest):
    if pair:
        first, second, own, other, *rest = rest
    else:
        first, second, *rest = rest
    uppers, lowers, centres = rest[0:2], rest[2:4], rest[4:6]
    out, whole, chosen, natural = rest[6:]
    rows, cols = centres[0].shape
    local = natural.shape[2]
    members = whole.shape[0]
    if pair:
        innovation = assemble_pair(first, second, own, other, whole)
    else:
        innovation = assemble(first, second, whole)
    down = lax.broadcasted_iota(jnp.int32, (members, members), 0)
    across = lax.broadcasted_iota(jnp.int32, (members, members), 1)
    identity = jnp.where(down == across, 1.0, 0.0)
    matrix = whole[...] + (members - 1.0) * identity
    parts = halves(matrix)
    square = dot3(parts, parts)
    squares = jnp.sum(jnp.sum(matrix * matrix, axis=1, keepdims=True), axis=0, keepdims=True)
    scaling = jnp.sqrt(squares)
    current = matrix * (1.0 / scaling)
    square = square * (1.0 / scaling) * (1.0 / scaling)
    inverse = None
    for repeat in range(0, ITERS, 2):
        if repeat:
            parts = halves(current)
            square = dot3(parts, parts)
        inner = 0.0625 * square - 0.5625 * current
        outer = 2.25 * identity - 2.4375 * current + 1.6875 * square
        both = outer + dot3(halves(square), halves(inner))
        both_parts = halves(both)
        if repeat + 2 < ITERS:
            twice = dot3(both_parts, both_parts)
            current = dot3(halves(current), halves(twice))
        inverse = both if inverse is None else dot3(halves(inverse), both_parts)
    once = jnp.sum(inverse * innovation, axis=1, keepdims=True)
    once_row = jnp.sum(jnp.where(down == across, once, 0.0), axis=0, keepdims=True)
    shifted = jnp.sum(inverse * once_row, axis=1, keepdims=True) * (1.0 / scaling)
    factor = jnp.sqrt((members - 1.0) / scaling)
    mixing = (factor * inverse + shifted)[:, :local]
    high, low = halves(mixing)
    chosen[:, :local] = high
    chosen[:, local:] = low
    many = grouping(rows)

    def block(b):
        for pieces, upper, lower in zip(layout, uppers, lowers):
            size = upper.shape[0] // rows
            at = pl.ds(b * many * size, many * size)
            value = dot(upper[at], chosen[...])
            value = value[:, :local] + value[:, local:] + dot(lower[at], chosen[:, :local])
            for i in range(many):
                for start, column, length in pieces:
                    natural[i, pl.ds(column, length)] = value[
                        i * size + start : i * size + start + length
                    ]
        for i in range(many):
            r = b * many + i
            middle_row = centres[0][pl.ds(r, 1)] + centres[1][pl.ds(r, 1)]
            out[pl.ds(r, local, stride=rows)] = natural[i].T + middle_row

    loop(rows // many, block)


def shift(value, axes, *moves):
    sizes = [lax.axis_size(a) for a in axes]
    pairs = []
    total = 1
    for s in sizes:
        total *= s
    for flat in range(total):
        rest, place = flat, []
        for s in reversed(sizes):
            place.append(rest % s)
            rest //= s
        place = place[::-1]
        to = 0
        for s, p, m in zip(sizes, place, moves):
            to = to * s + (p + m) % s
        pairs.append((flat, to))
    return lax.ppermute(value, axes if len(axes) > 1 else axes[0], pairs)


def trade(value, axis, first):
    size = lax.axis_size(axis)
    if size % 2:
        raise ValueError("odd ring")
    start = 1 if first else 0
    pairs = [(i % size, (i + 1) % size) for i in range(start, size, 2)]
    return lax.ppermute(value, axis, pairs + [(j, i) for i, j in pairs])


def role_sums(value, name="own"):
    size = lax.axis_size("role")
    if size & (size - 1) or size == 1:
        return [(lax.psum(value, "role"), jnp.zeros_like(value))]
    stages = []
    step = 1
    while step < size:
        with jax.named_scope(f"{name}_{step}"):
            other = lax.ppermute(value, "role", [(i, i ^ step) for i in range(size)])
        stages.append((value, other))
        value = value + other
        step *= 2
    return stages


def shards(
    ensemble,
    diffusion,
    drift_rows,
    drift_cols,
    observed_cells,
    observed_count,
    observed_values,
    observed_weights,
):
    groups = lax.axis_size("member")
    roles = lax.axis_size("role")
    local, rows, cols = ensemble.shape
    members = local * groups
    width = STEPS
    lanes = max(local, cols)
    cut, low, high = parted(cols)
    strip = struct(width * cut + 4 * width, lanes)
    rest = struct(width * (cols - cut) + 2 * width * width + 2 * width, lanes)
    edge = struct(rows * width + rows, lanes)
    field, kept, early, late, left, right = call(
        functools.partial(pack_kernel, "domain"),
        (struct(rows, cols, local), struct(3, rows, cols), strip, strip, edge, edge),
        ensemble.reshape(local * rows, cols),
        diffusion,
        drift_rows,
        drift_cols,
        name="pack",
        raw=4,
    )
    early = trade(early, "domain", True)
    late = trade(late, "domain", False)
    left, right = shift(right, ("role",), 1), shift(left, ("role",), -1)
    weight = call(
        functools.partial(weight_kernel, "role"),
        struct(cols, 2 * rows),
        observed_count.reshape(1, 1),
        observed_cells,
        observed_values,
        observed_weights,
        raw=4,
        name="weights",
    )
    early_rest, late_rest = call(
        functools.partial(turn_kernel, "domain"),
        (rest, rest),
        field,
        left,
        right,
        weight,
        name="turn",
    )
    early_rest = trade(early_rest, "domain", True)
    late_rest = trade(late_rest, "domain", False)
    padded = pltpu.VMEM((rows + 2 * width, cols + 2 * LEAD, local), jnp.float32)
    scratch = (
        padded,
        padded,
        pltpu.VMEM((4, rows + 2 * width, cols + 2 * LEAD, local), jnp.float32),
        pltpu.VMEM((5, 2 * width, cols), jnp.float32),
    )
    middle = call(
        functools.partial(middle_kernel, "domain"),
        struct(rows, high - low, local),
        field,
        kept,
        early,
        late,
        scratch=scratch,
        name="middle",
    )
    sides = call(
        functools.partial(sides_kernel, "domain"),
        struct(rows, cols - high + low, local),
        field,
        kept,
        early,
        late,
        left,
        right,
        early_rest,
        late_rest,
        scratch=scratch,
        name="sides",
    )

    def gathered(value):
        others = [shift(value, ("member",), s) for s in range(1, groups)]
        return jnp.concatenate(others, axis=0) if len(others) > 1 else others[0]

    middle_others = gathered(middle)
    sides_others = gathered(sides)
    layout = (
        ((0, low, high - low),),
        ((0, high, cols - high), (cols - high, 0, low)),
    )

    def deviations(columns):
        one = struct(rows * columns, members, kind=jnp.bfloat16)
        return one, one, struct(rows, cols)

    pair = groups == 2 and local % 128 == 0
    if pair:
        sided = rows * (cols - high + low)
        half = struct(local, sided, kind=jnp.bfloat16)
        alone, left_half, right_half, spread = call(
            functools.partial(own_gram_kernel, layout),
            (struct(local, local), half, half, struct(sided, local)),
            middle,
            sides,
            weight,
            name="own_gram",
        )
        stages = role_sums(alone)
        started = sum(stages[0])
        cross = struct(local + 8, local)
        upper_a, lower_a, centre_a, total = call(
            functools.partial(first_cross_kernel, layout[0]),
            (*deviations(high - low), cross),
            middle,
            middle_others,
            weight,
            started,
            name="first_cross",
        )
        alone, arriving = stages[-1]
        total, alone = lax.optimization_barrier((total, alone))
        alone = alone + arriving
        gram = call(
            last_cross_kernel,
            cross,
            sides,
            sides_others,
            left_half,
            right_half,
            spread,
            total,
            alone,
            name="last_cross",
        )
        gram, alone = lax.optimization_barrier((gram, alone))
        with jax.named_scope("facing"):
            facing = shift(alone, ("member",), 1)
        grams = (*role_sums(gram, "cross")[-1], alone, facing)
        upper_b, lower_b, centre_b = call(
            functools.partial(deviation_kernel, layout[1]),
            deviations(cols - high + low),
            sides,
            sides_others,
            gram,
            name="deviations",
        )
    else:
        blocks = members // 128
        size = blocks * (blocks + 1) // 2 * 128 + 8
        square = struct(members, members)
        vector = struct(1, members)
        upper_a, lower_a, centre_a, total, tilt = call(
            functools.partial(first_gram_kernel, groups, layout[0]),
            (*deviations(high - low), square, vector),
            middle,
            middle_others,
            weight,
            name="first_gram",
        )
        gram, upper_b, lower_b, centre_b = call(
            functools.partial(last_gram_kernel, groups, layout[1]),
            (struct(size, 128), *deviations(cols - high + low)),
            sides,
            sides_others,
            weight,
            total,
            tilt,
            scratch=(
                pltpu.VMEM((members, members), jnp.float32),
                pltpu.VMEM((1, members), jnp.float32),
            ),
            name="last_gram",
        )
        grams = role_sums(gram)[-1]
    return call(
        functools.partial(analysis_kernel, layout, pair),
        struct(local * rows, cols),
        *grams,
        upper_a,
        upper_b,
        lower_a,
        lower_b,
        centre_a,
        centre_b,
        scratch=(
            pltpu.VMEM((members, members), jnp.float32),
            pltpu.VMEM((members, 2 * local), jnp.bfloat16),
            pltpu.VMEM((4, cols, local), jnp.float32),
        ),
        name="analysis",
        result=True,
    ).reshape(local, rows, cols)


def solution(mesh):
    placed = (
        P("member", "domain", "role"),
        P("domain", "role"),
        P("domain", "role"),
        P("domain", "role"),
        P("domain", None),
        P("domain"),
        P("domain", None),
        P("domain", None),
    )
    return jax.shard_map(
        shards, mesh=mesh, in_specs=placed, out_specs=P("member", "domain", "role"), check_vma=False
    )
```

```python
import functools

import jax
import jax.numpy as jnp
from jax import lax
from jax.experimental import pallas as pl
from jax.experimental.pallas import tpu as pltpu
from jax.sharding import PartitionSpec as P


STEPS = 4
ITERS = 6
LEAD = 16


VMEM = pl.BlockSpec(memory_space=pltpu.VMEM)
SMEM = pl.BlockSpec(memory_space=pltpu.SMEM)
ROOM = 1 << 20


def struct(*shape, kind=jnp.float32):
    return jax.ShapeDtypeStruct(shape, kind)


def near(shape, kind):
    size = jnp.dtype(kind).itemsize
    for place, extent in enumerate(shape[::-1]):
        unit = (128, 32 // jnp.dtype(kind).itemsize, 1)[min(place, 2)]
        size *= -(-extent // unit) * unit
    return size <= ROOM


def call(body, outs, *args, scratch=(), scalars=0, raw=0, result=False):
    placed = list(args[: scalars + raw])
    for value in args[scalars + raw :]:
        if near(value.shape, value.dtype):
            value = pltpu.with_memory_space_constraint(value, pltpu.VMEM)
        placed.append(value)
    if not result:
        outs = jax.tree.map(
            lambda s: pltpu.VMEM(s.shape, s.dtype) if near(s.shape, s.dtype) else s, outs
        )
    return pl.pallas_call(
        body,
        out_shape=outs,
        in_specs=[SMEM] * scalars + [VMEM] * (len(args) - scalars),
        out_specs=tuple(VMEM for _ in outs) if isinstance(outs, tuple) else VMEM,
        scratch_shapes=scratch,
    )(*placed)


def halves(value):
    upper = value.astype(jnp.bfloat16)
    lower = (value - upper.astype(jnp.float32)).astype(jnp.bfloat16)
    return upper, lower


def dot(a, b, dims=((1,), (0,))):
    return lax.dot_general(a, b, (dims, ((), ())), preferred_element_type=jnp.float32)


def dot3(a, b, dims=((1,), (0,))):
    return dot(a[0], b[0], dims) + (dot(a[0], b[1], dims) + dot(a[1], b[0], dims))


def loop(count, body):
    if count <= 16:
        for i in range(count):
            body(i)
    else:
        lax.fori_loop(0, count, lambda i, c: (body(i), c)[1], 0)


def parted(cols):
    cut = (cols // 2 + 16) // 8 * 8
    return cut, 8, cut - 8


def parity(axis):
    return lax.rem(lax.axis_index(axis), 2)


def pack_kernel(axis, ens, diffusion, drift_rows, drift_cols, field, kept, early, late, left, right):
    odd = parity(axis)
    rows, cols, members = field.shape
    width = STEPS
    cut = parted(cols)[0]
    lanes = pl.ds(0, members)
    for r in range(rows):
        turned = ens[pl.ds(r, members, stride=rows)].T
        field[r] = turned
        part = pl.ds(r * width, width)
        left[part, lanes] = turned[:width]
        right[part, lanes] = turned[cols - width :]
    for i in range(width):
        part = pl.ds(i * cut, cut)
        early[part, lanes] = field[i + odd * (rows - width), pl.ds(0, cut)]
        late[part, lanes] = field[i + (1 - odd) * (rows - width), pl.ds(0, cut)]
    near_edge = jnp.zeros((rows, cols), jnp.float32)
    far_edge = near_edge
    lane = lax.broadcasted_iota(jnp.int32, (rows, cols), 1)
    for k, part in enumerate((diffusion, drift_rows, drift_cols)):
        at = pl.ds(width * cut + k * width, width)
        top, bottom = part[:width], part[rows - width :]
        early[at, pl.ds(0, cols)] = jnp.where(odd == 0, top, bottom)
        late[at, pl.ds(0, cols)] = jnp.where(odd == 0, bottom, top)
        value = part[...]
        kept[k] = value
        mine = (lane >= k * width) & (lane < (k + 1) * width)
        if k:
            near_edge = jnp.where(mine, pltpu.roll(value, k * width, 1), near_edge)
        else:
            near_edge = jnp.where(mine, value, near_edge)
        far_edge = jnp.where(mine, pltpu.roll(value, (k + 1) * width, 1), far_edge)
    left[pl.ds(rows * width, rows), pl.ds(0, cols)] = near_edge
    right[pl.ds(rows * width, rows), pl.ds(0, cols)] = far_edge


def turn_kernel(axis, field, left, right, after, early, late):
    rows, cols, members = field.shape
    odd = parity(axis)
    width = STEPS
    area = width * width
    cut = parted(cols)[0]
    size = cols - cut
    lanes = pl.ds(0, members)
    for i in range(width):
        at = pl.ds(i * size, size)
        early[at, lanes] = field[i + odd * (rows - width), pl.ds(cut, size)]
        late[at, lanes] = field[i + (1 - odd) * (rows - width), pl.ds(cut, size)]
    base = width * size
    for i, side in enumerate((left, right)):
        at = pl.ds(base + i * area, area)
        top, bottom = side[pl.ds(0, area)], side[pl.ds((rows - width) * width, area)]
        early[at] = jnp.where(odd == 0, top, bottom)
        late[at] = jnp.where(odd == 0, bottom, top)
        at = pl.ds(base + 2 * area + i * width, width)
        top = side[pl.ds(rows * width, width)]
        bottom = side[pl.ds(rows * width + rows - width, width)]
        early[at] = jnp.where(odd == 0, top, bottom)
        late[at] = jnp.where(odd == 0, bottom, top)


def widen(write, line, columns, members):
    for at, parts in columns:
        size = parts[0].shape[0]
        diffusion, rowwise, colwise = (
            jnp.broadcast_to(p[:, line : line + 1], (size, members)) for p in parts
        )
        here = pl.ds(at, size)
        write(0, here, 1.0 - 4.0 * diffusion - rowwise - colwise)
        write(1, here, diffusion)
        write(2, here, diffusion + rowwise)
        write(3, here, diffusion + colwise)


def spread_rows(spread, lines, columns, members):
    for line, row in lines:

        def write(k, here, value, row=row):
            spread[k, row, here] = value

        widen(write, line, columns, members)


def march(rows, even, odd, spread, ranges, finals, store):
    width = STEPS
    source, target = even, odd
    for step in range(1, STEPS + 1):
        last = step == STEPS

        def advance(r, source=source, target=target, last=last):
            for at, size in finals if last else ranges:
                here = pl.ds(at, size)
                value = (
                    spread[0, r, here] * source[r, here]
                    + spread[1, r, here] * (source[r + 1, here] + source[r, pl.ds(at + 1, size)])
                    + spread[2, r, here] * source[r - 1, here]
                    + spread[3, r, here] * source[r, pl.ds(at - 1, size)]
                )
                if last:
                    store(r - width, at, value)
                else:
                    target[r, here] = value

        loop(rows + 2 * width - 2 * step, lambda i: advance(i + step))
        source, target = target, source


def coefficient_rows(odd, kept, early, late, stage, cut):
    rows, cols = kept.shape[1:]
    width = STEPS
    for k in range(3):
        at = pl.ds(width * cut + k * width, width), pl.ds(0, cols)
        stage[k, pl.ds(0, width)] = jnp.where(odd == 0, early[at], late[at])
        stage[k, pl.ds(width, width)] = jnp.where(odd == 0, late[at], early[at])
    lines = [(i, i) for i in range(1, width)]
    lines += [(width + i, width + rows + i) for i in range(width - 1)]
    inside = [(r, width + r) for r in range(rows)]
    return [kept[k].T for k in range(3)], inside, [stage[k].T for k in range(3)], lines


def middle_kernel(axis, field, kept, early, late, out, one, two, spread, stage):
    rows, cols, members = field.shape
    width = STEPS
    cut, low, high = parted(cols)
    lanes = pl.ds(0, members)
    odd = parity(axis)
    own, inside, beyond, lines = coefficient_rows(odd, kept, early, late, stage, cut)
    for parts, places in ((beyond, lines), (own, inside)):
        spread_rows(spread, places, [(LEAD, [p[:cut] for p in parts])], members)
    here = pl.ds(LEAD, cut)
    for i in range(width):
        part = pl.ds(i * cut, cut)
        one[i + odd * (rows + width), here] = early[part, lanes]
        one[i + (1 - odd) * (rows + width), here] = late[part, lanes]
    for r in range(rows):
        one[width + r, here] = field[r, pl.ds(0, cut)]

    def store(r, at, value):
        out[r] = value

    march(rows, one, two, spread, [(LEAD, cut)], [(LEAD + low, high - low)], store)


def sides_kernel(
    axis,
    field,
    kept,
    early,
    late,
    left,
    right,
    early_rest,
    late_rest,
    out,
    one,
    two,
    spread,
    stage,
):
    rows, cols, members = field.shape
    width = STEPS
    area = width * width
    cut, low, high = parted(cols)
    first, second = low + 8, high - 8
    size = cols - cut
    base = width * size
    lanes = pl.ds(0, members)
    odd = parity(axis)
    own, inside, beyond, lines = coefficient_rows(odd, kept, early, late, stage, cut)
    for side in range(2):
        at = pl.ds(base + 2 * area + side * width, width), pl.ds(0, cols)
        stage[3 + side, pl.ds(0, width)] = jnp.where(odd == 0, early_rest[at], late_rest[at])
        stage[3 + side, pl.ds(width, width)] = jnp.where(odd == 0, late_rest[at], early_rest[at])
    edge = pl.ds(rows * width, rows), pl.ds(0, cols)
    for parts, near_part, far_part, places in (
        (beyond, stage[3].T, stage[4].T, lines),
        (own, left[edge].T, right[edge].T, inside),
    ):
        halo = [slice(k * width, (k + 1) * width) for k in range(3)]
        columns = [
            (LEAD - width, [near_part[h] for h in halo]),
            (LEAD, [p[:first] for p in parts]),
            (LEAD + second, [p[second:] for p in parts]),
            (LEAD + cols, [far_part[h] for h in halo]),
        ]
        spread_rows(spread, places, columns, members)
    before = pl.ds(LEAD - width, width)
    after = pl.ds(LEAD + cols, width)
    for i in range(width):
        for j, strip, rest in (
            (i + odd * (rows + width), early, early_rest),
            (i + (1 - odd) * (rows + width), late, late_rest),
        ):
            one[j, before] = rest[pl.ds(base + i * width, width), lanes]
            one[j, pl.ds(LEAD, first)] = strip[pl.ds(i * cut, first), lanes]
            one[j, pl.ds(LEAD + second, cut - second)] = strip[
                pl.ds(i * cut + second, cut - second), lanes
            ]
            one[j, pl.ds(LEAD + cut, size)] = rest[pl.ds(i * size, size), lanes]
            one[j, after] = rest[pl.ds(base + area + i * width, width), lanes]
    for r in range(rows):
        part = pl.ds(r * width, width)
        one[width + r, before] = left[part, lanes]
        one[width + r, pl.ds(LEAD, first)] = field[r, pl.ds(0, first)]
        one[width + r, pl.ds(LEAD + second, cols - second)] = field[
            r, pl.ds(second, cols - second)
        ]
        one[width + r, after] = right[part, lanes]

    def store(r, at, value):
        if at == LEAD:
            out[r, pl.ds(cols - high, low)] = value
        else:
            out[r, pl.ds(0, cols - high)] = value

    march(
        rows,
        one,
        two,
        spread,
        [(LEAD + second, cols - second + 8), (LEAD - 8, first + 8)],
        [(LEAD + high, cols - high), (LEAD, low)],
        store,
    )


def weight_kernel(axis, count, cells, values, weights, out):
    cols, twice = out.shape
    rows = twice // 2
    slots = cells.shape[1]
    full = cols * lax.axis_size(axis)
    cell = cells[...]
    if full & (full - 1):
        row_of = lax.div(cell, full)
    else:
        row_of = lax.shift_right_logical(cell, full.bit_length() - 1)
    col_of = cell - row_of * full - lax.axis_index(axis) * cols
    slot = lax.broadcasted_iota(jnp.int32, (1, slots), 1)
    plain = jnp.where(slot < count[...], weights[...], 0.0)
    valued = plain * values[...]
    here = lax.broadcasted_iota(jnp.int32, (cols, slots), 0) == col_of
    here = jnp.where(here, 1.0, 0.0).astype(jnp.bfloat16)
    line = lax.broadcasted_iota(jnp.int32, (rows, slots), 0) == row_of
    value = jnp.concatenate([jnp.where(line, plain, 0.0), jnp.where(line, valued, 0.0)], axis=0)
    total = jnp.zeros((cols, twice), jnp.float32)
    for _ in range(3):
        part = value.astype(jnp.bfloat16)
        value = value - part.astype(jnp.float32)
        total = total + dot(here, part, ((1,), (1,)))
    out[...] = total


def cell_weights(rows, pieces, weight, b, many):
    plain, valued = [], []
    for i in range(many):
        r = b * many + i
        for start, column, length in pieces:
            source = weight[pl.ds(column, length)]
            line = lax.broadcasted_iota(jnp.int32, source.shape, 1)
            plain.append(jnp.sum(jnp.where(line == r, source, 0.0), axis=1, keepdims=True))
            valued.append(jnp.sum(jnp.where(line == r + rows, source, 0.0), axis=1, keepdims=True))
    return jnp.concatenate(plain, axis=0), jnp.concatenate(valued, axis=0)


def lay_rows(pieces, column_of, size, centre, b, many):
    cols = centre.shape[1]
    for i in range(many):
        row = jnp.zeros((1, cols), jnp.float32)
        for start, column, length in pieces:
            place = lax.broadcasted_iota(jnp.int32, (length, cols), 0) + column
            here = place == lax.broadcasted_iota(jnp.int32, (length, cols), 1)
            part = column_of[i * size + start : i * size + start + length]
            row = row + jnp.sum(jnp.where(here, part, 0.0), axis=0, keepdims=True)
        centre[pl.ds(b * many + i, 1)] = row


def grouping(rows):
    return next(n for n in (4, 2, 1) if rows % n == 0)


def cells_of(ref, b, many, start=0):
    value = ref[pl.ds(start + b * many, many)]
    return value.reshape(many * value.shape[1], value.shape[2])


def lane_mean(value):
    return jnp.sum(value, axis=1, keepdims=True) * (1.0 / value.shape[1])


def wide(parts):
    return jnp.concatenate(parts, axis=1)


def dot_wide(a, both, size):
    value = dot(a[0], both)
    return value[:, :size] + value[:, size:] + dot(a[1], both[:, :size])


def gram_kernel(groups, pieces, own, others, weight, upper, lower, centre, total, tilt):
    rows, size, _ = own.shape
    many = grouping(rows)
    depth = many * size

    def block(b):
        parts = [cells_of(own, b, many)]
        parts += [cells_of(others, b, many, g * rows) for g in range(groups - 1)]
        value = wide(parts) if groups > 1 else parts[0]
        mean = lane_mean(value)
        deviation = value - mean
        plain, valued = cell_weights(rows, pieces, weight, b, many)
        lay_rows(pieces, mean, size, centre, b, many)
        high, low = halves(deviation)
        at = pl.ds(b * depth, depth)
        upper[at] = high
        lower[at] = low
        turned = (deviation * plain).T
        total[...] += dot3(halves(turned), (high, low))
        tilt[...] += jnp.sum(deviation * (valued - plain * mean), axis=0, keepdims=True)

    loop(rows // many, block)


def own_gram_kernel(layout, middle, sides, weight, total, left, right, spread):
    local = total.shape[0]
    total[...] = jnp.zeros_like(total)
    for pieces, own in zip(layout, (middle, sides)):
        rows, size, _ = own.shape
        many = grouping(rows)
        depth = many * size

        def block(b, pieces=pieces, own=own, rows=rows, many=many, depth=depth):
            value = cells_of(own, b, many)
            mean = lane_mean(value)
            deviation = value - mean
            plain, valued = cell_weights(rows, pieces, weight, b, many)
            turned = halves((deviation * plain).T)
            total[...] += dot_wide(turned, wide(halves(deviation)), local)
            if own is sides:
                at = pl.ds(b * depth, depth)
                left[:, at], right[:, at] = turned
                lane = lax.broadcasted_iota(jnp.int32, (depth, local), 1)
                spread[at] = jnp.where(lane == 0, plain, jnp.where(lane == 1, valued, mean))

        loop(rows // many, block)


def tally(total, local, value, partner, plain, valued, mean_own):
    mean_partner = lane_mean(partner)
    counter = partner - mean_partner
    mean = 0.5 * (mean_own + mean_partner)
    apart = 0.5 * (mean_own - mean_partner)
    deviation = value - mean
    pull = valued - plain * mean
    tie = plain * apart

    def add(row, columns):
        total[pl.ds(local + row, 1)] += jnp.sum(columns, axis=0, keepdims=True)

    add(0, deviation * pull)
    add(1, (partner - mean) * pull)
    add(2, deviation * tie)
    add(3, (mean - partner) * tie)
    add(4, jnp.broadcast_to(tie * apart, deviation.shape))
    return counter


def part_deviations(pieces, value, partner, size, upper, lower, centre, b, many):
    value = wide([value, partner])
    mean = lane_mean(value)
    lay_rows(pieces, mean, size, centre, b, many)
    at = pl.ds(b * many * size, many * size)
    upper[at], lower[at] = halves(value - mean)


def first_cross_kernel(pieces, own, other, weight, after, upper, lower, centre, total):
    total[...] = jnp.zeros_like(total)
    rows, size, local = own.shape
    many = grouping(rows)

    def block(b):
        value, partner = cells_of(own, b, many), cells_of(other, b, many)
        mean = lane_mean(value)
        plain, valued = cell_weights(rows, pieces, weight, b, many)
        counter = tally(total, local, value, partner, plain, valued, mean)
        part_deviations(pieces, value, partner, size, upper, lower, centre, b, many)
        turned = ((value - mean) * plain).T
        total[pl.ds(0, local)] += dot_wide(halves(turned), wide(halves(counter)), local)

    loop(rows // many, block)


def last_cross_kernel(own, other, left, right, spread, before, after, total):
    total[...] = before[...]
    rows, size, local = own.shape
    many = grouping(rows)
    depth = many * size

    def block(b):
        at = pl.ds(b * depth, depth)
        value, partner = cells_of(own, b, many), cells_of(other, b, many)
        counter = tally(total, local, value, partner, *(spread[at, i : i + 1] for i in range(3)))
        total[pl.ds(0, local)] += dot_wide(
            (left[:, at], right[:, at]), wide(halves(counter)), local
        )

    loop(rows // many, block)


def deviation_kernel(pieces, own, other, after, upper, lower, centre):
    rows, size, _ = own.shape
    many = grouping(rows)

    def block(b):
        value, partner = cells_of(own, b, many), cells_of(other, b, many)
        part_deviations(pieces, value, partner, size, upper, lower, centre, b, many)

    loop(rows // many, block)


def first_gram_kernel(groups, pieces, own, others, weight, upper, lower, centre, total, tilt):
    total[...] = jnp.zeros_like(total)
    tilt[...] = jnp.zeros_like(tilt)
    gram_kernel(groups, pieces, own, others, weight, upper, lower, centre, total, tilt)


def last_gram_kernel(
    groups, pieces, own, others, weight, before, tilted, gram, upper, lower, centre, total, tilt
):
    total[...] = before[...]
    tilt[...] = tilted[...]
    gram_kernel(groups, pieces, own, others, weight, upper, lower, centre, total, tilt)
    pull = gram.shape[0] - 8
    blocks = total.shape[0] // 128
    innovation = tilt[...]
    at = 0
    gram[pl.ds(pull, 8)] = jnp.zeros((8, 128), jnp.float32)
    for i in range(blocks):
        gram[pl.ds(pull + i, 1)] = innovation[:, i * 128 : (i + 1) * 128]
        for j in range(i, blocks):
            gram[pl.ds(at, 128)] = total[i * 128 : (i + 1) * 128, j * 128 : (j + 1) * 128]
            at += 128


def assemble(first, second, whole):
    blocks = whole.shape[0] // 128
    pull = first.shape[0] - 8
    at = 0
    for i in range(blocks):
        for j in range(i, blocks):
            block = first[pl.ds(at, 128)] + second[pl.ds(at, 128)]
            whole[i * 128 : (i + 1) * 128, j * 128 : (j + 1) * 128] = block
            if j > i:
                whole[j * 128 : (j + 1) * 128, i * 128 : (i + 1) * 128] = block.T
            at += 128
    return wide([first[pl.ds(pull + i, 1)] + second[pl.ds(pull + i, 1)] for i in range(blocks)])


def assemble_pair(first, second, own, other, whole):
    local = own.shape[1]
    cross = first[pl.ds(0, local)] + second[pl.ds(0, local)]
    rest = first[pl.ds(local, 8)] + second[pl.ds(local, 8)]
    square = rest[4:5]
    diagonal = lax.broadcasted_iota(jnp.int32, (local, local), 0) == lax.broadcasted_iota(
        jnp.int32, (local, local), 1
    )
    uprights = []
    for i, part in enumerate((own, other)):
        tie = rest[2 + i : 3 + i]
        upright = jnp.sum(jnp.where(diagonal, tie, 0.0), axis=1, keepdims=True)
        uprights.append(upright)
        at = slice(i * local, (i + 1) * local)
        whole[at, at] = part[...] + upright + (tie - square)
    cross = cross - uprights[0] + (square - rest[3:4])
    whole[:local, local:] = cross
    whole[local:, :local] = cross.T
    return wide([rest[0:1], rest[1:2]])


def analysis_kernel(layout, pair, *rest):
    if pair:
        first, second, own, other, *rest = rest
    else:
        first, second, *rest = rest
    uppers, lowers, centres = rest[0:2], rest[2:4], rest[4:6]
    out, whole, chosen, natural = rest[6:]
    rows, _ = centres[0].shape
    local = natural.shape[2]
    members = whole.shape[0]
    if pair:
        innovation = assemble_pair(first, second, own, other, whole)
    else:
        innovation = assemble(first, second, whole)
    down = lax.broadcasted_iota(jnp.int32, (members, members), 0)
    across = lax.broadcasted_iota(jnp.int32, (members, members), 1)
    identity = jnp.where(down == across, 1.0, 0.0)
    matrix = whole[...] + (members - 1.0) * identity
    parts = halves(matrix)
    square = dot3(parts, parts)
    squares = jnp.sum(jnp.sum(matrix * matrix, axis=1, keepdims=True), axis=0, keepdims=True)
    scaling = jnp.sqrt(squares)
    current = matrix * (1.0 / scaling)
    square = square * (1.0 / scaling) * (1.0 / scaling)
    inverse = None
    for repeat in range(0, ITERS, 2):
        if repeat:
            parts = halves(current)
            square = dot3(parts, parts)
        inner = 0.0625 * square - 0.5625 * current
        outer = 2.25 * identity - 2.4375 * current + 1.6875 * square
        both = outer + dot3(halves(square), halves(inner))
        both_parts = halves(both)
        if repeat + 2 < ITERS:
            twice = dot3(both_parts, both_parts)
            current = dot3(halves(current), halves(twice))
        inverse = both if inverse is None else dot3(halves(inverse), both_parts)
    once = jnp.sum(inverse * innovation, axis=1, keepdims=True)
    once_row = jnp.sum(jnp.where(down == across, once, 0.0), axis=0, keepdims=True)
    shifted = jnp.sum(inverse * once_row, axis=1, keepdims=True) * (1.0 / scaling)
    factor = jnp.sqrt((members - 1.0) / scaling)
    mixing = (factor * inverse + shifted)[:, :local]
    high, low = halves(mixing)
    chosen[:, :local] = high
    chosen[:, local:] = low
    many = grouping(rows)

    def block(b):
        for pieces, upper, lower in zip(layout, uppers, lowers):
            size = upper.shape[0] // rows
            at = pl.ds(b * many * size, many * size)
            value = dot(upper[at], chosen[...])
            value = value[:, :local] + value[:, local:] + dot(lower[at], chosen[:, :local])
            for i in range(many):
                for start, column, length in pieces:
                    natural[i, pl.ds(column, length)] = value[
                        i * size + start : i * size + start + length
                    ]
        for i in range(many):
            r = b * many + i
            middle_row = centres[0][pl.ds(r, 1)] + centres[1][pl.ds(r, 1)]
            out[pl.ds(r, local, stride=rows)] = natural[i].T + middle_row

    loop(rows // many, block)


def shift(value, axes, *moves):
    sizes = [lax.axis_size(a) for a in axes]
    pairs = []
    total = 1
    for s in sizes:
        total *= s
    for flat in range(total):
        rest, place = flat, []
        for s in reversed(sizes):
            place.append(rest % s)
            rest //= s
        place = place[::-1]
        to = 0
        for s, p, m in zip(sizes, place, moves):
            to = to * s + (p + m) % s
        pairs.append((flat, to))
    return lax.ppermute(value, axes if len(axes) > 1 else axes[0], pairs)


def trade(value, axis, first):
    size = lax.axis_size(axis)
    if size % 2:
        raise ValueError("odd ring")
    start = 1 if first else 0
    pairs = [(i % size, (i + 1) % size) for i in range(start, size, 2)]
    return lax.ppermute(value, axis, pairs + [(j, i) for i, j in pairs])


def role_sums(value):
    size = lax.axis_size("role")
    if size & (size - 1) or size == 1:
        return [(lax.psum(value, "role"), jnp.zeros_like(value))]
    stages = []
    step = 1
    while step < size:
        other = lax.ppermute(value, "role", [(i, i ^ step) for i in range(size)])
        stages.append((value, other))
        value = value + other
        step *= 2
    return stages


def shards(
    ensemble,
    diffusion,
    drift_rows,
    drift_cols,
    observed_cells,
    observed_count,
    observed_values,
    observed_weights,
):
    groups = lax.axis_size("member")
    local, rows, cols = ensemble.shape
    members = local * groups
    width = STEPS
    lanes = max(local, cols)
    cut, low, high = parted(cols)
    strip = struct(width * cut + 4 * width, lanes)
    rest = struct(width * (cols - cut) + 2 * width * width + 2 * width, lanes)
    edge = struct(rows * width + rows, lanes)
    field, kept, early, late, left, right = call(
        functools.partial(pack_kernel, "domain"),
        (struct(rows, cols, local), struct(3, rows, cols), strip, strip, edge, edge),
        ensemble.reshape(local * rows, cols),
        diffusion,
        drift_rows,
        drift_cols,
        raw=4,
    )
    early = trade(early, "domain", True)
    late = trade(late, "domain", False)
    left, right = shift(right, ("role",), 1), shift(left, ("role",), -1)
    weight = call(
        functools.partial(weight_kernel, "role"),
        struct(cols, 2 * rows),
        observed_count.reshape(1, 1),
        observed_cells,
        observed_values,
        observed_weights,
        raw=4,
    )
    early_rest, late_rest = call(
        functools.partial(turn_kernel, "domain"), (rest, rest), field, left, right, weight
    )
    early_rest = trade(early_rest, "domain", True)
    late_rest = trade(late_rest, "domain", False)
    padded = pltpu.VMEM((rows + 2 * width, cols + 2 * LEAD, local), jnp.float32)
    scratch = (
        padded,
        padded,
        pltpu.VMEM((4, rows + 2 * width, cols + 2 * LEAD, local), jnp.float32),
        pltpu.VMEM((5, 2 * width, cols), jnp.float32),
    )
    middle = call(
        functools.partial(middle_kernel, "domain"),
        struct(rows, high - low, local),
        field,
        kept,
        early,
        late,
        scratch=scratch,
    )
    sides = call(
        functools.partial(sides_kernel, "domain"),
        struct(rows, cols - high + low, local),
        field,
        kept,
        early,
        late,
        left,
        right,
        early_rest,
        late_rest,
        scratch=scratch,
    )

    def gathered(value):
        others = [shift(value, ("member",), s) for s in range(1, groups)]
        return jnp.concatenate(others, axis=0) if len(others) > 1 else others[0]

    middle_others = gathered(middle)
    sides_others = gathered(sides)
    layout = (
        ((0, low, high - low),),
        ((0, high, cols - high), (cols - high, 0, low)),
    )

    def deviations(columns):
        one = struct(rows * columns, members, kind=jnp.bfloat16)
        return one, one, struct(rows, cols)

    pair = groups == 2 and local % 128 == 0
    if pair:
        sided = rows * (cols - high + low)
        half = struct(local, sided, kind=jnp.bfloat16)
        alone, left_half, right_half, spread = call(
            functools.partial(own_gram_kernel, layout),
            (struct(local, local), half, half, struct(sided, local)),
            middle,
            sides,
            weight,
        )
        stages = role_sums(alone)
        started = sum(stages[0])
        cross = struct(local + 8, local)
        upper_a, lower_a, centre_a, total = call(
            functools.partial(first_cross_kernel, layout[0]),
            (*deviations(high - low), cross),
            middle,
            middle_others,
            weight,
            started,
        )
        alone, arriving = stages[-1]
        total, alone = lax.optimization_barrier((total, alone))
        alone = alone + arriving
        gram = call(
            last_cross_kernel,
            cross,
            sides,
            sides_others,
            left_half,
            right_half,
            spread,
            total,
            alone,
        )
        gram, alone = lax.optimization_barrier((gram, alone))
        facing = shift(alone, ("member",), 1)
        grams = (*role_sums(gram)[-1], alone, facing)
        upper_b, lower_b, centre_b = call(
            functools.partial(deviation_kernel, layout[1]),
            deviations(cols - high + low),
            sides,
            sides_others,
            gram,
        )
    else:
        blocks = members // 128
        size = blocks * (blocks + 1) // 2 * 128 + 8
        square = struct(members, members)
        vector = struct(1, members)
        upper_a, lower_a, centre_a, total, tilt = call(
            functools.partial(first_gram_kernel, groups, layout[0]),
            (*deviations(high - low), square, vector),
            middle,
            middle_others,
            weight,
        )
        gram, upper_b, lower_b, centre_b = call(
            functools.partial(last_gram_kernel, groups, layout[1]),
            (struct(size, 128), *deviations(cols - high + low)),
            sides,
            sides_others,
            weight,
            total,
            tilt,
            scratch=(
                pltpu.VMEM((members, members), jnp.float32),
                pltpu.VMEM((1, members), jnp.float32),
            ),
        )
        grams = role_sums(gram)[-1]
    return call(
        functools.partial(analysis_kernel, layout, pair),
        struct(local * rows, cols),
        *grams,
        upper_a,
        upper_b,
        lower_a,
        lower_b,
        centre_a,
        centre_b,
        scratch=(
            pltpu.VMEM((members, members), jnp.float32),
            pltpu.VMEM((members, 2 * local), jnp.bfloat16),
            pltpu.VMEM((4, cols, local), jnp.float32),
        ),
        result=True,
    ).reshape(local, rows, cols)


def solution(mesh):
    placed = (
        P("member", "domain", "role"),
        P("domain", "role"),
        P("domain", "role"),
        P("domain", "role"),
        P("domain", None),
        P("domain"),
        P("domain", None),
        P("domain", None),
    )
    return jax.shard_map(
        shards, mesh=mesh, in_specs=placed, out_specs=P("member", "domain", "role"), check_vma=False
    )
```

```python
import functools

import jax
import jax.numpy as jnp
from jax import lax
from jax.experimental import pallas as pl
from jax.experimental.pallas import tpu as pltpu
from jax.sharding import PartitionSpec as P


STEPS = 4
ITERS = 6
LEAD = 16


VMEM = pl.BlockSpec(memory_space=pltpu.VMEM)
SMEM = pl.BlockSpec(memory_space=pltpu.SMEM)
ROOM = 1 << 20


def struct(*shape, kind=jnp.float32):
    return jax.ShapeDtypeStruct(shape, kind)


def near(shape, kind):
    size = jnp.dtype(kind).itemsize
    for place, extent in enumerate(shape[::-1]):
        unit = (128, 32 // jnp.dtype(kind).itemsize, 1)[min(place, 2)]
        size *= -(-extent // unit) * unit
    return size <= ROOM


def call(body, outs, *args, scratch=(), scalars=0, raw=0, result=False):
    placed = list(args[: scalars + raw])
    for value in args[scalars + raw :]:
        if near(value.shape, value.dtype):
            value = pltpu.with_memory_space_constraint(value, pltpu.VMEM)
        placed.append(value)
    if not result:
        outs = jax.tree.map(
            lambda s: pltpu.VMEM(s.shape, s.dtype) if near(s.shape, s.dtype) else s, outs
        )
    return pl.pallas_call(
        body,
        out_shape=outs,
        in_specs=[SMEM] * scalars + [VMEM] * (len(args) - scalars),
        out_specs=tuple(VMEM for _ in outs) if isinstance(outs, tuple) else VMEM,
        scratch_shapes=scratch,
    )(*placed)


def halves(value):
    upper = value.astype(jnp.bfloat16)
    lower = (value - upper.astype(jnp.float32)).astype(jnp.bfloat16)
    return upper, lower


def dot(a, b, dims=((1,), (0,))):
    return lax.dot_general(a, b, (dims, ((), ())), preferred_element_type=jnp.float32)


def dot3(a, b, dims=((1,), (0,))):
    return dot(a[0], b[0], dims) + (dot(a[0], b[1], dims) + dot(a[1], b[0], dims))


def loop(count, body):
    if count <= 16:
        for i in range(count):
            body(i)
    else:
        lax.fori_loop(0, count, lambda i, c: (body(i), c)[1], 0)


EDGE = 8


def parted(cols):
    return cols * 3 // 8 // 8 * 8, cols * 3 // 4 // 8 * 8


def parity(axis):
    return lax.rem(lax.axis_index(axis), 2)


def pack_kernel(
    axis,
    ens,
    diffusion,
    drift_rows,
    drift_cols,
    field,
    kept,
    early,
    late,
    early_next,
    late_next,
    left,
    right,
):
    odd = parity(axis)
    rows, cols, members = field.shape
    width = STEPS
    cut, end = parted(cols)
    more = end - cut
    lanes = pl.ds(0, members)
    for r in range(rows):
        turned = ens[pl.ds(r, members, stride=rows)].T
        field[r] = turned
        part = pl.ds(r * width, width)
        left[part, lanes] = turned[:width]
        right[part, lanes] = turned[cols - width :]
    for i in range(width):
        part = pl.ds(i * cut, cut)
        early[part, lanes] = field[i + odd * (rows - width), pl.ds(0, cut)]
        late[part, lanes] = field[i + (1 - odd) * (rows - width), pl.ds(0, cut)]
        part = pl.ds(i * more, more)
        early_next[part, lanes] = field[i + odd * (rows - width), pl.ds(cut, more)]
        late_next[part, lanes] = field[i + (1 - odd) * (rows - width), pl.ds(cut, more)]
    near_edge = jnp.zeros((rows, cols), jnp.float32)
    far_edge = near_edge
    lane = lax.broadcasted_iota(jnp.int32, (rows, cols), 1)
    for k, part in enumerate((diffusion, drift_rows, drift_cols)):
        at = pl.ds(width * cut + k * width, width)
        top, bottom = part[:width], part[rows - width :]
        early[at, pl.ds(0, cols)] = jnp.where(odd == 0, top, bottom)
        late[at, pl.ds(0, cols)] = jnp.where(odd == 0, bottom, top)
        value = part[...]
        kept[k] = value
        mine = (lane >= k * width) & (lane < (k + 1) * width)
        if k:
            near_edge = jnp.where(mine, pltpu.roll(value, k * width, 1), near_edge)
        else:
            near_edge = jnp.where(mine, value, near_edge)
        far_edge = jnp.where(mine, pltpu.roll(value, (k + 1) * width, 1), far_edge)
    left[pl.ds(rows * width, rows), pl.ds(0, cols)] = near_edge
    right[pl.ds(rows * width, rows), pl.ds(0, cols)] = far_edge


def turn_kernel(axis, field, left, right, after, early, late):
    rows, cols, members = field.shape
    odd = parity(axis)
    width = STEPS
    area = width * width
    cut = parted(cols)[1]
    size = cols - cut
    lanes = pl.ds(0, members)
    for i in range(width):
        at = pl.ds(i * size, size)
        early[at, lanes] = field[i + odd * (rows - width), pl.ds(cut, size)]
        late[at, lanes] = field[i + (1 - odd) * (rows - width), pl.ds(cut, size)]
    base = width * size
    for i, side in enumerate((left, right)):
        at = pl.ds(base + i * area, area)
        top, bottom = side[pl.ds(0, area)], side[pl.ds((rows - width) * width, area)]
        early[at] = jnp.where(odd == 0, top, bottom)
        late[at] = jnp.where(odd == 0, bottom, top)
        at = pl.ds(base + 2 * area + i * width, width)
        top = side[pl.ds(rows * width, width)]
        bottom = side[pl.ds(rows * width + rows - width, width)]
        early[at] = jnp.where(odd == 0, top, bottom)
        late[at] = jnp.where(odd == 0, bottom, top)


def widen(write, line, columns, members):
    for at, parts in columns:
        size = parts[0].shape[0]
        diffusion, rowwise, colwise = (
            jnp.broadcast_to(p[:, line : line + 1], (size, members)) for p in parts
        )
        here = pl.ds(at, size)
        write(0, here, 1.0 - 4.0 * diffusion - rowwise - colwise)
        write(1, here, diffusion)
        write(2, here, diffusion + rowwise)
        write(3, here, diffusion + colwise)


def spread_rows(spread, lines, columns, members):
    for line, row in lines:

        def write(k, here, value, row=row):
            spread[k, row, here] = value

        widen(write, line, columns, members)


def march(rows, even, odd, spread, ranges, finals, store):
    width = STEPS
    source, target = even, odd
    for step in range(1, STEPS + 1):
        last = step == STEPS

        def advance(r, source=source, target=target, last=last):
            for at, size in finals if last else ranges:
                here = pl.ds(at, size)
                value = (
                    spread[0, r, here] * source[r, here]
                    + spread[1, r, here] * (source[r + 1, here] + source[r, pl.ds(at + 1, size)])
                    + spread[2, r, here] * source[r - 1, here]
                    + spread[3, r, here] * source[r, pl.ds(at - 1, size)]
                )
                if last:
                    store(r - width, at, value)
                else:
                    target[r, here] = value

        loop(rows + 2 * width - 2 * step, lambda i: advance(i + step))
        source, target = target, source


def coefficient_rows(odd, kept, early, late, stage, cut):
    rows, cols = kept.shape[1:]
    width = STEPS
    for k in range(3):
        at = pl.ds(width * cut + k * width, width), pl.ds(0, cols)
        stage[k, pl.ds(0, width)] = jnp.where(odd == 0, early[at], late[at])
        stage[k, pl.ds(width, width)] = jnp.where(odd == 0, late[at], early[at])
    lines = [(i, i) for i in range(1, width)]
    lines += [(width + i, width + rows + i) for i in range(width - 1)]
    inside = [(r, width + r) for r in range(rows)]
    return [kept[k].T for k in range(3)], inside, [stage[k].T for k in range(3)], lines


def middle_kernel(axis, low, high, pieces, after, field, kept, *refs):
    strips, (out, one, two, spread, stage) = refs[:-5], refs[-5:]
    rows, cols, members = field.shape
    width = STEPS
    lanes = pl.ds(0, members)
    odd = parity(axis)
    own, inside, beyond, lines = coefficient_rows(
        odd, kept, strips[0], strips[1], stage, parted(cols)[0]
    )
    start = pieces[0][3]
    end = pieces[-1][3] + pieces[-1][4]
    for parts, places in ((beyond, lines), (own, inside)):
        spread_rows(spread, places, [(LEAD + start, [p[start:end] for p in parts])], members)
    for pair, strip_cols, first, column, size in pieces:
        here = pl.ds(LEAD + column, size)
        for i in range(width):
            part = pl.ds(i * strip_cols + first, size)
            one[i + odd * (rows + width), here] = strips[2 * pair][part, lanes]
            one[i + (1 - odd) * (rows + width), here] = strips[2 * pair + 1][part, lanes]
    for r in range(rows):
        one[width + r, pl.ds(LEAD + start, end - start)] = field[r, pl.ds(start, end - start)]

    def store(r, at, value):
        out[r] = value

    march(
        rows,
        one,
        two,
        spread,
        [(LEAD + start, end - start)],
        [(LEAD + low, high - low)],
        store,
    )


def sides_kernel(
    axis,
    after,
    field,
    kept,
    early,
    late,
    early_next,
    late_next,
    left,
    right,
    early_rest,
    late_rest,
    out,
    one,
    two,
    spread,
    stage,
):
    rows, cols, members = field.shape
    odd = parity(axis)
    width = STEPS
    area = width * width
    cut, end = parted(cols)
    more = end - cut
    first, second, high = 2 * EDGE, end - 2 * EDGE, end - EDGE
    size = cols - end
    base = width * size
    lanes = pl.ds(0, members)
    own, inside, beyond, lines = coefficient_rows(odd, kept, early, late, stage, cut)
    for side in range(2):
        at = pl.ds(base + 2 * area + side * width, width), pl.ds(0, cols)
        stage[3 + side, pl.ds(0, width)] = jnp.where(odd == 0, early_rest[at], late_rest[at])
        stage[3 + side, pl.ds(width, width)] = jnp.where(odd == 0, late_rest[at], early_rest[at])
    edge = pl.ds(rows * width, rows), pl.ds(0, cols)
    for parts, near_part, far_part, places in (
        (beyond, stage[3].T, stage[4].T, lines),
        (own, left[edge].T, right[edge].T, inside),
    ):
        halo = [slice(k * width, (k + 1) * width) for k in range(3)]
        columns = [
            (LEAD - width, [near_part[h] for h in halo]),
            (LEAD, [p[:first] for p in parts]),
            (LEAD + second, [p[second:] for p in parts]),
            (LEAD + cols, [far_part[h] for h in halo]),
        ]
        spread_rows(spread, places, columns, members)
    before = pl.ds(LEAD - width, width)
    after = pl.ds(LEAD + cols, width)
    for i in range(width):
        for j, strip, following, rest in (
            (i + odd * (rows + width), early, early_next, early_rest),
            (i + (1 - odd) * (rows + width), late, late_next, late_rest),
        ):
            one[j, before] = rest[pl.ds(base + i * width, width), lanes]
            one[j, pl.ds(LEAD, first)] = strip[pl.ds(i * cut, first), lanes]
            one[j, pl.ds(LEAD + second, end - second)] = following[
                pl.ds(i * more + second - cut, end - second), lanes
            ]
            one[j, pl.ds(LEAD + end, size)] = rest[pl.ds(i * size, size), lanes]
            one[j, after] = rest[pl.ds(base + area + i * width, width), lanes]
    for r in range(rows):
        part = pl.ds(r * width, width)
        one[width + r, before] = left[part, lanes]
        one[width + r, pl.ds(LEAD, first)] = field[r, pl.ds(0, first)]
        one[width + r, pl.ds(LEAD + second, cols - second)] = field[
            r, pl.ds(second, cols - second)
        ]
        one[width + r, after] = right[part, lanes]

    def store(r, at, value):
        if at == LEAD:
            out[r, pl.ds(cols - high, EDGE)] = value
        else:
            out[r, pl.ds(0, cols - high)] = value

    march(
        rows,
        one,
        two,
        spread,
        [(LEAD + second, cols - second + 8), (LEAD - 8, first + 8)],
        [(LEAD + high, cols - high), (LEAD, EDGE)],
        store,
    )


def weight_kernel(axis, count, cells, values, weights, out):
    cols, twice = out.shape
    rows = twice // 2
    slots = cells.shape[1]
    full = cols * lax.axis_size(axis)
    cell = cells[...]
    if full & (full - 1):
        row_of = lax.div(cell, full)
    else:
        row_of = lax.shift_right_logical(cell, full.bit_length() - 1)
    col_of = cell - row_of * full - lax.axis_index(axis) * cols
    slot = lax.broadcasted_iota(jnp.int32, (1, slots), 1)
    plain = jnp.where(slot < count[...], weights[...], 0.0)
    valued = plain * values[...]
    here = lax.broadcasted_iota(jnp.int32, (cols, slots), 0) == col_of
    here = jnp.where(here, 1.0, 0.0).astype(jnp.bfloat16)
    line = lax.broadcasted_iota(jnp.int32, (rows, slots), 0) == row_of
    value = jnp.concatenate([jnp.where(line, plain, 0.0), jnp.where(line, valued, 0.0)], axis=0)
    total = jnp.zeros((cols, twice), jnp.float32)
    for _ in range(3):
        part = value.astype(jnp.bfloat16)
        value = value - part.astype(jnp.float32)
        total = total + dot(here, part, ((1,), (1,)))
    out[...] = total


def cell_weights(rows, pieces, weight, b, many):
    plain, valued = [], []
    for i in range(many):
        r = b * many + i
        for start, column, length in pieces:
            source = weight[pl.ds(column, length)]
            line = lax.broadcasted_iota(jnp.int32, source.shape, 1)
            plain.append(jnp.sum(jnp.where(line == r, source, 0.0), axis=1, keepdims=True))
            valued.append(jnp.sum(jnp.where(line == r + rows, source, 0.0), axis=1, keepdims=True))
    return jnp.concatenate(plain, axis=0), jnp.concatenate(valued, axis=0)


def lay_rows(pieces, column_of, size, centre, b, many):
    cols = centre.shape[1]
    for i in range(many):
        row = jnp.zeros((1, cols), jnp.float32)
        for start, column, length in pieces:
            place = lax.broadcasted_iota(jnp.int32, (length, cols), 0) + column
            here = place == lax.broadcasted_iota(jnp.int32, (length, cols), 1)
            part = column_of[i * size + start : i * size + start + length]
            row = row + jnp.sum(jnp.where(here, part, 0.0), axis=0, keepdims=True)
        centre[pl.ds(b * many + i, 1)] = row


def grouping(rows):
    return next(n for n in (8, 4, 2, 1) if rows % n == 0)


def cells_of(ref, b, many, start=0):
    value = ref[pl.ds(start + b * many, many)]
    return value.reshape(many * value.shape[1], value.shape[2])


def lane_mean(value):
    return jnp.sum(value, axis=1, keepdims=True) * (1.0 / value.shape[1])


def wide(parts):
    return jnp.concatenate(parts, axis=1)


def dot_wide(a, both, size):
    value = dot(a[0], both)
    return value[:, :size] + value[:, size:] + dot(a[1], both[:, :size])


def gram_kernel(groups, pieces, own, others, weight, upper, lower, centre, total, tilt):
    rows, size, _ = own.shape
    many = grouping(rows)
    depth = many * size

    def block(b):
        parts = [cells_of(own, b, many)]
        parts += [cells_of(others, b, many, g * rows) for g in range(groups - 1)]
        value = wide(parts) if groups > 1 else parts[0]
        mean = lane_mean(value)
        deviation = value - mean
        plain, valued = cell_weights(rows, pieces, weight, b, many)
        lay_rows(pieces, mean, size, centre, b, many)
        high, low = halves(deviation)
        at = pl.ds(b * depth, depth)
        upper[at] = high
        lower[at] = low
        turned = (deviation * plain).T
        total[...] += dot3(halves(turned), (high, low))
        tilt[...] += jnp.sum(deviation * (valued - plain * mean), axis=0, keepdims=True)

    loop(rows // many, block)


def own_gram_kernel(layout, first, second, sides, weight, total, left, right, spread):
    local = total.shape[0]
    total[...] = jnp.zeros_like(total)
    for pieces, own in zip(layout, (first, second, sides)):
        rows, size, _ = own.shape
        many = grouping(rows)
        depth = many * size

        def block(b, pieces=pieces, own=own, rows=rows, many=many, depth=depth):
            value = cells_of(own, b, many)
            mean = lane_mean(value)
            deviation = value - mean
            plain, valued = cell_weights(rows, pieces, weight, b, many)
            turned = halves((deviation * plain).T)
            total[...] += dot_wide(turned, wide(halves(deviation)), local)
            if own is sides:
                at = pl.ds(b * depth, depth)
                left[:, at], right[:, at] = turned
                lane = lax.broadcasted_iota(jnp.int32, (depth, local), 1)
                spread[at] = jnp.where(lane == 0, plain, jnp.where(lane == 1, valued, mean))

        loop(rows // many, block)


def tally(total, local, value, partner, plain, valued, mean_own):
    mean_partner = lane_mean(partner)
    counter = partner - mean_partner
    mean = 0.5 * (mean_own + mean_partner)
    apart = 0.5 * (mean_own - mean_partner)
    deviation = value - mean
    pull = valued - plain * mean
    tie = plain * apart

    def add(row, columns):
        total[pl.ds(local + row, 1)] += jnp.sum(columns, axis=0, keepdims=True)

    add(0, deviation * pull)
    add(1, (partner - mean) * pull)
    add(2, deviation * tie)
    add(3, (mean - partner) * tie)
    add(4, jnp.broadcast_to(tie * apart, deviation.shape))
    return counter


def part_deviations(pieces, value, partner, size, upper, lower, centre, b, many):
    value = wide([value, partner])
    mean = lane_mean(value)
    lay_rows(pieces, mean, size, centre, b, many)
    at = pl.ds(b * many * size, many * size)
    upper[at], lower[at] = halves(value - mean)


def part_cross_kernel(pieces, own, other, weight, after, *refs):
    before, (upper, lower, centre, total) = refs[:-4], refs[-4:]
    total[...] = before[0][...] if before else jnp.zeros_like(total)
    rows, size, local = own.shape
    many = grouping(rows)

    def block(b):
        value, partner = cells_of(own, b, many), cells_of(other, b, many)
        mean = lane_mean(value)
        plain, valued = cell_weights(rows, pieces, weight, b, many)
        counter = tally(total, local, value, partner, plain, valued, mean)
        part_deviations(pieces, value, partner, size, upper, lower, centre, b, many)
        turned = ((value - mean) * plain).T
        total[pl.ds(0, local)] += dot_wide(halves(turned), wide(halves(counter)), local)

    loop(rows // many, block)


def last_cross_kernel(own, other, left, right, spread, before, after, total):
    total[...] = before[...]
    rows, size, local = own.shape
    many = grouping(rows)
    depth = many * size

    def block(b):
        at = pl.ds(b * depth, depth)
        value, partner = cells_of(own, b, many), cells_of(other, b, many)
        counter = tally(total, local, value, partner, *(spread[at, i : i + 1] for i in range(3)))
        total[pl.ds(0, local)] += dot_wide(
            (left[:, at], right[:, at]), wide(halves(counter)), local
        )

    loop(rows // many, block)


def deviation_kernel(pieces, own, other, after, upper, lower, centre):
    rows, size, _ = own.shape
    many = grouping(rows)

    def block(b):
        value, partner = cells_of(own, b, many), cells_of(other, b, many)
        part_deviations(pieces, value, partner, size, upper, lower, centre, b, many)

    loop(rows // many, block)


def part_gram_kernel(groups, pieces, own, others, weight, *refs):
    before, (upper, lower, centre, total, tilt) = refs[:-5], refs[-5:]
    total[...] = before[0][...] if before else jnp.zeros_like(total)
    tilt[...] = before[1][...] if before else jnp.zeros_like(tilt)
    gram_kernel(groups, pieces, own, others, weight, upper, lower, centre, total, tilt)


def last_gram_kernel(
    groups, pieces, own, others, weight, before, tilted, gram, upper, lower, centre, total, tilt
):
    total[...] = before[...]
    tilt[...] = tilted[...]
    gram_kernel(groups, pieces, own, others, weight, upper, lower, centre, total, tilt)
    pull = gram.shape[0] - 8
    blocks = total.shape[0] // 128
    innovation = tilt[...]
    at = 0
    gram[pl.ds(pull, 8)] = jnp.zeros((8, 128), jnp.float32)
    for i in range(blocks):
        gram[pl.ds(pull + i, 1)] = innovation[:, i * 128 : (i + 1) * 128]
        for j in range(i, blocks):
            gram[pl.ds(at, 128)] = total[i * 128 : (i + 1) * 128, j * 128 : (j + 1) * 128]
            at += 128


def assemble(first, second, whole):
    blocks = whole.shape[0] // 128
    pull = first.shape[0] - 8
    at = 0
    for i in range(blocks):
        for j in range(i, blocks):
            block = first[pl.ds(at, 128)] + second[pl.ds(at, 128)]
            whole[i * 128 : (i + 1) * 128, j * 128 : (j + 1) * 128] = block
            if j > i:
                whole[j * 128 : (j + 1) * 128, i * 128 : (i + 1) * 128] = block.T
            at += 128
    return wide([first[pl.ds(pull + i, 1)] + second[pl.ds(pull + i, 1)] for i in range(blocks)])


def assemble_pair(first, second, own, other, whole):
    local = own.shape[1]
    cross = first[pl.ds(0, local)] + second[pl.ds(0, local)]
    rest = first[pl.ds(local, 8)] + second[pl.ds(local, 8)]
    square = rest[4:5]
    diagonal = lax.broadcasted_iota(jnp.int32, (local, local), 0) == lax.broadcasted_iota(
        jnp.int32, (local, local), 1
    )
    uprights = []
    for i, part in enumerate((own, other)):
        tie = rest[2 + i : 3 + i]
        upright = jnp.sum(jnp.where(diagonal, tie, 0.0), axis=1, keepdims=True)
        uprights.append(upright)
        at = slice(i * local, (i + 1) * local)
        whole[at, at] = part[...] + upright + (tie - square)
    cross = cross - uprights[0] + (square - rest[3:4])
    whole[:local, local:] = cross
    whole[local:, :local] = cross.T
    return wide([rest[0:1], rest[1:2]])


def analysis_kernel(layout, pair, *rest):
    if pair:
        first, second, own, other, *rest = rest
    else:
        first, second, *rest = rest
    count = len(layout)
    uppers, lowers, centres = (rest[i * count : (i + 1) * count] for i in range(3))
    out, whole, chosen, natural = rest[3 * count :]
    rows, _ = centres[0].shape
    local = natural.shape[2]
    members = whole.shape[0]
    if pair:
        innovation = assemble_pair(first, second, own, other, whole)
    else:
        innovation = assemble(first, second, whole)
    down = lax.broadcasted_iota(jnp.int32, (members, members), 0)
    across = lax.broadcasted_iota(jnp.int32, (members, members), 1)
    identity = jnp.where(down == across, 1.0, 0.0)
    matrix = whole[...] + (members - 1.0) * identity
    parts = halves(matrix)
    square = dot3(parts, parts)
    squares = jnp.sum(jnp.sum(matrix * matrix, axis=1, keepdims=True), axis=0, keepdims=True)
    scaling = jnp.sqrt(squares)
    current = matrix * (1.0 / scaling)
    square = square * (1.0 / scaling) * (1.0 / scaling)
    inverse = None
    for repeat in range(0, ITERS, 2):
        if repeat:
            parts = halves(current)
            square = dot3(parts, parts)
        inner = 0.0625 * square - 0.5625 * current
        outer = 2.25 * identity - 2.4375 * current + 1.6875 * square
        both = outer + dot3(halves(square), halves(inner))
        both_parts = halves(both)
        if repeat + 2 < ITERS:
            twice = dot3(both_parts, both_parts)
            current = dot3(halves(current), halves(twice))
        inverse = both if inverse is None else dot3(halves(inverse), both_parts)
    once = jnp.sum(inverse * innovation, axis=1, keepdims=True)
    once_row = jnp.sum(jnp.where(down == across, once, 0.0), axis=0, keepdims=True)
    shifted = jnp.sum(inverse * once_row, axis=1, keepdims=True) * (1.0 / scaling)
    factor = jnp.sqrt((members - 1.0) / scaling)
    mixing = (factor * inverse + shifted)[:, :local]
    high, low = halves(mixing)
    chosen[:, :local] = high
    chosen[:, local:] = low
    many = grouping(rows)

    def block(b):
        for pieces, upper, lower in zip(layout, uppers, lowers):
            size = upper.shape[0] // rows
            at = pl.ds(b * many * size, many * size)
            value = dot(upper[at], chosen[...])
            value = value[:, :local] + value[:, local:] + dot(lower[at], chosen[:, :local])
            for i in range(many):
                for start, column, length in pieces:
                    natural[i, pl.ds(column, length)] = value[
                        i * size + start : i * size + start + length
                    ]
        for i in range(many):
            r = b * many + i
            middle_row = sum(c[pl.ds(r, 1)] for c in centres)
            out[pl.ds(r, local, stride=rows)] = natural[i].T + middle_row

    loop(rows // many, block)


def shift(value, axes, *moves):
    sizes = [lax.axis_size(a) for a in axes]
    pairs = []
    total = 1
    for s in sizes:
        total *= s
    for flat in range(total):
        rest, place = flat, []
        for s in reversed(sizes):
            place.append(rest % s)
            rest //= s
        place = place[::-1]
        to = 0
        for s, p, m in zip(sizes, place, moves):
            to = to * s + (p + m) % s
        pairs.append((flat, to))
    return lax.ppermute(value, axes if len(axes) > 1 else axes[0], pairs)


def trade(value, axis, first):
    size = lax.axis_size(axis)
    if size % 2:
        raise ValueError("odd ring")
    start = 1 if first else 0
    pairs = [(i % size, (i + 1) % size) for i in range(start, size, 2)]
    return lax.ppermute(value, axis, pairs + [(j, i) for i, j in pairs])


def role_sums(value):
    size = lax.axis_size("role")
    if size & (size - 1) or size == 1:
        return [(lax.psum(value, "role"), jnp.zeros_like(value))]
    stages = []
    step = 1
    while step < size:
        other = lax.ppermute(value, "role", [(i, i ^ step) for i in range(size)])
        stages.append((value, other))
        value = value + other
        step *= 2
    return stages


def shards(
    ensemble,
    diffusion,
    drift_rows,
    drift_cols,
    observed_cells,
    observed_count,
    observed_values,
    observed_weights,
):
    groups = lax.axis_size("member")
    local, rows, cols = ensemble.shape
    members = local * groups
    width = STEPS
    lanes = max(local, cols)
    cut, end = parted(cols)
    strip = struct(width * cut + 4 * width, lanes)
    following = struct(width * (end - cut), lanes)
    rest = struct(width * (cols - end) + 2 * width * width + 2 * width, lanes)
    edge = struct(rows * width + rows, lanes)
    field, kept, early, late, early_next, late_next, left, right = call(
        functools.partial(pack_kernel, "domain"),
        (
            struct(rows, cols, local),
            struct(3, rows, cols),
            strip,
            strip,
            following,
            following,
            edge,
            edge,
        ),
        ensemble.reshape(local * rows, cols),
        diffusion,
        drift_rows,
        drift_cols,
        raw=4,
    )
    early = trade(early, "domain", True)
    late = trade(late, "domain", False)
    early_next = trade(early_next, "domain", True)
    late_next = trade(late_next, "domain", False)
    left, right = shift(right, ("role",), 1), shift(left, ("role",), -1)
    weight = call(
        functools.partial(weight_kernel, "role"),
        struct(cols, 2 * rows),
        observed_count.reshape(1, 1),
        observed_cells,
        observed_values,
        observed_weights,
        raw=4,
    )
    early_rest, late_rest = call(
        functools.partial(turn_kernel, "domain"), (rest, rest), field, left, right, weight
    )
    early_rest = trade(early_rest, "domain", True)
    late_rest = trade(late_rest, "domain", False)
    padded = pltpu.VMEM((rows + 2 * width, cols + 2 * LEAD, local), jnp.float32)
    scratch = (
        padded,
        padded,
        pltpu.VMEM((4, rows + 2 * width, cols + 2 * LEAD, local), jnp.float32),
        pltpu.VMEM((5, 2 * width, cols), jnp.float32),
    )
    ends = (EDGE, cut - EDGE, end - EDGE)

    def forecast(after, low, high, pieces, *strips):
        return call(
            functools.partial(middle_kernel, "domain", low, high, pieces),
            struct(rows, high - low, local),
            after,
            field,
            kept,
            *strips,
            scratch=scratch,
        )

    first = forecast(weight, *ends[:2], ((0, cut, 0, 0, cut),), early, late)
    back = 2 * EDGE
    pieces = (
        (0, cut, cut - back, cut - back, back),
        (1, end - cut, 0, cut, end - cut),
    )
    second = forecast(first, *ends[1:], pieces, early, late, early_next, late_next)
    sides = call(
        functools.partial(sides_kernel, "domain"),
        struct(rows, cols - end + 2 * EDGE, local),
        second,
        field,
        kept,
        early,
        late,
        early_next,
        late_next,
        left,
        right,
        early_rest,
        late_rest,
        scratch=scratch,
    )

    def gathered(value):
        others = [shift(value, ("member",), s) for s in range(1, groups)]
        return jnp.concatenate(others, axis=0) if len(others) > 1 else others[0]

    owns = (first, second, sides)
    theirs = []
    for value in owns:
        theirs.append(gathered(value))
    tail = cols - end + EDGE
    layout = (
        ((0, ends[0], ends[1] - ends[0]),),
        ((0, ends[1], ends[2] - ends[1]),),
        ((0, ends[2], tail), (tail, 0, EDGE)),
    )

    def deviations(value):
        one = struct(rows * value.shape[1], members, kind=jnp.bfloat16)
        return one, one, struct(rows, cols)

    made = []
    pair = groups == 2 and local % 128 == 0
    if pair:
        sided = rows * sides.shape[1]
        half = struct(local, sided, kind=jnp.bfloat16)
        alone, left_half, right_half, spread = call(
            functools.partial(own_gram_kernel, layout),
            (struct(local, local), half, half, struct(sided, local)),
            *owns,
            weight,
        )
        stages = role_sums(alone)
        started = sum(stages[0])
        cross = struct(local + 8, local)
        total = ()
        for i in range(2):
            *three, total = call(
                functools.partial(part_cross_kernel, layout[i]),
                (*deviations(owns[i]), cross),
                owns[i],
                theirs[i],
                weight,
                started,
                *total,
            )
            made.append(three)
            total = (total,)
        alone, arriving = stages[-1]
        total, alone = lax.optimization_barrier((total[0], alone))
        alone = alone + arriving
        gram = call(
            last_cross_kernel, cross, sides, theirs[-1], left_half, right_half, spread, total, alone
        )
        gram, alone = lax.optimization_barrier((gram, alone))
        facing = shift(alone, ("member",), 1)
        grams = (*role_sums(gram)[-1], alone, facing)
        three = call(
            functools.partial(deviation_kernel, layout[-1]),
            deviations(sides),
            sides,
            theirs[-1],
            gram,
        )
        made.append(three)
    else:
        blocks = members // 128
        size = blocks * (blocks + 1) // 2 * 128 + 8
        sums = struct(members, members), struct(1, members)
        totals = ()
        for i in range(2):
            *three, total, tilt = call(
                functools.partial(part_gram_kernel, groups, layout[i]),
                (*deviations(owns[i]), *sums),
                owns[i],
                theirs[i],
                weight,
                *totals,
            )
            made.append(three)
            totals = total, tilt
        gram, *three = call(
            functools.partial(last_gram_kernel, groups, layout[-1]),
            (struct(size, 128), *deviations(sides)),
            sides,
            theirs[-1],
            weight,
            *totals,
            scratch=tuple(pltpu.VMEM(v.shape, v.dtype) for v in sums),
        )
        made.append(three)
        grams = role_sums(gram)[-1]
    return call(
        functools.partial(analysis_kernel, layout, pair),
        struct(local * rows, cols),
        *grams,
        *(three[k] for k in range(3) for three in made),
        scratch=(
            pltpu.VMEM((members, members), jnp.float32),
            pltpu.VMEM((members, 2 * local), jnp.bfloat16),
            pltpu.VMEM((grouping(rows), cols, local), jnp.float32),
        ),
        result=True,
    ).reshape(local, rows, cols)


def solution(mesh):
    placed = (
        P("member", "domain", "role"),
        P("domain", "role"),
        P("domain", "role"),
        P("domain", "role"),
        P("domain", None),
        P("domain"),
        P("domain", None),
        P("domain", None),
    )
    return jax.shard_map(
        shards, mesh=mesh, in_specs=placed, out_specs=P("member", "domain", "role"), check_vma=False
    )
```

```python
import functools

import jax
import jax.numpy as jnp
from jax import lax
from jax.experimental import pallas as pl
from jax.experimental.pallas import tpu as pltpu
from jax.sharding import PartitionSpec as P


STEPS = 4
ITERS = 6
LEAD = 16


VMEM = pl.BlockSpec(memory_space=pltpu.VMEM)
SMEM = pl.BlockSpec(memory_space=pltpu.SMEM)
ROOM = 1 << 20


def struct(*shape, kind=jnp.float32):
    return jax.ShapeDtypeStruct(shape, kind)


def near(shape, kind):
    size = jnp.dtype(kind).itemsize
    for place, extent in enumerate(shape[::-1]):
        unit = (128, 32 // jnp.dtype(kind).itemsize, 1)[min(place, 2)]
        size *= -(-extent // unit) * unit
    return size <= ROOM


def call(body, outs, *args, scratch=(), scalars=0, raw=0, result=False):
    placed = list(args[: scalars + raw])
    for value in args[scalars + raw :]:
        if near(value.shape, value.dtype):
            value = pltpu.with_memory_space_constraint(value, pltpu.VMEM)
        placed.append(value)
    if not result:
        outs = jax.tree.map(
            lambda s: pltpu.VMEM(s.shape, s.dtype) if near(s.shape, s.dtype) else s, outs
        )
    return pl.pallas_call(
        body,
        out_shape=outs,
        in_specs=[SMEM] * scalars + [VMEM] * (len(args) - scalars),
        out_specs=tuple(VMEM for _ in outs) if isinstance(outs, tuple) else VMEM,
        scratch_shapes=scratch,
    )(*placed)


def halves(value):
    upper = value.astype(jnp.bfloat16)
    lower = (value - upper.astype(jnp.float32)).astype(jnp.bfloat16)
    return upper, lower


def dot(a, b, dims=((1,), (0,))):
    return lax.dot_general(a, b, (dims, ((), ())), preferred_element_type=jnp.float32)


def dot3(a, b, dims=((1,), (0,))):
    return dot(a[0], b[0], dims) + (dot(a[0], b[1], dims) + dot(a[1], b[0], dims))


def loop(count, body):
    if count <= 16:
        for i in range(count):
            body(i)
    else:
        lax.fori_loop(0, count, lambda i, c: (body(i), c)[1], 0)


EDGE = 8


def parted(cols):
    return cols * 3 // 8 // 8 * 8, cols * 3 // 4 // 8 * 8


def parity(axis):
    return lax.rem(lax.axis_index(axis), 2)


def pack_kernel(
    axis,
    ens,
    diffusion,
    drift_rows,
    drift_cols,
    field,
    kept,
    early,
    late,
    early_next,
    late_next,
    left,
    right,
):
    odd = parity(axis)
    rows, cols, members = field.shape
    width = STEPS
    cut, end = parted(cols)
    more = end - cut
    lanes = pl.ds(0, members)
    for r in range(rows):
        turned = ens[pl.ds(r, members, stride=rows)].T
        field[r] = turned
        part = pl.ds(r * width, width)
        left[part, lanes] = turned[:width]
        right[part, lanes] = turned[cols - width :]
    for i in range(width):
        part = pl.ds(i * cut, cut)
        early[part, lanes] = field[i + odd * (rows - width), pl.ds(0, cut)]
        late[part, lanes] = field[i + (1 - odd) * (rows - width), pl.ds(0, cut)]
        part = pl.ds(i * more, more)
        early_next[part, lanes] = field[i + odd * (rows - width), pl.ds(cut, more)]
        late_next[part, lanes] = field[i + (1 - odd) * (rows - width), pl.ds(cut, more)]
    near_edge = jnp.zeros((rows, cols), jnp.float32)
    far_edge = near_edge
    lane = lax.broadcasted_iota(jnp.int32, (rows, cols), 1)
    for k, part in enumerate((diffusion, drift_rows, drift_cols)):
        at = pl.ds(width * cut + k * width, width)
        top, bottom = part[:width], part[rows - width :]
        early[at, pl.ds(0, cols)] = jnp.where(odd == 0, top, bottom)
        late[at, pl.ds(0, cols)] = jnp.where(odd == 0, bottom, top)
        value = part[...]
        kept[k] = value
        mine = (lane >= k * width) & (lane < (k + 1) * width)
        if k:
            near_edge = jnp.where(mine, pltpu.roll(value, k * width, 1), near_edge)
        else:
            near_edge = jnp.where(mine, value, near_edge)
        far_edge = jnp.where(mine, pltpu.roll(value, (k + 1) * width, 1), far_edge)
    left[pl.ds(rows * width, rows), pl.ds(0, cols)] = near_edge
    right[pl.ds(rows * width, rows), pl.ds(0, cols)] = far_edge


def turn_kernel(axis, field, left, right, after, early, late):
    rows, cols, members = field.shape
    odd = parity(axis)
    width = STEPS
    area = width * width
    cut = parted(cols)[1]
    size = cols - cut
    lanes = pl.ds(0, members)
    for i in range(width):
        at = pl.ds(i * size, size)
        early[at, lanes] = field[i + odd * (rows - width), pl.ds(cut, size)]
        late[at, lanes] = field[i + (1 - odd) * (rows - width), pl.ds(cut, size)]
    base = width * size
    for i, side in enumerate((left, right)):
        at = pl.ds(base + i * area, area)
        top, bottom = side[pl.ds(0, area)], side[pl.ds((rows - width) * width, area)]
        early[at] = jnp.where(odd == 0, top, bottom)
        late[at] = jnp.where(odd == 0, bottom, top)
        at = pl.ds(base + 2 * area + i * width, width)
        top = side[pl.ds(rows * width, width)]
        bottom = side[pl.ds(rows * width + rows - width, width)]
        early[at] = jnp.where(odd == 0, top, bottom)
        late[at] = jnp.where(odd == 0, bottom, top)


def widen(write, line, columns, members):
    for at, parts in columns:
        size = parts[0].shape[0]
        diffusion, rowwise, colwise = (
            jnp.broadcast_to(p[:, line : line + 1], (size, members)) for p in parts
        )
        here = pl.ds(at, size)
        write(0, here, 1.0 - 4.0 * diffusion - rowwise - colwise)
        write(1, here, diffusion)
        write(2, here, diffusion + rowwise)
        write(3, here, diffusion + colwise)


def spread_rows(spread, lines, columns, members):
    for line, row in lines:

        def write(k, here, value, row=row):
            spread[k, row, here] = value

        widen(write, line, columns, members)


def march(rows, even, odd, spread, ranges, finals, store):
    width = STEPS
    source, target = even, odd
    for step in range(1, STEPS + 1):
        last = step == STEPS

        def advance(r, source=source, target=target, last=last):
            for at, size in finals if last else ranges:
                here = pl.ds(at, size)
                value = (
                    spread[0, r, here] * source[r, here]
                    + spread[1, r, here] * (source[r + 1, here] + source[r, pl.ds(at + 1, size)])
                    + spread[2, r, here] * source[r - 1, here]
                    + spread[3, r, here] * source[r, pl.ds(at - 1, size)]
                )
                if last:
                    store(r - width, at, value)
                else:
                    target[r, here] = value

        loop(rows + 2 * width - 2 * step, lambda i: advance(i + step))
        source, target = target, source


def coefficient_rows(odd, kept, early, late, stage, cut):
    rows, cols = kept.shape[1:]
    width = STEPS
    for k in range(3):
        at = pl.ds(width * cut + k * width, width), pl.ds(0, cols)
        stage[k, pl.ds(0, width)] = jnp.where(odd == 0, early[at], late[at])
        stage[k, pl.ds(width, width)] = jnp.where(odd == 0, late[at], early[at])
    lines = [(i, i) for i in range(1, width)]
    lines += [(width + i, width + rows + i) for i in range(width - 1)]
    inside = [(r, width + r) for r in range(rows)]
    return [kept[k].T for k in range(3)], inside, [stage[k].T for k in range(3)], lines


def middle_kernel(axis, low, high, pieces, after, field, kept, *refs):
    strips, (out, one, two, spread, stage) = refs[:-5], refs[-5:]
    rows, cols, members = field.shape
    width = STEPS
    lanes = pl.ds(0, members)
    odd = parity(axis)
    own, inside, beyond, lines = coefficient_rows(
        odd, kept, strips[0], strips[1], stage, parted(cols)[0]
    )
    start = pieces[0][3]
    end = pieces[-1][3] + pieces[-1][4]
    for parts, places in ((beyond, lines), (own, inside)):
        spread_rows(spread, places, [(LEAD + start, [p[start:end] for p in parts])], members)
    for pair, strip_cols, first, column, size in pieces:
        here = pl.ds(LEAD + column, size)
        for i in range(width):
            part = pl.ds(i * strip_cols + first, size)
            one[i + odd * (rows + width), here] = strips[2 * pair][part, lanes]
            one[i + (1 - odd) * (rows + width), here] = strips[2 * pair + 1][part, lanes]
    for r in range(rows):
        one[width + r, pl.ds(LEAD + start, end - start)] = field[r, pl.ds(start, end - start)]

    def store(r, at, value):
        out[r] = value

    march(
        rows,
        one,
        two,
        spread,
        [(LEAD + start, end - start)],
        [(LEAD + low, high - low)],
        store,
    )


def sides_kernel(
    axis,
    after,
    field,
    kept,
    early,
    late,
    early_next,
    late_next,
    left,
    right,
    early_rest,
    late_rest,
    out,
    one,
    two,
    spread,
    stage,
):
    rows, cols, members = field.shape
    odd = parity(axis)
    width = STEPS
    area = width * width
    cut, end = parted(cols)
    more = end - cut
    first, second, high = 2 * EDGE, end - 2 * EDGE, end - EDGE
    size = cols - end
    base = width * size
    lanes = pl.ds(0, members)
    own, inside, beyond, lines = coefficient_rows(odd, kept, early, late, stage, cut)
    for side in range(2):
        at = pl.ds(base + 2 * area + side * width, width), pl.ds(0, cols)
        stage[3 + side, pl.ds(0, width)] = jnp.where(odd == 0, early_rest[at], late_rest[at])
        stage[3 + side, pl.ds(width, width)] = jnp.where(odd == 0, late_rest[at], early_rest[at])
    edge = pl.ds(rows * width, rows), pl.ds(0, cols)
    for parts, near_part, far_part, places in (
        (beyond, stage[3].T, stage[4].T, lines),
        (own, left[edge].T, right[edge].T, inside),
    ):
        halo = [slice(k * width, (k + 1) * width) for k in range(3)]
        columns = [
            (LEAD - width, [near_part[h] for h in halo]),
            (LEAD, [p[:first] for p in parts]),
            (LEAD + second, [p[second:] for p in parts]),
            (LEAD + cols, [far_part[h] for h in halo]),
        ]
        spread_rows(spread, places, columns, members)
    before = pl.ds(LEAD - width, width)
    after = pl.ds(LEAD + cols, width)
    for i in range(width):
        for j, strip, following, rest in (
            (i + odd * (rows + width), early, early_next, early_rest),
            (i + (1 - odd) * (rows + width), late, late_next, late_rest),
        ):
            one[j, before] = rest[pl.ds(base + i * width, width), lanes]
            one[j, pl.ds(LEAD, first)] = strip[pl.ds(i * cut, first), lanes]
            one[j, pl.ds(LEAD + second, end - second)] = following[
                pl.ds(i * more + second - cut, end - second), lanes
            ]
            one[j, pl.ds(LEAD + end, size)] = rest[pl.ds(i * size, size), lanes]
            one[j, after] = rest[pl.ds(base + area + i * width, width), lanes]
    for r in range(rows):
        part = pl.ds(r * width, width)
        one[width + r, before] = left[part, lanes]
        one[width + r, pl.ds(LEAD, first)] = field[r, pl.ds(0, first)]
        one[width + r, pl.ds(LEAD + second, cols - second)] = field[
            r, pl.ds(second, cols - second)
        ]
        one[width + r, after] = right[part, lanes]

    def store(r, at, value):
        if at == LEAD:
            out[r, pl.ds(cols - high, EDGE)] = value
        else:
            out[r, pl.ds(0, cols - high)] = value

    march(
        rows,
        one,
        two,
        spread,
        [(LEAD + second, cols - second + 8), (LEAD - 8, first + 8)],
        [(LEAD + high, cols - high), (LEAD, EDGE)],
        store,
    )


def weight_kernel(axis, count, cells, values, weights, out):
    cols, twice = out.shape
    rows = twice // 2
    slots = cells.shape[1]
    full = cols * lax.axis_size(axis)
    cell = cells[...]
    if full & (full - 1):
        row_of = lax.div(cell, full)
    else:
        row_of = lax.shift_right_logical(cell, full.bit_length() - 1)
    col_of = cell - row_of * full - lax.axis_index(axis) * cols
    slot = lax.broadcasted_iota(jnp.int32, (1, slots), 1)
    plain = jnp.where(slot < count[0], weights[...], 0.0)
    valued = plain * values[...]
    here = lax.broadcasted_iota(jnp.int32, (cols, slots), 0) == col_of
    here = jnp.where(here, 1.0, 0.0).astype(jnp.bfloat16)
    line = lax.broadcasted_iota(jnp.int32, (rows, slots), 0) == row_of
    value = jnp.concatenate([jnp.where(line, plain, 0.0), jnp.where(line, valued, 0.0)], axis=0)
    total = jnp.zeros((cols, twice), jnp.float32)
    for _ in range(3):
        part = value.astype(jnp.bfloat16)
        value = value - part.astype(jnp.float32)
        total = total + dot(here, part, ((1,), (1,)))
    out[...] = total


def cell_weights(rows, pieces, weight, b, many):
    plain, valued = [], []
    for i in range(many):
        r = b * many + i
        for start, column, length in pieces:
            source = weight[pl.ds(column, length)]
            line = lax.broadcasted_iota(jnp.int32, source.shape, 1)
            plain.append(jnp.sum(jnp.where(line == r, source, 0.0), axis=1, keepdims=True))
            valued.append(jnp.sum(jnp.where(line == r + rows, source, 0.0), axis=1, keepdims=True))
    return jnp.concatenate(plain, axis=0), jnp.concatenate(valued, axis=0)


def lay_rows(pieces, column_of, size, centre, b, many):
    cols = centre.shape[1]
    for i in range(many):
        row = jnp.zeros((1, cols), jnp.float32)
        for start, column, length in pieces:
            place = lax.broadcasted_iota(jnp.int32, (length, cols), 0) + column
            here = place == lax.broadcasted_iota(jnp.int32, (length, cols), 1)
            part = column_of[i * size + start : i * size + start + length]
            row = row + jnp.sum(jnp.where(here, part, 0.0), axis=0, keepdims=True)
        centre[pl.ds(b * many + i, 1)] = row


def grouping(rows):
    return next(n for n in (8, 4, 2, 1) if rows % n == 0)


def cells_of(ref, b, many, start=0):
    value = ref[pl.ds(start + b * many, many)]
    return value.reshape(many * value.shape[1], value.shape[2])


def lane_mean(value):
    return jnp.sum(value, axis=1, keepdims=True) * (1.0 / value.shape[1])


def wide(parts):
    return jnp.concatenate(parts, axis=1)


def dot_wide(a, both, size):
    value = dot(a[0], both)
    return value[:, :size] + value[:, size:] + dot(a[1], both[:, :size])


def gram_kernel(groups, pieces, own, others, weight, upper, lower, centre, total, tilt):
    rows, size, _ = own.shape
    many = grouping(rows)
    depth = many * size

    def block(b):
        parts = [cells_of(own, b, many)]
        parts += [cells_of(others, b, many, g * rows) for g in range(groups - 1)]
        value = wide(parts) if groups > 1 else parts[0]
        mean = lane_mean(value)
        deviation = value - mean
        plain, valued = cell_weights(rows, pieces, weight, b, many)
        lay_rows(pieces, mean, size, centre, b, many)
        high, low = halves(deviation)
        at = pl.ds(b * depth, depth)
        upper[at] = high
        lower[at] = low
        turned = (deviation * plain).T
        total[...] += dot3(halves(turned), (high, low))
        tilt[...] += jnp.sum(deviation * (valued - plain * mean), axis=0, keepdims=True)

    loop(rows // many, block)


def own_gram_kernel(layout, first, second, sides, weight, total, left, right, spread):
    local = total.shape[0]
    total[...] = jnp.zeros_like(total)
    for pieces, own in zip(layout, (first, second, sides)):
        rows, size, _ = own.shape
        many = grouping(rows)
        depth = many * size

        def block(b, pieces=pieces, own=own, rows=rows, many=many, depth=depth):
            value = cells_of(own, b, many)
            mean = lane_mean(value)
            deviation = value - mean
            plain, valued = cell_weights(rows, pieces, weight, b, many)
            turned = halves((deviation * plain).T)
            total[...] += dot_wide(turned, wide(halves(deviation)), local)
            if own is sides:
                at = pl.ds(b * depth, depth)
                left[:, at], right[:, at] = turned
                lane = lax.broadcasted_iota(jnp.int32, (depth, local), 1)
                spread[at] = jnp.where(lane == 0, plain, jnp.where(lane == 1, valued, mean))

        loop(rows // many, block)


def tally(total, local, value, partner, plain, valued, mean_own):
    mean_partner = lane_mean(partner)
    counter = partner - mean_partner
    mean = 0.5 * (mean_own + mean_partner)
    apart = 0.5 * (mean_own - mean_partner)
    deviation = value - mean
    pull = valued - plain * mean
    tie = plain * apart

    def add(row, columns):
        total[pl.ds(local + row, 1)] += jnp.sum(columns, axis=0, keepdims=True)

    add(0, deviation * pull)
    add(1, (partner - mean) * pull)
    add(2, deviation * tie)
    add(3, (mean - partner) * tie)
    add(4, jnp.broadcast_to(tie * apart, deviation.shape))
    return counter


def part_deviations(pieces, value, partner, size, upper, lower, centre, b, many):
    value = wide([value, partner])
    mean = lane_mean(value)
    lay_rows(pieces, mean, size, centre, b, many)
    at = pl.ds(b * many * size, many * size)
    upper[at], lower[at] = halves(value - mean)


def part_cross_kernel(pieces, own, other, weight, after, *refs):
    before, (upper, lower, centre, total) = refs[:-4], refs[-4:]
    total[...] = before[0][...] if before else jnp.zeros_like(total)
    rows, size, local = own.shape
    many = grouping(rows)

    def block(b):
        value, partner = cells_of(own, b, many), cells_of(other, b, many)
        mean = lane_mean(value)
        plain, valued = cell_weights(rows, pieces, weight, b, many)
        counter = tally(total, local, value, partner, plain, valued, mean)
        part_deviations(pieces, value, partner, size, upper, lower, centre, b, many)
        turned = ((value - mean) * plain).T
        total[pl.ds(0, local)] += dot_wide(halves(turned), wide(halves(counter)), local)

    loop(rows // many, block)


def last_cross_kernel(own, other, left, right, spread, before, total):
    total[...] = before[...]
    rows, size, local = own.shape
    many = grouping(rows)
    depth = many * size

    def block(b):
        at = pl.ds(b * depth, depth)
        value, partner = cells_of(own, b, many), cells_of(other, b, many)
        counter = tally(total, local, value, partner, *(spread[at, i : i + 1] for i in range(3)))
        total[pl.ds(0, local)] += dot_wide(
            (left[:, at], right[:, at]), wide(halves(counter)), local
        )

    loop(rows // many, block)


def deviation_kernel(pieces, own, other, after, upper, lower, centre):
    rows, size, _ = own.shape
    many = grouping(rows)

    def block(b):
        value, partner = cells_of(own, b, many), cells_of(other, b, many)
        part_deviations(pieces, value, partner, size, upper, lower, centre, b, many)

    loop(rows // many, block)


def part_gram_kernel(groups, pieces, own, others, weight, *refs):
    before, (upper, lower, centre, total, tilt) = refs[:-5], refs[-5:]
    total[...] = before[0][...] if before else jnp.zeros_like(total)
    tilt[...] = before[1][...] if before else jnp.zeros_like(tilt)
    gram_kernel(groups, pieces, own, others, weight, upper, lower, centre, total, tilt)


def last_gram_kernel(
    groups, pieces, own, others, weight, before, tilted, gram, upper, lower, centre, total, tilt
):
    total[...] = before[...]
    tilt[...] = tilted[...]
    gram_kernel(groups, pieces, own, others, weight, upper, lower, centre, total, tilt)
    pull = gram.shape[0] - 8
    blocks = total.shape[0] // 128
    innovation = tilt[...]
    at = 0
    gram[pl.ds(pull, 8)] = jnp.zeros((8, 128), jnp.float32)
    for i in range(blocks):
        gram[pl.ds(pull + i, 1)] = innovation[:, i * 128 : (i + 1) * 128]
        for j in range(i, blocks):
            gram[pl.ds(at, 128)] = total[i * 128 : (i + 1) * 128, j * 128 : (j + 1) * 128]
            at += 128


def assemble(first, second, whole):
    blocks = whole.shape[0] // 128
    pull = first.shape[0] - 8
    at = 0
    for i in range(blocks):
        for j in range(i, blocks):
            block = first[pl.ds(at, 128)] + second[pl.ds(at, 128)]
            whole[i * 128 : (i + 1) * 128, j * 128 : (j + 1) * 128] = block
            if j > i:
                whole[j * 128 : (j + 1) * 128, i * 128 : (i + 1) * 128] = block.T
            at += 128
    return wide([first[pl.ds(pull + i, 1)] + second[pl.ds(pull + i, 1)] for i in range(blocks)])


def assemble_pair(first, second, own, other, whole):
    local = own.shape[1]
    cross = first[pl.ds(0, local)] + second[pl.ds(0, local)]
    rest = first[pl.ds(local, 8)] + second[pl.ds(local, 8)]
    square = rest[4:5]
    diagonal = lax.broadcasted_iota(jnp.int32, (local, local), 0) == lax.broadcasted_iota(
        jnp.int32, (local, local), 1
    )
    uprights = []
    for i, part in enumerate((own, other)):
        tie = rest[2 + i : 3 + i]
        upright = jnp.sum(jnp.where(diagonal, tie, 0.0), axis=1, keepdims=True)
        uprights.append(upright)
        at = slice(i * local, (i + 1) * local)
        whole[at, at] = part[...] + upright + (tie - square)
    cross = cross - uprights[0] + (square - rest[3:4])
    whole[:local, local:] = cross
    whole[local:, :local] = cross.T
    return wide([rest[0:1], rest[1:2]])


def analysis_kernel(layout, pair, *rest):
    if pair:
        first, second, own, other, *rest = rest
    else:
        first, second, *rest = rest
    count = len(layout)
    uppers, lowers, centres = (rest[i * count : (i + 1) * count] for i in range(3))
    out, whole, chosen, natural = rest[3 * count :]
    rows, _ = centres[0].shape
    local = natural.shape[2]
    members = whole.shape[0]
    if pair:
        innovation = assemble_pair(first, second, own, other, whole)
    else:
        innovation = assemble(first, second, whole)
    down = lax.broadcasted_iota(jnp.int32, (members, members), 0)
    across = lax.broadcasted_iota(jnp.int32, (members, members), 1)
    identity = jnp.where(down == across, 1.0, 0.0)
    matrix = whole[...] + (members - 1.0) * identity
    parts = halves(matrix)
    square = dot3(parts, parts)
    squares = jnp.sum(jnp.sum(matrix * matrix, axis=1, keepdims=True), axis=0, keepdims=True)
    scaling = jnp.sqrt(squares)
    current = matrix * (1.0 / scaling)
    square = square * (1.0 / scaling) * (1.0 / scaling)
    inverse = None
    for repeat in range(0, ITERS, 2):
        if repeat:
            parts = halves(current)
            square = dot3(parts, parts)
        inner = 0.0625 * square - 0.5625 * current
        outer = 2.25 * identity - 2.4375 * current + 1.6875 * square
        both = outer + dot3(halves(square), halves(inner))
        both_parts = halves(both)
        if repeat + 2 < ITERS:
            twice = dot3(both_parts, both_parts)
            current = dot3(halves(current), halves(twice))
        inverse = both if inverse is None else dot3(halves(inverse), both_parts)
    once = jnp.sum(inverse * innovation, axis=1, keepdims=True)
    once_row = jnp.sum(jnp.where(down == across, once, 0.0), axis=0, keepdims=True)
    shifted = jnp.sum(inverse * once_row, axis=1, keepdims=True) * (1.0 / scaling)
    factor = jnp.sqrt((members - 1.0) / scaling)
    mixing = (factor * inverse + shifted)[:, :local]
    high, low = halves(mixing)
    chosen[:, :local] = high
    chosen[:, local:] = low
    many = grouping(rows)

    def block(b):
        for pieces, upper, lower in zip(layout, uppers, lowers):
            size = upper.shape[0] // rows
            at = pl.ds(b * many * size, many * size)
            value = dot(upper[at], chosen[...])
            value = value[:, :local] + value[:, local:] + dot(lower[at], chosen[:, :local])
            for i in range(many):
                for start, column, length in pieces:
                    natural[i, pl.ds(column, length)] = value[
                        i * size + start : i * size + start + length
                    ]
        for i in range(many):
            r = b * many + i
            middle_row = sum(c[pl.ds(r, 1)] for c in centres)
            out[pl.ds(r, local, stride=rows)] = natural[i].T + middle_row

    loop(rows // many, block)


def shift(value, axes, *moves):
    sizes = [lax.axis_size(a) for a in axes]
    pairs = []
    total = 1
    for s in sizes:
        total *= s
    for flat in range(total):
        rest, place = flat, []
        for s in reversed(sizes):
            place.append(rest % s)
            rest //= s
        place = place[::-1]
        to = 0
        for s, p, m in zip(sizes, place, moves):
            to = to * s + (p + m) % s
        pairs.append((flat, to))
    return lax.ppermute(value, axes if len(axes) > 1 else axes[0], pairs)


def trade(value, axis, first):
    size = lax.axis_size(axis)
    if size % 2:
        raise ValueError("odd ring")
    start = 1 if first else 0
    pairs = [(i % size, (i + 1) % size) for i in range(start, size, 2)]
    return lax.ppermute(value, axis, pairs + [(j, i) for i, j in pairs])


def role_sums(value):
    size = lax.axis_size("role")
    if size & (size - 1) or size == 1:
        return [(lax.psum(value, "role"), jnp.zeros_like(value))]
    stages = []
    step = 1
    while step < size:
        other = lax.ppermute(value, "role", [(i, i ^ step) for i in range(size)])
        stages.append((value, other))
        value = value + other
        step *= 2
    return stages


def shards(
    ensemble,
    diffusion,
    drift_rows,
    drift_cols,
    observed_cells,
    observed_count,
    observed_values,
    observed_weights,
):
    groups = lax.axis_size("member")
    local, rows, cols = ensemble.shape
    members = local * groups
    width = STEPS
    lanes = max(local, cols)
    cut, end = parted(cols)
    strip = struct(width * cut + 4 * width, lanes)
    following = struct(width * (end - cut), lanes)
    rest = struct(width * (cols - end) + 2 * width * width + 2 * width, lanes)
    edge = struct(rows * width + rows, lanes)
    field, kept, early, late, early_next, late_next, left, right = call(
        functools.partial(pack_kernel, "domain"),
        (
            struct(rows, cols, local),
            struct(3, rows, cols),
            strip,
            strip,
            following,
            following,
            edge,
            edge,
        ),
        ensemble.reshape(local * rows, cols),
        diffusion,
        drift_rows,
        drift_cols,
        raw=4,
    )
    early = trade(early, "domain", True)
    late = trade(late, "domain", False)
    early_next = trade(early_next, "domain", True)
    late_next = trade(late_next, "domain", False)
    received = shift(right, ("role",), 1)
    right = shift(left, ("role",), -1)
    left = received
    weight = call(
        functools.partial(weight_kernel, "role"),
        struct(cols, 2 * rows),
        observed_count,
        observed_cells,
        observed_values,
        observed_weights,
        scalars=1,
    )
    early_rest, late_rest = call(
        functools.partial(turn_kernel, "domain"), (rest, rest), field, left, right, weight
    )
    early_rest = trade(early_rest, "domain", True)
    late_rest = trade(late_rest, "domain", False)
    padded = pltpu.VMEM((rows + 2 * width, cols + 2 * LEAD, local), jnp.float32)
    scratch = (
        padded,
        padded,
        pltpu.VMEM((4, rows + 2 * width, cols + 2 * LEAD, local), jnp.float32),
        pltpu.VMEM((5, 2 * width, cols), jnp.float32),
    )
    ends = (EDGE, cut - EDGE, end - EDGE)

    def forecast(after, low, high, pieces, *strips):
        return call(
            functools.partial(middle_kernel, "domain", low, high, pieces),
            struct(rows, high - low, local),
            after,
            field,
            kept,
            *strips,
            scratch=scratch,
        )

    first = forecast(weight, *ends[:2], ((0, cut, 0, 0, cut),), early, late)
    back = 2 * EDGE
    pieces = (
        (0, cut, cut - back, cut - back, back),
        (1, end - cut, 0, cut, end - cut),
    )
    second = forecast(first, *ends[1:], pieces, early, late, early_next, late_next)
    sides = call(
        functools.partial(sides_kernel, "domain"),
        struct(rows, cols - end + 2 * EDGE, local),
        second,
        field,
        kept,
        early,
        late,
        early_next,
        late_next,
        left,
        right,
        early_rest,
        late_rest,
        scratch=scratch,
    )

    def gathered(value):
        others = [shift(value, ("member",), s) for s in range(1, groups)]
        return jnp.concatenate(others, axis=0) if len(others) > 1 else others[0]

    owns = (first, second, sides)
    theirs = []
    for value in owns:
        theirs.append(gathered(value))
    tail = cols - end + EDGE
    layout = (
        ((0, ends[0], ends[1] - ends[0]),),
        ((0, ends[1], ends[2] - ends[1]),),
        ((0, ends[2], tail), (tail, 0, EDGE)),
    )

    def deviations(value):
        one = struct(rows * value.shape[1], members, kind=jnp.bfloat16)
        return one, one, struct(rows, cols)

    made = []
    pair = groups == 2 and local % 128 == 0
    if pair:
        sided = rows * sides.shape[1]
        half = struct(local, sided, kind=jnp.bfloat16)
        alone, left_half, right_half, spread = call(
            functools.partial(own_gram_kernel, layout),
            (struct(local, local), half, half, struct(sided, local)),
            *owns,
            weight,
        )
        stages = role_sums(alone)
        started = sum(stages[0])
        cross = struct(local + 8, local)
        total = ()
        for i in range(2):
            *three, total = call(
                functools.partial(part_cross_kernel, layout[i]),
                (*deviations(owns[i]), cross),
                owns[i],
                theirs[i],
                weight,
                started,
                *total,
            )
            made.append(three)
            total = (total,)
        alone, arriving = stages[-1]
        total, alone = lax.optimization_barrier((total[0], alone))
        alone = alone + arriving
        gram = call(
            last_cross_kernel, cross, sides, theirs[-1], left_half, right_half, spread, total
        )
        facing = shift(alone, ("member",), 1)
        grams = (*role_sums(gram)[-1], alone, facing)
        three = call(
            functools.partial(deviation_kernel, layout[-1]),
            deviations(sides),
            sides,
            theirs[-1],
            gram,
        )
        made.append(three)
    else:
        blocks = members // 128
        size = blocks * (blocks + 1) // 2 * 128 + 8
        sums = struct(members, members), struct(1, members)
        totals = ()
        for i in range(2):
            *three, total, tilt = call(
                functools.partial(part_gram_kernel, groups, layout[i]),
                (*deviations(owns[i]), *sums),
                owns[i],
                theirs[i],
                weight,
                *totals,
            )
            made.append(three)
            totals = total, tilt
        gram, *three = call(
            functools.partial(last_gram_kernel, groups, layout[-1]),
            (struct(size, 128), *deviations(sides)),
            sides,
            theirs[-1],
            weight,
            *totals,
            scratch=tuple(pltpu.VMEM(v.shape, v.dtype) for v in sums),
        )
        made.append(three)
        grams = role_sums(gram)[-1]
    return call(
        functools.partial(analysis_kernel, layout, pair),
        struct(local * rows, cols),
        *grams,
        *(three[k] for k in range(3) for three in made),
        scratch=(
            pltpu.VMEM((members, members), jnp.float32),
            pltpu.VMEM((members, 2 * local), jnp.bfloat16),
            pltpu.VMEM((grouping(rows), cols, local), jnp.float32),
        ),
        result=True,
    ).reshape(local, rows, cols)


def solution(mesh):
    placed = (
        P("member", "domain", "role"),
        P("domain", "role"),
        P("domain", "role"),
        P("domain", "role"),
        P("domain", None),
        P("domain"),
        P("domain", None),
        P("domain", None),
    )
    return jax.shard_map(
        shards, mesh=mesh, in_specs=placed, out_specs=P("member", "domain", "role"), check_vma=False
    )
```

```python
import functools

import jax
import jax.numpy as jnp
from jax import lax
from jax.experimental import pallas as pl
from jax.experimental.pallas import tpu as pltpu
from jax.sharding import PartitionSpec as P


STEPS = 4
ITERS = 6
LEAD = 16


VMEM = pl.BlockSpec(memory_space=pltpu.VMEM)
SMEM = pl.BlockSpec(memory_space=pltpu.SMEM)
ROOM = 1 << 20


def struct(*shape, kind=jnp.float32):
    return jax.ShapeDtypeStruct(shape, kind)


def near(shape, kind):
    size = jnp.dtype(kind).itemsize
    for place, extent in enumerate(shape[::-1]):
        unit = (128, 32 // jnp.dtype(kind).itemsize, 1)[min(place, 2)]
        size *= -(-extent // unit) * unit
    return size <= ROOM


def call(body, outs, *args, scratch=(), scalars=0, raw=0, result=False):
    placed = list(args[: scalars + raw])
    for value in args[scalars + raw :]:
        if near(value.shape, value.dtype):
            value = pltpu.with_memory_space_constraint(value, pltpu.VMEM)
        placed.append(value)
    if not result:
        outs = jax.tree.map(
            lambda s: pltpu.VMEM(s.shape, s.dtype) if near(s.shape, s.dtype) else s, outs
        )
    return pl.pallas_call(
        body,
        out_shape=outs,
        in_specs=[SMEM] * scalars + [VMEM] * (len(args) - scalars),
        out_specs=tuple(VMEM for _ in outs) if isinstance(outs, tuple) else VMEM,
        scratch_shapes=scratch,
    )(*placed)


def halves(value):
    upper = value.astype(jnp.bfloat16)
    lower = (value - upper.astype(jnp.float32)).astype(jnp.bfloat16)
    return upper, lower


def dot(a, b, dims=((1,), (0,))):
    return lax.dot_general(a, b, (dims, ((), ())), preferred_element_type=jnp.float32)


def dot3(a, b, dims=((1,), (0,))):
    return dot(a[0], b[0], dims) + (dot(a[0], b[1], dims) + dot(a[1], b[0], dims))


def loop(count, body):
    if count <= 16:
        for i in range(count):
            body(i)
    else:
        lax.fori_loop(0, count, lambda i, c: (body(i), c)[1], 0)


EDGE = 8


def parted(cols):
    return cols * 3 // 8 // 8 * 8, cols * 3 // 4 // 8 * 8


def parity(axis):
    return lax.rem(lax.axis_index(axis), 2)


def pack_kernel(
    axis,
    ens,
    diffusion,
    drift_rows,
    drift_cols,
    field,
    kept,
    early,
    late,
    early_next,
    late_next,
    left,
    right,
):
    odd = parity(axis)
    rows, cols, members = field.shape
    width = STEPS
    cut, end = parted(cols)
    more = end - cut
    lanes = pl.ds(0, members)
    for r in range(rows):
        turned = ens[pl.ds(r, members, stride=rows)].T
        field[r] = turned
        part = pl.ds(r * width, width)
        left[part, lanes] = turned[:width]
        right[part, lanes] = turned[cols - width :]
    for i in range(width):
        part = pl.ds(i * cut, cut)
        early[part, lanes] = field[i + odd * (rows - width), pl.ds(0, cut)]
        late[part, lanes] = field[i + (1 - odd) * (rows - width), pl.ds(0, cut)]
        part = pl.ds(i * more, more)
        early_next[part, lanes] = field[i + odd * (rows - width), pl.ds(cut, more)]
        late_next[part, lanes] = field[i + (1 - odd) * (rows - width), pl.ds(cut, more)]
    near_edge = jnp.zeros((rows, cols), jnp.float32)
    far_edge = near_edge
    lane = lax.broadcasted_iota(jnp.int32, (rows, cols), 1)
    for k, part in enumerate((diffusion, drift_rows, drift_cols)):
        at = pl.ds(width * cut + k * width, width)
        top, bottom = part[:width], part[rows - width :]
        early[at, pl.ds(0, cols)] = jnp.where(odd == 0, top, bottom)
        late[at, pl.ds(0, cols)] = jnp.where(odd == 0, bottom, top)
        value = part[...]
        kept[k] = value
        mine = (lane >= k * width) & (lane < (k + 1) * width)
        if k:
            near_edge = jnp.where(mine, pltpu.roll(value, k * width, 1), near_edge)
        else:
            near_edge = jnp.where(mine, value, near_edge)
        far_edge = jnp.where(mine, pltpu.roll(value, (k + 1) * width, 1), far_edge)
    left[pl.ds(rows * width, rows), pl.ds(0, cols)] = near_edge
    right[pl.ds(rows * width, rows), pl.ds(0, cols)] = far_edge


def turn_kernel(axis, field, left, right, early, late):
    rows, cols, members = field.shape
    odd = parity(axis)
    width = STEPS
    area = width * width
    cut = parted(cols)[1]
    size = cols - cut
    lanes = pl.ds(0, members)
    for i in range(width):
        at = pl.ds(i * size, size)
        early[at, lanes] = field[i + odd * (rows - width), pl.ds(cut, size)]
        late[at, lanes] = field[i + (1 - odd) * (rows - width), pl.ds(cut, size)]
    base = width * size
    for i, side in enumerate((left, right)):
        at = pl.ds(base + i * area, area)
        top, bottom = side[pl.ds(0, area)], side[pl.ds((rows - width) * width, area)]
        early[at] = jnp.where(odd == 0, top, bottom)
        late[at] = jnp.where(odd == 0, bottom, top)
        at = pl.ds(base + 2 * area + i * width, width)
        top = side[pl.ds(rows * width, width)]
        bottom = side[pl.ds(rows * width + rows - width, width)]
        early[at] = jnp.where(odd == 0, top, bottom)
        late[at] = jnp.where(odd == 0, bottom, top)


def widen(write, line, columns, members):
    for at, parts in columns:
        size = parts[0].shape[0]
        diffusion, rowwise, colwise = (
            jnp.broadcast_to(p[:, line : line + 1], (size, members)) for p in parts
        )
        here = pl.ds(at, size)
        write(0, here, 1.0 - 4.0 * diffusion - rowwise - colwise)
        write(1, here, diffusion)
        write(2, here, diffusion + rowwise)
        write(3, here, diffusion + colwise)


def spread_rows(spread, lines, columns, members):
    for line, row in lines:

        def write(k, here, value, row=row):
            spread[k, row, here] = value

        widen(write, line, columns, members)


def march(rows, even, odd, spread, ranges, finals, store):
    width = STEPS
    source, target = even, odd
    for step in range(1, STEPS + 1):
        last = step == STEPS

        def advance(r, source=source, target=target, last=last):
            for at, size in finals if last else ranges:
                here = pl.ds(at, size)
                value = (
                    spread[0, r, here] * source[r, here]
                    + spread[1, r, here] * (source[r + 1, here] + source[r, pl.ds(at + 1, size)])
                    + spread[2, r, here] * source[r - 1, here]
                    + spread[3, r, here] * source[r, pl.ds(at - 1, size)]
                )
                if last:
                    store(r - width, at, value)
                else:
                    target[r, here] = value

        loop(rows + 2 * width - 2 * step, lambda i: advance(i + step))
        source, target = target, source


def coefficient_rows(odd, kept, early, late, stage, cut):
    rows, cols = kept.shape[1:]
    width = STEPS
    for k in range(3):
        at = pl.ds(width * cut + k * width, width), pl.ds(0, cols)
        stage[k, pl.ds(0, width)] = jnp.where(odd == 0, early[at], late[at])
        stage[k, pl.ds(width, width)] = jnp.where(odd == 0, late[at], early[at])
    lines = [(i, i) for i in range(1, width)]
    lines += [(width + i, width + rows + i) for i in range(width - 1)]
    inside = [(r, width + r) for r in range(rows)]
    return [kept[k].T for k in range(3)], inside, [stage[k].T for k in range(3)], lines


def middle_kernel(axis, low, high, pieces, field, kept, *refs):
    strips, (out, one, two, spread, stage) = refs[:-5], refs[-5:]
    rows, cols, members = field.shape
    width = STEPS
    lanes = pl.ds(0, members)
    odd = parity(axis)
    own, inside, beyond, lines = coefficient_rows(
        odd, kept, strips[0], strips[1], stage, parted(cols)[0]
    )
    start = pieces[0][3]
    end = pieces[-1][3] + pieces[-1][4]
    for parts, places in ((beyond, lines), (own, inside)):
        spread_rows(spread, places, [(LEAD + start, [p[start:end] for p in parts])], members)
    for pair, strip_cols, first, column, size in pieces:
        here = pl.ds(LEAD + column, size)
        for i in range(width):
            part = pl.ds(i * strip_cols + first, size)
            one[i + odd * (rows + width), here] = strips[2 * pair][part, lanes]
            one[i + (1 - odd) * (rows + width), here] = strips[2 * pair + 1][part, lanes]
    for r in range(rows):
        one[width + r, pl.ds(LEAD + start, end - start)] = field[r, pl.ds(start, end - start)]

    def store(r, at, value):
        out[r] = value

    march(
        rows,
        one,
        two,
        spread,
        [(LEAD + start, end - start)],
        [(LEAD + low, high - low)],
        store,
    )


def sides_kernel(
    axis,
    after,
    field,
    kept,
    early,
    late,
    early_next,
    late_next,
    left,
    right,
    early_rest,
    late_rest,
    out,
    one,
    two,
    spread,
    stage,
):
    rows, cols, members = field.shape
    odd = parity(axis)
    width = STEPS
    area = width * width
    cut, end = parted(cols)
    more = end - cut
    first, second, high = 2 * EDGE, end - 2 * EDGE, end - EDGE
    size = cols - end
    base = width * size
    lanes = pl.ds(0, members)
    own, inside, beyond, lines = coefficient_rows(odd, kept, early, late, stage, cut)
    for side in range(2):
        at = pl.ds(base + 2 * area + side * width, width), pl.ds(0, cols)
        stage[3 + side, pl.ds(0, width)] = jnp.where(odd == 0, early_rest[at], late_rest[at])
        stage[3 + side, pl.ds(width, width)] = jnp.where(odd == 0, late_rest[at], early_rest[at])
    edge = pl.ds(rows * width, rows), pl.ds(0, cols)
    for parts, near_part, far_part, places in (
        (beyond, stage[3].T, stage[4].T, lines),
        (own, left[edge].T, right[edge].T, inside),
    ):
        halo = [slice(k * width, (k + 1) * width) for k in range(3)]
        columns = [
            (LEAD - width, [near_part[h] for h in halo]),
            (LEAD, [p[:first] for p in parts]),
            (LEAD + second, [p[second:] for p in parts]),
            (LEAD + cols, [far_part[h] for h in halo]),
        ]
        spread_rows(spread, places, columns, members)
    before = pl.ds(LEAD - width, width)
    after = pl.ds(LEAD + cols, width)
    for i in range(width):
        for j, strip, following, rest in (
            (i + odd * (rows + width), early, early_next, early_rest),
            (i + (1 - odd) * (rows + width), late, late_next, late_rest),
        ):
            one[j, before] = rest[pl.ds(base + i * width, width), lanes]
            one[j, pl.ds(LEAD, first)] = strip[pl.ds(i * cut, first), lanes]
            one[j, pl.ds(LEAD + second, end - second)] = following[
                pl.ds(i * more + second - cut, end - second), lanes
            ]
            one[j, pl.ds(LEAD + end, size)] = rest[pl.ds(i * size, size), lanes]
            one[j, after] = rest[pl.ds(base + area + i * width, width), lanes]
    for r in range(rows):
        part = pl.ds(r * width, width)
        one[width + r, before] = left[part, lanes]
        one[width + r, pl.ds(LEAD, first)] = field[r, pl.ds(0, first)]
        one[width + r, pl.ds(LEAD + second, cols - second)] = field[
            r, pl.ds(second, cols - second)
        ]
        one[width + r, after] = right[part, lanes]

    def store(r, at, value):
        if at == LEAD:
            out[r, pl.ds(cols - high, EDGE)] = value
        else:
            out[r, pl.ds(0, cols - high)] = value

    march(
        rows,
        one,
        two,
        spread,
        [(LEAD + second, cols - second + 8), (LEAD - 8, first + 8)],
        [(LEAD + high, cols - high), (LEAD, EDGE)],
        store,
    )


def weight_kernel(axis, count, cells, values, weights, after, out):
    cols, twice = out.shape
    rows = twice // 2
    slots = cells.shape[1]
    full = cols * lax.axis_size(axis)
    cell = cells[...]
    if full & (full - 1):
        row_of = lax.div(cell, full)
    else:
        row_of = lax.shift_right_logical(cell, full.bit_length() - 1)
    col_of = cell - row_of * full - lax.axis_index(axis) * cols
    slot = lax.broadcasted_iota(jnp.int32, (1, slots), 1)
    plain = jnp.where(slot < count[0], weights[...], 0.0)
    valued = plain * values[...]
    here = lax.broadcasted_iota(jnp.int32, (cols, slots), 0) == col_of
    here = jnp.where(here, 1.0, 0.0).astype(jnp.bfloat16)
    line = lax.broadcasted_iota(jnp.int32, (rows, slots), 0) == row_of
    value = jnp.concatenate([jnp.where(line, plain, 0.0), jnp.where(line, valued, 0.0)], axis=0)
    total = jnp.zeros((cols, twice), jnp.float32)
    for _ in range(3):
        part = value.astype(jnp.bfloat16)
        value = value - part.astype(jnp.float32)
        total = total + dot(here, part, ((1,), (1,)))
    out[...] = total


def cell_weights(rows, pieces, weight, b, many):
    plain, valued = [], []
    for i in range(many):
        r = b * many + i
        for start, column, length in pieces:
            source = weight[pl.ds(column, length)]
            line = lax.broadcasted_iota(jnp.int32, source.shape, 1)
            plain.append(jnp.sum(jnp.where(line == r, source, 0.0), axis=1, keepdims=True))
            valued.append(jnp.sum(jnp.where(line == r + rows, source, 0.0), axis=1, keepdims=True))
    return jnp.concatenate(plain, axis=0), jnp.concatenate(valued, axis=0)


def lay_rows(pieces, column_of, size, centre, b, many):
    cols = centre.shape[1]
    for i in range(many):
        row = jnp.zeros((1, cols), jnp.float32)
        for start, column, length in pieces:
            place = lax.broadcasted_iota(jnp.int32, (length, cols), 0) + column
            here = place == lax.broadcasted_iota(jnp.int32, (length, cols), 1)
            part = column_of[i * size + start : i * size + start + length]
            row = row + jnp.sum(jnp.where(here, part, 0.0), axis=0, keepdims=True)
        centre[pl.ds(b * many + i, 1)] = row


def grouping(rows):
    return next(n for n in (8, 4, 2, 1) if rows % n == 0)


def cells_of(ref, b, many, start=0):
    value = ref[pl.ds(start + b * many, many)]
    return value.reshape(many * value.shape[1], value.shape[2])


def lane_mean(value):
    return jnp.sum(value, axis=1, keepdims=True) * (1.0 / value.shape[1])


def wide(parts):
    return jnp.concatenate(parts, axis=1)


def dot_wide(a, both, size):
    value = dot(a[0], both)
    return value[:, :size] + value[:, size:] + dot(a[1], both[:, :size])


def gram_kernel(groups, pieces, own, others, weight, upper, lower, centre, total, tilt):
    rows, size, _ = own.shape
    many = grouping(rows)
    depth = many * size

    def block(b):
        parts = [cells_of(own, b, many)]
        parts += [cells_of(others, b, many, g * rows) for g in range(groups - 1)]
        value = wide(parts) if groups > 1 else parts[0]
        mean = lane_mean(value)
        deviation = value - mean
        plain, valued = cell_weights(rows, pieces, weight, b, many)
        lay_rows(pieces, mean, size, centre, b, many)
        high, low = halves(deviation)
        at = pl.ds(b * depth, depth)
        upper[at] = high
        lower[at] = low
        turned = (deviation * plain).T
        total[...] += dot3(halves(turned), (high, low))
        tilt[...] += jnp.sum(deviation * (valued - plain * mean), axis=0, keepdims=True)

    loop(rows // many, block)


def own_gram_kernel(layout, first, second, sides, weight, total, left, right, spread):
    local = total.shape[0]
    total[...] = jnp.zeros_like(total)
    for pieces, own in zip(layout, (first, second, sides)):
        rows, size, _ = own.shape
        many = grouping(rows)
        depth = many * size

        def block(b, pieces=pieces, own=own, rows=rows, many=many, depth=depth):
            value = cells_of(own, b, many)
            mean = lane_mean(value)
            deviation = value - mean
            plain, valued = cell_weights(rows, pieces, weight, b, many)
            turned = halves((deviation * plain).T)
            total[...] += dot_wide(turned, wide(halves(deviation)), local)
            if own is sides:
                at = pl.ds(b * depth, depth)
                left[:, at], right[:, at] = turned
                lane = lax.broadcasted_iota(jnp.int32, (depth, local), 1)
                spread[at] = jnp.where(lane == 0, plain, jnp.where(lane == 1, valued, mean))

        loop(rows // many, block)


def tally(total, local, value, partner, plain, valued, mean_own):
    mean_partner = lane_mean(partner)
    counter = partner - mean_partner
    mean = 0.5 * (mean_own + mean_partner)
    apart = 0.5 * (mean_own - mean_partner)
    deviation = value - mean
    pull = valued - plain * mean
    tie = plain * apart

    def add(row, columns):
        total[pl.ds(local + row, 1)] += jnp.sum(columns, axis=0, keepdims=True)

    add(0, deviation * pull)
    add(1, (partner - mean) * pull)
    add(2, deviation * tie)
    add(3, (mean - partner) * tie)
    add(4, jnp.broadcast_to(tie * apart, deviation.shape))
    return counter


def part_deviations(pieces, value, partner, size, upper, lower, centre, b, many):
    value = wide([value, partner])
    mean = lane_mean(value)
    lay_rows(pieces, mean, size, centre, b, many)
    at = pl.ds(b * many * size, many * size)
    upper[at], lower[at] = halves(value - mean)


def part_cross_kernel(pieces, own, other, weight, after, *refs):
    before, (upper, lower, centre, total) = refs[:-4], refs[-4:]
    total[...] = before[0][...] if before else jnp.zeros_like(total)
    rows, size, local = own.shape
    many = grouping(rows)

    def block(b):
        value, partner = cells_of(own, b, many), cells_of(other, b, many)
        mean = lane_mean(value)
        plain, valued = cell_weights(rows, pieces, weight, b, many)
        counter = tally(total, local, value, partner, plain, valued, mean)
        part_deviations(pieces, value, partner, size, upper, lower, centre, b, many)
        turned = ((value - mean) * plain).T
        total[pl.ds(0, local)] += dot_wide(halves(turned), wide(halves(counter)), local)

    loop(rows // many, block)


def last_cross_kernel(own, other, left, right, spread, before, total):
    total[...] = before[...]
    rows, size, local = own.shape
    many = grouping(rows)
    depth = many * size

    def block(b):
        at = pl.ds(b * depth, depth)
        value, partner = cells_of(own, b, many), cells_of(other, b, many)
        counter = tally(total, local, value, partner, *(spread[at, i : i + 1] for i in range(3)))
        total[pl.ds(0, local)] += dot_wide(
            (left[:, at], right[:, at]), wide(halves(counter)), local
        )

    loop(rows // many, block)


def deviation_kernel(pieces, own, other, after, upper, lower, centre):
    rows, size, _ = own.shape
    many = grouping(rows)

    def block(b):
        value, partner = cells_of(own, b, many), cells_of(other, b, many)
        part_deviations(pieces, value, partner, size, upper, lower, centre, b, many)

    loop(rows // many, block)


def part_gram_kernel(groups, pieces, own, others, weight, *refs):
    before, (upper, lower, centre, total, tilt) = refs[:-5], refs[-5:]
    total[...] = before[0][...] if before else jnp.zeros_like(total)
    tilt[...] = before[1][...] if before else jnp.zeros_like(tilt)
    gram_kernel(groups, pieces, own, others, weight, upper, lower, centre, total, tilt)


def last_gram_kernel(
    groups, pieces, own, others, weight, before, tilted, gram, upper, lower, centre, total, tilt
):
    total[...] = before[...]
    tilt[...] = tilted[...]
    gram_kernel(groups, pieces, own, others, weight, upper, lower, centre, total, tilt)
    pull = gram.shape[0] - 8
    blocks = total.shape[0] // 128
    innovation = tilt[...]
    at = 0
    gram[pl.ds(pull, 8)] = jnp.zeros((8, 128), jnp.float32)
    for i in range(blocks):
        gram[pl.ds(pull + i, 1)] = innovation[:, i * 128 : (i + 1) * 128]
        for j in range(i, blocks):
            gram[pl.ds(at, 128)] = total[i * 128 : (i + 1) * 128, j * 128 : (j + 1) * 128]
            at += 128


def assemble(first, second, whole):
    blocks = whole.shape[0] // 128
    pull = first.shape[0] - 8
    at = 0
    for i in range(blocks):
        for j in range(i, blocks):
            block = first[pl.ds(at, 128)] + second[pl.ds(at, 128)]
            whole[i * 128 : (i + 1) * 128, j * 128 : (j + 1) * 128] = block
            if j > i:
                whole[j * 128 : (j + 1) * 128, i * 128 : (i + 1) * 128] = block.T
            at += 128
    return wide([first[pl.ds(pull + i, 1)] + second[pl.ds(pull + i, 1)] for i in range(blocks)])


def assemble_pair(first, second, own, other, whole):
    local = own.shape[1]
    cross = first[pl.ds(0, local)] + second[pl.ds(0, local)]
    rest = first[pl.ds(local, 8)] + second[pl.ds(local, 8)]
    square = rest[4:5]
    diagonal = lax.broadcasted_iota(jnp.int32, (local, local), 0) == lax.broadcasted_iota(
        jnp.int32, (local, local), 1
    )
    uprights = []
    for i, part in enumerate((own, other)):
        tie = rest[2 + i : 3 + i]
        upright = jnp.sum(jnp.where(diagonal, tie, 0.0), axis=1, keepdims=True)
        uprights.append(upright)
        at = slice(i * local, (i + 1) * local)
        whole[at, at] = part[...] + upright + (tie - square)
    cross = cross - uprights[0] + (square - rest[3:4])
    whole[:local, local:] = cross
    whole[local:, :local] = cross.T
    return wide([rest[0:1], rest[1:2]])


def analysis_kernel(layout, pair, *rest):
    if pair:
        first, second, own, other, *rest = rest
    else:
        first, second, *rest = rest
    count = len(layout)
    uppers, lowers, centres = (rest[i * count : (i + 1) * count] for i in range(3))
    out, whole, chosen, natural = rest[3 * count :]
    rows, _ = centres[0].shape
    local = natural.shape[2]
    members = whole.shape[0]
    if pair:
        innovation = assemble_pair(first, second, own, other, whole)
    else:
        innovation = assemble(first, second, whole)
    down = lax.broadcasted_iota(jnp.int32, (members, members), 0)
    across = lax.broadcasted_iota(jnp.int32, (members, members), 1)
    identity = jnp.where(down == across, 1.0, 0.0)
    matrix = whole[...] + (members - 1.0) * identity
    parts = halves(matrix)
    square = dot3(parts, parts)
    squares = jnp.sum(jnp.sum(matrix * matrix, axis=1, keepdims=True), axis=0, keepdims=True)
    scaling = jnp.sqrt(squares)
    current = matrix * (1.0 / scaling)
    square = square * (1.0 / scaling) * (1.0 / scaling)
    inverse = None
    for repeat in range(0, ITERS, 2):
        if repeat:
            parts = halves(current)
            square = dot3(parts, parts)
        inner = 0.0625 * square - 0.5625 * current
        outer = 2.25 * identity - 2.4375 * current + 1.6875 * square
        both = outer + dot3(halves(square), halves(inner))
        both_parts = halves(both)
        if repeat + 2 < ITERS:
            twice = dot3(both_parts, both_parts)
            current = dot3(halves(current), halves(twice))
        inverse = both if inverse is None else dot3(halves(inverse), both_parts)
    once = jnp.sum(inverse * innovation, axis=1, keepdims=True)
    once_row = jnp.sum(jnp.where(down == across, once, 0.0), axis=0, keepdims=True)
    shifted = jnp.sum(inverse * once_row, axis=1, keepdims=True) * (1.0 / scaling)
    factor = jnp.sqrt((members - 1.0) / scaling)
    mixing = (factor * inverse + shifted)[:, :local]
    high, low = halves(mixing)
    chosen[:, :local] = high
    chosen[:, local:] = low
    many = grouping(rows)

    def block(b):
        for pieces, upper, lower in zip(layout, uppers, lowers):
            size = upper.shape[0] // rows
            at = pl.ds(b * many * size, many * size)
            value = dot(upper[at], chosen[...])
            value = value[:, :local] + value[:, local:] + dot(lower[at], chosen[:, :local])
            for i in range(many):
                for start, column, length in pieces:
                    natural[i, pl.ds(column, length)] = value[
                        i * size + start : i * size + start + length
                    ]
        for i in range(many):
            r = b * many + i
            middle_row = sum(c[pl.ds(r, 1)] for c in centres)
            out[pl.ds(r, local, stride=rows)] = natural[i].T + middle_row

    loop(rows // many, block)


def shift(value, axes, *moves):
    sizes = [lax.axis_size(a) for a in axes]
    pairs = []
    total = 1
    for s in sizes:
        total *= s
    for flat in range(total):
        rest, place = flat, []
        for s in reversed(sizes):
            place.append(rest % s)
            rest //= s
        place = place[::-1]
        to = 0
        for s, p, m in zip(sizes, place, moves):
            to = to * s + (p + m) % s
        pairs.append((flat, to))
    return lax.ppermute(value, axes if len(axes) > 1 else axes[0], pairs)


def trade(value, axis, first):
    size = lax.axis_size(axis)
    if size % 2:
        raise ValueError("odd ring")
    start = 1 if first else 0
    pairs = [(i % size, (i + 1) % size) for i in range(start, size, 2)]
    return lax.ppermute(value, axis, pairs + [(j, i) for i, j in pairs])


def role_sums(value):
    size = lax.axis_size("role")
    if size & (size - 1) or size == 1:
        return [(lax.psum(value, "role"), jnp.zeros_like(value))]
    stages = []
    step = 1
    while step < size:
        other = lax.ppermute(value, "role", [(i, i ^ step) for i in range(size)])
        stages.append((value, other))
        value = value + other
        step *= 2
    return stages


def shards(
    ensemble,
    diffusion,
    drift_rows,
    drift_cols,
    observed_cells,
    observed_count,
    observed_values,
    observed_weights,
):
    groups = lax.axis_size("member")
    local, rows, cols = ensemble.shape
    members = local * groups
    width = STEPS
    lanes = max(local, cols)
    cut, end = parted(cols)
    strip = struct(width * cut + 4 * width, lanes)
    following = struct(width * (end - cut), lanes)
    rest = struct(width * (cols - end) + 2 * width * width + 2 * width, lanes)
    edge = struct(rows * width + rows, lanes)
    field, kept, early, late, early_next, late_next, left, right = call(
        functools.partial(pack_kernel, "domain"),
        (
            struct(rows, cols, local),
            struct(3, rows, cols),
            strip,
            strip,
            following,
            following,
            edge,
            edge,
        ),
        ensemble.reshape(local * rows, cols),
        diffusion,
        drift_rows,
        drift_cols,
        raw=4,
    )
    early = trade(early, "domain", True)
    late = trade(late, "domain", False)
    early_next = trade(early_next, "domain", True)
    late_next = trade(late_next, "domain", False)
    received = shift(right, ("role",), 1)
    right = shift(left, ("role",), -1)
    left = received
    early_rest, late_rest = call(
        functools.partial(turn_kernel, "domain"), (rest, rest), field, left, right
    )
    early_rest = trade(early_rest, "domain", True)
    late_rest = trade(late_rest, "domain", False)
    padded = pltpu.VMEM((rows + 2 * width, cols + 2 * LEAD, local), jnp.float32)
    scratch = (
        padded,
        padded,
        pltpu.VMEM((4, rows + 2 * width, cols + 2 * LEAD, local), jnp.float32),
        pltpu.VMEM((5, 2 * width, cols), jnp.float32),
    )
    ends = (EDGE, cut - EDGE, end - EDGE)

    def forecast(low, high, pieces, *strips):
        return call(
            functools.partial(middle_kernel, "domain", low, high, pieces),
            struct(rows, high - low, local),
            field,
            kept,
            *strips,
            scratch=scratch,
        )

    first = forecast(*ends[:2], ((0, cut, 0, 0, cut),), early, late)
    back = 2 * EDGE
    pieces = (
        (0, cut, cut - back, cut - back, back),
        (1, end - cut, 0, cut, end - cut),
    )
    second = forecast(*ends[1:], pieces, early, late, early_next, late_next, first)
    limit = jnp.minimum(observed_count, observed_cells.shape[1])
    weight = call(
        functools.partial(weight_kernel, "role"),
        struct(cols, 2 * rows),
        limit,
        observed_cells,
        observed_values,
        observed_weights,
        second,
        scalars=1,
    )
    sides = call(
        functools.partial(sides_kernel, "domain"),
        struct(rows, cols - end + 2 * EDGE, local),
        weight,
        field,
        kept,
        early,
        late,
        early_next,
        late_next,
        left,
        right,
        early_rest,
        late_rest,
        scratch=scratch,
    )

    def gathered(value):
        others = [shift(value, ("member",), s) for s in range(1, groups)]
        return jnp.concatenate(others, axis=0) if len(others) > 1 else others[0]

    owns = (first, second, sides)
    theirs = []
    for value in owns:
        theirs.append(gathered(value))
    tail = cols - end + EDGE
    layout = (
        ((0, ends[0], ends[1] - ends[0]),),
        ((0, ends[1], ends[2] - ends[1]),),
        ((0, ends[2], tail), (tail, 0, EDGE)),
    )

    def deviations(value):
        one = struct(rows * value.shape[1], members, kind=jnp.bfloat16)
        return one, one, struct(rows, cols)

    made = []
    pair = groups == 2 and local % 128 == 0
    if pair:
        sided = rows * sides.shape[1]
        half = struct(local, sided, kind=jnp.bfloat16)
        alone, left_half, right_half, spread = call(
            functools.partial(own_gram_kernel, layout),
            (struct(local, local), half, half, struct(sided, local)),
            *owns,
            weight,
        )
        stages = role_sums(alone)
        started = sum(stages[0])
        cross = struct(local + 8, local)
        total = ()
        for i in range(2):
            *three, total = call(
                functools.partial(part_cross_kernel, layout[i]),
                (*deviations(owns[i]), cross),
                owns[i],
                theirs[i],
                weight,
                started,
                *total,
            )
            made.append(three)
            total = (total,)
        alone, arriving = stages[-1]
        total, alone = lax.optimization_barrier((total[0], alone))
        alone = alone + arriving
        gram = call(
            last_cross_kernel, cross, sides, theirs[-1], left_half, right_half, spread, total
        )
        facing = shift(alone, ("member",), 1)
        grams = (*role_sums(gram)[-1], alone, facing)
        three = call(
            functools.partial(deviation_kernel, layout[-1]),
            deviations(sides),
            sides,
            theirs[-1],
            gram,
        )
        made.append(three)
    else:
        blocks = members // 128
        size = blocks * (blocks + 1) // 2 * 128 + 8
        sums = struct(members, members), struct(1, members)
        totals = ()
        for i in range(2):
            *three, total, tilt = call(
                functools.partial(part_gram_kernel, groups, layout[i]),
                (*deviations(owns[i]), *sums),
                owns[i],
                theirs[i],
                weight,
                *totals,
            )
            made.append(three)
            totals = total, tilt
        gram, *three = call(
            functools.partial(last_gram_kernel, groups, layout[-1]),
            (struct(size, 128), *deviations(sides)),
            sides,
            theirs[-1],
            weight,
            *totals,
            scratch=tuple(pltpu.VMEM(v.shape, v.dtype) for v in sums),
        )
        made.append(three)
        grams = role_sums(gram)[-1]
    return call(
        functools.partial(analysis_kernel, layout, pair),
        struct(local * rows, cols),
        *grams,
        *(three[k] for k in range(3) for three in made),
        scratch=(
            pltpu.VMEM((members, members), jnp.float32),
            pltpu.VMEM((members, 2 * local), jnp.bfloat16),
            pltpu.VMEM((grouping(rows), cols, local), jnp.float32),
        ),
        result=True,
    ).reshape(local, rows, cols)


def solution(mesh):
    placed = (
        P("member", "domain", "role"),
        P("domain", "role"),
        P("domain", "role"),
        P("domain", "role"),
        P("domain", None),
        P("domain"),
        P("domain", None),
        P("domain", None),
    )
    return jax.shard_map(
        shards, mesh=mesh, in_specs=placed, out_specs=P("member", "domain", "role"), check_vma=False
    )
```

```python
import functools

import jax
import jax.numpy as jnp
from jax import lax
from jax.experimental import pallas as pl
from jax.experimental.pallas import tpu as pltpu
from jax.sharding import PartitionSpec as P


STEPS = 4
ITERS = 6
LEAD = 16


VMEM = pl.BlockSpec(memory_space=pltpu.VMEM)
SMEM = pl.BlockSpec(memory_space=pltpu.SMEM)
ROOM = 1 << 20


def struct(*shape, kind=jnp.float32):
    return jax.ShapeDtypeStruct(shape, kind)


def near(shape, kind):
    size = jnp.dtype(kind).itemsize
    for place, extent in enumerate(shape[::-1]):
        unit = (128, 32 // jnp.dtype(kind).itemsize, 1)[min(place, 2)]
        size *= -(-extent // unit) * unit
    return size <= ROOM


def call(body, outs, *args, scratch=(), scalars=0, raw=0, result=False):
    placed = list(args[: scalars + raw])
    for value in args[scalars + raw :]:
        if near(value.shape, value.dtype):
            value = pltpu.with_memory_space_constraint(value, pltpu.VMEM)
        placed.append(value)
    if not result:
        outs = jax.tree.map(
            lambda s: pltpu.VMEM(s.shape, s.dtype) if near(s.shape, s.dtype) else s, outs
        )
    return pl.pallas_call(
        body,
        out_shape=outs,
        in_specs=[SMEM] * scalars + [VMEM] * (len(args) - scalars),
        out_specs=tuple(VMEM for _ in outs) if isinstance(outs, tuple) else VMEM,
        scratch_shapes=scratch,
    )(*placed)


def halves(value):
    upper = value.astype(jnp.bfloat16)
    lower = (value - upper.astype(jnp.float32)).astype(jnp.bfloat16)
    return upper, lower


def dot(a, b, dims=((1,), (0,))):
    return lax.dot_general(a, b, (dims, ((), ())), preferred_element_type=jnp.float32)


def by_halves(product, *operands):
    half = operands[0].shape[0] // 2
    parts = [product(*(o[at] for o in operands)) for at in (slice(0, half), slice(half, None))]
    return jnp.concatenate(parts, axis=0)


def dot3(a, b):
    return by_halves(
        lambda high, low: (dot(high, b[0]) + dot(low, b[0])) + dot(high, b[1]), *a
    )


def loop(count, body):
    if count <= 16:
        for i in range(count):
            body(i)
    else:
        lax.fori_loop(0, count, lambda i, c: (body(i), c)[1], 0)


EDGE = 8


def parted(cols):
    return cols * 3 // 8 // 8 * 8, cols * 3 // 4 // 8 * 8


def parity(axis):
    return lax.rem(lax.axis_index(axis), 2)


def pack_kernel(
    axis,
    ens,
    diffusion,
    drift_rows,
    drift_cols,
    field,
    kept,
    early,
    late,
    early_next,
    late_next,
    left,
    right,
):
    odd = parity(axis)
    rows, cols, members = field.shape
    width = STEPS
    cut, end = parted(cols)
    more = end - cut
    lanes = pl.ds(0, members)
    for r in range(rows):
        turned = ens[pl.ds(r, members, stride=rows)].T
        field[r] = turned
        part = pl.ds(r * width, width)
        left[part, lanes] = turned[:width]
        right[part, lanes] = turned[cols - width :]
    for i in range(width):
        part = pl.ds(i * cut, cut)
        early[part, lanes] = field[i + odd * (rows - width), pl.ds(0, cut)]
        late[part, lanes] = field[i + (1 - odd) * (rows - width), pl.ds(0, cut)]
        part = pl.ds(i * more, more)
        early_next[part, lanes] = field[i + odd * (rows - width), pl.ds(cut, more)]
        late_next[part, lanes] = field[i + (1 - odd) * (rows - width), pl.ds(cut, more)]
    near_edge = jnp.zeros((rows, cols), jnp.float32)
    far_edge = near_edge
    lane = lax.broadcasted_iota(jnp.int32, (rows, cols), 1)
    for k, part in enumerate((diffusion, drift_rows, drift_cols)):
        at = pl.ds(width * cut + k * width, width)
        top, bottom = part[:width], part[rows - width :]
        early[at, pl.ds(0, cols)] = jnp.where(odd == 0, top, bottom)
        late[at, pl.ds(0, cols)] = jnp.where(odd == 0, bottom, top)
        value = part[...]
        kept[k] = value
        mine = (lane >= k * width) & (lane < (k + 1) * width)
        if k:
            near_edge = jnp.where(mine, pltpu.roll(value, k * width, 1), near_edge)
        else:
            near_edge = jnp.where(mine, value, near_edge)
        far_edge = jnp.where(mine, pltpu.roll(value, (k + 1) * width, 1), far_edge)
    left[pl.ds(rows * width, rows), pl.ds(0, cols)] = near_edge
    right[pl.ds(rows * width, rows), pl.ds(0, cols)] = far_edge


def turn_kernel(axis, field, left, right, after, early, late):
    rows, cols, members = field.shape
    odd = parity(axis)
    width = STEPS
    area = width * width
    cut = parted(cols)[1]
    size = cols - cut
    lanes = pl.ds(0, members)
    for i in range(width):
        at = pl.ds(i * size, size)
        early[at, lanes] = field[i + odd * (rows - width), pl.ds(cut, size)]
        late[at, lanes] = field[i + (1 - odd) * (rows - width), pl.ds(cut, size)]
    base = width * size
    for i, side in enumerate((left, right)):
        at = pl.ds(base + i * area, area)
        top, bottom = side[pl.ds(0, area)], side[pl.ds((rows - width) * width, area)]
        early[at] = jnp.where(odd == 0, top, bottom)
        late[at] = jnp.where(odd == 0, bottom, top)
        at = pl.ds(base + 2 * area + i * width, width)
        top = side[pl.ds(rows * width, width)]
        bottom = side[pl.ds(rows * width + rows - width, width)]
        early[at] = jnp.where(odd == 0, top, bottom)
        late[at] = jnp.where(odd == 0, bottom, top)


def widen(write, line, columns, members):
    for at, parts in columns:
        size = parts[0].shape[0]
        diffusion, rowwise, colwise = (
            jnp.broadcast_to(p[:, line : line + 1], (size, members)) for p in parts
        )
        here = pl.ds(at, size)
        write(0, here, 1.0 - 4.0 * diffusion - rowwise - colwise)
        write(1, here, diffusion)
        write(2, here, diffusion + rowwise)
        write(3, here, diffusion + colwise)


def spread_rows(spread, lines, columns, members):
    for line, row in lines:

        def write(k, here, value, row=row):
            spread[k, row, here] = value

        widen(write, line, columns, members)


def march(rows, even, odd, spread, ranges, finals, store):
    width = STEPS
    source, target = even, odd
    for step in range(1, STEPS + 1):
        last = step == STEPS

        def advance(r, source=source, target=target, last=last):
            for at, size in finals if last else ranges:
                here = pl.ds(at, size)
                value = (
                    spread[0, r, here] * source[r, here]
                    + spread[1, r, here] * (source[r + 1, here] + source[r, pl.ds(at + 1, size)])
                    + spread[2, r, here] * source[r - 1, here]
                    + spread[3, r, here] * source[r, pl.ds(at - 1, size)]
                )
                if last:
                    store(r - width, at, value)
                else:
                    target[r, here] = value

        loop(rows + 2 * width - 2 * step, lambda i: advance(i + step))
        source, target = target, source


def coefficient_rows(odd, kept, early, late, stage, cut):
    rows, cols = kept.shape[1:]
    width = STEPS
    for k in range(3):
        at = pl.ds(width * cut + k * width, width), pl.ds(0, cols)
        stage[k, pl.ds(0, width)] = jnp.where(odd == 0, early[at], late[at])
        stage[k, pl.ds(width, width)] = jnp.where(odd == 0, late[at], early[at])
    lines = [(i, i) for i in range(1, width)]
    lines += [(width + i, width + rows + i) for i in range(width - 1)]
    inside = [(r, width + r) for r in range(rows)]
    return [kept[k].T for k in range(3)], inside, [stage[k].T for k in range(3)], lines


def middle_kernel(axis, low, high, pieces, after, field, kept, *refs):
    strips, (out, one, two, spread, stage) = refs[:-5], refs[-5:]
    rows, cols, members = field.shape
    width = STEPS
    lanes = pl.ds(0, members)
    odd = parity(axis)
    own, inside, beyond, lines = coefficient_rows(
        odd, kept, strips[0], strips[1], stage, parted(cols)[0]
    )
    start = pieces[0][3]
    end = pieces[-1][3] + pieces[-1][4]
    for parts, places in ((beyond, lines), (own, inside)):
        spread_rows(spread, places, [(LEAD + start, [p[start:end] for p in parts])], members)
    for pair, strip_cols, first, column, size in pieces:
        here = pl.ds(LEAD + column, size)
        for i in range(width):
            part = pl.ds(i * strip_cols + first, size)
            one[i + odd * (rows + width), here] = strips[2 * pair][part, lanes]
            one[i + (1 - odd) * (rows + width), here] = strips[2 * pair + 1][part, lanes]
    for r in range(rows):
        one[width + r, pl.ds(LEAD + start, end - start)] = field[r, pl.ds(start, end - start)]

    def store(r, at, value):
        out[r] = value

    march(
        rows,
        one,
        two,
        spread,
        [(LEAD + start, end - start)],
        [(LEAD + low, high - low)],
        store,
    )


def sides_kernel(
    axis,
    after,
    field,
    kept,
    early,
    late,
    early_next,
    late_next,
    left,
    right,
    early_rest,
    late_rest,
    out,
    one,
    two,
    spread,
    stage,
):
    rows, cols, members = field.shape
    odd = parity(axis)
    width = STEPS
    area = width * width
    cut, end = parted(cols)
    more = end - cut
    first, second, high = 2 * EDGE, end - 2 * EDGE, end - EDGE
    size = cols - end
    base = width * size
    lanes = pl.ds(0, members)
    own, inside, beyond, lines = coefficient_rows(odd, kept, early, late, stage, cut)
    for side in range(2):
        at = pl.ds(base + 2 * area + side * width, width), pl.ds(0, cols)
        stage[3 + side, pl.ds(0, width)] = jnp.where(odd == 0, early_rest[at], late_rest[at])
        stage[3 + side, pl.ds(width, width)] = jnp.where(odd == 0, late_rest[at], early_rest[at])
    edge = pl.ds(rows * width, rows), pl.ds(0, cols)
    for parts, near_part, far_part, places in (
        (beyond, stage[3].T, stage[4].T, lines),
        (own, left[edge].T, right[edge].T, inside),
    ):
        halo = [slice(k * width, (k + 1) * width) for k in range(3)]
        columns = [
            (LEAD - width, [near_part[h] for h in halo]),
            (LEAD, [p[:first] for p in parts]),
            (LEAD + second, [p[second:] for p in parts]),
            (LEAD + cols, [far_part[h] for h in halo]),
        ]
        spread_rows(spread, places, columns, members)
    before = pl.ds(LEAD - width, width)
    after = pl.ds(LEAD + cols, width)
    for i in range(width):
        for j, strip, following, rest in (
            (i + odd * (rows + width), early, early_next, early_rest),
            (i + (1 - odd) * (rows + width), late, late_next, late_rest),
        ):
            one[j, before] = rest[pl.ds(base + i * width, width), lanes]
            one[j, pl.ds(LEAD, first)] = strip[pl.ds(i * cut, first), lanes]
            one[j, pl.ds(LEAD + second, end - second)] = following[
                pl.ds(i * more + second - cut, end - second), lanes
            ]
            one[j, pl.ds(LEAD + end, size)] = rest[pl.ds(i * size, size), lanes]
            one[j, after] = rest[pl.ds(base + area + i * width, width), lanes]
    for r in range(rows):
        part = pl.ds(r * width, width)
        one[width + r, before] = left[part, lanes]
        one[width + r, pl.ds(LEAD, first)] = field[r, pl.ds(0, first)]
        one[width + r, pl.ds(LEAD + second, cols - second)] = field[
            r, pl.ds(second, cols - second)
        ]
        one[width + r, after] = right[part, lanes]

    def store(r, at, value):
        if at == LEAD:
            out[r, pl.ds(cols - high, EDGE)] = value
        else:
            out[r, pl.ds(0, cols - high)] = value

    march(
        rows,
        one,
        two,
        spread,
        [(LEAD + second, cols - second + 8), (LEAD - 8, first + 8)],
        [(LEAD + high, cols - high), (LEAD, EDGE)],
        store,
    )


def weight_kernel(axis, count, cells, values, weights, out):
    cols, twice = out.shape
    rows = twice // 2
    slots = cells.shape[1]
    full = cols * lax.axis_size(axis)
    cell = cells[...]
    if full & (full - 1):
        row_of = lax.div(cell, full)
    else:
        row_of = lax.shift_right_logical(cell, full.bit_length() - 1)
    col_of = cell - row_of * full - lax.axis_index(axis) * cols
    slot = lax.broadcasted_iota(jnp.int32, (1, slots), 1)
    plain = jnp.where(slot < count[0], weights[...], 0.0)
    valued = plain * values[...]
    here = lax.broadcasted_iota(jnp.int32, (cols, slots), 0) == col_of
    here = jnp.where(here, 1.0, 0.0).astype(jnp.bfloat16)
    line = lax.broadcasted_iota(jnp.int32, (rows, slots), 0) == row_of
    value = jnp.concatenate([jnp.where(line, plain, 0.0), jnp.where(line, valued, 0.0)], axis=0)
    total = jnp.zeros((cols, twice), jnp.float32)
    for _ in range(3):
        part = value.astype(jnp.bfloat16)
        value = value - part.astype(jnp.float32)
        total = total + dot(here, part, ((1,), (1,)))
    out[...] = total


def cell_weights(rows, pieces, weight, b, many):
    plain, valued = [], []
    for i in range(many):
        r = b * many + i
        for start, column, length in pieces:
            source = weight[pl.ds(column, length)]
            line = lax.broadcasted_iota(jnp.int32, source.shape, 1)
            plain.append(jnp.sum(jnp.where(line == r, source, 0.0), axis=1, keepdims=True))
            valued.append(jnp.sum(jnp.where(line == r + rows, source, 0.0), axis=1, keepdims=True))
    return jnp.concatenate(plain, axis=0), jnp.concatenate(valued, axis=0)


def lay_rows(pieces, column_of, size, centre, b, many):
    cols = centre.shape[1]
    for i in range(many):
        row = jnp.zeros((1, cols), jnp.float32)
        for start, column, length in pieces:
            place = lax.broadcasted_iota(jnp.int32, (length, cols), 0) + column
            here = place == lax.broadcasted_iota(jnp.int32, (length, cols), 1)
            part = column_of[i * size + start : i * size + start + length]
            row = row + jnp.sum(jnp.where(here, part, 0.0), axis=0, keepdims=True)
        centre[pl.ds(b * many + i, 1)] = row


def grouping(rows):
    return next(n for n in (8, 4, 2, 1) if rows % n == 0)


def cells_of(ref, b, many, start=0):
    value = ref[pl.ds(start + b * many, many)]
    return value.reshape(many * value.shape[1], value.shape[2])


def lane_mean(value):
    return jnp.sum(value, axis=1, keepdims=True) * (1.0 / value.shape[1])


def wide(parts):
    return jnp.concatenate(parts, axis=1)


def dot_wide(a, both, size):
    value = dot(a[0], both)
    return value[:, :size] + value[:, size:] + dot(a[1], both[:, :size])


def gram_kernel(groups, pieces, own, others, weight, upper, lower, centre, total, tilt):
    rows, size, _ = own.shape
    many = grouping(rows)
    depth = many * size

    def block(b):
        parts = [cells_of(own, b, many)]
        parts += [cells_of(others, b, many, g * rows) for g in range(groups - 1)]
        value = wide(parts) if groups > 1 else parts[0]
        mean = lane_mean(value)
        deviation = value - mean
        plain, valued = cell_weights(rows, pieces, weight, b, many)
        lay_rows(pieces, mean, size, centre, b, many)
        high, low = halves(deviation)
        at = pl.ds(b * depth, depth)
        upper[at] = high
        lower[at] = low
        turned = (deviation * plain).T
        total[...] += dot3(halves(turned), (high, low))
        tilt[...] += jnp.sum(deviation * (valued - plain * mean), axis=0, keepdims=True)

    loop(rows // many, block)


def own_gram_kernel(layout, first, second, sides, weight, total, left, right, spread):
    local = total.shape[0]
    total[...] = jnp.zeros_like(total)
    for pieces, own in zip(layout, (first, second, sides)):
        rows, size, _ = own.shape
        many = grouping(rows)
        depth = many * size

        def block(b, pieces=pieces, own=own, rows=rows, many=many, depth=depth):
            value = cells_of(own, b, many)
            mean = lane_mean(value)
            deviation = value - mean
            plain, valued = cell_weights(rows, pieces, weight, b, many)
            turned = halves((deviation * plain).T)
            total[...] += dot_wide(turned, wide(halves(deviation)), local)
            if own is sides:
                at = pl.ds(b * depth, depth)
                left[:, at], right[:, at] = turned
                lane = lax.broadcasted_iota(jnp.int32, (depth, local), 1)
                spread[at] = jnp.where(lane == 0, plain, jnp.where(lane == 1, valued, mean))

        loop(rows // many, block)


def tally(total, local, value, partner, plain, valued, mean_own):
    mean_partner = lane_mean(partner)
    counter = partner - mean_partner
    mean = 0.5 * (mean_own + mean_partner)
    apart = 0.5 * (mean_own - mean_partner)
    deviation = value - mean
    pull = valued - plain * mean
    tie = plain * apart

    def add(row, columns):
        total[pl.ds(local + row, 1)] += jnp.sum(columns, axis=0, keepdims=True)

    add(0, deviation * pull)
    add(1, (partner - mean) * pull)
    add(2, deviation * tie)
    add(3, (mean - partner) * tie)
    add(4, jnp.broadcast_to(tie * apart, deviation.shape))
    return counter


def part_deviations(pieces, value, partner, size, upper, lower, centre, b, many):
    value = wide([value, partner])
    mean = lane_mean(value)
    lay_rows(pieces, mean, size, centre, b, many)
    at = pl.ds(b * many * size, many * size)
    upper[at], lower[at] = halves(value - mean)


def part_cross_kernel(pieces, own, other, weight, after, *refs):
    before, (upper, lower, centre, total) = refs[:-4], refs[-4:]
    total[...] = before[0][...] if before else jnp.zeros_like(total)
    rows, size, local = own.shape
    many = grouping(rows)

    def block(b):
        value, partner = cells_of(own, b, many), cells_of(other, b, many)
        mean = lane_mean(value)
        plain, valued = cell_weights(rows, pieces, weight, b, many)
        counter = tally(total, local, value, partner, plain, valued, mean)
        part_deviations(pieces, value, partner, size, upper, lower, centre, b, many)
        turned = ((value - mean) * plain).T
        total[pl.ds(0, local)] += dot_wide(halves(turned), wide(halves(counter)), local)

    loop(rows // many, block)


def last_cross_kernel(own, other, left, right, spread, before, total):
    total[...] = before[...]
    rows, size, local = own.shape
    many = grouping(rows)
    depth = many * size

    def block(b):
        at = pl.ds(b * depth, depth)
        value, partner = cells_of(own, b, many), cells_of(other, b, many)
        counter = tally(total, local, value, partner, *(spread[at, i : i + 1] for i in range(3)))
        total[pl.ds(0, local)] += dot_wide(
            (left[:, at], right[:, at]), wide(halves(counter)), local
        )

    loop(rows // many, block)


def deviation_kernel(pieces, own, other, after, upper, lower, centre):
    rows, size, _ = own.shape
    many = grouping(rows)

    def block(b):
        value, partner = cells_of(own, b, many), cells_of(other, b, many)
        part_deviations(pieces, value, partner, size, upper, lower, centre, b, many)

    loop(rows // many, block)


def part_gram_kernel(groups, pieces, own, others, weight, *refs):
    before, (upper, lower, centre, total, tilt) = refs[:-5], refs[-5:]
    total[...] = before[0][...] if before else jnp.zeros_like(total)
    tilt[...] = before[1][...] if before else jnp.zeros_like(tilt)
    gram_kernel(groups, pieces, own, others, weight, upper, lower, centre, total, tilt)


def last_gram_kernel(
    groups, pieces, own, others, weight, before, tilted, gram, upper, lower, centre, total, tilt
):
    total[...] = before[...]
    tilt[...] = tilted[...]
    gram_kernel(groups, pieces, own, others, weight, upper, lower, centre, total, tilt)
    pull = gram.shape[0] - 8
    blocks = total.shape[0] // 128
    innovation = tilt[...]
    at = 0
    gram[pl.ds(pull, 8)] = jnp.zeros((8, 128), jnp.float32)
    for i in range(blocks):
        gram[pl.ds(pull + i, 1)] = innovation[:, i * 128 : (i + 1) * 128]
        for j in range(i, blocks):
            gram[pl.ds(at, 128)] = total[i * 128 : (i + 1) * 128, j * 128 : (j + 1) * 128]
            at += 128


def assemble(first, second, whole):
    blocks = whole.shape[0] // 128
    pull = first.shape[0] - 8
    at = 0
    for i in range(blocks):
        for j in range(i, blocks):
            block = first[pl.ds(at, 128)] + second[pl.ds(at, 128)]
            whole[i * 128 : (i + 1) * 128, j * 128 : (j + 1) * 128] = block
            if j > i:
                whole[j * 128 : (j + 1) * 128, i * 128 : (i + 1) * 128] = block.T
            at += 128
    return wide([first[pl.ds(pull + i, 1)] + second[pl.ds(pull + i, 1)] for i in range(blocks)])


def assemble_pair(first, second, own, other, whole):
    local = own.shape[1]
    cross = first[pl.ds(0, local)] + second[pl.ds(0, local)]
    rest = first[pl.ds(local, 8)] + second[pl.ds(local, 8)]
    square = rest[4:5]
    diagonal = lax.broadcasted_iota(jnp.int32, (local, local), 0) == lax.broadcasted_iota(
        jnp.int32, (local, local), 1
    )
    uprights = []
    for i, part in enumerate((own, other)):
        tie = rest[2 + i : 3 + i]
        upright = jnp.sum(jnp.where(diagonal, tie, 0.0), axis=1, keepdims=True)
        uprights.append(upright)
        at = slice(i * local, (i + 1) * local)
        whole[at, at] = part[...] + upright + (tie - square)
    cross = cross - uprights[0] + (square - rest[3:4])
    whole[:local, local:] = cross
    whole[local:, :local] = cross.T
    return wide([rest[0:1], rest[1:2]])


def analysis_kernel(layout, pair, *rest):
    if pair:
        first, second, own, other, *rest = rest
    else:
        first, second, *rest = rest
    count = len(layout)
    uppers, lowers, centres = (rest[i * count : (i + 1) * count] for i in range(3))
    out, whole, chosen, natural = rest[3 * count :]
    rows, _ = centres[0].shape
    local = natural.shape[2]
    members = whole.shape[0]
    if pair:
        innovation = assemble_pair(first, second, own, other, whole)
    else:
        innovation = assemble(first, second, whole)
    down = lax.broadcasted_iota(jnp.int32, (members, members), 0)
    across = lax.broadcasted_iota(jnp.int32, (members, members), 1)
    identity = jnp.where(down == across, 1.0, 0.0)
    matrix = whole[...] + (members - 1.0) * identity
    parts = halves(matrix)
    square = dot3(parts, parts)
    squares = jnp.sum(jnp.sum(matrix * matrix, axis=1, keepdims=True), axis=0, keepdims=True)
    scaling = jnp.sqrt(squares)
    current = matrix * (1.0 / scaling)
    square = square * (1.0 / scaling) * (1.0 / scaling)
    inverse = None
    for repeat in range(0, ITERS, 2):
        if repeat:
            parts = halves(current)
            square = dot3(parts, parts)
        inner = 0.0625 * square - 0.5625 * current
        outer = 2.25 * identity - 2.4375 * current + 1.6875 * square
        both = outer + dot3(halves(square), halves(inner))
        both_parts = halves(both)
        if repeat + 2 < ITERS:
            twice = dot3(both_parts, both_parts)
            current = dot3(halves(current), halves(twice))
        inverse = both if inverse is None else dot3(halves(inverse), both_parts)
    once = jnp.sum(inverse * innovation, axis=1, keepdims=True)
    once_row = jnp.sum(jnp.where(down == across, once, 0.0), axis=0, keepdims=True)
    shifted = jnp.sum(inverse * once_row, axis=1, keepdims=True) * (1.0 / scaling)
    factor = jnp.sqrt((members - 1.0) / scaling)
    mixing = (factor * inverse + shifted)[:, :local]
    high, low = halves(mixing)
    chosen[:, :local] = high
    chosen[:, local:] = low
    many = grouping(rows)

    def block(b):
        for pieces, upper, lower in zip(layout, uppers, lowers):
            size = upper.shape[0] // rows
            at = pl.ds(b * many * size, many * size)
            value = dot(upper[at], chosen[...])
            value = value[:, :local] + value[:, local:] + dot(lower[at], chosen[:, :local])
            for i in range(many):
                for start, column, length in pieces:
                    natural[i, pl.ds(column, length)] = value[
                        i * size + start : i * size + start + length
                    ]
        for i in range(many):
            r = b * many + i
            middle_row = sum(c[pl.ds(r, 1)] for c in centres)
            out[pl.ds(r, local, stride=rows)] = natural[i].T + middle_row

    loop(rows // many, block)


def shift(value, axes, *moves):
    sizes = [lax.axis_size(a) for a in axes]
    pairs = []
    total = 1
    for s in sizes:
        total *= s
    for flat in range(total):
        rest, place = flat, []
        for s in reversed(sizes):
            place.append(rest % s)
            rest //= s
        place = place[::-1]
        to = 0
        for s, p, m in zip(sizes, place, moves):
            to = to * s + (p + m) % s
        pairs.append((flat, to))
    return lax.ppermute(value, axes if len(axes) > 1 else axes[0], pairs)


def trade(value, axis, first):
    size = lax.axis_size(axis)
    if size % 2:
        raise ValueError("odd ring")
    start = 1 if first else 0
    pairs = [(i % size, (i + 1) % size) for i in range(start, size, 2)]
    return lax.ppermute(value, axis, pairs + [(j, i) for i, j in pairs])


def role_sums(value):
    size = lax.axis_size("role")
    if size & (size - 1) or size == 1:
        return [(lax.psum(value, "role"), jnp.zeros_like(value))]
    stages = []
    step = 1
    while step < size:
        other = lax.ppermute(value, "role", [(i, i ^ step) for i in range(size)])
        stages.append((value, other))
        value = value + other
        step *= 2
    return stages


def shards(
    ensemble,
    diffusion,
    drift_rows,
    drift_cols,
    observed_cells,
    observed_count,
    observed_values,
    observed_weights,
):
    groups = lax.axis_size("member")
    local, rows, cols = ensemble.shape
    members = local * groups
    width = STEPS
    lanes = max(local, cols)
    cut, end = parted(cols)
    strip = struct(width * cut + 4 * width, lanes)
    following = struct(width * (end - cut), lanes)
    rest = struct(width * (cols - end) + 2 * width * width + 2 * width, lanes)
    edge = struct(rows * width + rows, lanes)
    field, kept, early, late, early_next, late_next, left, right = call(
        functools.partial(pack_kernel, "domain"),
        (
            struct(rows, cols, local),
            struct(3, rows, cols),
            strip,
            strip,
            following,
            following,
            edge,
            edge,
        ),
        ensemble.reshape(local * rows, cols),
        diffusion,
        drift_rows,
        drift_cols,
        raw=4,
    )
    early = trade(early, "domain", True)
    late = trade(late, "domain", False)
    early_next = trade(early_next, "domain", True)
    late_next = trade(late_next, "domain", False)
    received = shift(right, ("role",), 1)
    right = shift(left, ("role",), -1)
    left = received
    weight = call(
        functools.partial(weight_kernel, "role"),
        struct(cols, 2 * rows),
        observed_count,
        observed_cells,
        observed_values,
        observed_weights,
        scalars=1,
    )
    early_rest, late_rest = call(
        functools.partial(turn_kernel, "domain"), (rest, rest), field, left, right, weight
    )
    early_rest = trade(early_rest, "domain", True)
    late_rest = trade(late_rest, "domain", False)
    padded = pltpu.VMEM((rows + 2 * width, cols + 2 * LEAD, local), jnp.float32)
    scratch = (
        padded,
        padded,
        pltpu.VMEM((4, rows + 2 * width, cols + 2 * LEAD, local), jnp.float32),
        pltpu.VMEM((5, 2 * width, cols), jnp.float32),
    )
    ends = (EDGE, cut - EDGE, end - EDGE)

    def forecast(after, low, high, pieces, *strips):
        return call(
            functools.partial(middle_kernel, "domain", low, high, pieces),
            struct(rows, high - low, local),
            after,
            field,
            kept,
            *strips,
            scratch=scratch,
        )

    first = forecast(weight, *ends[:2], ((0, cut, 0, 0, cut),), early, late)
    back = 2 * EDGE
    pieces = (
        (0, cut, cut - back, cut - back, back),
        (1, end - cut, 0, cut, end - cut),
    )
    second = forecast(first, *ends[1:], pieces, early, late, early_next, late_next)
    sides = call(
        functools.partial(sides_kernel, "domain"),
        struct(rows, cols - end + 2 * EDGE, local),
        second,
        field,
        kept,
        early,
        late,
        early_next,
        late_next,
        left,
        right,
        early_rest,
        late_rest,
        scratch=scratch,
    )

    def gathered(value):
        others = [shift(value, ("member",), s) for s in range(1, groups)]
        return jnp.concatenate(others, axis=0) if len(others) > 1 else others[0]

    owns = (first, second, sides)
    theirs = []
    for value in owns:
        theirs.append(gathered(value))
    tail = cols - end + EDGE
    layout = (
        ((0, ends[0], ends[1] - ends[0]),),
        ((0, ends[1], ends[2] - ends[1]),),
        ((0, ends[2], tail), (tail, 0, EDGE)),
    )

    def deviations(value):
        one = struct(rows * value.shape[1], members, kind=jnp.bfloat16)
        return one, one, struct(rows, cols)

    made = []
    pair = groups == 2 and local % 128 == 0
    if pair:
        sided = rows * sides.shape[1]
        half = struct(local, sided, kind=jnp.bfloat16)
        alone, left_half, right_half, spread = call(
            functools.partial(own_gram_kernel, layout),
            (struct(local, local), half, half, struct(sided, local)),
            *owns,
            weight,
        )
        stages = role_sums(alone)
        started = sum(stages[0])
        cross = struct(local + 8, local)
        total = ()
        for i in range(2):
            *three, total = call(
                functools.partial(part_cross_kernel, layout[i]),
                (*deviations(owns[i]), cross),
                owns[i],
                theirs[i],
                weight,
                started,
                *total,
            )
            made.append(three)
            total = (total,)
        alone, arriving = stages[-1]
        total, alone = lax.optimization_barrier((total[0], alone))
        alone = alone + arriving
        gram = call(
            last_cross_kernel, cross, sides, theirs[-1], left_half, right_half, spread, total
        )
        facing = shift(alone, ("member",), 1)
        grams = (*role_sums(gram)[-1], alone, facing)
        three = call(
            functools.partial(deviation_kernel, layout[-1]),
            deviations(sides),
            sides,
            theirs[-1],
            gram,
        )
        made.append(three)
    else:
        blocks = members // 128
        size = blocks * (blocks + 1) // 2 * 128 + 8
        sums = struct(members, members), struct(1, members)
        totals = ()
        for i in range(2):
            *three, total, tilt = call(
                functools.partial(part_gram_kernel, groups, layout[i]),
                (*deviations(owns[i]), *sums),
                owns[i],
                theirs[i],
                weight,
                *totals,
            )
            made.append(three)
            totals = total, tilt
        gram, *three = call(
            functools.partial(last_gram_kernel, groups, layout[-1]),
            (struct(size, 128), *deviations(sides)),
            sides,
            theirs[-1],
            weight,
            *totals,
            scratch=tuple(pltpu.VMEM(v.shape, v.dtype) for v in sums),
        )
        made.append(three)
        grams = role_sums(gram)[-1]
    return call(
        functools.partial(analysis_kernel, layout, pair),
        struct(local * rows, cols),
        *grams,
        *(three[k] for k in range(3) for three in made),
        scratch=(
            pltpu.VMEM((members, members), jnp.float32),
            pltpu.VMEM((members, 2 * local), jnp.bfloat16),
            pltpu.VMEM((grouping(rows), cols, local), jnp.float32),
        ),
        result=True,
    ).reshape(local, rows, cols)


def solution(mesh):
    placed = (
        P("member", "domain", "role"),
        P("domain", "role"),
        P("domain", "role"),
        P("domain", "role"),
        P("domain", None),
        P("domain"),
        P("domain", None),
        P("domain", None),
    )
    return jax.shard_map(
        shards, mesh=mesh, in_specs=placed, out_specs=P("member", "domain", "role"), check_vma=False
    )
```

```python
import functools

import jax
import jax.numpy as jnp
from jax import lax
from jax.experimental import pallas as pl
from jax.experimental.pallas import tpu as pltpu
from jax.sharding import PartitionSpec as P


STEPS = 4
ITERS = 6
LEAD = 16


VMEM = pl.BlockSpec(memory_space=pltpu.VMEM)
SMEM = pl.BlockSpec(memory_space=pltpu.SMEM)
ROOM = 1 << 20


def struct(*shape, kind=jnp.float32):
    return jax.ShapeDtypeStruct(shape, kind)


def near(shape, kind):
    size = jnp.dtype(kind).itemsize
    for place, extent in enumerate(shape[::-1]):
        unit = (128, 32 // jnp.dtype(kind).itemsize, 1)[min(place, 2)]
        size *= -(-extent // unit) * unit
    return size <= ROOM


def call(body, outs, *args, scratch=(), scalars=0, raw=0, result=False):
    placed = list(args[: scalars + raw])
    for value in args[scalars + raw :]:
        if near(value.shape, value.dtype):
            value = pltpu.with_memory_space_constraint(value, pltpu.VMEM)
        placed.append(value)
    if not result:
        outs = jax.tree.map(
            lambda s: pltpu.VMEM(s.shape, s.dtype) if near(s.shape, s.dtype) else s, outs
        )
    return pl.pallas_call(
        body,
        out_shape=outs,
        in_specs=[SMEM] * scalars + [VMEM] * (len(args) - scalars),
        out_specs=tuple(VMEM for _ in outs) if isinstance(outs, tuple) else VMEM,
        scratch_shapes=scratch,
    )(*placed)


def halves(value):
    upper = value.astype(jnp.bfloat16)
    lower = (value - upper.astype(jnp.float32)).astype(jnp.bfloat16)
    return upper, lower


def dot(a, b, dims=((1,), (0,))):
    return lax.dot_general(a, b, (dims, ((), ())), preferred_element_type=jnp.float32)


def by_halves(product, *operands):
    half = operands[0].shape[0] // 2
    parts = [product(*(o[at] for o in operands)) for at in (slice(0, half), slice(half, None))]
    return jnp.concatenate(parts, axis=0)


def dot3(a, b):
    return by_halves(
        lambda high, low: (dot(high, b[0]) + dot(low, b[0])) + dot(high, b[1]), *a
    )


def loop(count, body):
    if count <= 16:
        for i in range(count):
            body(i)
    else:
        lax.fori_loop(0, count, lambda i, c: (body(i), c)[1], 0)


EDGE = 8


def parted(cols):
    return cols * 7 // 16 // 8 * 8, cols * 13 // 16 // 8 * 8


def parity(axis):
    return lax.rem(lax.axis_index(axis), 2)


def pack_kernel(
    axis,
    ens,
    diffusion,
    drift_rows,
    drift_cols,
    field,
    kept,
    early,
    late,
    early_next,
    late_next,
    left,
    right,
):
    odd = parity(axis)
    rows, cols, members = field.shape
    width = STEPS
    cut, end = parted(cols)
    more = end - cut
    lanes = pl.ds(0, members)
    for r in range(rows):
        turned = ens[pl.ds(r, members, stride=rows)].T
        field[r] = turned
        part = pl.ds(r * width, width)
        left[part, lanes] = turned[:width]
        right[part, lanes] = turned[cols - width :]
    for i in range(width):
        part = pl.ds(i * cut, cut)
        early[part, lanes] = field[i + odd * (rows - width), pl.ds(0, cut)]
        late[part, lanes] = field[i + (1 - odd) * (rows - width), pl.ds(0, cut)]
        part = pl.ds(i * more, more)
        early_next[part, lanes] = field[i + odd * (rows - width), pl.ds(cut, more)]
        late_next[part, lanes] = field[i + (1 - odd) * (rows - width), pl.ds(cut, more)]
    near_edge = jnp.zeros((rows, cols), jnp.float32)
    far_edge = near_edge
    lane = lax.broadcasted_iota(jnp.int32, (rows, cols), 1)
    for k, part in enumerate((diffusion, drift_rows, drift_cols)):
        at = pl.ds(width * cut + k * width, width)
        top, bottom = part[:width], part[rows - width :]
        early[at, pl.ds(0, cols)] = jnp.where(odd == 0, top, bottom)
        late[at, pl.ds(0, cols)] = jnp.where(odd == 0, bottom, top)
        value = part[...]
        kept[k] = value
        mine = (lane >= k * width) & (lane < (k + 1) * width)
        if k:
            near_edge = jnp.where(mine, pltpu.roll(value, k * width, 1), near_edge)
        else:
            near_edge = jnp.where(mine, value, near_edge)
        far_edge = jnp.where(mine, pltpu.roll(value, (k + 1) * width, 1), far_edge)
    left[pl.ds(rows * width, rows), pl.ds(0, cols)] = near_edge
    right[pl.ds(rows * width, rows), pl.ds(0, cols)] = far_edge


def turn_kernel(axis, field, left, right, after, early, late):
    rows, cols, members = field.shape
    odd = parity(axis)
    width = STEPS
    area = width * width
    cut = parted(cols)[1]
    size = cols - cut
    lanes = pl.ds(0, members)
    for i in range(width):
        at = pl.ds(i * size, size)
        early[at, lanes] = field[i + odd * (rows - width), pl.ds(cut, size)]
        late[at, lanes] = field[i + (1 - odd) * (rows - width), pl.ds(cut, size)]
    base = width * size
    for i, side in enumerate((left, right)):
        at = pl.ds(base + i * area, area)
        top, bottom = side[pl.ds(0, area)], side[pl.ds((rows - width) * width, area)]
        early[at] = jnp.where(odd == 0, top, bottom)
        late[at] = jnp.where(odd == 0, bottom, top)
        at = pl.ds(base + 2 * area + i * width, width)
        top = side[pl.ds(rows * width, width)]
        bottom = side[pl.ds(rows * width + rows - width, width)]
        early[at] = jnp.where(odd == 0, top, bottom)
        late[at] = jnp.where(odd == 0, bottom, top)


def widen(write, line, columns, members):
    for at, parts in columns:
        size = parts[0].shape[0]
        diffusion, rowwise, colwise = (
            jnp.broadcast_to(p[:, line : line + 1], (size, members)) for p in parts
        )
        here = pl.ds(at, size)
        write(0, here, 1.0 - 4.0 * diffusion - rowwise - colwise)
        write(1, here, diffusion)
        write(2, here, diffusion + rowwise)
        write(3, here, diffusion + colwise)


def spread_rows(spread, lines, columns, members):
    for line, row in lines:

        def write(k, here, value, row=row):
            spread[k, row, here] = value

        widen(write, line, columns, members)


def march(rows, even, odd, spread, ranges, finals, store):
    width = STEPS
    source, target = even, odd
    for step in range(1, STEPS + 1):
        last = step == STEPS

        def advance(r, source=source, target=target, last=last):
            for at, size in finals if last else ranges:
                here = pl.ds(at, size)
                value = (
                    spread[0, r, here] * source[r, here]
                    + spread[1, r, here] * (source[r + 1, here] + source[r, pl.ds(at + 1, size)])
                    + spread[2, r, here] * source[r - 1, here]
                    + spread[3, r, here] * source[r, pl.ds(at - 1, size)]
                )
                if last:
                    store(r - width, at, value)
                else:
                    target[r, here] = value

        loop(rows + 2 * width - 2 * step, lambda i: advance(i + step))
        source, target = target, source


def coefficient_rows(odd, kept, early, late, stage, cut):
    rows, cols = kept.shape[1:]
    width = STEPS
    for k in range(3):
        at = pl.ds(width * cut + k * width, width), pl.ds(0, cols)
        stage[k, pl.ds(0, width)] = jnp.where(odd == 0, early[at], late[at])
        stage[k, pl.ds(width, width)] = jnp.where(odd == 0, late[at], early[at])
    lines = [(i, i) for i in range(1, width)]
    lines += [(width + i, width + rows + i) for i in range(width - 1)]
    inside = [(r, width + r) for r in range(rows)]
    return [kept[k].T for k in range(3)], inside, [stage[k].T for k in range(3)], lines


def middle_kernel(axis, low, high, pieces, after, field, kept, *refs):
    strips, (out, one, two, spread, stage) = refs[:-5], refs[-5:]
    rows, cols, members = field.shape
    width = STEPS
    lanes = pl.ds(0, members)
    odd = parity(axis)
    own, inside, beyond, lines = coefficient_rows(
        odd, kept, strips[0], strips[1], stage, parted(cols)[0]
    )
    start = pieces[0][3]
    end = pieces[-1][3] + pieces[-1][4]
    for parts, places in ((beyond, lines), (own, inside)):
        spread_rows(spread, places, [(LEAD + start, [p[start:end] for p in parts])], members)
    for pair, strip_cols, first, column, size in pieces:
        here = pl.ds(LEAD + column, size)
        for i in range(width):
            part = pl.ds(i * strip_cols + first, size)
            one[i + odd * (rows + width), here] = strips[2 * pair][part, lanes]
            one[i + (1 - odd) * (rows + width), here] = strips[2 * pair + 1][part, lanes]
    for r in range(rows):
        one[width + r, pl.ds(LEAD + start, end - start)] = field[r, pl.ds(start, end - start)]

    def store(r, at, value):
        out[r] = value

    march(
        rows,
        one,
        two,
        spread,
        [(LEAD + start, end - start)],
        [(LEAD + low, high - low)],
        store,
    )


def sides_kernel(
    axis,
    after,
    field,
    kept,
    early,
    late,
    early_next,
    late_next,
    left,
    right,
    early_rest,
    late_rest,
    out,
    one,
    two,
    spread,
    stage,
):
    rows, cols, members = field.shape
    odd = parity(axis)
    width = STEPS
    area = width * width
    cut, end = parted(cols)
    more = end - cut
    first, second, high = 2 * EDGE, end - 2 * EDGE, end - EDGE
    size = cols - end
    base = width * size
    lanes = pl.ds(0, members)
    own, inside, beyond, lines = coefficient_rows(odd, kept, early, late, stage, cut)
    for side in range(2):
        at = pl.ds(base + 2 * area + side * width, width), pl.ds(0, cols)
        stage[3 + side, pl.ds(0, width)] = jnp.where(odd == 0, early_rest[at], late_rest[at])
        stage[3 + side, pl.ds(width, width)] = jnp.where(odd == 0, late_rest[at], early_rest[at])
    edge = pl.ds(rows * width, rows), pl.ds(0, cols)
    for parts, near_part, far_part, places in (
        (beyond, stage[3].T, stage[4].T, lines),
        (own, left[edge].T, right[edge].T, inside),
    ):
        halo = [slice(k * width, (k + 1) * width) for k in range(3)]
        columns = [
            (LEAD - width, [near_part[h] for h in halo]),
            (LEAD, [p[:first] for p in parts]),
            (LEAD + second, [p[second:] for p in parts]),
            (LEAD + cols, [far_part[h] for h in halo]),
        ]
        spread_rows(spread, places, columns, members)
    before = pl.ds(LEAD - width, width)
    after = pl.ds(LEAD + cols, width)
    for i in range(width):
        for j, strip, following, rest in (
            (i + odd * (rows + width), early, early_next, early_rest),
            (i + (1 - odd) * (rows + width), late, late_next, late_rest),
        ):
            one[j, before] = rest[pl.ds(base + i * width, width), lanes]
            one[j, pl.ds(LEAD, first)] = strip[pl.ds(i * cut, first), lanes]
            one[j, pl.ds(LEAD + second, end - second)] = following[
                pl.ds(i * more + second - cut, end - second), lanes
            ]
            one[j, pl.ds(LEAD + end, size)] = rest[pl.ds(i * size, size), lanes]
            one[j, after] = rest[pl.ds(base + area + i * width, width), lanes]
    for r in range(rows):
        part = pl.ds(r * width, width)
        one[width + r, before] = left[part, lanes]
        one[width + r, pl.ds(LEAD, first)] = field[r, pl.ds(0, first)]
        one[width + r, pl.ds(LEAD + second, cols - second)] = field[
            r, pl.ds(second, cols - second)
        ]
        one[width + r, after] = right[part, lanes]

    def store(r, at, value):
        if at == LEAD:
            out[r, pl.ds(cols - high, EDGE)] = value
        else:
            out[r, pl.ds(0, cols - high)] = value

    march(
        rows,
        one,
        two,
        spread,
        [(LEAD + second, cols - second + 8), (LEAD - 8, first + 8)],
        [(LEAD + high, cols - high), (LEAD, EDGE)],
        store,
    )


def weight_kernel(axis, count, cells, values, weights, out):
    cols, twice = out.shape
    rows = twice // 2
    slots = cells.shape[1]
    full = cols * lax.axis_size(axis)
    cell = cells[...]
    if full & (full - 1):
        row_of = lax.div(cell, full)
    else:
        row_of = lax.shift_right_logical(cell, full.bit_length() - 1)
    col_of = cell - row_of * full - lax.axis_index(axis) * cols
    slot = lax.broadcasted_iota(jnp.int32, (1, slots), 1)
    plain = jnp.where(slot < count[0], weights[...], 0.0)
    valued = plain * values[...]
    here = lax.broadcasted_iota(jnp.int32, (cols, slots), 0) == col_of
    here = jnp.where(here, 1.0, 0.0).astype(jnp.bfloat16)
    line = lax.broadcasted_iota(jnp.int32, (rows, slots), 0) == row_of
    value = jnp.concatenate([jnp.where(line, plain, 0.0), jnp.where(line, valued, 0.0)], axis=0)
    total = jnp.zeros((cols, twice), jnp.float32)
    for _ in range(3):
        part = value.astype(jnp.bfloat16)
        value = value - part.astype(jnp.float32)
        total = total + dot(here, part, ((1,), (1,)))
    out[...] = total


def cell_weights(rows, pieces, weight, b, many):
    plain, valued = [], []
    for i in range(many):
        r = b * many + i
        for start, column, length in pieces:
            source = weight[pl.ds(column, length)]
            line = lax.broadcasted_iota(jnp.int32, source.shape, 1)
            plain.append(jnp.sum(jnp.where(line == r, source, 0.0), axis=1, keepdims=True))
            valued.append(jnp.sum(jnp.where(line == r + rows, source, 0.0), axis=1, keepdims=True))
    return jnp.concatenate(plain, axis=0), jnp.concatenate(valued, axis=0)


def lay_rows(pieces, column_of, size, centre, b, many):
    cols = centre.shape[1]
    for i in range(many):
        row = jnp.zeros((1, cols), jnp.float32)
        for start, column, length in pieces:
            place = lax.broadcasted_iota(jnp.int32, (length, cols), 0) + column
            here = place == lax.broadcasted_iota(jnp.int32, (length, cols), 1)
            part = column_of[i * size + start : i * size + start + length]
            row = row + jnp.sum(jnp.where(here, part, 0.0), axis=0, keepdims=True)
        centre[pl.ds(b * many + i, 1)] = row


def grouping(rows):
    return next(n for n in (8, 4, 2, 1) if rows % n == 0)


def cells_of(ref, b, many, start=0):
    value = ref[pl.ds(start + b * many, many)]
    return value.reshape(many * value.shape[1], value.shape[2])


def lane_mean(value):
    return jnp.sum(value, axis=1, keepdims=True) * (1.0 / value.shape[1])


def wide(parts):
    return jnp.concatenate(parts, axis=1)


def dot_wide(a, both, size):
    value = dot(a[0], both)
    return value[:, :size] + value[:, size:] + dot(a[1], both[:, :size])


def gram_kernel(groups, pieces, own, others, weight, upper, lower, centre, total, tilt):
    rows, size, _ = own.shape
    many = grouping(rows)
    depth = many * size

    def block(b):
        parts = [cells_of(own, b, many)]
        parts += [cells_of(others, b, many, g * rows) for g in range(groups - 1)]
        value = wide(parts) if groups > 1 else parts[0]
        mean = lane_mean(value)
        deviation = value - mean
        plain, valued = cell_weights(rows, pieces, weight, b, many)
        lay_rows(pieces, mean, size, centre, b, many)
        high, low = halves(deviation)
        at = pl.ds(b * depth, depth)
        upper[at] = high
        lower[at] = low
        turned = (deviation * plain).T
        total[...] += dot3(halves(turned), (high, low))
        tilt[...] += jnp.sum(deviation * (valued - plain * mean), axis=0, keepdims=True)

    loop(rows // many, block)


def own_gram_kernel(layout, first, second, sides, weight, total, left, right, spread):
    local = total.shape[0]
    total[...] = jnp.zeros_like(total)
    for pieces, own in zip(layout, (first, second, sides)):
        rows, size, _ = own.shape
        many = grouping(rows)
        depth = many * size

        def block(b, pieces=pieces, own=own, rows=rows, many=many, depth=depth):
            value = cells_of(own, b, many)
            mean = lane_mean(value)
            deviation = value - mean
            plain, valued = cell_weights(rows, pieces, weight, b, many)
            turned = halves((deviation * plain).T)
            total[...] += dot_wide(turned, wide(halves(deviation)), local)
            if own is sides:
                at = pl.ds(b * depth, depth)
                left[:, at], right[:, at] = turned
                for i, column in enumerate((plain, valued, mean)):
                    spread[i, at] = jnp.broadcast_to(column, (depth, local))

        loop(rows // many, block)


def tally(total, local, value, partner, plain, valued, mean_own):
    mean_partner = lane_mean(partner)
    counter = partner - mean_partner
    mean = 0.5 * (mean_own + mean_partner)
    apart = 0.5 * (mean_own - mean_partner)
    deviation = value - mean
    pull = valued - plain * mean
    tie = plain * apart

    def add(row, columns):
        total[pl.ds(local + row, 1)] += jnp.sum(columns, axis=0, keepdims=True)

    add(0, deviation * pull)
    add(1, (partner - mean) * pull)
    add(2, deviation * tie)
    add(3, (mean - partner) * tie)
    add(4, jnp.broadcast_to(tie * apart, deviation.shape))
    return counter


def part_deviations(pieces, value, partner, size, upper, lower, centre, b, many):
    value = wide([value, partner])
    mean = lane_mean(value)
    lay_rows(pieces, mean, size, centre, b, many)
    at = pl.ds(b * many * size, many * size)
    upper[at], lower[at] = halves(value - mean)


def part_cross_kernel(pieces, own, other, weight, after, *refs):
    before, (upper, lower, centre, total) = refs[:-4], refs[-4:]
    total[...] = before[0][...] if before else jnp.zeros_like(total)
    rows, size, local = own.shape
    many = grouping(rows)

    def block(b):
        value, partner = cells_of(own, b, many), cells_of(other, b, many)
        mean = lane_mean(value)
        plain, valued = cell_weights(rows, pieces, weight, b, many)
        counter = tally(total, local, value, partner, plain, valued, mean)
        part_deviations(pieces, value, partner, size, upper, lower, centre, b, many)
        turned = ((value - mean) * plain).T
        total[pl.ds(0, local)] += dot_wide(halves(turned), wide(halves(counter)), local)

    loop(rows // many, block)


def last_cross_kernel(own, other, left, right, spread, before, total):
    total[...] = before[...]
    rows, size, local = own.shape
    many = grouping(rows)
    depth = many * size

    def block(b):
        at = pl.ds(b * depth, depth)
        value, partner = cells_of(own, b, many), cells_of(other, b, many)
        counter = tally(total, local, value, partner, *(spread[i, at] for i in range(3)))
        total[pl.ds(0, local)] += dot_wide(
            (left[:, at], right[:, at]), wide(halves(counter)), local
        )

    loop(rows // many, block)


def deviation_kernel(pieces, own, other, after, upper, lower, centre):
    rows, size, _ = own.shape
    many = grouping(rows)

    def block(b):
        value, partner = cells_of(own, b, many), cells_of(other, b, many)
        part_deviations(pieces, value, partner, size, upper, lower, centre, b, many)

    loop(rows // many, block)


def part_gram_kernel(groups, pieces, own, others, weight, *refs):
    before, (upper, lower, centre, total, tilt) = refs[:-5], refs[-5:]
    total[...] = before[0][...] if before else jnp.zeros_like(total)
    tilt[...] = before[1][...] if before else jnp.zeros_like(tilt)
    gram_kernel(groups, pieces, own, others, weight, upper, lower, centre, total, tilt)


def last_gram_kernel(
    groups, pieces, own, others, weight, before, tilted, gram, upper, lower, centre, total, tilt
):
    total[...] = before[...]
    tilt[...] = tilted[...]
    gram_kernel(groups, pieces, own, others, weight, upper, lower, centre, total, tilt)
    pull = gram.shape[0] - 8
    blocks = total.shape[0] // 128
    innovation = tilt[...]
    at = 0
    gram[pl.ds(pull, 8)] = jnp.zeros((8, 128), jnp.float32)
    for i in range(blocks):
        gram[pl.ds(pull + i, 1)] = innovation[:, i * 128 : (i + 1) * 128]
        for j in range(i, blocks):
            gram[pl.ds(at, 128)] = total[i * 128 : (i + 1) * 128, j * 128 : (j + 1) * 128]
            at += 128


def assemble(first, second, whole):
    blocks = whole.shape[0] // 128
    pull = first.shape[0] - 8
    at = 0
    for i in range(blocks):
        for j in range(i, blocks):
            block = first[pl.ds(at, 128)] + second[pl.ds(at, 128)]
            whole[i * 128 : (i + 1) * 128, j * 128 : (j + 1) * 128] = block
            if j > i:
                whole[j * 128 : (j + 1) * 128, i * 128 : (i + 1) * 128] = block.T
            at += 128
    return wide([first[pl.ds(pull + i, 1)] + second[pl.ds(pull + i, 1)] for i in range(blocks)])


def assemble_pair(first, second, own, other, whole):
    local = own.shape[1]
    cross = first[pl.ds(0, local)] + second[pl.ds(0, local)]
    rest = first[pl.ds(local, 8)] + second[pl.ds(local, 8)]
    square = rest[4:5]
    diagonal = lax.broadcasted_iota(jnp.int32, (local, local), 0) == lax.broadcasted_iota(
        jnp.int32, (local, local), 1
    )
    uprights = []
    for i, part in enumerate((own, other)):
        tie = rest[2 + i : 3 + i]
        upright = jnp.sum(jnp.where(diagonal, tie, 0.0), axis=1, keepdims=True)
        uprights.append(upright)
        at = slice(i * local, (i + 1) * local)
        whole[at, at] = part[...] + upright + (tie - square)
    cross = cross - uprights[0] + (square - rest[3:4])
    whole[:local, local:] = cross
    whole[local:, :local] = cross.T
    return wide([rest[0:1], rest[1:2]])


def analysis_kernel(layout, pair, *rest):
    if pair:
        first, second, own, other, *rest = rest
    else:
        first, second, *rest = rest
    count = len(layout)
    uppers, lowers, centres = (rest[i * count : (i + 1) * count] for i in range(3))
    out, whole, chosen, natural = rest[3 * count :]
    rows, _ = centres[0].shape
    local = natural.shape[2]
    members = whole.shape[0]
    if pair:
        innovation = assemble_pair(first, second, own, other, whole)
    else:
        innovation = assemble(first, second, whole)
    down = lax.broadcasted_iota(jnp.int32, (members, members), 0)
    across = lax.broadcasted_iota(jnp.int32, (members, members), 1)
    identity = jnp.where(down == across, 1.0, 0.0)
    matrix = whole[...] + (members - 1.0) * identity
    parts = halves(matrix)
    square = dot3(parts, parts)
    squares = jnp.sum(jnp.sum(matrix * matrix, axis=1, keepdims=True), axis=0, keepdims=True)
    scaling = jnp.sqrt(squares)
    current = matrix * (1.0 / scaling)
    square = square * (1.0 / scaling) * (1.0 / scaling)
    inverse = None
    for repeat in range(0, ITERS, 2):
        if repeat:
            parts = halves(current)
            square = dot3(parts, parts)
        inner = 0.0625 * square - 0.5625 * current
        outer = 2.25 * identity - 2.4375 * current + 1.6875 * square
        both = outer + dot3(halves(square), halves(inner))
        both_parts = halves(both)
        if repeat + 2 < ITERS:
            twice = dot3(both_parts, both_parts)
            current = dot3(halves(current), halves(twice))
        inverse = both if inverse is None else dot3(halves(inverse), both_parts)
    once = jnp.sum(inverse * innovation, axis=1, keepdims=True)
    once_row = jnp.sum(jnp.where(down == across, once, 0.0), axis=0, keepdims=True)
    shifted = jnp.sum(inverse * once_row, axis=1, keepdims=True) * (1.0 / scaling)
    factor = jnp.sqrt((members - 1.0) / scaling)
    mixing = (factor * inverse + shifted)[:, :local]
    high, low = halves(mixing)
    chosen[:, :local] = high
    chosen[:, local:] = low
    many = grouping(rows)

    def block(b):
        for pieces, upper, lower in zip(layout, uppers, lowers):
            size = upper.shape[0] // rows
            at = pl.ds(b * many * size, many * size)
            value = dot(upper[at], chosen[...])
            value = value[:, :local] + value[:, local:] + dot(lower[at], chosen[:, :local])
            for i in range(many):
                for start, column, length in pieces:
                    natural[i, pl.ds(column, length)] = value[
                        i * size + start : i * size + start + length
                    ]
        for i in range(many):
            r = b * many + i
            middle_row = sum(c[pl.ds(r, 1)] for c in centres)
            out[pl.ds(r, local, stride=rows)] = natural[i].T + middle_row

    loop(rows // many, block)


def shift(value, axes, *moves):
    sizes = [lax.axis_size(a) for a in axes]
    pairs = []
    total = 1
    for s in sizes:
        total *= s
    for flat in range(total):
        rest, place = flat, []
        for s in reversed(sizes):
            place.append(rest % s)
            rest //= s
        place = place[::-1]
        to = 0
        for s, p, m in zip(sizes, place, moves):
            to = to * s + (p + m) % s
        pairs.append((flat, to))
    return lax.ppermute(value, axes if len(axes) > 1 else axes[0], pairs)


def trade(value, axis, first):
    size = lax.axis_size(axis)
    if size % 2:
        raise ValueError("odd ring")
    start = 1 if first else 0
    pairs = [(i % size, (i + 1) % size) for i in range(start, size, 2)]
    return lax.ppermute(value, axis, pairs + [(j, i) for i, j in pairs])


def role_sums(value):
    size = lax.axis_size("role")
    if size & (size - 1) or size == 1:
        return [(lax.psum(value, "role"), jnp.zeros_like(value))]
    stages = []
    step = 1
    while step < size:
        other = lax.ppermute(value, "role", [(i, i ^ step) for i in range(size)])
        stages.append((value, other))
        value = value + other
        step *= 2
    return stages


def shards(
    ensemble,
    diffusion,
    drift_rows,
    drift_cols,
    observed_cells,
    observed_count,
    observed_values,
    observed_weights,
):
    groups = lax.axis_size("member")
    local, rows, cols = ensemble.shape
    members = local * groups
    width = STEPS
    lanes = max(local, cols)
    cut, end = parted(cols)
    strip = struct(width * cut + 4 * width, lanes)
    following = struct(width * (end - cut), lanes)
    rest = struct(width * (cols - end) + 2 * width * width + 2 * width, lanes)
    edge = struct(rows * width + rows, lanes)
    field, kept, early, late, early_next, late_next, left, right = call(
        functools.partial(pack_kernel, "domain"),
        (
            struct(rows, cols, local),
            struct(3, rows, cols),
            strip,
            strip,
            following,
            following,
            edge,
            edge,
        ),
        ensemble.reshape(local * rows, cols),
        diffusion,
        drift_rows,
        drift_cols,
        raw=4,
    )
    early = trade(early, "domain", True)
    late = trade(late, "domain", False)
    early_next = trade(early_next, "domain", True)
    late_next = trade(late_next, "domain", False)
    received = shift(right, ("role",), 1)
    right = shift(left, ("role",), -1)
    left = received
    weight = call(
        functools.partial(weight_kernel, "role"),
        struct(cols, 2 * rows),
        observed_count,
        observed_cells,
        observed_values,
        observed_weights,
        scalars=1,
    )
    early_rest, late_rest = call(
        functools.partial(turn_kernel, "domain"), (rest, rest), field, left, right, weight
    )
    early_rest = trade(early_rest, "domain", True)
    late_rest = trade(late_rest, "domain", False)
    padded = pltpu.VMEM((rows + 2 * width, cols + 2 * LEAD, local), jnp.float32)
    scratch = (
        padded,
        padded,
        pltpu.VMEM((4, rows + 2 * width, cols + 2 * LEAD, local), jnp.float32),
        pltpu.VMEM((5, 2 * width, cols), jnp.float32),
    )
    ends = (EDGE, cut - EDGE, end - EDGE)

    def forecast(after, low, high, pieces, *strips):
        return call(
            functools.partial(middle_kernel, "domain", low, high, pieces),
            struct(rows, high - low, local),
            after,
            field,
            kept,
            *strips,
            scratch=scratch,
        )

    first = forecast(weight, *ends[:2], ((0, cut, 0, 0, cut),), early, late)
    back = 2 * EDGE
    pieces = (
        (0, cut, cut - back, cut - back, back),
        (1, end - cut, 0, cut, end - cut),
    )
    second = forecast(first, *ends[1:], pieces, early, late, early_next, late_next)
    sides = call(
        functools.partial(sides_kernel, "domain"),
        struct(rows, cols - end + 2 * EDGE, local),
        second,
        field,
        kept,
        early,
        late,
        early_next,
        late_next,
        left,
        right,
        early_rest,
        late_rest,
        scratch=scratch,
    )

    def gathered(value):
        others = [shift(value, ("member",), s) for s in range(1, groups)]
        return jnp.concatenate(others, axis=0) if len(others) > 1 else others[0]

    owns = (first, second, sides)
    theirs = []
    for value in owns:
        theirs.append(gathered(value))
    tail = cols - end + EDGE
    layout = (
        ((0, ends[0], ends[1] - ends[0]),),
        ((0, ends[1], ends[2] - ends[1]),),
        ((0, ends[2], tail), (tail, 0, EDGE)),
    )

    def deviations(value):
        one = struct(rows * value.shape[1], members, kind=jnp.bfloat16)
        return one, one, struct(rows, cols)

    made = []
    pair = groups == 2 and local % 128 == 0
    if pair:
        sided = rows * sides.shape[1]
        half = struct(local, sided, kind=jnp.bfloat16)
        alone, left_half, right_half, spread = call(
            functools.partial(own_gram_kernel, layout),
            (struct(local, local), half, half, struct(3, sided, local)),
            *owns,
            weight,
        )
        stages = role_sums(alone)
        started = sum(stages[0])
        cross = struct(local + 8, local)
        total = ()
        for i in range(2):
            *three, total = call(
                functools.partial(part_cross_kernel, layout[i]),
                (*deviations(owns[i]), cross),
                owns[i],
                theirs[i],
                weight,
                started,
                *total,
            )
            made.append(three)
            total = (total,)
        alone, arriving = stages[-1]
        total, alone = lax.optimization_barrier((total[0], alone))
        alone = alone + arriving
        gram = call(
            last_cross_kernel, cross, sides, theirs[-1], left_half, right_half, spread, total
        )
        facing = shift(alone, ("member",), 1)
        grams = (*role_sums(gram)[-1], alone, facing)
        three = call(
            functools.partial(deviation_kernel, layout[-1]),
            deviations(sides),
            sides,
            theirs[-1],
            gram,
        )
        made.append(three)
    else:
        blocks = members // 128
        size = blocks * (blocks + 1) // 2 * 128 + 8
        sums = struct(members, members), struct(1, members)
        totals = ()
        for i in range(2):
            *three, total, tilt = call(
                functools.partial(part_gram_kernel, groups, layout[i]),
                (*deviations(owns[i]), *sums),
                owns[i],
                theirs[i],
                weight,
                *totals,
            )
            made.append(three)
            totals = total, tilt
        gram, *three = call(
            functools.partial(last_gram_kernel, groups, layout[-1]),
            (struct(size, 128), *deviations(sides)),
            sides,
            theirs[-1],
            weight,
            *totals,
            scratch=tuple(pltpu.VMEM(v.shape, v.dtype) for v in sums),
        )
        made.append(three)
        grams = role_sums(gram)[-1]
    return call(
        functools.partial(analysis_kernel, layout, pair),
        struct(local * rows, cols),
        *grams,
        *(three[k] for k in range(3) for three in made),
        scratch=(
            pltpu.VMEM((members, members), jnp.float32),
            pltpu.VMEM((members, 2 * local), jnp.bfloat16),
            pltpu.VMEM((grouping(rows), cols, local), jnp.float32),
        ),
        result=True,
    ).reshape(local, rows, cols)


def solution(mesh):
    placed = (
        P("member", "domain", "role"),
        P("domain", "role"),
        P("domain", "role"),
        P("domain", "role"),
        P("domain", None),
        P("domain"),
        P("domain", None),
        P("domain", None),
    )
    return jax.shard_map(
        shards, mesh=mesh, in_specs=placed, out_specs=P("member", "domain", "role"), check_vma=False
    )
```

```python
import functools

import jax
import jax.numpy as jnp
from jax import lax
from jax.experimental import pallas as pl
from jax.experimental.pallas import tpu as pltpu
from jax.sharding import PartitionSpec as P


STEPS = 4
ITERS = 6
LEAD = 16


VMEM = pl.BlockSpec(memory_space=pltpu.VMEM)
SMEM = pl.BlockSpec(memory_space=pltpu.SMEM)
ROOM = 1 << 20


def struct(*shape, kind=jnp.float32):
    return jax.ShapeDtypeStruct(shape, kind)


def near(shape, kind):
    size = jnp.dtype(kind).itemsize
    for place, extent in enumerate(shape[::-1]):
        unit = (128, 32 // jnp.dtype(kind).itemsize, 1)[min(place, 2)]
        size *= -(-extent // unit) * unit
    return size <= ROOM


def call(body, outs, *args, scratch=(), scalars=0, raw=0, result=False):
    placed = list(args[: scalars + raw])
    for value in args[scalars + raw :]:
        if near(value.shape, value.dtype):
            value = pltpu.with_memory_space_constraint(value, pltpu.VMEM)
        placed.append(value)
    if not result:
        outs = jax.tree.map(
            lambda s: pltpu.VMEM(s.shape, s.dtype) if near(s.shape, s.dtype) else s, outs
        )
    return pl.pallas_call(
        body,
        out_shape=outs,
        in_specs=[SMEM] * scalars + [VMEM] * (len(args) - scalars),
        out_specs=tuple(VMEM for _ in outs) if isinstance(outs, tuple) else VMEM,
        scratch_shapes=scratch,
    )(*placed)


def halves(value):
    upper = value.astype(jnp.bfloat16)
    lower = (value - upper.astype(jnp.float32)).astype(jnp.bfloat16)
    return upper, lower


def dot(a, b, dims=((1,), (0,))):
    return lax.dot_general(a, b, (dims, ((), ())), preferred_element_type=jnp.float32)


def by_halves(product, *operands):
    half = operands[0].shape[0] // 2
    parts = [product(*(o[at] for o in operands)) for at in (slice(0, half), slice(half, None))]
    return jnp.concatenate(parts, axis=0)


def dot3(a, b):
    return by_halves(
        lambda high, low: (dot(high, b[0]) + dot(low, b[0])) + dot(high, b[1]), *a
    )


def loop(count, body):
    if count <= 16:
        for i in range(count):
            body(i)
    else:
        lax.fori_loop(0, count, lambda i, c: (body(i), c)[1], 0)


EDGE = 8


def parted(cols):
    return cols * 3 // 8 // 8 * 8, cols * 3 // 4 // 8 * 8


def parity(axis):
    return lax.rem(lax.axis_index(axis), 2)


def pack_kernel(
    axis,
    ens,
    diffusion,
    drift_rows,
    drift_cols,
    field,
    kept,
    early,
    late,
    early_next,
    late_next,
    left,
    right,
):
    odd = parity(axis)
    rows, cols, members = field.shape
    width = STEPS
    cut, end = parted(cols)
    more = end - cut
    lanes = pl.ds(0, members)
    for r in range(rows):
        turned = ens[pl.ds(r, members, stride=rows)].T
        field[r] = turned
        part = pl.ds(r * width, width)
        left[part, lanes] = turned[:width]
        right[part, lanes] = turned[cols - width :]
    for i in range(width):
        part = pl.ds(i * cut, cut)
        early[part, lanes] = field[i + odd * (rows - width), pl.ds(0, cut)]
        late[part, lanes] = field[i + (1 - odd) * (rows - width), pl.ds(0, cut)]
        part = pl.ds(i * more, more)
        early_next[part, lanes] = field[i + odd * (rows - width), pl.ds(cut, more)]
        late_next[part, lanes] = field[i + (1 - odd) * (rows - width), pl.ds(cut, more)]
    near_edge = jnp.zeros((rows, cols), jnp.float32)
    far_edge = near_edge
    lane = lax.broadcasted_iota(jnp.int32, (rows, cols), 1)
    for k, part in enumerate((diffusion, drift_rows, drift_cols)):
        at = pl.ds(width * cut + k * width, width)
        top, bottom = part[:width], part[rows - width :]
        early[at, pl.ds(0, cols)] = jnp.where(odd == 0, top, bottom)
        late[at, pl.ds(0, cols)] = jnp.where(odd == 0, bottom, top)
        value = part[...]
        kept[k] = value
        mine = (lane >= k * width) & (lane < (k + 1) * width)
        if k:
            near_edge = jnp.where(mine, pltpu.roll(value, k * width, 1), near_edge)
        else:
            near_edge = jnp.where(mine, value, near_edge)
        far_edge = jnp.where(mine, pltpu.roll(value, (k + 1) * width, 1), far_edge)
    left[pl.ds(rows * width, rows), pl.ds(0, cols)] = near_edge
    right[pl.ds(rows * width, rows), pl.ds(0, cols)] = far_edge


def turn_kernel(axis, field, left, right, after, early, late):
    rows, cols, members = field.shape
    odd = parity(axis)
    width = STEPS
    area = width * width
    cut = parted(cols)[1]
    size = cols - cut
    lanes = pl.ds(0, members)
    for i in range(width):
        at = pl.ds(i * size, size)
        early[at, lanes] = field[i + odd * (rows - width), pl.ds(cut, size)]
        late[at, lanes] = field[i + (1 - odd) * (rows - width), pl.ds(cut, size)]
    base = width * size
    for i, side in enumerate((left, right)):
        at = pl.ds(base + i * area, area)
        top, bottom = side[pl.ds(0, area)], side[pl.ds((rows - width) * width, area)]
        early[at] = jnp.where(odd == 0, top, bottom)
        late[at] = jnp.where(odd == 0, bottom, top)
        at = pl.ds(base + 2 * area + i * width, width)
        top = side[pl.ds(rows * width, width)]
        bottom = side[pl.ds(rows * width + rows - width, width)]
        early[at] = jnp.where(odd == 0, top, bottom)
        late[at] = jnp.where(odd == 0, bottom, top)


def widen(write, line, columns, members):
    for at, parts in columns:
        size = parts[0].shape[0]
        diffusion, rowwise, colwise = (
            jnp.broadcast_to(p[:, line : line + 1], (size, members)) for p in parts
        )
        here = pl.ds(at, size)
        write(0, here, 1.0 - 4.0 * diffusion - rowwise - colwise)
        write(1, here, diffusion)
        write(2, here, diffusion + rowwise)
        write(3, here, diffusion + colwise)


def spread_rows(spread, lines, columns, members):
    for line, row in lines:

        def write(k, here, value, row=row):
            spread[k, row, here] = value

        widen(write, line, columns, members)


def march(rows, even, odd, spread, ranges, finals, store):
    width = STEPS
    source, target = even, odd
    for step in range(1, STEPS + 1):
        last = step == STEPS

        def advance(r, source=source, target=target, last=last):
            for at, size in finals if last else ranges:
                here = pl.ds(at, size)
                value = (
                    spread[0, r, here] * source[r, here]
                    + spread[1, r, here] * (source[r + 1, here] + source[r, pl.ds(at + 1, size)])
                    + spread[2, r, here] * source[r - 1, here]
                    + spread[3, r, here] * source[r, pl.ds(at - 1, size)]
                )
                if last:
                    store(r - width, at, value)
                else:
                    target[r, here] = value

        loop(rows + 2 * width - 2 * step, lambda i: advance(i + step))
        source, target = target, source


def coefficient_rows(odd, kept, early, late, stage, cut):
    rows, cols = kept.shape[1:]
    width = STEPS
    for k in range(3):
        at = pl.ds(width * cut + k * width, width), pl.ds(0, cols)
        stage[k, pl.ds(0, width)] = jnp.where(odd == 0, early[at], late[at])
        stage[k, pl.ds(width, width)] = jnp.where(odd == 0, late[at], early[at])
    lines = [(i, i) for i in range(1, width)]
    lines += [(width + i, width + rows + i) for i in range(width - 1)]
    inside = [(r, width + r) for r in range(rows)]
    return [kept[k].T for k in range(3)], inside, [stage[k].T for k in range(3)], lines


def middle_kernel(axis, low, high, pieces, after, field, kept, *refs):
    strips, (out, one, two, spread, stage) = refs[:-5], refs[-5:]
    rows, cols, members = field.shape
    width = STEPS
    lanes = pl.ds(0, members)
    odd = parity(axis)
    own, inside, beyond, lines = coefficient_rows(
        odd, kept, strips[0], strips[1], stage, parted(cols)[0]
    )
    start = pieces[0][3]
    end = pieces[-1][3] + pieces[-1][4]
    for parts, places in ((beyond, lines), (own, inside)):
        spread_rows(spread, places, [(LEAD + start, [p[start:end] for p in parts])], members)
    for pair, strip_cols, first, column, size in pieces:
        here = pl.ds(LEAD + column, size)
        for i in range(width):
            part = pl.ds(i * strip_cols + first, size)
            one[i + odd * (rows + width), here] = strips[2 * pair][part, lanes]
            one[i + (1 - odd) * (rows + width), here] = strips[2 * pair + 1][part, lanes]
    for r in range(rows):
        one[width + r, pl.ds(LEAD + start, end - start)] = field[r, pl.ds(start, end - start)]

    def store(r, at, value):
        out[r] = value

    march(
        rows,
        one,
        two,
        spread,
        [(LEAD + start, end - start)],
        [(LEAD + low, high - low)],
        store,
    )


def sides_kernel(
    axis,
    after,
    field,
    kept,
    early,
    late,
    early_next,
    late_next,
    left,
    right,
    early_rest,
    late_rest,
    out,
    one,
    two,
    spread,
    stage,
):
    rows, cols, members = field.shape
    odd = parity(axis)
    width = STEPS
    area = width * width
    cut, end = parted(cols)
    more = end - cut
    first, second, high = 2 * EDGE, end - 2 * EDGE, end - EDGE
    size = cols - end
    base = width * size
    lanes = pl.ds(0, members)
    own, inside, beyond, lines = coefficient_rows(odd, kept, early, late, stage, cut)
    for side in range(2):
        at = pl.ds(base + 2 * area + side * width, width), pl.ds(0, cols)
        stage[3 + side, pl.ds(0, width)] = jnp.where(odd == 0, early_rest[at], late_rest[at])
        stage[3 + side, pl.ds(width, width)] = jnp.where(odd == 0, late_rest[at], early_rest[at])
    edge = pl.ds(rows * width, rows), pl.ds(0, cols)
    for parts, near_part, far_part, places in (
        (beyond, stage[3].T, stage[4].T, lines),
        (own, left[edge].T, right[edge].T, inside),
    ):
        halo = [slice(k * width, (k + 1) * width) for k in range(3)]
        columns = [
            (LEAD - width, [near_part[h] for h in halo]),
            (LEAD, [p[:first] for p in parts]),
            (LEAD + second, [p[second:] for p in parts]),
            (LEAD + cols, [far_part[h] for h in halo]),
        ]
        spread_rows(spread, places, columns, members)
    before = pl.ds(LEAD - width, width)
    after = pl.ds(LEAD + cols, width)
    for i in range(width):
        for j, strip, following, rest in (
            (i + odd * (rows + width), early, early_next, early_rest),
            (i + (1 - odd) * (rows + width), late, late_next, late_rest),
        ):
            one[j, before] = rest[pl.ds(base + i * width, width), lanes]
            one[j, pl.ds(LEAD, first)] = strip[pl.ds(i * cut, first), lanes]
            one[j, pl.ds(LEAD + second, end - second)] = following[
                pl.ds(i * more + second - cut, end - second), lanes
            ]
            one[j, pl.ds(LEAD + end, size)] = rest[pl.ds(i * size, size), lanes]
            one[j, after] = rest[pl.ds(base + area + i * width, width), lanes]
    for r in range(rows):
        part = pl.ds(r * width, width)
        one[width + r, before] = left[part, lanes]
        one[width + r, pl.ds(LEAD, first)] = field[r, pl.ds(0, first)]
        one[width + r, pl.ds(LEAD + second, cols - second)] = field[
            r, pl.ds(second, cols - second)
        ]
        one[width + r, after] = right[part, lanes]

    def store(r, at, value):
        if at == LEAD:
            out[r, pl.ds(cols - high, EDGE)] = value
        else:
            out[r, pl.ds(0, cols - high)] = value

    march(
        rows,
        one,
        two,
        spread,
        [(LEAD + second, cols - second + 8), (LEAD - 8, first + 8)],
        [(LEAD + high, cols - high), (LEAD, EDGE)],
        store,
    )


def weight_kernel(axis, count, cells, values, weights, out):
    cols, twice = out.shape
    rows = twice // 2
    slots = cells.shape[1]
    full = cols * lax.axis_size(axis)
    cell = cells[...]
    if full & (full - 1):
        row_of = lax.div(cell, full)
    else:
        row_of = lax.shift_right_logical(cell, full.bit_length() - 1)
    col_of = cell - row_of * full - lax.axis_index(axis) * cols
    slot = lax.broadcasted_iota(jnp.int32, (1, slots), 1)
    plain = jnp.where(slot < count[0], weights[...], 0.0)
    valued = plain * values[...]
    here = lax.broadcasted_iota(jnp.int32, (cols, slots), 0) == col_of
    here = jnp.where(here, 1.0, 0.0).astype(jnp.bfloat16)
    line = lax.broadcasted_iota(jnp.int32, (rows, slots), 0) == row_of
    value = jnp.concatenate([jnp.where(line, plain, 0.0), jnp.where(line, valued, 0.0)], axis=0)
    total = jnp.zeros((cols, twice), jnp.float32)
    for _ in range(3):
        part = value.astype(jnp.bfloat16)
        value = value - part.astype(jnp.float32)
        total = total + dot(here, part, ((1,), (1,)))
    out[...] = total


def cell_weights(rows, pieces, weight, b, many):
    plain, valued = [], []
    for i in range(many):
        r = b * many + i
        for start, column, length in pieces:
            source = weight[pl.ds(column, length)]
            line = lax.broadcasted_iota(jnp.int32, source.shape, 1)
            plain.append(jnp.sum(jnp.where(line == r, source, 0.0), axis=1, keepdims=True))
            valued.append(jnp.sum(jnp.where(line == r + rows, source, 0.0), axis=1, keepdims=True))
    return jnp.concatenate(plain, axis=0), jnp.concatenate(valued, axis=0)


def lay_rows(pieces, column_of, size, centre, b, many):
    cols = centre.shape[1]
    for i in range(many):
        row = jnp.zeros((1, cols), jnp.float32)
        for start, column, length in pieces:
            place = lax.broadcasted_iota(jnp.int32, (length, cols), 0) + column
            here = place == lax.broadcasted_iota(jnp.int32, (length, cols), 1)
            part = column_of[i * size + start : i * size + start + length]
            row = row + jnp.sum(jnp.where(here, part, 0.0), axis=0, keepdims=True)
        centre[pl.ds(b * many + i, 1)] = row


def grouping(rows):
    return next(n for n in (8, 4, 2, 1) if rows % n == 0)


def cells_of(ref, b, many, start=0):
    value = ref[pl.ds(start + b * many, many)]
    return value.reshape(many * value.shape[1], value.shape[2])


def lane_mean(value):
    return jnp.sum(value, axis=1, keepdims=True) * (1.0 / value.shape[1])


def wide(parts):
    return jnp.concatenate(parts, axis=1)


def dot_wide(a, both, size):
    value = dot(a[0], both)
    return value[:, :size] + value[:, size:] + dot(a[1], both[:, :size])


def gram_kernel(groups, pieces, own, others, weight, upper, lower, centre, total, tilt):
    rows, size, _ = own.shape
    many = grouping(rows)
    depth = many * size

    def block(b):
        parts = [cells_of(own, b, many)]
        parts += [cells_of(others, b, many, g * rows) for g in range(groups - 1)]
        value = wide(parts) if groups > 1 else parts[0]
        mean = lane_mean(value)
        deviation = value - mean
        plain, valued = cell_weights(rows, pieces, weight, b, many)
        lay_rows(pieces, mean, size, centre, b, many)
        high, low = halves(deviation)
        at = pl.ds(b * depth, depth)
        upper[at] = high
        lower[at] = low
        turned = (deviation * plain).T
        total[...] += dot3(halves(turned), (high, low))
        tilt[...] += jnp.sum(deviation * (valued - plain * mean), axis=0, keepdims=True)

    loop(rows // many, block)


def own_gram_kernel(layout, first, second, sides, weight, total, left, right, spread):
    local = total.shape[0]
    total[...] = jnp.zeros_like(total)
    for pieces, own in zip(layout, (first, second, sides)):
        rows, size, _ = own.shape
        many = grouping(rows)
        depth = many * size

        def block(b, pieces=pieces, own=own, rows=rows, many=many, depth=depth):
            value = cells_of(own, b, many)
            mean = lane_mean(value)
            deviation = value - mean
            plain, valued = cell_weights(rows, pieces, weight, b, many)
            turned = halves((deviation * plain).T)
            total[...] += dot_wide(turned, wide(halves(deviation)), local)
            if own is sides:
                at = pl.ds(b * depth, depth)
                left[:, at], right[:, at] = turned
                for i, column in enumerate((plain, valued, mean)):
                    spread[i, at] = jnp.broadcast_to(column, (depth, local))

        loop(rows // many, block)


def tally(total, local, value, partner, plain, valued, mean_own):
    mean_partner = lane_mean(partner)
    counter = partner - mean_partner
    mean = 0.5 * (mean_own + mean_partner)
    apart = 0.5 * (mean_own - mean_partner)
    deviation = value - mean
    pull = valued - plain * mean
    tie = plain * apart

    def add(row, columns):
        total[pl.ds(local + row, 1)] += jnp.sum(columns, axis=0, keepdims=True)

    add(0, deviation * pull)
    add(1, (partner - mean) * pull)
    add(2, deviation * tie)
    add(3, (mean - partner) * tie)
    add(4, jnp.broadcast_to(tie * apart, deviation.shape))
    return counter


def part_deviations(pieces, value, partner, size, upper, lower, centre, b, many):
    value = wide([value, partner])
    mean = lane_mean(value)
    lay_rows(pieces, mean, size, centre, b, many)
    at = pl.ds(b * many * size, many * size)
    upper[at], lower[at] = halves(value - mean)


def part_cross_kernel(pieces, own, other, weight, after, *refs):
    before, (upper, lower, centre, total) = refs[:-4], refs[-4:]
    total[...] = before[0][...] if before else jnp.zeros_like(total)
    rows, size, local = own.shape
    many = grouping(rows)

    def block(b):
        value, partner = cells_of(own, b, many), cells_of(other, b, many)
        mean = lane_mean(value)
        plain, valued = cell_weights(rows, pieces, weight, b, many)
        counter = tally(total, local, value, partner, plain, valued, mean)
        part_deviations(pieces, value, partner, size, upper, lower, centre, b, many)
        turned = ((value - mean) * plain).T
        total[pl.ds(0, local)] += dot_wide(halves(turned), wide(halves(counter)), local)

    loop(rows // many, block)


def last_cross_kernel(own, other, left, right, spread, before, total):
    total[...] = before[...]
    rows, size, local = own.shape
    many = grouping(rows)
    depth = many * size

    def block(b):
        at = pl.ds(b * depth, depth)
        value, partner = cells_of(own, b, many), cells_of(other, b, many)
        counter = tally(total, local, value, partner, *(spread[i, at] for i in range(3)))
        total[pl.ds(0, local)] += dot_wide(
            (left[:, at], right[:, at]), wide(halves(counter)), local
        )

    loop(rows // many, block)


def deviation_kernel(pieces, own, other, after, upper, lower, centre):
    rows, size, _ = own.shape
    many = grouping(rows)

    def block(b):
        value, partner = cells_of(own, b, many), cells_of(other, b, many)
        part_deviations(pieces, value, partner, size, upper, lower, centre, b, many)

    loop(rows // many, block)


def part_gram_kernel(groups, pieces, own, others, weight, *refs):
    before, (upper, lower, centre, total, tilt) = refs[:-5], refs[-5:]
    total[...] = before[0][...] if before else jnp.zeros_like(total)
    tilt[...] = before[1][...] if before else jnp.zeros_like(tilt)
    gram_kernel(groups, pieces, own, others, weight, upper, lower, centre, total, tilt)


def last_gram_kernel(
    groups, pieces, own, others, weight, before, tilted, gram, upper, lower, centre, total, tilt
):
    total[...] = before[...]
    tilt[...] = tilted[...]
    gram_kernel(groups, pieces, own, others, weight, upper, lower, centre, total, tilt)
    pull = gram.shape[0] - 8
    blocks = total.shape[0] // 128
    innovation = tilt[...]
    at = 0
    gram[pl.ds(pull, 8)] = jnp.zeros((8, 128), jnp.float32)
    for i in range(blocks):
        gram[pl.ds(pull + i, 1)] = innovation[:, i * 128 : (i + 1) * 128]
        for j in range(i, blocks):
            gram[pl.ds(at, 128)] = total[i * 128 : (i + 1) * 128, j * 128 : (j + 1) * 128]
            at += 128


def assemble(first, second, whole):
    blocks = whole.shape[0] // 128
    pull = first.shape[0] - 8
    at = 0
    for i in range(blocks):
        for j in range(i, blocks):
            block = first[pl.ds(at, 128)] + second[pl.ds(at, 128)]
            whole[i * 128 : (i + 1) * 128, j * 128 : (j + 1) * 128] = block
            if j > i:
                whole[j * 128 : (j + 1) * 128, i * 128 : (i + 1) * 128] = block.T
            at += 128
    return wide([first[pl.ds(pull + i, 1)] + second[pl.ds(pull + i, 1)] for i in range(blocks)])


def assemble_pair(first, second, own, other, whole):
    local = own.shape[1]
    cross = first[pl.ds(0, local)] + second[pl.ds(0, local)]
    rest = first[pl.ds(local, 8)] + second[pl.ds(local, 8)]
    square = rest[4:5]
    diagonal = lax.broadcasted_iota(jnp.int32, (local, local), 0) == lax.broadcasted_iota(
        jnp.int32, (local, local), 1
    )
    uprights = []
    for i, part in enumerate((own, other)):
        tie = rest[2 + i : 3 + i]
        upright = jnp.sum(jnp.where(diagonal, tie, 0.0), axis=1, keepdims=True)
        uprights.append(upright)
        at = slice(i * local, (i + 1) * local)
        whole[at, at] = part[...] + upright + (tie - square)
    cross = cross - uprights[0] + (square - rest[3:4])
    whole[:local, local:] = cross
    whole[local:, :local] = cross.T
    return wide([rest[0:1], rest[1:2]])


def analysis_kernel(layout, pair, *rest):
    if pair:
        first, second, own, other, *rest = rest
    else:
        first, second, *rest = rest
    count = len(layout)
    uppers, lowers, centres = (rest[i * count : (i + 1) * count] for i in range(3))
    out, whole, chosen, natural = rest[3 * count :]
    rows, _ = centres[0].shape
    local = natural.shape[2]
    members = whole.shape[0]
    if pair:
        innovation = assemble_pair(first, second, own, other, whole)
    else:
        innovation = assemble(first, second, whole)
    down = lax.broadcasted_iota(jnp.int32, (members, members), 0)
    across = lax.broadcasted_iota(jnp.int32, (members, members), 1)
    identity = jnp.where(down == across, 1.0, 0.0)
    matrix = whole[...] + (members - 1.0) * identity
    parts = halves(matrix)
    square = dot3(parts, parts)
    squares = jnp.sum(jnp.sum(matrix * matrix, axis=1, keepdims=True), axis=0, keepdims=True)
    scaling = jnp.sqrt(squares)
    current = matrix * (1.0 / scaling)
    square = square * (1.0 / scaling) * (1.0 / scaling)
    inverse = None
    for repeat in range(0, ITERS, 2):
        if repeat:
            parts = halves(current)
            square = dot3(parts, parts)
        inner = 0.0625 * square - 0.5625 * current
        outer = 2.25 * identity - 2.4375 * current + 1.6875 * square
        both = outer + dot3(halves(square), halves(inner))
        both_parts = halves(both)
        if repeat + 2 < ITERS:
            twice = dot3(both_parts, both_parts)
            current = dot3(halves(current), halves(twice))
        inverse = both if inverse is None else dot3(halves(inverse), both_parts)
    once = jnp.sum(inverse * innovation, axis=1, keepdims=True)
    once_row = jnp.sum(jnp.where(down == across, once, 0.0), axis=0, keepdims=True)
    shifted = jnp.sum(inverse * once_row, axis=1, keepdims=True) * (1.0 / scaling)
    factor = jnp.sqrt((members - 1.0) / scaling)
    mixing = (factor * inverse + shifted)[:, :local]
    high, low = halves(mixing)
    chosen[:, :local] = high
    chosen[:, local:] = low
    many = grouping(rows)

    def block(b):
        for pieces, upper, lower in zip(layout, uppers, lowers):
            size = upper.shape[0] // rows
            at = pl.ds(b * many * size, many * size)
            value = dot(upper[at], chosen[...])
            value = value[:, :local] + value[:, local:] + dot(lower[at], chosen[:, :local])
            for i in range(many):
                for start, column, length in pieces:
                    natural[i, pl.ds(column, length)] = value[
                        i * size + start : i * size + start + length
                    ]
        for i in range(many):
            r = b * many + i
            middle_row = sum(c[pl.ds(r, 1)] for c in centres)
            out[pl.ds(r, local, stride=rows)] = natural[i].T + middle_row

    loop(rows // many, block)


def shift(value, axes, *moves):
    sizes = [lax.axis_size(a) for a in axes]
    pairs = []
    total = 1
    for s in sizes:
        total *= s
    for flat in range(total):
        rest, place = flat, []
        for s in reversed(sizes):
            place.append(rest % s)
            rest //= s
        place = place[::-1]
        to = 0
        for s, p, m in zip(sizes, place, moves):
            to = to * s + (p + m) % s
        pairs.append((flat, to))
    return lax.ppermute(value, axes if len(axes) > 1 else axes[0], pairs)


def trade(value, axis, first):
    size = lax.axis_size(axis)
    if size % 2:
        raise ValueError("odd ring")
    start = 1 if first else 0
    pairs = [(i % size, (i + 1) % size) for i in range(start, size, 2)]
    return lax.ppermute(value, axis, pairs + [(j, i) for i, j in pairs])


def role_sums(value, far_first=False):
    size = lax.axis_size("role")
    if size & (size - 1) or size == 1:
        return [(lax.psum(value, "role"), jnp.zeros_like(value))]
    steps = [1 << i for i in range(size.bit_length() - 1)]
    stages = []
    for step in steps[::-1] if far_first else steps:
        other = lax.ppermute(value, "role", [(k, k ^ step) for k in range(size)])
        stages.append((value, other))
        value = value + other
    return stages


def shards(
    ensemble,
    diffusion,
    drift_rows,
    drift_cols,
    observed_cells,
    observed_count,
    observed_values,
    observed_weights,
):
    groups = lax.axis_size("member")
    local, rows, cols = ensemble.shape
    members = local * groups
    width = STEPS
    lanes = max(local, cols)
    cut, end = parted(cols)
    strip = struct(width * cut + 4 * width, lanes)
    following = struct(width * (end - cut), lanes)
    rest = struct(width * (cols - end) + 2 * width * width + 2 * width, lanes)
    edge = struct(rows * width + rows, lanes)
    field, kept, early, late, early_next, late_next, left, right = call(
        functools.partial(pack_kernel, "domain"),
        (
            struct(rows, cols, local),
            struct(3, rows, cols),
            strip,
            strip,
            following,
            following,
            edge,
            edge,
        ),
        ensemble.reshape(local * rows, cols),
        diffusion,
        drift_rows,
        drift_cols,
        raw=4,
    )
    early = trade(early, "domain", True)
    late = trade(late, "domain", False)
    early_next = trade(early_next, "domain", True)
    late_next = trade(late_next, "domain", False)
    received = shift(right, ("role",), 1)
    right = shift(left, ("role",), -1)
    left = received
    weight = call(
        functools.partial(weight_kernel, "role"),
        struct(cols, 2 * rows),
        observed_count,
        observed_cells,
        observed_values,
        observed_weights,
        scalars=1,
    )
    early_rest, late_rest = call(
        functools.partial(turn_kernel, "domain"), (rest, rest), field, left, right, weight
    )
    early_rest = trade(early_rest, "domain", True)
    late_rest = trade(late_rest, "domain", False)
    padded = pltpu.VMEM((rows + 2 * width, cols + 2 * LEAD, local), jnp.float32)
    scratch = (
        padded,
        padded,
        pltpu.VMEM((4, rows + 2 * width, cols + 2 * LEAD, local), jnp.float32),
        pltpu.VMEM((5, 2 * width, cols), jnp.float32),
    )
    ends = (EDGE, cut - EDGE, end - EDGE)

    def forecast(after, low, high, pieces, *strips):
        return call(
            functools.partial(middle_kernel, "domain", low, high, pieces),
            struct(rows, high - low, local),
            after,
            field,
            kept,
            *strips,
            scratch=scratch,
        )

    first = forecast(weight, *ends[:2], ((0, cut, 0, 0, cut),), early, late)
    back = 2 * EDGE
    pieces = (
        (0, cut, cut - back, cut - back, back),
        (1, end - cut, 0, cut, end - cut),
    )
    second = forecast(first, *ends[1:], pieces, early, late, early_next, late_next)
    sides = call(
        functools.partial(sides_kernel, "domain"),
        struct(rows, cols - end + 2 * EDGE, local),
        second,
        field,
        kept,
        early,
        late,
        early_next,
        late_next,
        left,
        right,
        early_rest,
        late_rest,
        scratch=scratch,
    )

    def gathered(value):
        others = [shift(value, ("member",), s) for s in range(1, groups)]
        return jnp.concatenate(others, axis=0) if len(others) > 1 else others[0]

    owns = (first, second, sides)
    theirs = []
    for value in owns:
        theirs.append(gathered(value))
    tail = cols - end + EDGE
    layout = (
        ((0, ends[0], ends[1] - ends[0]),),
        ((0, ends[1], ends[2] - ends[1]),),
        ((0, ends[2], tail), (tail, 0, EDGE)),
    )

    def deviations(value):
        one = struct(rows * value.shape[1], members, kind=jnp.bfloat16)
        return one, one, struct(rows, cols)

    made = []
    pair = groups == 2 and local % 128 == 0
    if pair:
        sided = rows * sides.shape[1]
        half = struct(local, sided, kind=jnp.bfloat16)
        alone, left_half, right_half, spread = call(
            functools.partial(own_gram_kernel, layout),
            (struct(local, local), half, half, struct(3, sided, local)),
            *owns,
            weight,
        )
        stages = role_sums(alone)
        started = sum(stages[0])
        cross = struct(local + 8, local)
        total = ()
        for i in range(2):
            *three, total = call(
                functools.partial(part_cross_kernel, layout[i]),
                (*deviations(owns[i]), cross),
                owns[i],
                theirs[i],
                weight,
                started,
                *total,
            )
            made.append(three)
            total = (total,)
        alone, arriving = stages[-1]
        total, alone = lax.optimization_barrier((total[0], alone))
        alone = alone + arriving
        gram = call(
            last_cross_kernel, cross, sides, theirs[-1], left_half, right_half, spread, total
        )
        facing = shift(alone, ("member",), 1)
        grams = (*role_sums(gram, True)[-1], alone, facing)
        three = call(
            functools.partial(deviation_kernel, layout[-1]),
            deviations(sides),
            sides,
            theirs[-1],
            gram,
        )
        made.append(three)
    else:
        blocks = members // 128
        size = blocks * (blocks + 1) // 2 * 128 + 8
        sums = struct(members, members), struct(1, members)
        totals = ()
        for i in range(2):
            *three, total, tilt = call(
                functools.partial(part_gram_kernel, groups, layout[i]),
                (*deviations(owns[i]), *sums),
                owns[i],
                theirs[i],
                weight,
                *totals,
            )
            made.append(three)
            totals = total, tilt
        gram, *three = call(
            functools.partial(last_gram_kernel, groups, layout[-1]),
            (struct(size, 128), *deviations(sides)),
            sides,
            theirs[-1],
            weight,
            *totals,
            scratch=tuple(pltpu.VMEM(v.shape, v.dtype) for v in sums),
        )
        made.append(three)
        grams = role_sums(gram)[-1]
    return call(
        functools.partial(analysis_kernel, layout, pair),
        struct(local * rows, cols),
        *grams,
        *(three[k] for k in range(3) for three in made),
        scratch=(
            pltpu.VMEM((members, members), jnp.float32),
            pltpu.VMEM((members, 2 * local), jnp.bfloat16),
            pltpu.VMEM((grouping(rows), cols, local), jnp.float32),
        ),
        result=True,
    ).reshape(local, rows, cols)


def solution(mesh):
    placed = (
        P("member", "domain", "role"),
        P("domain", "role"),
        P("domain", "role"),
        P("domain", "role"),
        P("domain", None),
        P("domain"),
        P("domain", None),
        P("domain", None),
    )
    return jax.shard_map(
        shards, mesh=mesh, in_specs=placed, out_specs=P("member", "domain", "role"), check_vma=False
    )
```

```python
import functools

import jax
import jax.numpy as jnp
from jax import lax
from jax.experimental import pallas as pl
from jax.experimental.pallas import tpu as pltpu
from jax.sharding import PartitionSpec as P


STEPS = 4
ITERS = 6
LEAD = 16


VMEM = pl.BlockSpec(memory_space=pltpu.VMEM)
SMEM = pl.BlockSpec(memory_space=pltpu.SMEM)
ROOM = 1 << 20


def struct(*shape, kind=jnp.float32):
    return jax.ShapeDtypeStruct(shape, kind)


def near(shape, kind):
    size = jnp.dtype(kind).itemsize
    for place, extent in enumerate(shape[::-1]):
        unit = (128, 32 // jnp.dtype(kind).itemsize, 1)[min(place, 2)]
        size *= -(-extent // unit) * unit
    return size <= ROOM


def call(body, outs, *args, scratch=(), scalars=0, raw=0, result=False):
    placed = list(args[: scalars + raw])
    for value in args[scalars + raw :]:
        if near(value.shape, value.dtype):
            value = pltpu.with_memory_space_constraint(value, pltpu.VMEM)
        placed.append(value)
    if not result:
        outs = jax.tree.map(
            lambda s: pltpu.VMEM(s.shape, s.dtype) if near(s.shape, s.dtype) else s, outs
        )
    return pl.pallas_call(
        body,
        out_shape=outs,
        in_specs=[SMEM] * scalars + [VMEM] * (len(args) - scalars),
        out_specs=tuple(VMEM for _ in outs) if isinstance(outs, tuple) else VMEM,
        scratch_shapes=scratch,
    )(*placed)


def halves(value):
    upper = value.astype(jnp.bfloat16)
    lower = (value - upper.astype(jnp.float32)).astype(jnp.bfloat16)
    return upper, lower


def dot(a, b, dims=((1,), (0,))):
    return lax.dot_general(a, b, (dims, ((), ())), preferred_element_type=jnp.float32)


def by_halves(product, *operands):
    half = operands[0].shape[0] // 2
    parts = [product(*(o[at] for o in operands)) for at in (slice(0, half), slice(half, None))]
    return jnp.concatenate(parts, axis=0)


def dot3(a, b):
    return by_halves(
        lambda high, low: (dot(high, b[0]) + dot(low, b[0])) + dot(high, b[1]), *a
    )


def loop(count, body):
    if count <= 16:
        for i in range(count):
            body(i)
    else:
        lax.fori_loop(0, count, lambda i, c: (body(i), c)[1], 0)


EDGE = 8


def parted(cols):
    return cols * 3 // 8 // 8 * 8, cols * 3 // 4 // 8 * 8


def parity(axis):
    return lax.rem(lax.axis_index(axis), 2)


def pack_kernel(
    axis,
    ens,
    diffusion,
    drift_rows,
    drift_cols,
    field,
    kept,
    early,
    late,
    early_next,
    late_next,
    left,
    right,
):
    odd = parity(axis)
    rows, cols, members = field.shape
    width = STEPS
    cut, end = parted(cols)
    more = end - cut
    lanes = pl.ds(0, members)
    for r in range(rows):
        turned = ens[pl.ds(r, members, stride=rows)].T
        field[r] = turned
        part = pl.ds(r * width, width)
        left[part, lanes] = turned[:width]
        right[part, lanes] = turned[cols - width :]
    for i in range(width):
        part = pl.ds(i * cut, cut)
        early[part, lanes] = field[i + odd * (rows - width), pl.ds(0, cut)]
        late[part, lanes] = field[i + (1 - odd) * (rows - width), pl.ds(0, cut)]
        part = pl.ds(i * more, more)
        early_next[part, lanes] = field[i + odd * (rows - width), pl.ds(cut, more)]
        late_next[part, lanes] = field[i + (1 - odd) * (rows - width), pl.ds(cut, more)]
    near_edge = jnp.zeros((rows, cols), jnp.float32)
    far_edge = near_edge
    lane = lax.broadcasted_iota(jnp.int32, (rows, cols), 1)
    for k, part in enumerate((diffusion, drift_rows, drift_cols)):
        at = pl.ds(width * cut + k * width, width)
        top, bottom = part[:width], part[rows - width :]
        early[at, pl.ds(0, cols)] = jnp.where(odd == 0, top, bottom)
        late[at, pl.ds(0, cols)] = jnp.where(odd == 0, bottom, top)
        value = part[...]
        kept[k] = value
        mine = (lane >= k * width) & (lane < (k + 1) * width)
        if k:
            near_edge = jnp.where(mine, pltpu.roll(value, k * width, 1), near_edge)
        else:
            near_edge = jnp.where(mine, value, near_edge)
        far_edge = jnp.where(mine, pltpu.roll(value, (k + 1) * width, 1), far_edge)
    left[pl.ds(rows * width, rows), pl.ds(0, cols)] = near_edge
    right[pl.ds(rows * width, rows), pl.ds(0, cols)] = far_edge


def turn_kernel(axis, field, left, right, early, late):
    rows, cols, members = field.shape
    odd = parity(axis)
    width = STEPS
    area = width * width
    cut = parted(cols)[1]
    size = cols - cut
    lanes = pl.ds(0, members)
    for i in range(width):
        at = pl.ds(i * size, size)
        early[at, lanes] = field[i + odd * (rows - width), pl.ds(cut, size)]
        late[at, lanes] = field[i + (1 - odd) * (rows - width), pl.ds(cut, size)]
    base = width * size
    for i, side in enumerate((left, right)):
        at = pl.ds(base + i * area, area)
        top, bottom = side[pl.ds(0, area)], side[pl.ds((rows - width) * width, area)]
        early[at] = jnp.where(odd == 0, top, bottom)
        late[at] = jnp.where(odd == 0, bottom, top)
        at = pl.ds(base + 2 * area + i * width, width)
        top = side[pl.ds(rows * width, width)]
        bottom = side[pl.ds(rows * width + rows - width, width)]
        early[at] = jnp.where(odd == 0, top, bottom)
        late[at] = jnp.where(odd == 0, bottom, top)


def widen(write, line, columns, members):
    for at, parts in columns:
        size = parts[0].shape[0]
        diffusion, rowwise, colwise = (
            jnp.broadcast_to(p[:, line : line + 1], (size, members)) for p in parts
        )
        here = pl.ds(at, size)
        write(0, here, 1.0 - 4.0 * diffusion - rowwise - colwise)
        write(1, here, diffusion)
        write(2, here, diffusion + rowwise)
        write(3, here, diffusion + colwise)


def spread_rows(spread, lines, columns, members):
    for line, row in lines:

        def write(k, here, value, row=row):
            spread[k, row, here] = value

        widen(write, line, columns, members)


def march(rows, even, odd, spread, ranges, finals, store):
    width = STEPS
    source, target = even, odd
    for step in range(1, STEPS + 1):
        last = step == STEPS

        def advance(r, source=source, target=target, last=last):
            for at, size in finals if last else ranges:
                here = pl.ds(at, size)
                value = (
                    spread[0, r, here] * source[r, here]
                    + spread[1, r, here] * (source[r + 1, here] + source[r, pl.ds(at + 1, size)])
                    + spread[2, r, here] * source[r - 1, here]
                    + spread[3, r, here] * source[r, pl.ds(at - 1, size)]
                )
                if last:
                    store(r - width, at, value)
                else:
                    target[r, here] = value

        loop(rows + 2 * width - 2 * step, lambda i: advance(i + step))
        source, target = target, source


def coefficient_rows(odd, kept, early, late, stage, cut):
    rows, cols = kept.shape[1:]
    width = STEPS
    for k in range(3):
        at = pl.ds(width * cut + k * width, width), pl.ds(0, cols)
        stage[k, pl.ds(0, width)] = jnp.where(odd == 0, early[at], late[at])
        stage[k, pl.ds(width, width)] = jnp.where(odd == 0, late[at], early[at])
    lines = [(i, i) for i in range(1, width)]
    lines += [(width + i, width + rows + i) for i in range(width - 1)]
    inside = [(r, width + r) for r in range(rows)]
    return [kept[k].T for k in range(3)], inside, [stage[k].T for k in range(3)], lines


def middle_kernel(axis, low, high, pieces, field, kept, *refs):
    strips, (out, one, two, spread, stage) = refs[:-5], refs[-5:]
    rows, cols, members = field.shape
    width = STEPS
    lanes = pl.ds(0, members)
    odd = parity(axis)
    own, inside, beyond, lines = coefficient_rows(
        odd, kept, strips[0], strips[1], stage, parted(cols)[0]
    )
    start = pieces[0][3]
    end = pieces[-1][3] + pieces[-1][4]
    for parts, places in ((beyond, lines), (own, inside)):
        spread_rows(spread, places, [(LEAD + start, [p[start:end] for p in parts])], members)
    for pair, strip_cols, first, column, size in pieces:
        here = pl.ds(LEAD + column, size)
        for i in range(width):
            part = pl.ds(i * strip_cols + first, size)
            one[i + odd * (rows + width), here] = strips[2 * pair][part, lanes]
            one[i + (1 - odd) * (rows + width), here] = strips[2 * pair + 1][part, lanes]
    for r in range(rows):
        one[width + r, pl.ds(LEAD + start, end - start)] = field[r, pl.ds(start, end - start)]

    def store(r, at, value):
        out[r] = value

    march(
        rows,
        one,
        two,
        spread,
        [(LEAD + start, end - start)],
        [(LEAD + low, high - low)],
        store,
    )


def sides_kernel(
    axis,
    after,
    field,
    kept,
    early,
    late,
    early_next,
    late_next,
    left,
    right,
    early_rest,
    late_rest,
    out,
    one,
    two,
    spread,
    stage,
):
    rows, cols, members = field.shape
    odd = parity(axis)
    width = STEPS
    area = width * width
    cut, end = parted(cols)
    more = end - cut
    first, second, high = 2 * EDGE, end - 2 * EDGE, end - EDGE
    size = cols - end
    base = width * size
    lanes = pl.ds(0, members)
    own, inside, beyond, lines = coefficient_rows(odd, kept, early, late, stage, cut)
    for side in range(2):
        at = pl.ds(base + 2 * area + side * width, width), pl.ds(0, cols)
        stage[3 + side, pl.ds(0, width)] = jnp.where(odd == 0, early_rest[at], late_rest[at])
        stage[3 + side, pl.ds(width, width)] = jnp.where(odd == 0, late_rest[at], early_rest[at])
    edge = pl.ds(rows * width, rows), pl.ds(0, cols)
    for parts, near_part, far_part, places in (
        (beyond, stage[3].T, stage[4].T, lines),
        (own, left[edge].T, right[edge].T, inside),
    ):
        halo = [slice(k * width, (k + 1) * width) for k in range(3)]
        columns = [
            (LEAD - width, [near_part[h] for h in halo]),
            (LEAD, [p[:first] for p in parts]),
            (LEAD + second, [p[second:] for p in parts]),
            (LEAD + cols, [far_part[h] for h in halo]),
        ]
        spread_rows(spread, places, columns, members)
    before = pl.ds(LEAD - width, width)
    after = pl.ds(LEAD + cols, width)
    for i in range(width):
        for j, strip, following, rest in (
            (i + odd * (rows + width), early, early_next, early_rest),
            (i + (1 - odd) * (rows + width), late, late_next, late_rest),
        ):
            one[j, before] = rest[pl.ds(base + i * width, width), lanes]
            one[j, pl.ds(LEAD, first)] = strip[pl.ds(i * cut, first), lanes]
            one[j, pl.ds(LEAD + second, end - second)] = following[
                pl.ds(i * more + second - cut, end - second), lanes
            ]
            one[j, pl.ds(LEAD + end, size)] = rest[pl.ds(i * size, size), lanes]
            one[j, after] = rest[pl.ds(base + area + i * width, width), lanes]
    for r in range(rows):
        part = pl.ds(r * width, width)
        one[width + r, before] = left[part, lanes]
        one[width + r, pl.ds(LEAD, first)] = field[r, pl.ds(0, first)]
        one[width + r, pl.ds(LEAD + second, cols - second)] = field[
            r, pl.ds(second, cols - second)
        ]
        one[width + r, after] = right[part, lanes]

    def store(r, at, value):
        if at == LEAD:
            out[r, pl.ds(cols - high, EDGE)] = value
        else:
            out[r, pl.ds(0, cols - high)] = value

    march(
        rows,
        one,
        two,
        spread,
        [(LEAD + second, cols - second + 8), (LEAD - 8, first + 8)],
        [(LEAD + high, cols - high), (LEAD, EDGE)],
        store,
    )


def weight_kernel(axis, count, cells, values, weights, after, out):
    cols, twice = out.shape
    rows = twice // 2
    slots = cells.shape[1]
    full = cols * lax.axis_size(axis)
    cell = cells[...]
    if full & (full - 1):
        row_of = lax.div(cell, full)
    else:
        row_of = lax.shift_right_logical(cell, full.bit_length() - 1)
    col_of = cell - row_of * full - lax.axis_index(axis) * cols
    slot = lax.broadcasted_iota(jnp.int32, (1, slots), 1)
    plain = jnp.where(slot < count[0], weights[...], 0.0)
    valued = plain * values[...]
    here = lax.broadcasted_iota(jnp.int32, (cols, slots), 0) == col_of
    here = jnp.where(here, 1.0, 0.0).astype(jnp.bfloat16)
    line = lax.broadcasted_iota(jnp.int32, (rows, slots), 0) == row_of
    value = jnp.concatenate([jnp.where(line, plain, 0.0), jnp.where(line, valued, 0.0)], axis=0)
    total = jnp.zeros((cols, twice), jnp.float32)
    for _ in range(3):
        part = value.astype(jnp.bfloat16)
        value = value - part.astype(jnp.float32)
        total = total + dot(here, part, ((1,), (1,)))
    out[...] = total


def cell_weights(rows, pieces, weight, b, many):
    plain, valued = [], []
    for i in range(many):
        r = b * many + i
        for start, column, length in pieces:
            source = weight[pl.ds(column, length)]
            line = lax.broadcasted_iota(jnp.int32, source.shape, 1)
            plain.append(jnp.sum(jnp.where(line == r, source, 0.0), axis=1, keepdims=True))
            valued.append(jnp.sum(jnp.where(line == r + rows, source, 0.0), axis=1, keepdims=True))
    return jnp.concatenate(plain, axis=0), jnp.concatenate(valued, axis=0)


def lay_rows(pieces, column_of, size, centre, b, many):
    cols = centre.shape[1]
    for i in range(many):
        row = jnp.zeros((1, cols), jnp.float32)
        for start, column, length in pieces:
            place = lax.broadcasted_iota(jnp.int32, (length, cols), 0) + column
            here = place == lax.broadcasted_iota(jnp.int32, (length, cols), 1)
            part = column_of[i * size + start : i * size + start + length]
            row = row + jnp.sum(jnp.where(here, part, 0.0), axis=0, keepdims=True)
        centre[pl.ds(b * many + i, 1)] = row


def grouping(rows):
    return next(n for n in (8, 4, 2, 1) if rows % n == 0)


def cells_of(ref, b, many, start=0):
    value = ref[pl.ds(start + b * many, many)]
    return value.reshape(many * value.shape[1], value.shape[2])


def lane_mean(value):
    return jnp.sum(value, axis=1, keepdims=True) * (1.0 / value.shape[1])


def wide(parts):
    return jnp.concatenate(parts, axis=1)


def dot_wide(a, both, size):
    value = dot(a[0], both)
    return value[:, :size] + value[:, size:] + dot(a[1], both[:, :size])


def gram_kernel(groups, pieces, own, others, weight, upper, lower, centre, total, tilt):
    rows, size, _ = own.shape
    many = grouping(rows)
    depth = many * size

    def block(b):
        parts = [cells_of(own, b, many)]
        parts += [cells_of(others, b, many, g * rows) for g in range(groups - 1)]
        value = wide(parts) if groups > 1 else parts[0]
        mean = lane_mean(value)
        deviation = value - mean
        plain, valued = cell_weights(rows, pieces, weight, b, many)
        lay_rows(pieces, mean, size, centre, b, many)
        high, low = halves(deviation)
        at = pl.ds(b * depth, depth)
        upper[at] = high
        lower[at] = low
        turned = (deviation * plain).T
        total[...] += dot3(halves(turned), (high, low))
        tilt[...] += jnp.sum(deviation * (valued - plain * mean), axis=0, keepdims=True)

    loop(rows // many, block)


def own_gram_kernel(layout, first, second, sides, weight, total, left, right, spread):
    local = total.shape[0]
    total[...] = jnp.zeros_like(total)
    for pieces, own in zip(layout, (first, second, sides)):
        rows, size, _ = own.shape
        many = grouping(rows)
        depth = many * size

        def block(b, pieces=pieces, own=own, rows=rows, many=many, depth=depth):
            value = cells_of(own, b, many)
            mean = lane_mean(value)
            deviation = value - mean
            plain, valued = cell_weights(rows, pieces, weight, b, many)
            turned = halves((deviation * plain).T)
            total[...] += dot_wide(turned, wide(halves(deviation)), local)
            if own is sides:
                at = pl.ds(b * depth, depth)
                left[:, at], right[:, at] = turned
                for i, column in enumerate((plain, valued, mean)):
                    spread[i, at] = jnp.broadcast_to(column, (depth, local))

        loop(rows // many, block)


def tally(total, local, value, partner, plain, valued, mean_own):
    mean_partner = lane_mean(partner)
    counter = partner - mean_partner
    mean = 0.5 * (mean_own + mean_partner)
    apart = 0.5 * (mean_own - mean_partner)
    deviation = value - mean
    pull = valued - plain * mean
    tie = plain * apart

    def add(row, columns):
        total[pl.ds(local + row, 1)] += jnp.sum(columns, axis=0, keepdims=True)

    add(0, deviation * pull)
    add(1, (partner - mean) * pull)
    add(2, deviation * tie)
    add(3, (mean - partner) * tie)
    add(4, jnp.broadcast_to(tie * apart, deviation.shape))
    return counter


def part_deviations(pieces, value, partner, size, upper, lower, centre, b, many):
    value = wide([value, partner])
    mean = lane_mean(value)
    lay_rows(pieces, mean, size, centre, b, many)
    at = pl.ds(b * many * size, many * size)
    upper[at], lower[at] = halves(value - mean)


def part_cross_kernel(pieces, own, other, weight, after, *refs):
    before, (upper, lower, centre, total) = refs[:-4], refs[-4:]
    total[...] = before[0][...] if before else jnp.zeros_like(total)
    rows, size, local = own.shape
    many = grouping(rows)

    def block(b):
        value, partner = cells_of(own, b, many), cells_of(other, b, many)
        mean = lane_mean(value)
        plain, valued = cell_weights(rows, pieces, weight, b, many)
        counter = tally(total, local, value, partner, plain, valued, mean)
        part_deviations(pieces, value, partner, size, upper, lower, centre, b, many)
        turned = ((value - mean) * plain).T
        total[pl.ds(0, local)] += dot_wide(halves(turned), wide(halves(counter)), local)

    loop(rows // many, block)


def last_cross_kernel(own, other, left, right, spread, before, total):
    total[...] = before[...]
    rows, size, local = own.shape
    many = grouping(rows)
    depth = many * size

    def block(b):
        at = pl.ds(b * depth, depth)
        value, partner = cells_of(own, b, many), cells_of(other, b, many)
        counter = tally(total, local, value, partner, *(spread[i, at] for i in range(3)))
        total[pl.ds(0, local)] += dot_wide(
            (left[:, at], right[:, at]), wide(halves(counter)), local
        )

    loop(rows // many, block)


def deviation_kernel(pieces, own, other, after, upper, lower, centre):
    rows, size, _ = own.shape
    many = grouping(rows)

    def block(b):
        value, partner = cells_of(own, b, many), cells_of(other, b, many)
        part_deviations(pieces, value, partner, size, upper, lower, centre, b, many)

    loop(rows // many, block)


def part_gram_kernel(groups, pieces, own, others, weight, *refs):
    before, (upper, lower, centre, total, tilt) = refs[:-5], refs[-5:]
    total[...] = before[0][...] if before else jnp.zeros_like(total)
    tilt[...] = before[1][...] if before else jnp.zeros_like(tilt)
    gram_kernel(groups, pieces, own, others, weight, upper, lower, centre, total, tilt)


def last_gram_kernel(
    groups, pieces, own, others, weight, before, tilted, gram, upper, lower, centre, total, tilt
):
    total[...] = before[...]
    tilt[...] = tilted[...]
    gram_kernel(groups, pieces, own, others, weight, upper, lower, centre, total, tilt)
    pull = gram.shape[0] - 8
    blocks = total.shape[0] // 128
    innovation = tilt[...]
    at = 0
    gram[pl.ds(pull, 8)] = jnp.zeros((8, 128), jnp.float32)
    for i in range(blocks):
        gram[pl.ds(pull + i, 1)] = innovation[:, i * 128 : (i + 1) * 128]
        for j in range(i, blocks):
            gram[pl.ds(at, 128)] = total[i * 128 : (i + 1) * 128, j * 128 : (j + 1) * 128]
            at += 128


def assemble(first, second, whole):
    blocks = whole.shape[0] // 128
    pull = first.shape[0] - 8
    at = 0
    for i in range(blocks):
        for j in range(i, blocks):
            block = first[pl.ds(at, 128)] + second[pl.ds(at, 128)]
            whole[i * 128 : (i + 1) * 128, j * 128 : (j + 1) * 128] = block
            if j > i:
                whole[j * 128 : (j + 1) * 128, i * 128 : (i + 1) * 128] = block.T
            at += 128
    return wide([first[pl.ds(pull + i, 1)] + second[pl.ds(pull + i, 1)] for i in range(blocks)])


def assemble_pair(first, second, own, other, whole):
    local = own.shape[1]
    cross = first[pl.ds(0, local)] + second[pl.ds(0, local)]
    rest = first[pl.ds(local, 8)] + second[pl.ds(local, 8)]
    square = rest[4:5]
    diagonal = lax.broadcasted_iota(jnp.int32, (local, local), 0) == lax.broadcasted_iota(
        jnp.int32, (local, local), 1
    )
    uprights = []
    for i, part in enumerate((own, other)):
        tie = rest[2 + i : 3 + i]
        upright = jnp.sum(jnp.where(diagonal, tie, 0.0), axis=1, keepdims=True)
        uprights.append(upright)
        at = slice(i * local, (i + 1) * local)
        whole[at, at] = part[...] + upright + (tie - square)
    cross = cross - uprights[0] + (square - rest[3:4])
    whole[:local, local:] = cross
    whole[local:, :local] = cross.T
    return wide([rest[0:1], rest[1:2]])


def analysis_kernel(layout, pair, *rest):
    if pair:
        first, second, own, other, *rest = rest
    else:
        first, second, *rest = rest
    count = len(layout)
    uppers, lowers, centres = (rest[i * count : (i + 1) * count] for i in range(3))
    out, whole, chosen, natural = rest[3 * count :]
    rows, _ = centres[0].shape
    local = natural.shape[2]
    members = whole.shape[0]
    if pair:
        innovation = assemble_pair(first, second, own, other, whole)
    else:
        innovation = assemble(first, second, whole)
    down = lax.broadcasted_iota(jnp.int32, (members, members), 0)
    across = lax.broadcasted_iota(jnp.int32, (members, members), 1)
    identity = jnp.where(down == across, 1.0, 0.0)
    matrix = whole[...] + (members - 1.0) * identity
    parts = halves(matrix)
    square = dot3(parts, parts)
    squares = jnp.sum(jnp.sum(matrix * matrix, axis=1, keepdims=True), axis=0, keepdims=True)
    scaling = jnp.sqrt(squares)
    current = matrix * (1.0 / scaling)
    square = square * (1.0 / scaling) * (1.0 / scaling)
    inverse = None
    for repeat in range(0, ITERS, 2):
        if repeat:
            parts = halves(current)
            square = dot3(parts, parts)
        inner = 0.0625 * square - 0.5625 * current
        outer = 2.25 * identity - 2.4375 * current + 1.6875 * square
        both = outer + dot3(halves(square), halves(inner))
        both_parts = halves(both)
        if repeat + 2 < ITERS:
            twice = dot3(both_parts, both_parts)
            current = dot3(halves(current), halves(twice))
        inverse = both if inverse is None else dot3(halves(inverse), both_parts)
    once = jnp.sum(inverse * innovation, axis=1, keepdims=True)
    once_row = jnp.sum(jnp.where(down == across, once, 0.0), axis=0, keepdims=True)
    shifted = jnp.sum(inverse * once_row, axis=1, keepdims=True) * (1.0 / scaling)
    factor = jnp.sqrt((members - 1.0) / scaling)
    mixing = (factor * inverse + shifted)[:, :local]
    high, low = halves(mixing)
    chosen[:, :local] = high
    chosen[:, local:] = low
    many = grouping(rows)

    def block(b):
        for pieces, upper, lower in zip(layout, uppers, lowers):
            size = upper.shape[0] // rows
            at = pl.ds(b * many * size, many * size)
            value = dot(upper[at], chosen[...])
            value = value[:, :local] + value[:, local:] + dot(lower[at], chosen[:, :local])
            for i in range(many):
                for start, column, length in pieces:
                    natural[i, pl.ds(column, length)] = value[
                        i * size + start : i * size + start + length
                    ]
        for i in range(many):
            r = b * many + i
            middle_row = sum(c[pl.ds(r, 1)] for c in centres)
            out[pl.ds(r, local, stride=rows)] = natural[i].T + middle_row

    loop(rows // many, block)


def shift(value, axes, *moves):
    sizes = [lax.axis_size(a) for a in axes]
    pairs = []
    total = 1
    for s in sizes:
        total *= s
    for flat in range(total):
        rest, place = flat, []
        for s in reversed(sizes):
            place.append(rest % s)
            rest //= s
        place = place[::-1]
        to = 0
        for s, p, m in zip(sizes, place, moves):
            to = to * s + (p + m) % s
        pairs.append((flat, to))
    return lax.ppermute(value, axes if len(axes) > 1 else axes[0], pairs)


def trade(value, axis, first):
    size = lax.axis_size(axis)
    if size % 2:
        raise ValueError("odd ring")
    start = 1 if first else 0
    pairs = [(i % size, (i + 1) % size) for i in range(start, size, 2)]
    return lax.ppermute(value, axis, pairs + [(j, i) for i, j in pairs])


def role_sums(value):
    size = lax.axis_size("role")
    if size & (size - 1) or size == 1:
        return [(lax.psum(value, "role"), jnp.zeros_like(value))]
    stages = []
    step = 1
    while step < size:
        other = lax.ppermute(value, "role", [(i, i ^ step) for i in range(size)])
        stages.append((value, other))
        value = value + other
        step *= 2
    return stages


def shards(
    ensemble,
    diffusion,
    drift_rows,
    drift_cols,
    observed_cells,
    observed_count,
    observed_values,
    observed_weights,
):
    groups = lax.axis_size("member")
    local, rows, cols = ensemble.shape
    members = local * groups
    width = STEPS
    lanes = max(local, cols)
    cut, end = parted(cols)
    strip = struct(width * cut + 4 * width, lanes)
    following = struct(width * (end - cut), lanes)
    rest = struct(width * (cols - end) + 2 * width * width + 2 * width, lanes)
    edge = struct(rows * width + rows, lanes)
    field, kept, early, late, early_next, late_next, left, right = call(
        functools.partial(pack_kernel, "domain"),
        (
            struct(rows, cols, local),
            struct(3, rows, cols),
            strip,
            strip,
            following,
            following,
            edge,
            edge,
        ),
        ensemble.reshape(local * rows, cols),
        diffusion,
        drift_rows,
        drift_cols,
        raw=4,
    )
    early = trade(early, "domain", True)
    late = trade(late, "domain", False)
    early_next = trade(early_next, "domain", True)
    late_next = trade(late_next, "domain", False)
    received = shift(right, ("role",), 1)
    right = shift(left, ("role",), -1)
    left = received
    early_rest, late_rest = call(
        functools.partial(turn_kernel, "domain"), (rest, rest), field, left, right
    )
    early_rest = trade(early_rest, "domain", True)
    late_rest = trade(late_rest, "domain", False)
    padded = pltpu.VMEM((rows + 2 * width, cols + 2 * LEAD, local), jnp.float32)
    scratch = (
        padded,
        padded,
        pltpu.VMEM((4, rows + 2 * width, cols + 2 * LEAD, local), jnp.float32),
        pltpu.VMEM((5, 2 * width, cols), jnp.float32),
    )
    ends = (EDGE, cut - EDGE, end - EDGE)

    def forecast(low, high, pieces, *strips):
        return call(
            functools.partial(middle_kernel, "domain", low, high, pieces),
            struct(rows, high - low, local),
            field,
            kept,
            *strips,
            scratch=scratch,
        )

    first = forecast(*ends[:2], ((0, cut, 0, 0, cut),), early, late)
    back = 2 * EDGE
    pieces = (
        (0, cut, cut - back, cut - back, back),
        (1, end - cut, 0, cut, end - cut),
    )
    second = forecast(*ends[1:], pieces, early, late, early_next, late_next, first)
    limit = jnp.minimum(observed_count, observed_cells.shape[1])
    weight = call(
        functools.partial(weight_kernel, "role"),
        struct(cols, 2 * rows),
        limit,
        observed_cells,
        observed_values,
        observed_weights,
        second,
        scalars=1,
    )
    sides = call(
        functools.partial(sides_kernel, "domain"),
        struct(rows, cols - end + 2 * EDGE, local),
        weight,
        field,
        kept,
        early,
        late,
        early_next,
        late_next,
        left,
        right,
        early_rest,
        late_rest,
        scratch=scratch,
    )

    def gathered(value):
        others = [shift(value, ("member",), s) for s in range(1, groups)]
        return jnp.concatenate(others, axis=0) if len(others) > 1 else others[0]

    owns = (first, second, sides)
    theirs = []
    for value in owns:
        theirs.append(gathered(value))
    tail = cols - end + EDGE
    layout = (
        ((0, ends[0], ends[1] - ends[0]),),
        ((0, ends[1], ends[2] - ends[1]),),
        ((0, ends[2], tail), (tail, 0, EDGE)),
    )

    def deviations(value):
        one = struct(rows * value.shape[1], members, kind=jnp.bfloat16)
        return one, one, struct(rows, cols)

    made = []
    pair = groups == 2 and local % 128 == 0
    if pair:
        sided = rows * sides.shape[1]
        half = struct(local, sided, kind=jnp.bfloat16)
        alone, left_half, right_half, spread = call(
            functools.partial(own_gram_kernel, layout),
            (struct(local, local), half, half, struct(3, sided, local)),
            *owns,
            weight,
        )
        stages = role_sums(alone)
        started = sum(stages[0])
        cross = struct(local + 8, local)
        total = ()
        for i in range(2):
            *three, total = call(
                functools.partial(part_cross_kernel, layout[i]),
                (*deviations(owns[i]), cross),
                owns[i],
                theirs[i],
                weight,
                started,
                *total,
            )
            made.append(three)
            total = (total,)
        alone, arriving = stages[-1]
        total, alone = lax.optimization_barrier((total[0], alone))
        alone = alone + arriving
        gram = call(
            last_cross_kernel, cross, sides, theirs[-1], left_half, right_half, spread, total
        )
        facing = shift(alone, ("member",), 1)
        grams = (*role_sums(gram)[-1], alone, facing)
        three = call(
            functools.partial(deviation_kernel, layout[-1]),
            deviations(sides),
            sides,
            theirs[-1],
            gram,
        )
        made.append(three)
    else:
        blocks = members // 128
        size = blocks * (blocks + 1) // 2 * 128 + 8
        sums = struct(members, members), struct(1, members)
        totals = ()
        for i in range(2):
            *three, total, tilt = call(
                functools.partial(part_gram_kernel, groups, layout[i]),
                (*deviations(owns[i]), *sums),
                owns[i],
                theirs[i],
                weight,
                *totals,
            )
            made.append(three)
            totals = total, tilt
        gram, *three = call(
            functools.partial(last_gram_kernel, groups, layout[-1]),
            (struct(size, 128), *deviations(sides)),
            sides,
            theirs[-1],
            weight,
            *totals,
            scratch=tuple(pltpu.VMEM(v.shape, v.dtype) for v in sums),
        )
        made.append(three)
        grams = role_sums(gram)[-1]
    return call(
        functools.partial(analysis_kernel, layout, pair),
        struct(local * rows, cols),
        *grams,
        *(three[k] for k in range(3) for three in made),
        scratch=(
            pltpu.VMEM((members, members), jnp.float32),
            pltpu.VMEM((members, 2 * local), jnp.bfloat16),
            pltpu.VMEM((grouping(rows), cols, local), jnp.float32),
        ),
        result=True,
    ).reshape(local, rows, cols)


def solution(mesh):
    placed = (
        P("member", "domain", "role"),
        P("domain", "role"),
        P("domain", "role"),
        P("domain", "role"),
        P("domain", None),
        P("domain"),
        P("domain", None),
        P("domain", None),
    )
    return jax.shard_map(
        shards, mesh=mesh, in_specs=placed, out_specs=P("member", "domain", "role"), check_vma=False
    )
```

```python
import functools

import jax
import jax.numpy as jnp
from jax import lax
from jax.experimental import pallas as pl
from jax.experimental.pallas import tpu as pltpu
from jax.sharding import PartitionSpec as P


STEPS = 4
ITERS = 6
LEAD = 16


VMEM = pl.BlockSpec(memory_space=pltpu.VMEM)
SMEM = pl.BlockSpec(memory_space=pltpu.SMEM)
ROOM = 1 << 20


def struct(*shape, kind=jnp.float32):
    return jax.ShapeDtypeStruct(shape, kind)


def near(shape, kind):
    size = jnp.dtype(kind).itemsize
    for place, extent in enumerate(shape[::-1]):
        unit = (128, 32 // jnp.dtype(kind).itemsize, 1)[min(place, 2)]
        size *= -(-extent // unit) * unit
    return size <= ROOM


def call(body, outs, *args, scratch=(), scalars=0, raw=0, result=False):
    placed = list(args[: scalars + raw])
    for value in args[scalars + raw :]:
        if near(value.shape, value.dtype):
            value = pltpu.with_memory_space_constraint(value, pltpu.VMEM)
        placed.append(value)
    if not result:
        outs = jax.tree.map(
            lambda s: pltpu.VMEM(s.shape, s.dtype) if near(s.shape, s.dtype) else s, outs
        )
    return pl.pallas_call(
        body,
        out_shape=outs,
        in_specs=[SMEM] * scalars + [VMEM] * (len(args) - scalars),
        out_specs=tuple(VMEM for _ in outs) if isinstance(outs, tuple) else VMEM,
        scratch_shapes=scratch,
    )(*placed)


def halves(value):
    upper = value.astype(jnp.bfloat16)
    lower = (value - upper.astype(jnp.float32)).astype(jnp.bfloat16)
    return upper, lower


def dot(a, b, dims=((1,), (0,))):
    return lax.dot_general(a, b, (dims, ((), ())), preferred_element_type=jnp.float32)


def by_halves(product, *operands):
    half = operands[0].shape[0] // 2
    parts = [product(*(o[at] for o in operands)) for at in (slice(0, half), slice(half, None))]
    return jnp.concatenate(parts, axis=0)


def dot3(a, b):
    return by_halves(
        lambda high, low: (dot(high, b[0]) + dot(low, b[0])) + dot(high, b[1]), *a
    )


def loop(count, body):
    if count <= 16:
        for i in range(count):
            body(i)
    else:
        lax.fori_loop(0, count, lambda i, c: (body(i), c)[1], 0)


EDGE = 8


def parted(cols):
    return cols * 3 // 8 // 8 * 8, cols * 3 // 4 // 8 * 8


def parity(axis):
    return lax.rem(lax.axis_index(axis), 2)


def pack_kernel(
    axis,
    ens,
    diffusion,
    drift_rows,
    drift_cols,
    field,
    kept,
    early,
    late,
    early_next,
    late_next,
    left,
    right,
):
    odd = parity(axis)
    rows, cols, members = field.shape
    width = STEPS
    cut, end = parted(cols)
    more = end - cut
    lanes = pl.ds(0, members)
    for r in range(rows):
        turned = ens[pl.ds(r, members, stride=rows)].T
        field[r] = turned
        part = pl.ds(r * width, width)
        left[part, lanes] = turned[:width]
        right[part, lanes] = turned[cols - width :]
    for i in range(width):
        part = pl.ds(i * cut, cut)
        early[part, lanes] = field[i + odd * (rows - width), pl.ds(0, cut)]
        late[part, lanes] = field[i + (1 - odd) * (rows - width), pl.ds(0, cut)]
        part = pl.ds(i * more, more)
        early_next[part, lanes] = field[i + odd * (rows - width), pl.ds(cut, more)]
        late_next[part, lanes] = field[i + (1 - odd) * (rows - width), pl.ds(cut, more)]
    near_edge = jnp.zeros((rows, cols), jnp.float32)
    far_edge = near_edge
    lane = lax.broadcasted_iota(jnp.int32, (rows, cols), 1)
    for k, part in enumerate((diffusion, drift_rows, drift_cols)):
        at = pl.ds(width * cut + k * width, width)
        top, bottom = part[:width], part[rows - width :]
        early[at, pl.ds(0, cols)] = jnp.where(odd == 0, top, bottom)
        late[at, pl.ds(0, cols)] = jnp.where(odd == 0, bottom, top)
        value = part[...]
        kept[k] = value
        mine = (lane >= k * width) & (lane < (k + 1) * width)
        if k:
            near_edge = jnp.where(mine, pltpu.roll(value, k * width, 1), near_edge)
        else:
            near_edge = jnp.where(mine, value, near_edge)
        far_edge = jnp.where(mine, pltpu.roll(value, (k + 1) * width, 1), far_edge)
    left[pl.ds(rows * width, rows), pl.ds(0, cols)] = near_edge
    right[pl.ds(rows * width, rows), pl.ds(0, cols)] = far_edge


def turn_kernel(axis, field, left, right, after, early, late):
    rows, cols, members = field.shape
    odd = parity(axis)
    width = STEPS
    area = width * width
    cut = parted(cols)[1]
    size = cols - cut
    lanes = pl.ds(0, members)
    for i in range(width):
        at = pl.ds(i * size, size)
        early[at, lanes] = field[i + odd * (rows - width), pl.ds(cut, size)]
        late[at, lanes] = field[i + (1 - odd) * (rows - width), pl.ds(cut, size)]
    base = width * size
    for i, side in enumerate((left, right)):
        at = pl.ds(base + i * area, area)
        top, bottom = side[pl.ds(0, area)], side[pl.ds((rows - width) * width, area)]
        early[at] = jnp.where(odd == 0, top, bottom)
        late[at] = jnp.where(odd == 0, bottom, top)
        at = pl.ds(base + 2 * area + i * width, width)
        top = side[pl.ds(rows * width, width)]
        bottom = side[pl.ds(rows * width + rows - width, width)]
        early[at] = jnp.where(odd == 0, top, bottom)
        late[at] = jnp.where(odd == 0, bottom, top)


def widen(write, line, columns, members):
    for at, parts in columns:
        size = parts[0].shape[0]
        diffusion, rowwise, colwise = (
            jnp.broadcast_to(p[:, line : line + 1], (size, members)) for p in parts
        )
        here = pl.ds(at, size)
        write(0, here, 1.0 - 4.0 * diffusion - rowwise - colwise)
        write(1, here, diffusion)
        write(2, here, diffusion + rowwise)
        write(3, here, diffusion + colwise)


def spread_rows(spread, lines, columns, members):
    for line, row in lines:

        def write(k, here, value, row=row):
            spread[k, row, here] = value

        widen(write, line, columns, members)


def march(rows, even, odd, spread, ranges, finals, store):
    width = STEPS
    source, target = even, odd
    for step in range(1, STEPS + 1):
        last = step == STEPS

        def advance(r, source=source, target=target, last=last):
            for at, size in finals if last else ranges:
                here = pl.ds(at, size)
                value = (
                    spread[0, r, here] * source[r, here]
                    + spread[1, r, here] * (source[r + 1, here] + source[r, pl.ds(at + 1, size)])
                    + spread[2, r, here] * source[r - 1, here]
                    + spread[3, r, here] * source[r, pl.ds(at - 1, size)]
                )
                if last:
                    store(r - width, at, value)
                else:
                    target[r, here] = value

        loop(rows + 2 * width - 2 * step, lambda i: advance(i + step))
        source, target = target, source


def coefficient_rows(odd, kept, early, late, stage, cut):
    rows, cols = kept.shape[1:]
    width = STEPS
    for k in range(3):
        at = pl.ds(width * cut + k * width, width), pl.ds(0, cols)
        stage[k, pl.ds(0, width)] = jnp.where(odd == 0, early[at], late[at])
        stage[k, pl.ds(width, width)] = jnp.where(odd == 0, late[at], early[at])
    lines = [(i, i) for i in range(1, width)]
    lines += [(width + i, width + rows + i) for i in range(width - 1)]
    inside = [(r, width + r) for r in range(rows)]
    return [kept[k].T for k in range(3)], inside, [stage[k].T for k in range(3)], lines


def middle_kernel(axis, low, high, pieces, after, field, kept, *refs):
    strips, (out, one, two, spread, stage) = refs[:-5], refs[-5:]
    rows, cols, members = field.shape
    width = STEPS
    lanes = pl.ds(0, members)
    odd = parity(axis)
    own, inside, beyond, lines = coefficient_rows(
        odd, kept, strips[0], strips[1], stage, parted(cols)[0]
    )
    start = pieces[0][3]
    end = pieces[-1][3] + pieces[-1][4]
    for parts, places in ((beyond, lines), (own, inside)):
        spread_rows(spread, places, [(LEAD + start, [p[start:end] for p in parts])], members)
    for pair, strip_cols, first, column, size in pieces:
        here = pl.ds(LEAD + column, size)
        for i in range(width):
            part = pl.ds(i * strip_cols + first, size)
            one[i + odd * (rows + width), here] = strips[2 * pair][part, lanes]
            one[i + (1 - odd) * (rows + width), here] = strips[2 * pair + 1][part, lanes]
    for r in range(rows):
        one[width + r, pl.ds(LEAD + start, end - start)] = field[r, pl.ds(start, end - start)]

    def store(r, at, value):
        out[r] = value

    march(
        rows,
        one,
        two,
        spread,
        [(LEAD + start, end - start)],
        [(LEAD + low, high - low)],
        store,
    )


def sides_kernel(
    axis,
    after,
    field,
    kept,
    early,
    late,
    early_next,
    late_next,
    left,
    right,
    early_rest,
    late_rest,
    out,
    one,
    two,
    spread,
    stage,
):
    rows, cols, members = field.shape
    odd = parity(axis)
    width = STEPS
    area = width * width
    cut, end = parted(cols)
    more = end - cut
    first, second, high = 2 * EDGE, end - 2 * EDGE, end - EDGE
    size = cols - end
    base = width * size
    lanes = pl.ds(0, members)
    own, inside, beyond, lines = coefficient_rows(odd, kept, early, late, stage, cut)
    for side in range(2):
        at = pl.ds(base + 2 * area + side * width, width), pl.ds(0, cols)
        stage[3 + side, pl.ds(0, width)] = jnp.where(odd == 0, early_rest[at], late_rest[at])
        stage[3 + side, pl.ds(width, width)] = jnp.where(odd == 0, late_rest[at], early_rest[at])
    edge = pl.ds(rows * width, rows), pl.ds(0, cols)
    for parts, near_part, far_part, places in (
        (beyond, stage[3].T, stage[4].T, lines),
        (own, left[edge].T, right[edge].T, inside),
    ):
        halo = [slice(k * width, (k + 1) * width) for k in range(3)]
        columns = [
            (LEAD - width, [near_part[h] for h in halo]),
            (LEAD, [p[:first] for p in parts]),
            (LEAD + second, [p[second:] for p in parts]),
            (LEAD + cols, [far_part[h] for h in halo]),
        ]
        spread_rows(spread, places, columns, members)
    before = pl.ds(LEAD - width, width)
    after = pl.ds(LEAD + cols, width)
    for i in range(width):
        for j, strip, following, rest in (
            (i + odd * (rows + width), early, early_next, early_rest),
            (i + (1 - odd) * (rows + width), late, late_next, late_rest),
        ):
            one[j, before] = rest[pl.ds(base + i * width, width), lanes]
            one[j, pl.ds(LEAD, first)] = strip[pl.ds(i * cut, first), lanes]
            one[j, pl.ds(LEAD + second, end - second)] = following[
                pl.ds(i * more + second - cut, end - second), lanes
            ]
            one[j, pl.ds(LEAD + end, size)] = rest[pl.ds(i * size, size), lanes]
            one[j, after] = rest[pl.ds(base + area + i * width, width), lanes]
    for r in range(rows):
        part = pl.ds(r * width, width)
        one[width + r, before] = left[part, lanes]
        one[width + r, pl.ds(LEAD, first)] = field[r, pl.ds(0, first)]
        one[width + r, pl.ds(LEAD + second, cols - second)] = field[
            r, pl.ds(second, cols - second)
        ]
        one[width + r, after] = right[part, lanes]

    def store(r, at, value):
        if at == LEAD:
            out[r, pl.ds(cols - high, EDGE)] = value
        else:
            out[r, pl.ds(0, cols - high)] = value

    march(
        rows,
        one,
        two,
        spread,
        [(LEAD + second, cols - second + 8), (LEAD - 8, first + 8)],
        [(LEAD + high, cols - high), (LEAD, EDGE)],
        store,
    )


def weight_kernel(axis, count, cells, values, weights, out):
    cols, twice = out.shape
    rows = twice // 2
    slots = cells.shape[1]
    full = cols * lax.axis_size(axis)
    cell = cells[...]
    if full & (full - 1):
        row_of = lax.div(cell, full)
    else:
        row_of = lax.shift_right_logical(cell, full.bit_length() - 1)
    col_of = cell - row_of * full - lax.axis_index(axis) * cols
    slot = lax.broadcasted_iota(jnp.int32, (1, slots), 1)
    plain = jnp.where(slot < count[0], weights[...], 0.0)
    valued = plain * values[...]
    here = lax.broadcasted_iota(jnp.int32, (cols, slots), 0) == col_of
    here = jnp.where(here, 1.0, 0.0).astype(jnp.bfloat16)
    line = lax.broadcasted_iota(jnp.int32, (rows, slots), 0) == row_of
    value = jnp.concatenate([jnp.where(line, plain, 0.0), jnp.where(line, valued, 0.0)], axis=0)
    total = jnp.zeros((cols, twice), jnp.float32)
    for _ in range(3):
        part = value.astype(jnp.bfloat16)
        value = value - part.astype(jnp.float32)
        total = total + dot(here, part, ((1,), (1,)))
    out[...] = total


def cell_weights(rows, pieces, weight, b, many):
    plain, valued = [], []
    for i in range(many):
        r = b * many + i
        for start, column, length in pieces:
            source = weight[pl.ds(column, length)]
            line = lax.broadcasted_iota(jnp.int32, source.shape, 1)
            plain.append(jnp.sum(jnp.where(line == r, source, 0.0), axis=1, keepdims=True))
            valued.append(jnp.sum(jnp.where(line == r + rows, source, 0.0), axis=1, keepdims=True))
    return jnp.concatenate(plain, axis=0), jnp.concatenate(valued, axis=0)


def lay_rows(pieces, column_of, size, centre, b, many):
    cols = centre.shape[1]
    for i in range(many):
        row = jnp.zeros((1, cols), jnp.float32)
        for start, column, length in pieces:
            place = lax.broadcasted_iota(jnp.int32, (length, cols), 0) + column
            here = place == lax.broadcasted_iota(jnp.int32, (length, cols), 1)
            part = column_of[i * size + start : i * size + start + length]
            row = row + jnp.sum(jnp.where(here, part, 0.0), axis=0, keepdims=True)
        centre[pl.ds(b * many + i, 1)] = row


def grouping(rows):
    return next(n for n in (8, 4, 2, 1) if rows % n == 0)


def cells_of(ref, b, many, start=0):
    value = ref[pl.ds(start + b * many, many)]
    return value.reshape(many * value.shape[1], value.shape[2])


def lane_mean(value):
    return jnp.sum(value, axis=1, keepdims=True) * (1.0 / value.shape[1])


def wide(parts):
    return jnp.concatenate(parts, axis=1)


def dot_wide(a, both, size):
    value = dot(a[0], both)
    return value[:, :size] + value[:, size:] + dot(a[1], both[:, :size])


def gram_kernel(groups, pieces, own, others, weight, upper, lower, centre, total, tilt):
    rows, size, _ = own.shape
    many = grouping(rows)
    depth = many * size

    def block(b):
        parts = [cells_of(own, b, many)]
        parts += [cells_of(others, b, many, g * rows) for g in range(groups - 1)]
        value = wide(parts) if groups > 1 else parts[0]
        mean = lane_mean(value)
        deviation = value - mean
        plain, valued = cell_weights(rows, pieces, weight, b, many)
        lay_rows(pieces, mean, size, centre, b, many)
        high, low = halves(deviation)
        at = pl.ds(b * depth, depth)
        upper[at] = high
        lower[at] = low
        turned = (deviation * plain).T
        total[...] += dot3(halves(turned), (high, low))
        tilt[...] += jnp.sum(deviation * (valued - plain * mean), axis=0, keepdims=True)

    loop(rows // many, block)


def own_gram_kernel(layout, first, second, sides, weight, total):
    local = total.shape[0]
    total[...] = jnp.zeros_like(total)
    for pieces, own in zip(layout, (first, second, sides)):
        rows, size, _ = own.shape
        many = grouping(rows)
        depth = many * size

        def block(b, pieces=pieces, own=own, rows=rows, many=many, depth=depth):
            value = cells_of(own, b, many)
            mean = lane_mean(value)
            deviation = value - mean
            plain, _ = cell_weights(rows, pieces, weight, b, many)
            turned = halves((deviation * plain).T)
            total[...] += dot_wide(turned, wide(halves(deviation)), local)

        loop(rows // many, block)


def prepare_kernel(pieces, own, weight, after, left, right, spread):
    rows, size, local = own.shape
    many = grouping(rows)
    depth = many * size

    def block(b):
        value = cells_of(own, b, many)
        mean = lane_mean(value)
        plain, valued = cell_weights(rows, pieces, weight, b, many)
        at = pl.ds(b * depth, depth)
        left[:, at], right[:, at] = halves(((value - mean) * plain).T)
        for i, column in enumerate((plain, valued, mean)):
            spread[i, at] = jnp.broadcast_to(column, (depth, local))

    loop(rows // many, block)


def tally(total, local, value, partner, plain, valued, mean_own):
    mean_partner = lane_mean(partner)
    counter = partner - mean_partner
    mean = 0.5 * (mean_own + mean_partner)
    apart = 0.5 * (mean_own - mean_partner)
    deviation = value - mean
    pull = valued - plain * mean
    tie = plain * apart

    def add(row, columns):
        total[pl.ds(local + row, 1)] += jnp.sum(columns, axis=0, keepdims=True)

    add(0, deviation * pull)
    add(1, (partner - mean) * pull)
    add(2, deviation * tie)
    add(3, (mean - partner) * tie)
    add(4, jnp.broadcast_to(tie * apart, deviation.shape))
    return counter


def part_deviations(pieces, value, partner, size, upper, lower, centre, b, many):
    value = wide([value, partner])
    mean = lane_mean(value)
    lay_rows(pieces, mean, size, centre, b, many)
    at = pl.ds(b * many * size, many * size)
    upper[at], lower[at] = halves(value - mean)


def part_cross_kernel(pieces, own, other, weight, after, *refs):
    before, (upper, lower, centre, total) = refs[:-4], refs[-4:]
    total[...] = before[0][...] if before else jnp.zeros_like(total)
    rows, size, local = own.shape
    many = grouping(rows)

    def block(b):
        value, partner = cells_of(own, b, many), cells_of(other, b, many)
        mean = lane_mean(value)
        plain, valued = cell_weights(rows, pieces, weight, b, many)
        counter = tally(total, local, value, partner, plain, valued, mean)
        part_deviations(pieces, value, partner, size, upper, lower, centre, b, many)
        turned = ((value - mean) * plain).T
        total[pl.ds(0, local)] += dot_wide(halves(turned), wide(halves(counter)), local)

    loop(rows // many, block)


def last_cross_kernel(own, other, left, right, spread, before, total):
    total[...] = before[...]
    rows, size, local = own.shape
    many = grouping(rows)
    depth = many * size

    def block(b):
        at = pl.ds(b * depth, depth)
        value, partner = cells_of(own, b, many), cells_of(other, b, many)
        counter = tally(total, local, value, partner, *(spread[i, at] for i in range(3)))
        total[pl.ds(0, local)] += dot_wide(
            (left[:, at], right[:, at]), wide(halves(counter)), local
        )

    loop(rows // many, block)


def deviation_kernel(pieces, own, other, after, upper, lower, centre):
    rows, size, _ = own.shape
    many = grouping(rows)

    def block(b):
        value, partner = cells_of(own, b, many), cells_of(other, b, many)
        part_deviations(pieces, value, partner, size, upper, lower, centre, b, many)

    loop(rows // many, block)


def part_gram_kernel(groups, pieces, own, others, weight, *refs):
    before, (upper, lower, centre, total, tilt) = refs[:-5], refs[-5:]
    total[...] = before[0][...] if before else jnp.zeros_like(total)
    tilt[...] = before[1][...] if before else jnp.zeros_like(tilt)
    gram_kernel(groups, pieces, own, others, weight, upper, lower, centre, total, tilt)


def last_gram_kernel(
    groups, pieces, own, others, weight, before, tilted, gram, upper, lower, centre, total, tilt
):
    total[...] = before[...]
    tilt[...] = tilted[...]
    gram_kernel(groups, pieces, own, others, weight, upper, lower, centre, total, tilt)
    pull = gram.shape[0] - 8
    blocks = total.shape[0] // 128
    innovation = tilt[...]
    at = 0
    gram[pl.ds(pull, 8)] = jnp.zeros((8, 128), jnp.float32)
    for i in range(blocks):
        gram[pl.ds(pull + i, 1)] = innovation[:, i * 128 : (i + 1) * 128]
        for j in range(i, blocks):
            gram[pl.ds(at, 128)] = total[i * 128 : (i + 1) * 128, j * 128 : (j + 1) * 128]
            at += 128


def assemble(first, second, whole):
    blocks = whole.shape[0] // 128
    pull = first.shape[0] - 8
    at = 0
    for i in range(blocks):
        for j in range(i, blocks):
            block = first[pl.ds(at, 128)] + second[pl.ds(at, 128)]
            whole[i * 128 : (i + 1) * 128, j * 128 : (j + 1) * 128] = block
            if j > i:
                whole[j * 128 : (j + 1) * 128, i * 128 : (i + 1) * 128] = block.T
            at += 128
    return wide([first[pl.ds(pull + i, 1)] + second[pl.ds(pull + i, 1)] for i in range(blocks)])


def assemble_pair(first, second, own, other, whole):
    local = own.shape[1]
    cross = first[pl.ds(0, local)] + second[pl.ds(0, local)]
    rest = first[pl.ds(local, 8)] + second[pl.ds(local, 8)]
    square = rest[4:5]
    diagonal = lax.broadcasted_iota(jnp.int32, (local, local), 0) == lax.broadcasted_iota(
        jnp.int32, (local, local), 1
    )
    uprights = []
    for i, part in enumerate((own, other)):
        tie = rest[2 + i : 3 + i]
        upright = jnp.sum(jnp.where(diagonal, tie, 0.0), axis=1, keepdims=True)
        uprights.append(upright)
        at = slice(i * local, (i + 1) * local)
        whole[at, at] = part[...] + upright + (tie - square)
    cross = cross - uprights[0] + (square - rest[3:4])
    whole[:local, local:] = cross
    whole[local:, :local] = cross.T
    return wide([rest[0:1], rest[1:2]])


def analysis_kernel(layout, pair, *rest):
    if pair:
        first, second, own, other, *rest = rest
    else:
        first, second, *rest = rest
    count = len(layout)
    uppers, lowers, centres = (rest[i * count : (i + 1) * count] for i in range(3))
    out, whole, chosen, natural = rest[3 * count :]
    rows, _ = centres[0].shape
    local = natural.shape[2]
    members = whole.shape[0]
    if pair:
        innovation = assemble_pair(first, second, own, other, whole)
    else:
        innovation = assemble(first, second, whole)
    down = lax.broadcasted_iota(jnp.int32, (members, members), 0)
    across = lax.broadcasted_iota(jnp.int32, (members, members), 1)
    identity = jnp.where(down == across, 1.0, 0.0)
    matrix = whole[...] + (members - 1.0) * identity
    parts = halves(matrix)
    square = dot3(parts, parts)
    squares = jnp.sum(jnp.sum(matrix * matrix, axis=1, keepdims=True), axis=0, keepdims=True)
    scaling = jnp.sqrt(squares)
    current = matrix * (1.0 / scaling)
    square = square * (1.0 / scaling) * (1.0 / scaling)
    inverse = None
    for repeat in range(0, ITERS, 2):
        if repeat:
            parts = halves(current)
            square = dot3(parts, parts)
        inner = 0.0625 * square - 0.5625 * current
        outer = 2.25 * identity - 2.4375 * current + 1.6875 * square
        both = outer + dot3(halves(square), halves(inner))
        both_parts = halves(both)
        if repeat + 2 < ITERS:
            twice = dot3(both_parts, both_parts)
            current = dot3(halves(current), halves(twice))
        inverse = both if inverse is None else dot3(halves(inverse), both_parts)
    once = jnp.sum(inverse * innovation, axis=1, keepdims=True)
    once_row = jnp.sum(jnp.where(down == across, once, 0.0), axis=0, keepdims=True)
    shifted = jnp.sum(inverse * once_row, axis=1, keepdims=True) * (1.0 / scaling)
    factor = jnp.sqrt((members - 1.0) / scaling)
    mixing = (factor * inverse + shifted)[:, :local]
    high, low = halves(mixing)
    chosen[:, :local] = high
    chosen[:, local:] = low
    many = grouping(rows)

    def block(b):
        for pieces, upper, lower in zip(layout, uppers, lowers):
            size = upper.shape[0] // rows
            at = pl.ds(b * many * size, many * size)
            value = dot(upper[at], chosen[...])
            value = value[:, :local] + value[:, local:] + dot(lower[at], chosen[:, :local])
            for i in range(many):
                for start, column, length in pieces:
                    natural[i, pl.ds(column, length)] = value[
                        i * size + start : i * size + start + length
                    ]
        for i in range(many):
            r = b * many + i
            middle_row = sum(c[pl.ds(r, 1)] for c in centres)
            out[pl.ds(r, local, stride=rows)] = natural[i].T + middle_row

    loop(rows // many, block)


def shift(value, axes, *moves):
    sizes = [lax.axis_size(a) for a in axes]
    pairs = []
    total = 1
    for s in sizes:
        total *= s
    for flat in range(total):
        rest, place = flat, []
        for s in reversed(sizes):
            place.append(rest % s)
            rest //= s
        place = place[::-1]
        to = 0
        for s, p, m in zip(sizes, place, moves):
            to = to * s + (p + m) % s
        pairs.append((flat, to))
    return lax.ppermute(value, axes if len(axes) > 1 else axes[0], pairs)


def trade(value, axis, first):
    size = lax.axis_size(axis)
    if size % 2:
        raise ValueError("odd ring")
    start = 1 if first else 0
    pairs = [(i % size, (i + 1) % size) for i in range(start, size, 2)]
    return lax.ppermute(value, axis, pairs + [(j, i) for i, j in pairs])


def role_sums(value):
    size = lax.axis_size("role")
    if size & (size - 1) or size == 1:
        return [(lax.psum(value, "role"), jnp.zeros_like(value))]
    stages = []
    step = 1
    while step < size:
        other = lax.ppermute(value, "role", [(i, i ^ step) for i in range(size)])
        stages.append((value, other))
        value = value + other
        step *= 2
    return stages


def shards(
    ensemble,
    diffusion,
    drift_rows,
    drift_cols,
    observed_cells,
    observed_count,
    observed_values,
    observed_weights,
):
    groups = lax.axis_size("member")
    local, rows, cols = ensemble.shape
    members = local * groups
    width = STEPS
    lanes = max(local, cols)
    cut, end = parted(cols)
    strip = struct(width * cut + 4 * width, lanes)
    following = struct(width * (end - cut), lanes)
    rest = struct(width * (cols - end) + 2 * width * width + 2 * width, lanes)
    edge = struct(rows * width + rows, lanes)
    field, kept, early, late, early_next, late_next, left, right = call(
        functools.partial(pack_kernel, "domain"),
        (
            struct(rows, cols, local),
            struct(3, rows, cols),
            strip,
            strip,
            following,
            following,
            edge,
            edge,
        ),
        ensemble.reshape(local * rows, cols),
        diffusion,
        drift_rows,
        drift_cols,
        raw=4,
    )
    early = trade(early, "domain", True)
    late = trade(late, "domain", False)
    early_next = trade(early_next, "domain", True)
    late_next = trade(late_next, "domain", False)
    received = shift(right, ("role",), 1)
    right = shift(left, ("role",), -1)
    left = received
    weight = call(
        functools.partial(weight_kernel, "role"),
        struct(cols, 2 * rows),
        observed_count,
        observed_cells,
        observed_values,
        observed_weights,
        scalars=1,
    )
    early_rest, late_rest = call(
        functools.partial(turn_kernel, "domain"), (rest, rest), field, left, right, weight
    )
    early_rest = trade(early_rest, "domain", True)
    late_rest = trade(late_rest, "domain", False)
    padded = pltpu.VMEM((rows + 2 * width, cols + 2 * LEAD, local), jnp.float32)
    scratch = (
        padded,
        padded,
        pltpu.VMEM((4, rows + 2 * width, cols + 2 * LEAD, local), jnp.float32),
        pltpu.VMEM((5, 2 * width, cols), jnp.float32),
    )
    ends = (EDGE, cut - EDGE, end - EDGE)

    def forecast(after, low, high, pieces, *strips):
        return call(
            functools.partial(middle_kernel, "domain", low, high, pieces),
            struct(rows, high - low, local),
            after,
            field,
            kept,
            *strips,
            scratch=scratch,
        )

    first = forecast(weight, *ends[:2], ((0, cut, 0, 0, cut),), early, late)
    back = 2 * EDGE
    pieces = (
        (0, cut, cut - back, cut - back, back),
        (1, end - cut, 0, cut, end - cut),
    )
    second = forecast(first, *ends[1:], pieces, early, late, early_next, late_next)
    sides = call(
        functools.partial(sides_kernel, "domain"),
        struct(rows, cols - end + 2 * EDGE, local),
        second,
        field,
        kept,
        early,
        late,
        early_next,
        late_next,
        left,
        right,
        early_rest,
        late_rest,
        scratch=scratch,
    )

    def gathered(value):
        others = [shift(value, ("member",), s) for s in range(1, groups)]
        return jnp.concatenate(others, axis=0) if len(others) > 1 else others[0]

    owns = (first, second, sides)
    theirs = []
    for value in owns:
        theirs.append(gathered(value))
    tail = cols - end + EDGE
    layout = (
        ((0, ends[0], ends[1] - ends[0]),),
        ((0, ends[1], ends[2] - ends[1]),),
        ((0, ends[2], tail), (tail, 0, EDGE)),
    )

    def deviations(value):
        one = struct(rows * value.shape[1], members, kind=jnp.bfloat16)
        return one, one, struct(rows, cols)

    made = []
    pair = groups == 2 and local % 128 == 0
    if pair:
        sided = rows * sides.shape[1]
        half = struct(local, sided, kind=jnp.bfloat16)
        alone = call(
            functools.partial(own_gram_kernel, layout), struct(local, local), *owns, weight
        )
        stages = role_sums(alone)
        started = sum(stages[0])
        left_half, right_half, spread = call(
            functools.partial(prepare_kernel, layout[-1]),
            (half, half, struct(3, sided, local)),
            sides,
            weight,
            started,
        )
        cross = struct(local + 8, local)
        total = ()
        for i in range(2):
            *three, total = call(
                functools.partial(part_cross_kernel, layout[i]),
                (*deviations(owns[i]), cross),
                owns[i],
                theirs[i],
                weight,
                started,
                *total,
            )
            made.append(three)
            total = (total,)
        alone, arriving = stages[-1]
        total, alone = lax.optimization_barrier((total[0], alone))
        alone = alone + arriving
        gram = call(
            last_cross_kernel, cross, sides, theirs[-1], left_half, right_half, spread, total
        )
        facing = shift(alone, ("member",), 1)
        grams = (*role_sums(gram)[-1], alone, facing)
        three = call(
            functools.partial(deviation_kernel, layout[-1]),
            deviations(sides),
            sides,
            theirs[-1],
            gram,
        )
        made.append(three)
    else:
        blocks = members // 128
        size = blocks * (blocks + 1) // 2 * 128 + 8
        sums = struct(members, members), struct(1, members)
        totals = ()
        for i in range(2):
            *three, total, tilt = call(
                functools.partial(part_gram_kernel, groups, layout[i]),
                (*deviations(owns[i]), *sums),
                owns[i],
                theirs[i],
                weight,
                *totals,
            )
            made.append(three)
            totals = total, tilt
        gram, *three = call(
            functools.partial(last_gram_kernel, groups, layout[-1]),
            (struct(size, 128), *deviations(sides)),
            sides,
            theirs[-1],
            weight,
            *totals,
            scratch=tuple(pltpu.VMEM(v.shape, v.dtype) for v in sums),
        )
        made.append(three)
        grams = role_sums(gram)[-1]
    return call(
        functools.partial(analysis_kernel, layout, pair),
        struct(local * rows, cols),
        *grams,
        *(three[k] for k in range(3) for three in made),
        scratch=(
            pltpu.VMEM((members, members), jnp.float32),
            pltpu.VMEM((members, 2 * local), jnp.bfloat16),
            pltpu.VMEM((grouping(rows), cols, local), jnp.float32),
        ),
        result=True,
    ).reshape(local, rows, cols)


def solution(mesh):
    placed = (
        P("member", "domain", "role"),
        P("domain", "role"),
        P("domain", "role"),
        P("domain", "role"),
        P("domain", None),
        P("domain"),
        P("domain", None),
        P("domain", None),
    )
    return jax.shard_map(
        shards, mesh=mesh, in_specs=placed, out_specs=P("member", "domain", "role"), check_vma=False
    )
```
